32 devices in a mesh: seq: 8 (over y, x, core), tp: 4 (over z).
Axes of the slice: x: 2, y: 2, z: 4, core: 2. Of those that a mesh axis runs over, the one named last changes fastest.
Arguments:
- layer_input: bfloat16 [4, 2048, 1536], P('tp', 'seq'), may hold values from -6 to 6
- doc_ids: int32 [4, 2048], P('tp', 'seq'), may hold values from 0 to 3, as said below
- positions: int32 [4, 2048], P('tp', 'seq'), may hold values from 0 to 4088, as said below
- first_gain: bfloat16 [1536], P(('seq', 'tp')), may hold values from 0.099609375 to 1.8984375
- query_weight: bfloat16 [1536, 1536], P(('seq', 'tp')), may hold values from -0.15625 to 0.15625
- key_weight: bfloat16 [1536, 768], P(('seq', 'tp')), may hold values from -0.15625 to 0.15625
- value_weight: bfloat16 [1536, 768], P(('seq', 'tp')), may hold values from -0.15625 to 0.15625
- output_weight: bfloat16 [1536, 1536], P(('seq', 'tp')), may hold values from -0.625 to 0.625
- second_gain: bfloat16 [1536], P(('seq', 'tp')), may hold values from 0.099609375 to 1.8984375
- gate_weight: bfloat16 [1536, 4096], P('seq', 'tp'), may hold values from -0.15625 to 0.15625
- up_weight: bfloat16 [1536, 4096], P('seq', 'tp'), may hold values from -0.15625 to 0.15625
- down_weight: bfloat16 [1536, 4096], P('seq', 'tp'), may hold values from -0.09375 to 0.09375
- out_grad: bfloat16 [4, 2048, 1536], P('tp', 'seq'), may hold values from -6 to 6
Outputs:
- layer_output: bfloat16 [4, 2048, 1536], P('tp', 'seq')
- input_grad: float32 [4, 2048, 1536], P('tp', 'seq')
- first_gain_grad: float32 [1536], P(('seq', 'tp'))
- query_grad: float32 [1536, 1536], P(('seq', 'tp'))
- key_grad: float32 [1536, 768], P(('seq', 'tp'))
- value_grad: float32 [1536, 768], P(('seq', 'tp'))
- output_grad: float32 [1536, 1536], P(('seq', 'tp'))
- second_gain_grad: float32 [1536], P(('seq', 'tp'))
- gate_grad: float32 [1536, 4096], P('seq', 'tp')
- up_grad: float32 [1536, 4096], P('seq', 'tp')
- down_grad: float32 [1536, 4096], P('seq', 'tp')
The draws below stay inside these ranges and needn't reach their ends.
Inputs may be any that keep to these rules, and one draw needn't show every extreme that they name: `doc_ids`: within each sequence the ids never fall, start at 0, and each of 0 to 3 holds one contiguous run of tokens. `positions`: 0 at each document's first token; within a document it rises by 1 or 2 from one token to the next.
All inputs are finite; a program needn't handle non-finite values.
Results may differ from the reference program's by a relative error of at most 0.018.
Values may be sent and summed in bfloat16 or wider, within the bound.
A program may use at most 256 MiB of HBM per device.

```python
import math
import jax
import jax.numpy as jnp
from jax import lax

D = 1536
QUERY_HEADS = 16
KEY_VALUE_HEADS = 8
HEAD_SIZE = 96
FF = 4096
DOCS = 4
HQD = 1536
KVD = 768
SEQS = 4
LENGTH = 2048


def doc_layout(key):
    base = jax.random.fold_in(key, 11)
    cut_key, step_key = jax.random.split(base)
    index = jnp.arange(LENGTH, dtype=jnp.int32)

    def one_cuts(seq_key):
        order = jax.random.permutation(seq_key, LENGTH - 1).astype(jnp.int32) + 1
        return jnp.sort(order[:DOCS - 1]).astype(jnp.int32)
    cuts_all = jax.vmap(one_cuts)(jax.random.split(cut_key, SEQS)).astype(jnp.int32)
    forced_cuts = (LENGTH - DOCS + 1 + jnp.arange(DOCS - 1, dtype=jnp.int32)).astype(jnp.int32)
    cuts_all = cuts_all.at[0].set(forced_cuts)
    identity = jnp.sum((index[None, :, None] >= cuts_all[:, None, :]).astype(jnp.int32), axis=2).astype(jnp.int32)
    increments = jax.random.randint(step_key, (SEQS, LENGTH), 1, 3).astype(jnp.int32)
    increments = increments.at[0].set(jnp.full((LENGTH,), 2, jnp.int32))
    climbed = jnp.cumsum(increments, axis=1)
    before = climbed - increments
    previous = jnp.concatenate([jnp.full((SEQS, 1), -1, jnp.int32), identity[:, :-1]], axis=1)
    starting = identity != previous
    offsets = lax.cummax(jnp.where(starting, before, 0), axis=1)
    return (identity, (before - offsets).astype(jnp.int32))


def draw_doc_ids(key, part):
    return doc_layout(key)[0]


def draw_positions(key, part):
    return doc_layout(key)[1]


def block_scale(key, shape, pieces, smallest, largest):
    def one(dim, parts):
        draws = jax.random.uniform(jax.random.fold_in(jax.random.fold_in(key, 6), dim), (parts,), jnp.float32, smallest / len(pieces), largest / len(pieces))
        return jnp.repeat(jnp.exp(draws), shape[dim] // parts).reshape((-1,) + (1,) * (len(shape) - dim - 1))

    factor_of = one(*pieces[0])
    for cut in pieces[1:]:
        factor_of = factor_of * one(*cut)
    return factor_of


def noise(own_key, dims, deviation, limit, cuts=(), held_as=jnp.bfloat16):
    result = deviation * jax.random.normal(own_key, dims, jnp.float32)
    if cuts:
        result = result * block_scale(own_key, dims, cuts, -0.22, 0.18)
    return jnp.clip(result, -limit, limit).astype(held_as)


def setup_inputs(seed: int = 0) -> dict:
    key_of = jax.random.split(jax.random.key(seed), 14)
    layer_input = noise(key_of[0], (SEQS, LENGTH, D), 1.0, 6.0, ((0, 4), (1, 8)))
    doc_ids = draw_doc_ids(jax.random.fold_in(key_of[13], 71), 0)
    positions = draw_positions(jax.random.fold_in(key_of[13], 71), 0)
    first_gain = jnp.clip(1.0 + 0.18 * jax.random.normal(key_of[3], (D,), jnp.float32), 0.099609375, 1.8984375).astype(jnp.bfloat16)
    query_weight = noise(key_of[4], (D, HQD), D ** -0.5, 0.15625, ((0, 32),))
    key_weight = noise(key_of[5], (D, KVD), D ** -0.5, 0.15625, ((0, 32),))
    value_weight = noise(key_of[6], (D, KVD), D ** -0.5, 0.15625, ((0, 32),))
    output_weight = noise(key_of[7], (HQD, D), (HQD // 16) ** -0.5, 0.625, ((0, 32),))
    second_gain = jnp.clip(1.0 + 0.18 * jax.random.normal(key_of[8], (D,), jnp.float32), 0.099609375, 1.8984375).astype(jnp.bfloat16)
    gate_weight = noise(key_of[9], (D, FF), D ** -0.5, 0.15625, ((0, 8), (1, 4)))
    up_weight = noise(key_of[10], (D, FF), D ** -0.5, 0.15625, ((0, 8), (1, 4)))
    down_weight = noise(key_of[11], (D, FF), FF ** -0.5, 0.09375, ((0, 8), (1, 4)))
    out_grad = noise(key_of[12], (SEQS, LENGTH, D), 1.0, 6.0, ((0, 4), (1, 8)))
    return {"layer_input": layer_input, "doc_ids": doc_ids, "positions": positions, "first_gain": first_gain, "query_weight": query_weight, "key_weight": key_weight, "value_weight": value_weight, "output_weight": output_weight, "second_gain": second_gain, "gate_weight": gate_weight, "up_weight": up_weight, "down_weight": down_weight, "out_grad": out_grad}


@jax.custom_vjp
def lower_precision(v):
    return lax.optimization_barrier(v.astype(jnp.bfloat16)).astype(jnp.float32)

@jax.custom_vjp
def lower_backward(v):
    return v

def low_keep(v):
    return (lower_precision(v), None)

def low_pass(kept, grad):
    return (grad,)

def back_keep(v):
    return (v, None)

def back_low(kept, grad):
    return (lower_precision(grad),)
lower_precision.defvjp(low_keep, low_pass)
lower_backward.defvjp(back_keep, back_low)
norm_epsilon = 1e-05
rope_base = 100000.0
mask_fill_value = -1e+30

def rope_tables(places):
    half = HEAD_SIZE // 2
    inverse = rope_base ** (-(jnp.arange(half, dtype=jnp.float32) * 2.0 / HEAD_SIZE))
    angles = places.astype(jnp.float32)[:, None] * inverse[None, :]
    return (jnp.cos(angles), jnp.sin(angles))

def apply_rotary(value_rows, cosine_table, sine_table, heads):
    sequence_length = value_rows.shape[0]
    split = value_rows.reshape(sequence_length, heads, 2, HEAD_SIZE // 2)
    first = split[:, :, 0]
    second = split[:, :, 1]
    cosine = cosine_table[:, None, :]
    sine = sine_table[:, None, :]
    turned = jnp.stack([first * cosine - second * sine, second * cosine + first * sine], axis=2)
    return turned.reshape(sequence_length, heads * HEAD_SIZE)

def layer_sequence(inputs, documents, places, weight_set):
    gain_one, query_w, key_projection_weight, value_w, output_w, gain_two, gate_w, up_w, down_w = weight_set
    highest_precision = lax.Precision.HIGHEST
    sequence_length = inputs.shape[0]
    query_groups = QUERY_HEADS // KEY_VALUE_HEADS
    scale_of_scores = 1.0 / math.sqrt(HEAD_SIZE)
    scale_one = lax.rsqrt(lax.optimization_barrier(jnp.mean(inputs * inputs, axis=-1, keepdims=True)) + norm_epsilon)
    first_normalized = lower_precision(inputs * scale_one * gain_one)
    cosine_table, sine_table = rope_tables(places)
    query_rows = lower_precision(apply_rotary(lower_backward(jnp.dot(first_normalized, query_w, precision=highest_precision)), cosine_table, sine_table, QUERY_HEADS))
    key_rows = lower_precision(apply_rotary(lower_backward(jnp.dot(first_normalized, key_projection_weight, precision=highest_precision)), cosine_table, sine_table, KEY_VALUE_HEADS))
    value_rows = lower_precision(lower_backward(jnp.dot(first_normalized, value_w, precision=highest_precision)))
    block_number = math.gcd(512, sequence_length)
    block_count = sequence_length // block_number
    index = jnp.arange(sequence_length, dtype=jnp.int32)
    blocks_of_query = query_rows.reshape(block_count, block_number, KEY_VALUE_HEADS, query_groups, HEAD_SIZE)
    heads_of_key = key_rows.reshape(sequence_length, KEY_VALUE_HEADS, HEAD_SIZE)
    heads_of_value = value_rows.reshape(sequence_length, KEY_VALUE_HEADS, HEAD_SIZE)

    def attend(item):
        query_block, index_block, doc_block = item
        raw = jnp.einsum('tgrd,kgd->tgrk', query_block, heads_of_key, precision=highest_precision)
        scores = lower_backward(raw * scale_of_scores)
        allowed = ((index[None, :] <= index_block[:, None]) & (documents[None, :] == doc_block[:, None]))[:, None, None, :]
        masked = jnp.where(allowed, scores, mask_fill_value)
        top = lax.optimization_barrier(jnp.max(masked, axis=3, keepdims=True))
        log_total = top + jnp.log(lax.optimization_barrier(jnp.sum(jnp.where(allowed, jnp.exp(masked - top), 0.0), axis=3, keepdims=True)))
        probs = jnp.where(allowed, jnp.exp(masked - log_total), 0.0)
        return jnp.einsum('tgrk,kgd->tgrd', lower_precision(probs), heads_of_value, precision=highest_precision)
    heads = lax.map(jax.checkpoint(attend), (blocks_of_query, index.reshape(block_count, block_number), documents.reshape(block_count, block_number)))
    attn_low = lower_precision(lower_backward(heads.reshape(sequence_length, QUERY_HEADS * HEAD_SIZE)))
    branch = lower_backward(jnp.dot(attn_low, output_w, precision=highest_precision))
    resid = inputs + branch
    scale_two = lax.rsqrt(lax.optimization_barrier(jnp.mean(resid * resid, axis=-1, keepdims=True)) + norm_epsilon)
    normed_two = lower_precision(resid * scale_two * gain_two)
    gate = lower_backward(jnp.dot(normed_two, gate_w, precision=highest_precision))
    up_part = lower_backward(jnp.dot(normed_two, up_w, precision=highest_precision))
    hidden = lower_precision(gate * jax.nn.sigmoid(gate) * up_part)
    mixed = lower_backward(jnp.dot(hidden, down_w.T, precision=highest_precision))
    return resid + mixed

def reference(layer_input, doc_ids, positions, first_gain, query_weight, key_weight, value_weight, output_weight, second_gain, gate_weight, up_weight, down_weight, out_grad):
    weight_set = tuple((w.astype(jnp.float32) for w in (first_gain, query_weight, key_weight, value_weight, output_weight, second_gain, gate_weight, up_weight, down_weight)))
    inputs_f = layer_input.astype(jnp.float32)
    cotangent = out_grad.astype(jnp.float32)
    checked = jax.checkpoint(layer_sequence)

    def forward(inputs_all, weights_all):

        def one_sequence(carry, item):
            inputs, documents, places = item
            return (carry, checked(inputs, documents, places, weights_all))
        unused_result, outputs = lax.scan(one_sequence, jnp.zeros((), jnp.float32), (inputs_all, doc_ids, positions))
        return outputs
    outputs, pullback = jax.vjp(forward, inputs_f, weight_set)
    input_grad, grads = pullback(cotangent)
    return (outputs.astype(jnp.bfloat16), input_grad, grads[0], grads[1], grads[2], grads[3], grads[4], grads[5], grads[6], grads[7], grads[8])
```

```python
import functools
import math

import jax
import jax.numpy as jnp
from jax import lax
from jax.experimental import pallas as pl
from jax.experimental.pallas import tpu as pltpu
from jax.sharding import PartitionSpec as P

QUERY_HEADS = 16
KEY_VALUE_HEADS = 8
HEAD_SIZE = 96


norm_epsilon = 1e-05
rope_base = 100000.0
mask_fill_value = -1e30


def rope_tables(places):
    half = HEAD_SIZE // 2
    inverse = rope_base ** (-(jnp.arange(half, dtype=jnp.float32) * 2.0 / HEAD_SIZE))
    angles = places.astype(jnp.float32)[:, None] * inverse[None, :]
    return (jnp.cos(angles), jnp.sin(angles))


def apply_rotary(value_rows, cosine_table, sine_table, heads, direction):
    sequence_length = value_rows.shape[0]
    split = value_rows.reshape(sequence_length, heads, 2, HEAD_SIZE // 2)
    first = split[:, :, 0]
    second = split[:, :, 1]
    cosine = cosine_table[:, None, :]
    sine = direction * sine_table[:, None, :]
    turned = jnp.stack([first * cosine - second * sine, second * cosine + first * sine], axis=2)
    return turned.reshape(sequence_length, heads * HEAD_SIZE)


def outer_product(left, right):
    return lax.dot_general(
        left, right, (((0,), (0,)), ((), ())), preferred_element_type=jnp.float32
    )


def times_transpose(left, right):
    return lax.dot_general(
        left, right, (((1,), (1,)), ((), ())), preferred_element_type=jnp.float32
    )


def norm_backward(inputs, scale, gain, upstream):
    inner = gain * upstream
    moment = jnp.mean(inputs * inner, axis=1, keepdims=True)
    return (
        scale * inner - inputs * scale * scale * scale * moment,
        jnp.sum(upstream * inputs * scale, axis=0),
    )


def on_device(
    layer_input,
    doc_ids,
    positions,
    first_gain,
    query_weight,
    key_weight,
    value_weight,
    output_weight,
    second_gain,
    gate_weight,
    up_weight,
    down_weight,
    out_grad,
):
    token_rows = layer_input.shape[1]
    query_groups = QUERY_HEADS // KEY_VALUE_HEADS
    scale_of_scores = 1.0 / math.sqrt(HEAD_SIZE)
    inputs_f = layer_input[0].astype(jnp.float32)
    my_docs = doc_ids[0]
    gain_one, query_full, complete_keys, value_full, output_full, gain_two = (
        lax.all_gather(first_gain, ("seq", "tp"), axis=0, tiled=True),
        lax.all_gather(query_weight, ("seq", "tp"), axis=0, tiled=True),
        lax.all_gather(key_weight, ("seq", "tp"), axis=0, tiled=True),
        lax.all_gather(value_weight, ("seq", "tp"), axis=0, tiled=True),
        lax.all_gather(output_weight, ("seq", "tp"), axis=0, tiled=True),
        lax.all_gather(second_gain, ("seq", "tp"), axis=0, tiled=True),
    )
    gain_one_f = gain_one.astype(jnp.float32)
    gain_two_f = gain_two.astype(jnp.float32)
    scale_one = lax.rsqrt(jnp.mean(inputs_f * inputs_f, axis=1, keepdims=True) + norm_epsilon)
    first_normalized = (inputs_f * scale_one * gain_one_f).astype(jnp.bfloat16)
    cosine_table, sine_table = rope_tables(positions[0])
    rotated_query = apply_rotary(
        jnp.dot(first_normalized, query_full, preferred_element_type=jnp.float32),
        cosine_table,
        sine_table,
        QUERY_HEADS,
        1.0,
    ).astype(jnp.bfloat16)
    key_rot = apply_rotary(
        jnp.dot(first_normalized, complete_keys, preferred_element_type=jnp.float32),
        cosine_table,
        sine_table,
        KEY_VALUE_HEADS,
        1.0,
    ).astype(jnp.bfloat16)
    value_low = jnp.dot(first_normalized, value_full, preferred_element_type=jnp.float32).astype(
        jnp.bfloat16
    )
    gathered_keys, gathered_values, doc_all = (
        lax.all_gather(key_rot, "seq", axis=0, tiled=True),
        lax.all_gather(value_low, "seq", axis=0, tiled=True),
        lax.all_gather(my_docs.astype(jnp.bfloat16), "seq", axis=0, tiled=True),
    )
    sequence_length = gathered_keys.shape[0]
    block_number = math.gcd(512, sequence_length)
    block_count = sequence_length // block_number
    query_index = lax.axis_index("seq") * token_rows + jnp.arange(token_rows, dtype=jnp.int32)
    my_doc_f = my_docs.astype(jnp.float32)
    heads_of_query = rotated_query.reshape(token_rows, KEY_VALUE_HEADS, query_groups, HEAD_SIZE)
    layer_entries = (
        gathered_keys.reshape(block_count, block_number, KEY_VALUE_HEADS, HEAD_SIZE),
        gathered_values.reshape(block_count, block_number, KEY_VALUE_HEADS, HEAD_SIZE),
        doc_all.astype(jnp.float32).reshape(block_count, block_number),
        jnp.arange(block_count, dtype=jnp.int32) * block_number,
    )

    def allowed_of(doc_piece, start):
        key_index = start + jnp.arange(block_number, dtype=jnp.int32)
        return (key_index[None, :] <= query_index[:, None]) & (
            doc_piece[None, :] == my_doc_f[:, None]
        )

    def scores_of(key_piece, allowed):
        raw = (
            jnp.einsum(
                "tgrd,kgd->tgrk", heads_of_query, key_piece, preferred_element_type=jnp.float32
            )
            * scale_of_scores
        )
        return jnp.where(allowed[:, None, None, :], raw, mask_fill_value)

    def total_step(carry, item):
        key_piece, value_piece, doc_piece, start = item
        allowed = allowed_of(doc_piece, start)

        def total_work(state):
            top, total = state
            scores = scores_of(key_piece, allowed)
            new_top = jnp.maximum(top, jnp.max(scores, axis=3))
            weights = jnp.where(
                allowed[:, None, None, :], jnp.exp(scores - new_top[..., None]), 0.0
            )
            return (new_top, total * jnp.exp(top - new_top) + jnp.sum(weights, axis=3))

        return (lax.cond(jnp.any(allowed), total_work, lambda state: state, carry), None)

    start_state = (
        jnp.full((token_rows, KEY_VALUE_HEADS, query_groups), mask_fill_value, jnp.float32),
        jnp.zeros((token_rows, KEY_VALUE_HEADS, query_groups), jnp.float32),
    )
    (top, total), unused_result = lax.scan(total_step, start_state, layer_entries)
    log_total = top + jnp.log(total)

    def probs_of(key_piece, allowed):
        scores = scores_of(key_piece, allowed)
        return jnp.where(allowed[:, None, None, :], jnp.exp(scores - log_total[..., None]), 0.0)

    def output_update(accum, item):
        key_piece, value_piece, doc_piece, start = item
        allowed = allowed_of(doc_piece, start)

        def output_work(state):
            probs = probs_of(key_piece, allowed).astype(jnp.bfloat16)
            return state + jnp.einsum(
                "tgrk,kgd->tgrd", probs, value_piece, preferred_element_type=jnp.float32
            )

        return (lax.cond(jnp.any(allowed), output_work, lambda state: state, accum), None)

    heads_output, unused_result = lax.scan(
        output_update,
        jnp.zeros((token_rows, KEY_VALUE_HEADS, query_groups, HEAD_SIZE), jnp.float32),
        layer_entries,
    )
    attn_low = heads_output.reshape(token_rows, QUERY_HEADS * HEAD_SIZE).astype(jnp.bfloat16)
    resid = inputs_f + jnp.dot(attn_low, output_full, preferred_element_type=jnp.float32)
    scale_two = lax.rsqrt(jnp.mean(resid * resid, axis=1, keepdims=True) + norm_epsilon)
    normed_two = (resid * scale_two * gain_two_f).astype(jnp.bfloat16)
    rows_all = lax.all_gather(normed_two, "tp", axis=0, tiled=True)
    gate_cols, up_cols, down_cols = (
        lax.all_gather(gate_weight, "seq", axis=0, tiled=True),
        lax.all_gather(up_weight, "seq", axis=0, tiled=True),
        lax.all_gather(down_weight, "seq", axis=0, tiled=True),
    )
    gate_pre = jnp.dot(rows_all, gate_cols, preferred_element_type=jnp.float32)
    up_pre = jnp.dot(rows_all, up_cols, preferred_element_type=jnp.float32)
    gate_sig = jax.nn.sigmoid(gate_pre)
    gate_act = gate_pre * gate_sig
    hidden = (gate_act * up_pre).astype(jnp.bfloat16)
    mixed = lax.psum_scatter(
        times_transpose(hidden, down_cols).astype(jnp.bfloat16),
        "tp",
        scatter_dimension=0,
        tiled=True,
    ).astype(jnp.float32)
    layer_output = (resid + mixed).astype(jnp.bfloat16)[None]
    grad_low = out_grad[0]
    grad_f = grad_low.astype(jnp.float32)
    grad_all = lax.all_gather(grad_low, "tp", axis=0, tiled=True)
    dhidden = jnp.dot(grad_all, down_cols, preferred_element_type=jnp.float32)
    dgate = (dhidden * up_pre * gate_sig * (1.0 + gate_pre * (1.0 - gate_sig))).astype(jnp.bfloat16)
    dup = (dhidden * gate_act).astype(jnp.bfloat16)
    gate_term = outer_product(rows_all, dgate)
    up_term = outer_product(rows_all, dup)
    down_term_grad = outer_product(grad_all, hidden)
    dnorm_two = lax.psum_scatter(
        (times_transpose(dgate, gate_cols) + times_transpose(dup, up_cols)).astype(jnp.bfloat16),
        "tp",
        scatter_dimension=0,
        tiled=True,
    ).astype(jnp.float32)
    gate_grad, up_grad, down_grad = (
        lax.psum_scatter(
            gate_term.astype(jnp.bfloat16), "seq", scatter_dimension=0, tiled=True
        ).astype(jnp.float32),
        lax.psum_scatter(
            up_term.astype(jnp.bfloat16), "seq", scatter_dimension=0, tiled=True
        ).astype(jnp.float32),
        lax.psum_scatter(
            down_term_grad.astype(jnp.bfloat16), "seq", scatter_dimension=0, tiled=True
        ).astype(jnp.float32),
    )
    resid_part, gain_two_term = norm_backward(resid, scale_two, gain_two_f, dnorm_two)
    dresid = grad_f + resid_part
    dbranch = dresid.astype(jnp.bfloat16)
    output_term = outer_product(attn_low, dbranch)
    heads_gradient = times_transpose(dbranch, output_full).astype(jnp.bfloat16)
    grouped_heads_gradient = heads_gradient.reshape(
        token_rows, KEY_VALUE_HEADS, query_groups, HEAD_SIZE
    )
    delta = jnp.sum(grouped_heads_gradient.astype(jnp.float32) * heads_output, axis=3)

    def gradient_update(dquery, item):
        key_piece, value_piece, doc_piece, start = item
        allowed = allowed_of(doc_piece, start)

        def gradient_work(state):
            probs = probs_of(key_piece, allowed)
            value_piece_grad = jnp.einsum(
                "tgrk,tgrd->kgd",
                probs.astype(jnp.bfloat16),
                grouped_heads_gradient,
                preferred_element_type=jnp.float32,
            )
            prob_grad = jnp.einsum(
                "tgrd,kgd->tgrk",
                grouped_heads_gradient,
                value_piece,
                preferred_element_type=jnp.float32,
            )
            score_grad = (probs * (prob_grad - delta[..., None])).astype(jnp.bfloat16)
            key_piece_grad = jnp.einsum(
                "tgrk,tgrd->kgd", score_grad, heads_of_query, preferred_element_type=jnp.float32
            )
            updated = state + jnp.einsum(
                "tgrk,kgd->tgrd", score_grad, key_piece, preferred_element_type=jnp.float32
            )
            return (updated, (key_piece_grad, value_piece_grad))

        def skip(state):
            blank_tensor = jnp.zeros((block_number, KEY_VALUE_HEADS, HEAD_SIZE), jnp.float32)
            return (state, (blank_tensor, blank_tensor))

        return lax.cond(jnp.any(allowed), gradient_work, skip, dquery)

    dquery, (key_contributions, value_contributions) = lax.scan(
        gradient_update,
        jnp.zeros((token_rows, KEY_VALUE_HEADS, query_groups, HEAD_SIZE), jnp.float32),
        layer_entries,
    )
    gathered_key_contributions = (
        key_contributions.reshape(sequence_length, KEY_VALUE_HEADS * HEAD_SIZE) * scale_of_scores
    )
    gathered_value_contributions = value_contributions.reshape(
        sequence_length, KEY_VALUE_HEADS * HEAD_SIZE
    )
    local_keys, value_mine = (
        lax.psum_scatter(
            gathered_key_contributions.astype(jnp.bfloat16), "seq", scatter_dimension=0, tiled=True
        ).astype(jnp.float32),
        lax.psum_scatter(
            gathered_value_contributions.astype(jnp.bfloat16),
            "seq",
            scatter_dimension=0,
            tiled=True,
        ).astype(jnp.float32),
    )
    dq_pre = apply_rotary(
        dquery.reshape(token_rows, QUERY_HEADS * HEAD_SIZE) * scale_of_scores,
        cosine_table,
        sine_table,
        QUERY_HEADS,
        -1.0,
    ).astype(jnp.bfloat16)
    key_gradient_unrotated = apply_rotary(
        local_keys, cosine_table, sine_table, KEY_VALUE_HEADS, -1.0
    ).astype(jnp.bfloat16)
    dv_pre = value_mine.astype(jnp.bfloat16)
    dnorm_one = (
        times_transpose(dq_pre, query_full)
        + times_transpose(key_gradient_unrotated, complete_keys)
        + times_transpose(dv_pre, value_full)
    )
    input_part, gain_one_term = norm_backward(inputs_f, scale_one, gain_one_f, dnorm_one)
    input_grad = (dresid + input_part)[None]
    query_term = outer_product(first_normalized, dq_pre)
    key_term = outer_product(first_normalized, key_gradient_unrotated)
    value_term = outer_product(first_normalized, dv_pre)
    first_gain_grad, query_grad, key_grad, value_grad, output_grad, second_gain_grad = (
        lax.psum_scatter(gain_one_term, ("seq", "tp"), scatter_dimension=0, tiled=True),
        lax.psum_scatter(query_term, ("seq", "tp"), scatter_dimension=0, tiled=True),
        lax.psum_scatter(key_term, ("seq", "tp"), scatter_dimension=0, tiled=True),
        lax.psum_scatter(value_term, ("seq", "tp"), scatter_dimension=0, tiled=True),
        lax.psum_scatter(output_term, ("seq", "tp"), scatter_dimension=0, tiled=True),
        lax.psum_scatter(gain_two_term, ("seq", "tp"), scatter_dimension=0, tiled=True),
    )
    return (
        layer_output,
        input_grad,
        first_gain_grad,
        query_grad,
        key_grad,
        value_grad,
        output_grad,
        second_gain_grad,
        gate_grad,
        up_grad,
        down_grad,
    )


MESH = pl.DeviceIdType.MESH
ANY = pl.ANY
HALF = HEAD_SIZE // 2
LANES = 128
SLOT = LANES // 2
f32 = jnp.float32
bf16 = jnp.bfloat16


class Plane:
    def __init__(self, n, m):
        self.n, self.m, self.chips = n, m, n // 2
        self.s = lax.axis_index("seq")
        self.t = lax.axis_index("tp")
        self.q = self.s // 2
        self.c = lax.rem(self.s, 2)

    def device(self, s):
        return (s, self.t)

    def sibling(self):
        return (2 * self.q + 1 - self.c, self.t)

    def ahead(self, k):
        return lax.rem(self.q + k, self.chips)

    def behind(self, k):
        return lax.rem(self.q + self.chips - k, self.chips)

    def seq_ahead(self, k):
        return lax.rem(self.s + k, self.n)

    def seq_behind(self, k):
        return lax.rem(self.s + self.n - k, self.n)

    def tp_ahead(self, k):
        return (self.s, lax.rem(self.t + k, self.m))

    def tp_behind(self, k):
        return lax.rem(self.t + self.m - k, self.m)


def enter_plane(plane, with_tp):
    barrier = pltpu.get_barrier_semaphore()
    for k in range(1, plane.n):
        pl.semaphore_signal(
            barrier, inc=1, device_id=plane.device(plane.seq_ahead(k)), device_id_type=MESH
        )
    count = plane.n - 1
    if with_tp:
        for k in range(1, plane.m):
            pl.semaphore_signal(barrier, inc=1, device_id=plane.tp_ahead(k), device_id_type=MESH)
        count += plane.m - 1
    pl.semaphore_wait(barrier, count)


def remote(src, dst, send, recv, device):
    return pltpu.make_async_remote_copy(
        src_ref=src,
        dst_ref=dst,
        send_sem=send,
        recv_sem=recv,
        device_id=device,
        device_id_type=MESH,
    )


class Gather:
    def __init__(self, plane, src, dst, send, recv, local):
        chips = plane.chips
        self.own = pltpu.make_async_copy(src, dst.at[plane.s], local)
        self.out = [remote(src, dst.at[plane.s], send.at[0], recv.at[0], plane.sibling())]
        self.forward = []
        for k in range(1, chips):
            peer = 2 * plane.ahead(k) + plane.c
            self.out.append(
                remote(src, dst.at[plane.s], send.at[k], recv.at[k], plane.device(peer))
            )
            came = 2 * plane.behind(k) + plane.c
            self.forward.append(
                remote(
                    dst.at[came],
                    dst.at[came],
                    send.at[chips - 1 + k],
                    recv.at[chips - 1 + k],
                    plane.sibling(),
                )
            )

    def start(self):
        for copy in self.out[1:]:
            copy.start()
        self.out[0].start()
        self.own.start()

    def relay(self):
        for copy, onward in zip(self.out[1:], self.forward):
            copy.wait_recv()
            onward.start()

    def finish(self):
        self.own.wait()
        self.out[0].wait()
        for copy in self.out[1:]:
            copy.wait_send()
        for onward in self.forward:
            onward.wait()


def exchange(plane, src_of, dst_of, send, recv, local):
    own = pltpu.make_async_copy(src_of(plane.s), dst_of(plane.s), local)
    copies = []
    for k in range(1, plane.n):
        peer = plane.seq_ahead(k)
        copies.append(
            remote(
                src_of(peer), dst_of(plane.s), send.at[k - 1], recv.at[k - 1], plane.device(peer)
            )
        )
    return [own] + copies


def entry_body(
    n, m, x, places, wqkv, wg, wu, wd, x_all, places_all, wqkv_all, ffn, sems_x, rem, loc
):
    plane = Plane(n, m)
    enter_plane(plane, True)
    width = wg.shape[1] // n
    rows = wg.shape[0]
    step = n - 1
    mine = wqkv_all.at[plane.t]
    a = exchange(
        plane,
        lambda i: wqkv.at[i],
        lambda i: mine.at[i],
        rem.at[0, 0],
        rem.at[0, 1],
        loc.at[0],
    )
    b = exchange(
        plane,
        lambda i: places,
        lambda i: places_all.at[i],
        rem.at[1, 0],
        rem.at[1, 1],
        loc.at[1],
    )
    gather = Gather(plane, x, x_all, sems_x.at[0], sems_x.at[1], loc.at[2])
    for copy in a + b:
        copy.start()
    gather.start()
    f = []
    for j, w in enumerate((wg, wu, wd)):
        f += exchange(
            plane,
            lambda i, w=w: w.at[:, pl.ds(pl.multiple_of(i * width, width), width)],
            lambda i, j=j: ffn.at[j, pl.ds(pl.multiple_of(i * rows, rows), rows), :],
            rem.at[2 + j, 0],
            rem.at[2 + j, 1],
            loc.at[3 + j],
        )
    for copy in f:
        copy.start()
    for copy in a:
        copy.wait()
    z = []
    for k in range(1, m):
        z.append(
            remote(mine, mine, rem.at[5, 0].at[k - 1], rem.at[5, 1].at[k - 1], plane.tp_ahead(k))
        )
    for copy in z:
        copy.start()
    gather.relay()
    for copy in b + f + z:
        copy.wait()
    gather.finish()


def entry(n, m, x, places, wqkv, wg, wu, wd):
    rows, width = wg.shape
    return pl.pallas_call(
        functools.partial(entry_body, n, m),
        out_shape=(
            jax.ShapeDtypeStruct((n,) + x.shape, x.dtype),
            jax.ShapeDtypeStruct((n,) + places.shape, places.dtype),
            jax.ShapeDtypeStruct((m,) + wqkv.shape, wqkv.dtype),
            jax.ShapeDtypeStruct((3, rows * n, width // n), wg.dtype),
        ),
        in_specs=[pl.BlockSpec(memory_space=ANY)] * 6,
        out_specs=[pl.BlockSpec(memory_space=ANY)] * 4,
        scratch_shapes=[
            pltpu.SemaphoreType.DMA((2, n)),
            pltpu.SemaphoreType.DMA((6, 2, n - 1)),
            pltpu.SemaphoreType.DMA((6,)),
        ],
        compiler_params=pltpu.CompilerParams(collective_id=0, has_side_effects=True),
        cost_estimate=pl.CostEstimate(flops=0, transcendentals=0, bytes_accessed=150_000_000),
        name="entry",
    )(x, places, wqkv, wg, wu, wd)


def gather_body(n, m, src, dst, sems, loc):
    plane = Plane(n, m)
    enter_plane(plane, False)
    gather = Gather(plane, src, dst, sems.at[0], sems.at[1], loc.at[0])
    gather.start()
    gather.relay()
    gather.finish()


def plane_gather(n, m, block, ident):
    return pl.pallas_call(
        functools.partial(gather_body, n, m),
        out_shape=jax.ShapeDtypeStruct((n,) + block.shape, block.dtype),
        in_specs=[pl.BlockSpec(memory_space=ANY)],
        out_specs=pl.BlockSpec(memory_space=ANY),
        scratch_shapes=[pltpu.SemaphoreType.DMA((2, n)), pltpu.SemaphoreType.DMA((1,))],
        compiler_params=pltpu.CompilerParams(collective_id=ident, has_side_effects=True),
        cost_estimate=pl.CostEstimate(flops=0, transcendentals=0, bytes_accessed=120_000_000),
        name="plane_gather",
    )(block)


def swap_body(n, m, src, dst, sems, loc):
    plane = Plane(n, m)
    enter_plane(plane, False)
    copies = exchange(
        plane, lambda i: src.at[i], lambda i: dst.at[i], sems.at[0], sems.at[1], loc.at[0]
    )
    for copy in copies:
        copy.start()
    for copy in copies:
        copy.wait()


def plane_swap(n, m, blocks, ident):
    return pl.pallas_call(
        functools.partial(swap_body, n, m),
        out_shape=jax.ShapeDtypeStruct(blocks.shape, blocks.dtype),
        in_specs=[pl.BlockSpec(memory_space=ANY)],
        out_specs=pl.BlockSpec(memory_space=ANY),
        scratch_shapes=[pltpu.SemaphoreType.DMA((2, n - 1)), pltpu.SemaphoreType.DMA((1,))],
        compiler_params=pltpu.CompilerParams(collective_id=ident, has_side_effects=True),
        cost_estimate=pl.CostEstimate(flops=0, transcendentals=0, bytes_accessed=40_000_000),
        name="plane_swap",
    )(blocks)


def final_body(n, m, ffn, qkv, ffn_out, qkv_out, sems, loc):
    plane = Plane(n, m)
    enter_plane(plane, False)
    rows = ffn_out.shape[1]
    width = ffn.shape[2]
    a = exchange(
        plane,
        lambda i: ffn.at[:, pl.ds(pl.multiple_of(i * rows, rows), rows), :],
        lambda i: ffn_out.at[:, :, pl.ds(pl.multiple_of(i * width, width), width)],
        sems.at[0],
        sems.at[1],
        loc.at[0],
    )
    b = exchange(
        plane, lambda i: qkv.at[i], lambda i: qkv_out.at[i], sems.at[2], sems.at[3], loc.at[1]
    )
    for copy in a + b:
        copy.start()
    for copy in a + b:
        copy.wait()


def final_swap(n, m, ffn, qkv, ident):
    return pl.pallas_call(
        functools.partial(final_body, n, m),
        out_shape=(
            jax.ShapeDtypeStruct((3, ffn.shape[1] // n, ffn.shape[2] * n), ffn.dtype),
            jax.ShapeDtypeStruct(qkv.shape, qkv.dtype),
        ),
        in_specs=[pl.BlockSpec(memory_space=ANY)] * 2,
        out_specs=[pl.BlockSpec(memory_space=ANY)] * 2,
        scratch_shapes=[pltpu.SemaphoreType.DMA((4, n - 1)), pltpu.SemaphoreType.DMA((2,))],
        compiler_params=pltpu.CompilerParams(collective_id=ident, has_side_effects=True),
        cost_estimate=pl.CostEstimate(flops=0, transcendentals=0, bytes_accessed=40_000_000),
        name="final_swap",
    )(ffn, qkv)


def reduce_body(n, m, parts, total, pair, near, far, sems, loc):
    plane = Plane(n, m)
    enter_plane(plane, False)
    chips = plane.chips
    rows = parts.shape[1]
    order = list(range(1, chips)) + [0]
    loads, swaps, sends = {}, {}, {}
    for k in order:
        chip = plane.ahead(k)
        swaps[k] = remote(
            parts.at[2 * chip + 1 - plane.c],
            near.at[k],
            sems.at[0, k],
            sems.at[1, k],
            plane.sibling(),
        )
        loads[k] = pltpu.make_async_copy(parts.at[2 * chip + plane.c], pair.at[k], loc.at[k])
        swaps[k].start()
        loads[k].start()
        if k:
            sends[k] = remote(
                pair.at[k],
                far.at[k - 1],
                sems.at[2, k],
                sems.at[3, k],
                plane.device(2 * chip + plane.c),
            )
    tile = 16

    def spans(body):
        def one(i, carry):
            body(pl.ds(pl.multiple_of(i * tile, tile), tile))
            return carry

        lax.fori_loop(0, rows // tile, one, 0)

    for k in order:
        swaps[k].wait()
        loads[k].wait()
        if k:

            def add(at, k=k):
                both = pair[k, at, :].astype(f32) + near[k, at, :].astype(f32)
                pair[k, at, :] = both.astype(bf16)

            spans(add)
            sends[k].start()
        else:

            def first(at):
                total[at, :] = pair[0, at, :].astype(f32) + near[0, at, :].astype(f32)

            spans(first)
    for k in range(1, chips):
        sends[k].wait()

    def last(at):
        value = total[at, :]
        for k in range(1, chips):
            value = value + far[k - 1, at, :].astype(f32)
        total[at, :] = value

    spans(last)


def plane_reduce(n, m, parts, ident):
    rows, width = parts.shape[1:]
    chips = n // 2
    return pl.pallas_call(
        functools.partial(reduce_body, n, m),
        out_shape=jax.ShapeDtypeStruct((rows, width), f32),
        in_specs=[pl.BlockSpec(memory_space=ANY)],
        out_specs=pl.BlockSpec(memory_space=pltpu.VMEM),
        scratch_shapes=[
            pltpu.VMEM((chips, rows, width), bf16),
            pltpu.VMEM((chips, rows, width), bf16),
            pltpu.VMEM((chips - 1, rows, width), bf16),
            pltpu.SemaphoreType.DMA((4, chips)),
            pltpu.SemaphoreType.DMA((chips,)),
        ],
        compiler_params=pltpu.CompilerParams(
            collective_id=ident, has_side_effects=True, vmem_limit_bytes=32 << 20
        ),
        cost_estimate=pl.CostEstimate(flops=0, transcendentals=0, bytes_accessed=120_000_000),
        name="plane_reduce",
    )(parts)


def project_body(heads, x, gain, w, cosine, sine, norm, q, k, v):
    value = x[...].astype(f32)
    scale = lax.rsqrt(jnp.mean(value * value, axis=1, keepdims=True) + norm_epsilon)
    low = (value * scale * gain[...]).astype(bf16)
    norm[...] = low
    out = jnp.dot(low, w[...], preferred_element_type=f32)
    cos, sin = cosine[...], sine[...]
    for h in range(heads + 1):
        part = out[:, h * LANES : (h + 1) * LANES]
        turned = (part * cos + pltpu.roll(part, SLOT, 1) * sin).astype(bf16)
        if h < heads:
            q[h] = turned
        else:
            k[...] = turned
    v[...] = out[:, (heads + 1) * LANES :].astype(bf16)


def project(heads, x_all, gain, w, cosine, sine):
    length, width = x_all.shape
    tile = 256
    wide = w.shape[1]
    return pl.pallas_call(
        functools.partial(project_body, heads),
        grid=(length // tile,),
        out_shape=(
            jax.ShapeDtypeStruct((length, width), bf16),
            jax.ShapeDtypeStruct((heads, length, LANES), bf16),
            jax.ShapeDtypeStruct((length, LANES), bf16),
            jax.ShapeDtypeStruct((length, LANES), bf16),
        ),
        in_specs=[
            pl.BlockSpec((tile, width), lambda i: (i, 0)),
            pl.BlockSpec((1, width), lambda i: (0, 0)),
            pl.BlockSpec((width, wide), lambda i: (0, 0)),
            pl.BlockSpec((tile, LANES), lambda i: (i, 0)),
            pl.BlockSpec((tile, LANES), lambda i: (i, 0)),
        ],
        out_specs=[
            pl.BlockSpec((tile, width), lambda i: (i, 0)),
            pl.BlockSpec((heads, tile, LANES), lambda i: (0, i, 0)),
            pl.BlockSpec((tile, LANES), lambda i: (i, 0)),
            pl.BlockSpec((tile, LANES), lambda i: (i, 0)),
        ],
        cost_estimate=pl.CostEstimate(
            flops=2 * length * width * wide, transcendentals=0, bytes_accessed=18_000_000
        ),
        name="project",
    )(x_all, gain, w, cosine, sine)


BLOCK = 512
NT = (((1,), (1,)), ((), ()))
LOG2E = 1.4426950408889634


def allowed_block(first_key, first_query, begin, causal):
    keys = first_key + lax.broadcasted_iota(jnp.int32, (BLOCK, BLOCK), 0)
    ok = keys >= begin
    if causal:
        queries = first_query + lax.broadcasted_iota(jnp.int32, (BLOCK, BLOCK), 1)
        ok = ok & (keys <= queries)
    return ok


def attend_body(factor, q, k, v, begin, o, low, lse, vt, top, total, acc):
    i = pl.program_id(1)

    @pl.when((i == 0) & (pl.program_id(0) == 0))
    def _():
        vt[...] = v[...].astype(f32).T.astype(bf16)

    top[...] = jnp.full_like(top, mask_fill_value)
    total[...] = jnp.zeros_like(total)
    acc[...] = jnp.zeros_like(acc)
    query = q[0]
    start = begin[...]

    def step(j, causal):
        at = pl.ds(pl.multiple_of(j * BLOCK, BLOCK), BLOCK)
        raw = lax.dot_general(k[at, :], query, NT, preferred_element_type=f32)
        ok = allowed_block(j * BLOCK, i * BLOCK, start, causal)
        scores = jnp.where(ok, raw * factor, mask_fill_value)
        new_top = jnp.maximum(top[...], jnp.max(scores, axis=0, keepdims=True))
        weights = jnp.exp2(scores - new_top)
        keep = jnp.exp2(top[...] - new_top)
        total[...] = total[...] * keep + jnp.sum(weights, axis=0, keepdims=True)
        acc[...] = acc[...] * keep + jnp.dot(
            vt[:, at], weights.astype(bf16), preferred_element_type=f32
        )
        top[...] = new_top

    def loop(j, carry):
        step(j, False)
        return carry

    lax.fori_loop(0, i, loop, 0)
    step(i, True)
    out = (acc[...] / total[...]).T
    o[0] = out
    low[...] = out.astype(bf16)
    lse[0] = top[...] + jnp.log2(total[...])


def attend(factor, q, k, v, begin):
    heads, length, _ = q.shape
    blocks = length // BLOCK
    pairs = heads * BLOCK * BLOCK * blocks * (blocks + 1) // 2
    return pl.pallas_call(
        functools.partial(attend_body, factor),
        grid=(heads, blocks),
        out_shape=(
            jax.ShapeDtypeStruct((heads, length, LANES), f32),
            jax.ShapeDtypeStruct((length, heads * LANES), bf16),
            jax.ShapeDtypeStruct((heads, 1, length), f32),
        ),
        in_specs=[
            pl.BlockSpec((1, BLOCK, LANES), lambda h, i: (h, i, 0)),
            pl.BlockSpec((length, LANES), lambda h, i: (0, 0)),
            pl.BlockSpec((length, LANES), lambda h, i: (0, 0)),
            pl.BlockSpec((1, BLOCK), lambda h, i: (0, i)),
        ],
        out_specs=[
            pl.BlockSpec((1, BLOCK, LANES), lambda h, i: (h, i, 0)),
            pl.BlockSpec((BLOCK, LANES), lambda h, i: (i, h)),
            pl.BlockSpec((1, 1, BLOCK), lambda h, i: (h, 0, i)),
        ],
        scratch_shapes=[
            pltpu.VMEM((LANES, length), bf16),
            pltpu.VMEM((1, BLOCK), f32),
            pltpu.VMEM((1, BLOCK), f32),
            pltpu.VMEM((LANES, BLOCK), f32),
        ],
        cost_estimate=pl.CostEstimate(
            flops=pairs * 4 * LANES * 3, transcendentals=pairs, bytes_accessed=6_000_000
        ),
        name="attend",
    )(q, k, v, begin)


def attend_back_body(
    factor, scale, heads, q, k, v, go, o, lse, begin, cosine, sine, out, kt, dqt, dk, dv, delta
):
    h = pl.program_id(0)
    j = pl.program_id(1)
    blocks = pl.num_programs(1)

    @pl.when((h == 0) & (j == 0))
    def _():
        kt[...] = k[...].astype(f32).T.astype(bf16)
        dk[...] = jnp.zeros_like(dk)
        dv[...] = jnp.zeros_like(dv)

    @pl.when(j == 0)
    def _():
        dqt[...] = jnp.zeros_like(dqt)

        def deltas(i, carry):
            at = pl.ds(pl.multiple_of(i * BLOCK, BLOCK), BLOCK)
            both = (go[at, :].astype(f32) * o[0, at, :]).T
            delta[:, at] = jnp.sum(both, axis=0, keepdims=True)
            return carry

        lax.fori_loop(0, blocks, deltas, 0)

    keys_at = pl.ds(pl.multiple_of(j * BLOCK, BLOCK), BLOCK)
    key = k[keys_at, :]
    value = v[keys_at, :]

    def step(i, causal):
        at = pl.ds(pl.multiple_of(i * BLOCK, BLOCK), BLOCK)
        query = q[0, at, :]
        raw = lax.dot_general(key, query, NT, preferred_element_type=f32)
        ok = allowed_block(j * BLOCK, i * BLOCK, begin[:, at], causal)
        probs = jnp.where(ok, jnp.exp2(raw * factor - lse[0, :, at]), 0.0)
        grads = go[at, :]
        dprob = lax.dot_general(value, grads, NT, preferred_element_type=f32)
        dscore = (probs * (dprob - delta[:, at])).astype(bf16)
        dv[keys_at, :] += jnp.dot(probs.astype(bf16), grads, preferred_element_type=f32)
        dk[keys_at, :] += jnp.dot(dscore, query, preferred_element_type=f32)
        dqt[:, at] += jnp.dot(kt[:, keys_at], dscore, preferred_element_type=f32)

    step(j, True)

    def loop(i, carry):
        step(i, False)
        return carry

    lax.fori_loop(j + 1, blocks, loop, 0)

    def unturn(value, at):
        return value * cosine[at, :] - pltpu.roll(value, SLOT, 1) * sine[at, :]

    @pl.when(j == blocks - 1)
    def _():
        def write(i, carry):
            at = pl.ds(pl.multiple_of(i * BLOCK, BLOCK), BLOCK)
            got = unturn(dqt[:, at].T * scale, at).astype(bf16)
            for which in range(heads):

                @pl.when(h == which)
                def _(which=which):
                    out[at, which * LANES : (which + 1) * LANES] = got

            return carry

        lax.fori_loop(0, blocks, write, 0)

    @pl.when((h == heads - 1) & (j == blocks - 1))
    def _():
        def write(i, carry):
            at = pl.ds(pl.multiple_of(i * BLOCK, BLOCK), BLOCK)
            out[at, heads * LANES : (heads + 1) * LANES] = unturn(dk[at, :] * scale, at).astype(
                bf16
            )
            out[at, (heads + 1) * LANES :] = dv[at, :].astype(bf16)
            return carry

        lax.fori_loop(0, blocks, write, 0)


def attend_back(factor, scale, q, k, v, go, o, lse, begin, cosine, sine):
    heads, length, _ = q.shape
    blocks = length // BLOCK
    pairs = heads * BLOCK * BLOCK * blocks * (blocks + 1) // 2
    whole = pl.BlockSpec((length, LANES), lambda h, j: (0, 0))
    one = pl.BlockSpec((1, length, LANES), lambda h, j: (h, 0, 0))
    return pl.pallas_call(
        functools.partial(attend_back_body, factor, scale, heads),
        grid=(heads, blocks),
        out_shape=jax.ShapeDtypeStruct((length, (heads + 2) * LANES), bf16),
        in_specs=[
            one,
            whole,
            whole,
            pl.BlockSpec((length, LANES), lambda h, j: (0, h)),
            one,
            pl.BlockSpec((1, 1, length), lambda h, j: (h, 0, 0)),
            pl.BlockSpec((1, length), lambda h, j: (0, 0)),
            whole,
            whole,
        ],
        out_specs=pl.BlockSpec((length, (heads + 2) * LANES), lambda h, j: (0, 0)),
        scratch_shapes=[
            pltpu.VMEM((LANES, length), bf16),
            pltpu.VMEM((LANES, length), f32),
            pltpu.VMEM((length, LANES), f32),
            pltpu.VMEM((length, LANES), f32),
            pltpu.VMEM((1, length), f32),
        ],
        cost_estimate=pl.CostEstimate(
            flops=pairs * 10 * LANES * 2, transcendentals=pairs, bytes_accessed=12_000_000
        ),
        name="attend_back",
    )(q, k, v, go, o, lse, begin, cosine, sine)


def split_heads(w, groups):
    rows = w.shape[0]
    return w.reshape(rows, groups, -1).transpose(1, 0, 2)


def spread(blocks):
    lead = blocks.shape[:-1]
    halves = blocks.reshape(lead + (-1, HALF))
    pad = [(0, 0)] * len(lead) + [(0, 0), (0, SLOT - HALF)]
    wide = jnp.pad(halves, pad)
    return wide.reshape(lead + (-1,))


def gathered(wide):
    lead = wide.shape[:-1]
    halves = wide.reshape(lead + (-1, SLOT))[..., :HALF]
    return halves.reshape(lead + (-1,))


def fast_layer(n, m):
    def on_plane(
        layer_input,
        doc_ids,
        positions,
        first_gain,
        query_weight,
        key_weight,
        value_weight,
        output_weight,
        second_gain,
        gate_weight,
        up_weight,
        down_weight,
        out_grad,
    ):
        x = layer_input[0]
        rows, width = x.shape
        length = rows * n
        heads = QUERY_HEADS // n
        scale = 1.0 / math.sqrt(HEAD_SIZE)
        factor = scale * LOG2E
        strip = query_weight.shape[0]
        hid = gate_weight.shape[1] // n

        packed = jnp.concatenate(
            [split_heads(w, n) for w in (query_weight, key_weight, value_weight)], axis=2
        )
        cols = packed.shape[2]
        gains = jnp.concatenate([first_gain, second_gain])
        gain_rows = jnp.pad(gains[None, :], ((0, 7), (0, cols - 2 * strip)))
        packed = jnp.concatenate(
            [packed, jnp.broadcast_to(gain_rows[None], (n, 8, cols))], axis=1
        )
        places = jnp.concatenate([doc_ids, positions], axis=0)
        output_full = lax.all_gather(output_weight, ("seq", "tp"), axis=0, tiled=True)

        x_all, places_all, w_all, ffn_mine = entry(
            n, m, x, places, packed, gate_weight, up_weight, down_weight
        )
        ffn_all = lax.all_gather(ffn_mine, "tp", axis=0, tiled=False)
        x_all = x_all.reshape(length, width)
        docs = places_all[:, 0].reshape(1, length)
        places_seq = places_all[:, 1].reshape(length, 1).astype(f32)

        ordered = w_all.transpose(1, 0, 2, 3)
        wqkv = spread(ordered[:, :, :strip].reshape(width, cols))
        gain_one = ordered[:, :, strip, :strip].reshape(1, width).astype(f32)
        gain_two = ordered[:, :, strip, strip : 2 * strip].reshape(1, width).astype(f32)

        lane = jnp.arange(SLOT)
        inverse = jnp.where(
            lane < HALF, rope_base ** (-(lane.astype(f32) * 2.0 / HEAD_SIZE)), 0.0
        )
        angles = places_seq * inverse[None, :]
        cos, sin = jnp.cos(angles), jnp.sin(angles)
        cosine = jnp.concatenate([cos, cos], axis=1)
        sine = jnp.concatenate([-sin, sin], axis=1)
        begin = jnp.zeros((1, length), jnp.int32)
        for d in range(3):
            begin = begin + jnp.where(docs > d, jnp.sum((docs == d).astype(jnp.int32)), 0)

        norm_one, q, k, v = project(heads, x_all, gain_one, wqkv, cosine, sine)
        o, low, lse = attend(factor, q, k, v, begin)
        mine = plane_swap(n, m, low.reshape(n, rows, heads * LANES), 1)
        attn_low = gathered(mine.transpose(1, 0, 2).reshape(rows, n * heads * LANES))

        x_f = x.astype(f32)
        resid = x_f + jnp.dot(attn_low, output_full, preferred_element_type=f32)
        scale_two = lax.rsqrt(jnp.mean(resid * resid, axis=1, keepdims=True) + norm_epsilon)
        norm_two = (resid * scale_two * gain_two).astype(bf16)
        rows_all = plane_gather(n, m, norm_two, 2).reshape(length, width)
        grad_low = out_grad[0]
        grad_all = lax.all_gather(grad_low, "seq", axis=0, tiled=True)

        gate_w, up_w, down_w = [
            ffn_all[:, i].transpose(1, 0, 2).reshape(width, m * hid) for i in range(3)
        ]
        gate_pre = jnp.dot(rows_all, gate_w, preferred_element_type=f32)
        up_pre = jnp.dot(rows_all, up_w, preferred_element_type=f32)
        gate_sig = jax.nn.sigmoid(gate_pre)
        gate_act = gate_pre * gate_sig
        hidden = (gate_act * up_pre).astype(bf16)
        mixed = times_transpose(hidden, down_w).astype(bf16)
        dhidden = jnp.dot(grad_all, down_w, preferred_element_type=f32)
        dgate = (dhidden * up_pre * gate_sig * (1.0 + gate_pre * (1.0 - gate_sig))).astype(bf16)
        dup = (dhidden * gate_act).astype(bf16)
        dnorm_part = (times_transpose(dgate, gate_w) + times_transpose(dup, up_w)).astype(bf16)
        dnorm_two = plane_reduce(n, m, dnorm_part.reshape(n, rows, width), 3)

        terms = [
            outer_product(a, b).astype(bf16).reshape(width, m, hid).transpose(1, 0, 2)
            for a, b in ((rows_all, dgate), (rows_all, dup), (grad_all, hidden))
        ]
        ffn_terms = jnp.stack(terms, axis=1)
        ffn_sum = lax.psum_scatter(ffn_terms, "tp", scatter_dimension=0, tiled=False)

        mixed_sum = plane_reduce(n, m, mixed.reshape(n, rows, width), 4)
        layer_output = (resid + mixed_sum).astype(bf16)[None]

        inner = gain_two * dnorm_two
        moment = jnp.mean(resid * inner, axis=1, keepdims=True)
        dresid = (
            grad_low.astype(f32)
            + scale_two * inner
            - resid * scale_two * scale_two * scale_two * moment
        )
        dbranch = dresid.astype(bf16)
        output_term = outer_product(attn_low, dbranch)
        output_grad = lax.psum_scatter(
            output_term.astype(bf16), ("seq", "tp"), scatter_dimension=0, tiled=True
        ).astype(f32)
        dheads = spread(times_transpose(dbranch, output_full).astype(bf16))
        dheads = dheads.reshape(rows, n, heads * LANES).transpose(1, 0, 2)
        go = plane_swap(n, m, dheads, 5).reshape(length, heads * LANES)

        dqkv = attend_back(factor, scale, q, k, v, go, o, lse, begin, cosine, sine)
        dnorm_one_part = times_transpose(dqkv, wqkv).astype(bf16)
        qkv_term = gathered(outer_product(norm_one, dqkv).astype(bf16))
        qkv_term = qkv_term.reshape(n, m, strip, cols).transpose(1, 0, 2, 3)
        qkv_sum = lax.psum_scatter(qkv_term, "tp", scatter_dimension=0, tiled=False)
        dnorm_one = plane_reduce(n, m, dnorm_one_part.reshape(n, rows, width), 6)

        scale_one = lax.rsqrt(jnp.mean(x_f * x_f, axis=1, keepdims=True) + norm_epsilon)
        inner = gain_one * dnorm_one
        moment = jnp.mean(x_f * inner, axis=1, keepdims=True)
        input_grad = (
            dresid + scale_one * inner - x_f * scale_one * scale_one * scale_one * moment
        )[None]

        ffn_out, qkv_out = final_swap(n, m, ffn_sum, qkv_sum, 7)
        gate_grad, up_grad, down_grad = [ffn_out[i].astype(f32) for i in range(3)]
        kv = HEAD_SIZE * KEY_VALUE_HEADS // n
        split = heads * HEAD_SIZE

        def columns(a, b):
            return qkv_out[:, :, a:b].transpose(1, 0, 2).reshape(strip, -1).astype(f32)

        query_grad = columns(0, split)
        key_grad = columns(split, split + kv)
        value_grad = columns(split + kv, cols)

        one = (
            jnp.sum(query_weight.astype(f32) * query_grad, axis=1)
            + jnp.sum(key_weight.astype(f32) * key_grad, axis=1)
            + jnp.sum(value_weight.astype(f32) * value_grad, axis=1)
        )
        first_gain_grad = one / first_gain.astype(f32)
        two = jnp.sum(
            gate_weight.astype(f32) * gate_grad + up_weight.astype(f32) * up_grad, axis=1
        )
        second_gain_grad = lax.psum_scatter(
            two, "tp", scatter_dimension=0, tiled=True
        ) / second_gain.astype(f32)
        return (
            layer_output,
            input_grad,
            first_gain_grad,
            query_grad,
            key_grad,
            value_grad,
            output_grad,
            second_gain_grad,
            gate_grad,
            up_grad,
            down_grad,
        )

    return on_plane


def solution(mesh):
    n, m = mesh.shape["seq"], mesh.shape["tp"]
    fits = KEY_VALUE_HEADS == n
    return jax.shard_map(
        fast_layer(n, m) if fits else on_device,
        mesh=mesh,
        in_specs=(
            P("tp", "seq", None),
            P("tp", "seq"),
            P("tp", "seq"),
            P(("seq", "tp")),
            P(("seq", "tp"), None),
            P(("seq", "tp"), None),
            P(("seq", "tp"), None),
            P(("seq", "tp"), None),
            P(("seq", "tp")),
            P("seq", "tp"),
            P("seq", "tp"),
            P("seq", "tp"),
            P("tp", "seq", None),
        ),
        out_specs=(
            P("tp", "seq", None),
            P("tp", "seq", None),
            P(("seq", "tp")),
            P(("seq", "tp"), None),
            P(("seq", "tp"), None),
            P(("seq", "tp"), None),
            P(("seq", "tp"), None),
            P(("seq", "tp")),
            P("seq", "tp"),
            P("seq", "tp"),
            P("seq", "tp"),
        ),
        check_vma=False,
    )
```

```python
import functools
import math

import jax
import jax.numpy as jnp
from jax import lax
from jax.experimental import pallas as pl
from jax.experimental.pallas import tpu as pltpu
from jax.sharding import PartitionSpec as P

QUERY_HEADS = 16
KEY_VALUE_HEADS = 8
HEAD_SIZE = 96


norm_epsilon = 1e-05
rope_base = 100000.0
mask_fill_value = -1e30


def rope_tables(places):
    half = HEAD_SIZE // 2
    inverse = rope_base ** (-(jnp.arange(half, dtype=jnp.float32) * 2.0 / HEAD_SIZE))
    angles = places.astype(jnp.float32)[:, None] * inverse[None, :]
    return (jnp.cos(angles), jnp.sin(angles))


def apply_rotary(value_rows, cosine_table, sine_table, heads, direction):
    sequence_length = value_rows.shape[0]
    split = value_rows.reshape(sequence_length, heads, 2, HEAD_SIZE // 2)
    first = split[:, :, 0]
    second = split[:, :, 1]
    cosine = cosine_table[:, None, :]
    sine = direction * sine_table[:, None, :]
    turned = jnp.stack([first * cosine - second * sine, second * cosine + first * sine], axis=2)
    return turned.reshape(sequence_length, heads * HEAD_SIZE)


def outer_product(left, right):
    return lax.dot_general(
        left, right, (((0,), (0,)), ((), ())), preferred_element_type=jnp.float32
    )


def times_transpose(left, right):
    return lax.dot_general(
        left, right, (((1,), (1,)), ((), ())), preferred_element_type=jnp.float32
    )


def norm_backward(inputs, scale, gain, upstream):
    inner = gain * upstream
    moment = jnp.mean(inputs * inner, axis=1, keepdims=True)
    return (
        scale * inner - inputs * scale * scale * scale * moment,
        jnp.sum(upstream * inputs * scale, axis=0),
    )


def on_device(
    layer_input,
    doc_ids,
    positions,
    first_gain,
    query_weight,
    key_weight,
    value_weight,
    output_weight,
    second_gain,
    gate_weight,
    up_weight,
    down_weight,
    out_grad,
):
    token_rows = layer_input.shape[1]
    query_groups = QUERY_HEADS // KEY_VALUE_HEADS
    scale_of_scores = 1.0 / math.sqrt(HEAD_SIZE)
    inputs_f = layer_input[0].astype(jnp.float32)
    my_docs = doc_ids[0]
    gain_one, query_full, complete_keys, value_full, output_full, gain_two = (
        lax.all_gather(first_gain, ("seq", "tp"), axis=0, tiled=True),
        lax.all_gather(query_weight, ("seq", "tp"), axis=0, tiled=True),
        lax.all_gather(key_weight, ("seq", "tp"), axis=0, tiled=True),
        lax.all_gather(value_weight, ("seq", "tp"), axis=0, tiled=True),
        lax.all_gather(output_weight, ("seq", "tp"), axis=0, tiled=True),
        lax.all_gather(second_gain, ("seq", "tp"), axis=0, tiled=True),
    )
    gain_one_f = gain_one.astype(jnp.float32)
    gain_two_f = gain_two.astype(jnp.float32)
    scale_one = lax.rsqrt(jnp.mean(inputs_f * inputs_f, axis=1, keepdims=True) + norm_epsilon)
    first_normalized = (inputs_f * scale_one * gain_one_f).astype(jnp.bfloat16)
    cosine_table, sine_table = rope_tables(positions[0])
    rotated_query = apply_rotary(
        jnp.dot(first_normalized, query_full, preferred_element_type=jnp.float32),
        cosine_table,
        sine_table,
        QUERY_HEADS,
        1.0,
    ).astype(jnp.bfloat16)
    key_rot = apply_rotary(
        jnp.dot(first_normalized, complete_keys, preferred_element_type=jnp.float32),
        cosine_table,
        sine_table,
        KEY_VALUE_HEADS,
        1.0,
    ).astype(jnp.bfloat16)
    value_low = jnp.dot(first_normalized, value_full, preferred_element_type=jnp.float32).astype(
        jnp.bfloat16
    )
    gathered_keys, gathered_values, doc_all = (
        lax.all_gather(key_rot, "seq", axis=0, tiled=True),
        lax.all_gather(value_low, "seq", axis=0, tiled=True),
        lax.all_gather(my_docs.astype(jnp.bfloat16), "seq", axis=0, tiled=True),
    )
    sequence_length = gathered_keys.shape[0]
    block_number = math.gcd(512, sequence_length)
    block_count = sequence_length // block_number
    query_index = lax.axis_index("seq") * token_rows + jnp.arange(token_rows, dtype=jnp.int32)
    my_doc_f = my_docs.astype(jnp.float32)
    heads_of_query = rotated_query.reshape(token_rows, KEY_VALUE_HEADS, query_groups, HEAD_SIZE)
    layer_entries = (
        gathered_keys.reshape(block_count, block_number, KEY_VALUE_HEADS, HEAD_SIZE),
        gathered_values.reshape(block_count, block_number, KEY_VALUE_HEADS, HEAD_SIZE),
        doc_all.astype(jnp.float32).reshape(block_count, block_number),
        jnp.arange(block_count, dtype=jnp.int32) * block_number,
    )

    def allowed_of(doc_piece, start):
        key_index = start + jnp.arange(block_number, dtype=jnp.int32)
        return (key_index[None, :] <= query_index[:, None]) & (
            doc_piece[None, :] == my_doc_f[:, None]
        )

    def scores_of(key_piece, allowed):
        raw = (
            jnp.einsum(
                "tgrd,kgd->tgrk", heads_of_query, key_piece, preferred_element_type=jnp.float32
            )
            * scale_of_scores
        )
        return jnp.where(allowed[:, None, None, :], raw, mask_fill_value)

    def total_step(carry, item):
        key_piece, value_piece, doc_piece, start = item
        allowed = allowed_of(doc_piece, start)

        def total_work(state):
            top, total = state
            scores = scores_of(key_piece, allowed)
            new_top = jnp.maximum(top, jnp.max(scores, axis=3))
            weights = jnp.where(
                allowed[:, None, None, :], jnp.exp(scores - new_top[..., None]), 0.0
            )
            return (new_top, total * jnp.exp(top - new_top) + jnp.sum(weights, axis=3))

        return (lax.cond(jnp.any(allowed), total_work, lambda state: state, carry), None)

    start_state = (
        jnp.full((token_rows, KEY_VALUE_HEADS, query_groups), mask_fill_value, jnp.float32),
        jnp.zeros((token_rows, KEY_VALUE_HEADS, query_groups), jnp.float32),
    )
    (top, total), unused_result = lax.scan(total_step, start_state, layer_entries)
    log_total = top + jnp.log(total)

    def probs_of(key_piece, allowed):
        scores = scores_of(key_piece, allowed)
        return jnp.where(allowed[:, None, None, :], jnp.exp(scores - log_total[..., None]), 0.0)

    def output_update(accum, item):
        key_piece, value_piece, doc_piece, start = item
        allowed = allowed_of(doc_piece, start)

        def output_work(state):
            probs = probs_of(key_piece, allowed).astype(jnp.bfloat16)
            return state + jnp.einsum(
                "tgrk,kgd->tgrd", probs, value_piece, preferred_element_type=jnp.float32
            )

        return (lax.cond(jnp.any(allowed), output_work, lambda state: state, accum), None)

    heads_output, unused_result = lax.scan(
        output_update,
        jnp.zeros((token_rows, KEY_VALUE_HEADS, query_groups, HEAD_SIZE), jnp.float32),
        layer_entries,
    )
    attn_low = heads_output.reshape(token_rows, QUERY_HEADS * HEAD_SIZE).astype(jnp.bfloat16)
    resid = inputs_f + jnp.dot(attn_low, output_full, preferred_element_type=jnp.float32)
    scale_two = lax.rsqrt(jnp.mean(resid * resid, axis=1, keepdims=True) + norm_epsilon)
    normed_two = (resid * scale_two * gain_two_f).astype(jnp.bfloat16)
    rows_all = lax.all_gather(normed_two, "tp", axis=0, tiled=True)
    gate_cols, up_cols, down_cols = (
        lax.all_gather(gate_weight, "seq", axis=0, tiled=True),
        lax.all_gather(up_weight, "seq", axis=0, tiled=True),
        lax.all_gather(down_weight, "seq", axis=0, tiled=True),
    )
    gate_pre = jnp.dot(rows_all, gate_cols, preferred_element_type=jnp.float32)
    up_pre = jnp.dot(rows_all, up_cols, preferred_element_type=jnp.float32)
    gate_sig = jax.nn.sigmoid(gate_pre)
    gate_act = gate_pre * gate_sig
    hidden = (gate_act * up_pre).astype(jnp.bfloat16)
    mixed = lax.psum_scatter(
        times_transpose(hidden, down_cols).astype(jnp.bfloat16),
        "tp",
        scatter_dimension=0,
        tiled=True,
    ).astype(jnp.float32)
    layer_output = (resid + mixed).astype(jnp.bfloat16)[None]
    grad_low = out_grad[0]
    grad_f = grad_low.astype(jnp.float32)
    grad_all = lax.all_gather(grad_low, "tp", axis=0, tiled=True)
    dhidden = jnp.dot(grad_all, down_cols, preferred_element_type=jnp.float32)
    dgate = (dhidden * up_pre * gate_sig * (1.0 + gate_pre * (1.0 - gate_sig))).astype(jnp.bfloat16)
    dup = (dhidden * gate_act).astype(jnp.bfloat16)
    gate_term = outer_product(rows_all, dgate)
    up_term = outer_product(rows_all, dup)
    down_term_grad = outer_product(grad_all, hidden)
    dnorm_two = lax.psum_scatter(
        (times_transpose(dgate, gate_cols) + times_transpose(dup, up_cols)).astype(jnp.bfloat16),
        "tp",
        scatter_dimension=0,
        tiled=True,
    ).astype(jnp.float32)
    gate_grad, up_grad, down_grad = (
        lax.psum_scatter(
            gate_term.astype(jnp.bfloat16), "seq", scatter_dimension=0, tiled=True
        ).astype(jnp.float32),
        lax.psum_scatter(
            up_term.astype(jnp.bfloat16), "seq", scatter_dimension=0, tiled=True
        ).astype(jnp.float32),
        lax.psum_scatter(
            down_term_grad.astype(jnp.bfloat16), "seq", scatter_dimension=0, tiled=True
        ).astype(jnp.float32),
    )
    resid_part, gain_two_term = norm_backward(resid, scale_two, gain_two_f, dnorm_two)
    dresid = grad_f + resid_part
    dbranch = dresid.astype(jnp.bfloat16)
    output_term = outer_product(attn_low, dbranch)
    heads_gradient = times_transpose(dbranch, output_full).astype(jnp.bfloat16)
    grouped_heads_gradient = heads_gradient.reshape(
        token_rows, KEY_VALUE_HEADS, query_groups, HEAD_SIZE
    )
    delta = jnp.sum(grouped_heads_gradient.astype(jnp.float32) * heads_output, axis=3)

    def gradient_update(dquery, item):
        key_piece, value_piece, doc_piece, start = item
        allowed = allowed_of(doc_piece, start)

        def gradient_work(state):
            probs = probs_of(key_piece, allowed)
            value_piece_grad = jnp.einsum(
                "tgrk,tgrd->kgd",
                probs.astype(jnp.bfloat16),
                grouped_heads_gradient,
                preferred_element_type=jnp.float32,
            )
            prob_grad = jnp.einsum(
                "tgrd,kgd->tgrk",
                grouped_heads_gradient,
                value_piece,
                preferred_element_type=jnp.float32,
            )
            score_grad = (probs * (prob_grad - delta[..., None])).astype(jnp.bfloat16)
            key_piece_grad = jnp.einsum(
                "tgrk,tgrd->kgd", score_grad, heads_of_query, preferred_element_type=jnp.float32
            )
            updated = state + jnp.einsum(
                "tgrk,kgd->tgrd", score_grad, key_piece, preferred_element_type=jnp.float32
            )
            return (updated, (key_piece_grad, value_piece_grad))

        def skip(state):
            blank_tensor = jnp.zeros((block_number, KEY_VALUE_HEADS, HEAD_SIZE), jnp.float32)
            return (state, (blank_tensor, blank_tensor))

        return lax.cond(jnp.any(allowed), gradient_work, skip, dquery)

    dquery, (key_contributions, value_contributions) = lax.scan(
        gradient_update,
        jnp.zeros((token_rows, KEY_VALUE_HEADS, query_groups, HEAD_SIZE), jnp.float32),
        layer_entries,
    )
    gathered_key_contributions = (
        key_contributions.reshape(sequence_length, KEY_VALUE_HEADS * HEAD_SIZE) * scale_of_scores
    )
    gathered_value_contributions = value_contributions.reshape(
        sequence_length, KEY_VALUE_HEADS * HEAD_SIZE
    )
    local_keys, value_mine = (
        lax.psum_scatter(
            gathered_key_contributions.astype(jnp.bfloat16), "seq", scatter_dimension=0, tiled=True
        ).astype(jnp.float32),
        lax.psum_scatter(
            gathered_value_contributions.astype(jnp.bfloat16),
            "seq",
            scatter_dimension=0,
            tiled=True,
        ).astype(jnp.float32),
    )
    dq_pre = apply_rotary(
        dquery.reshape(token_rows, QUERY_HEADS * HEAD_SIZE) * scale_of_scores,
        cosine_table,
        sine_table,
        QUERY_HEADS,
        -1.0,
    ).astype(jnp.bfloat16)
    key_gradient_unrotated = apply_rotary(
        local_keys, cosine_table, sine_table, KEY_VALUE_HEADS, -1.0
    ).astype(jnp.bfloat16)
    dv_pre = value_mine.astype(jnp.bfloat16)
    dnorm_one = (
        times_transpose(dq_pre, query_full)
        + times_transpose(key_gradient_unrotated, complete_keys)
        + times_transpose(dv_pre, value_full)
    )
    input_part, gain_one_term = norm_backward(inputs_f, scale_one, gain_one_f, dnorm_one)
    input_grad = (dresid + input_part)[None]
    query_term = outer_product(first_normalized, dq_pre)
    key_term = outer_product(first_normalized, key_gradient_unrotated)
    value_term = outer_product(first_normalized, dv_pre)
    first_gain_grad, query_grad, key_grad, value_grad, output_grad, second_gain_grad = (
        lax.psum_scatter(gain_one_term, ("seq", "tp"), scatter_dimension=0, tiled=True),
        lax.psum_scatter(query_term, ("seq", "tp"), scatter_dimension=0, tiled=True),
        lax.psum_scatter(key_term, ("seq", "tp"), scatter_dimension=0, tiled=True),
        lax.psum_scatter(value_term, ("seq", "tp"), scatter_dimension=0, tiled=True),
        lax.psum_scatter(output_term, ("seq", "tp"), scatter_dimension=0, tiled=True),
        lax.psum_scatter(gain_two_term, ("seq", "tp"), scatter_dimension=0, tiled=True),
    )
    return (
        layer_output,
        input_grad,
        first_gain_grad,
        query_grad,
        key_grad,
        value_grad,
        output_grad,
        second_gain_grad,
        gate_grad,
        up_grad,
        down_grad,
    )


MESH = pl.DeviceIdType.MESH
ANY = pl.ANY
HALF = HEAD_SIZE // 2
LANES = 128
SLOT = LANES // 2
f32 = jnp.float32
bf16 = jnp.bfloat16


class Plane:
    def __init__(self, n, m):
        self.n, self.m, self.chips = n, m, n // 2
        self.s = lax.axis_index("seq")
        self.t = lax.axis_index("tp")
        self.q = self.s // 2
        self.c = lax.rem(self.s, 2)

        across = self.q + 1 - 2 * lax.rem(self.q, 2)
        along = lax.rem(self.q + 2, 4)
        self.to = across * (1 - self.c) + along * self.c
        self.fro = across * self.c + along * (1 - self.c)
        self.far = 3 - self.q
        self.order = (self.q, self.to, self.fro, self.far)

    def device(self, s):
        return (s, self.t)

    def same(self, chip):
        return (2 * chip + self.c, self.t)

    def sibling(self):
        return (2 * self.q + 1 - self.c, self.t)

    def ahead(self, k):
        return lax.rem(self.q + k, self.chips)

    def behind(self, k):
        return lax.rem(self.q + self.chips - k, self.chips)

    def seq_ahead(self, k):
        return lax.rem(self.s + k, self.n)

    def seq_behind(self, k):
        return lax.rem(self.s + self.n - k, self.n)

    def tp_ahead(self, k):
        return (self.s, lax.rem(self.t + k, self.m))

    def tp_behind(self, k):
        return lax.rem(self.t + self.m - k, self.m)


def enter_plane(plane, with_tp):
    barrier = pltpu.get_barrier_semaphore()
    for k in range(1, plane.n):
        pl.semaphore_signal(
            barrier, inc=1, device_id=plane.device(plane.seq_ahead(k)), device_id_type=MESH
        )
    count = plane.n - 1
    if with_tp:
        for k in range(1, plane.m):
            pl.semaphore_signal(barrier, inc=1, device_id=plane.tp_ahead(k), device_id_type=MESH)
        count += plane.m - 1
    pl.semaphore_wait(barrier, count)


def remote(src, dst, send, recv, device):
    return pltpu.make_async_remote_copy(
        src_ref=src,
        dst_ref=dst,
        send_sem=send,
        recv_sem=recv,
        device_id=device,
        device_id_type=MESH,
    )


class Gather:
    COPIES = 7

    def __init__(self, plane, src, dst, send, recv, local):
        to, fro, far, c = plane.to, plane.fro, plane.far, plane.c
        here = dst.at[plane.s]
        self.own = pltpu.make_async_copy(src, here, local)

        def block(chip):
            return dst.at[2 * chip + c]

        def copy(i, a, b, device):
            return remote(a, b, send.at[i], recv.at[i], device)

        sibling = plane.sibling()
        self.swap = copy(0, src, here, sibling)
        self.ahead = copy(1, src, here, plane.same(to))
        self.back = copy(2, src, here, plane.same(fro))
        self.relay = copy(3, block(fro), block(fro), plane.same(to))
        self.share = [
            copy(4, block(to), block(to), sibling),
            copy(5, block(fro), block(fro), sibling),
            copy(6, block(far), block(far), sibling),
        ]

    def start(self):
        self.back.start()
        self.ahead.start()
        self.swap.start()
        self.own.start()

    def relay_near(self):
        self.back.wait_recv()
        self.relay.start()
        self.share[1].start()
        self.ahead.wait_recv()
        self.share[0].start()

    def relay_far(self):
        self.relay.wait_recv()
        self.share[2].start()

    def finish(self):
        self.own.wait()
        self.swap.wait()
        self.ahead.wait_send()
        self.back.wait_send()
        self.relay.wait_send()
        for copy in self.share:
            copy.wait()

    def run(self):
        self.start()
        self.relay_near()
        self.relay_far()
        self.finish()


def fan(plane, src_of, dst_of, send, recv):
    copies = []
    for k in range(1, plane.m):
        device = plane.tp_ahead(k)
        copies.append(
            remote(src_of(device[1]), dst_of(plane.t), send.at[k - 1], recv.at[k - 1], device)
        )
    return copies


def exchange(plane, src_of, dst_of, send, recv, local):
    own = pltpu.make_async_copy(src_of(plane.s), dst_of(plane.s), local)
    copies = []
    for k in range(1, plane.n):
        peer = plane.seq_ahead(k)
        copies.append(
            remote(
                src_of(peer), dst_of(plane.s), send.at[k - 1], recv.at[k - 1], plane.device(peer)
            )
        )
    return [own] + copies


def entry_body(n, m, x, places, wqkv, gains, x_all, places_all, w_all, gains_all, sx, rem, sz, loc):
    plane = Plane(n, m)
    enter_plane(plane, True)
    gather = Gather(plane, x, x_all, sx.at[0], sx.at[1], loc.at[0])
    copies = exchange(
        plane,
        lambda i: wqkv.at[i],
        lambda i: w_all.at[i, plane.t],
        rem.at[0, 0],
        rem.at[0, 1],
        loc.at[1],
    )
    copies += exchange(
        plane,
        lambda i: gains,
        lambda i: gains_all.at[i, plane.t],
        rem.at[1, 0],
        rem.at[1, 1],
        loc.at[2],
    )
    few = exchange(
        plane, lambda i: places, lambda i: places_all.at[i], rem.at[2, 0], rem.at[2, 1], loc.at[3]
    )
    for copy in copies:
        copy.start()
    gather.start()
    for copy in few:
        copy.start()
    for copy in copies:
        copy.wait()
    across = []
    for i, ref in enumerate((w_all, gains_all)):

        def slot(t, ref=ref):
            return ref.at[:, plane.t]

        across += fan(plane, slot, slot, sz.at[i, 0], sz.at[i, 1])
    for copy in across:
        copy.start()
    gather.relay_near()
    gather.relay_far()
    for copy in few + across:
        copy.wait()
    gather.finish()


def entry(n, m, x, places, wqkv, gains):
    return pl.pallas_call(
        functools.partial(entry_body, n, m),
        out_shape=(
            jax.ShapeDtypeStruct((n,) + x.shape, x.dtype),
            jax.ShapeDtypeStruct((n,) + places.shape, places.dtype),
            jax.ShapeDtypeStruct((n, m) + wqkv.shape[1:], wqkv.dtype),
            jax.ShapeDtypeStruct((n, m) + gains.shape, gains.dtype),
        ),
        in_specs=[pl.BlockSpec(memory_space=ANY)] * 4,
        out_specs=[pl.BlockSpec(memory_space=ANY)] * 4,
        scratch_shapes=[
            pltpu.SemaphoreType.DMA((2, Gather.COPIES)),
            pltpu.SemaphoreType.DMA((3, 2, n - 1)),
            pltpu.SemaphoreType.DMA((2, 2, m - 1)),
            pltpu.SemaphoreType.DMA((4,)),
        ],
        compiler_params=pltpu.CompilerParams(collective_id=0, has_side_effects=True),
        cost_estimate=pl.CostEstimate(flops=0, transcendentals=0, bytes_accessed=100_000_000),
        name="entry",
    )(x, places, wqkv, gains)


def swap_body(n, m, count, *refs):
    plane = Plane(n, m)
    enter_plane(plane, False)
    sems, loc = refs[2 * count :]
    copies = []
    for i in range(count):
        src, dst = refs[i], refs[count + i]
        copies += exchange(
            plane,
            lambda k, src=src: src.at[k],
            lambda k, dst=dst: dst.at[k],
            sems.at[i, 0],
            sems.at[i, 1],
            loc.at[i],
        )
    for copy in copies:
        copy.start()
    for copy in copies:
        copy.wait()


def plane_swap(n, m, ident, *arrays):
    count = len(arrays)
    return pl.pallas_call(
        functools.partial(swap_body, n, m, count),
        out_shape=tuple(jax.ShapeDtypeStruct(a.shape, a.dtype) for a in arrays),
        in_specs=[pl.BlockSpec(memory_space=ANY)] * count,
        out_specs=[pl.BlockSpec(memory_space=ANY)] * count,
        scratch_shapes=[
            pltpu.SemaphoreType.DMA((count, 2, n - 1)),
            pltpu.SemaphoreType.DMA((count,)),
        ],
        compiler_params=pltpu.CompilerParams(collective_id=ident, has_side_effects=True),
        cost_estimate=pl.CostEstimate(flops=0, transcendentals=0, bytes_accessed=40_000_000),
        name="plane_swap",
    )(*arrays)


TILE = 16


def in_tiles(rows, body):
    def one(i, carry):
        body(pl.ds(pl.multiple_of(i * TILE, TILE), TILE))
        return carry

    lax.fori_loop(0, rows // TILE, one, 0)


class Reduce:
    SLOTS = (4, 4, 3)

    THEIRS = (0, 2, 1, 3)

    def __init__(self, plane, part_of, pair, near, far, sems, loc, stage=None):
        c = plane.c
        self.pair, self.near, self.far = pair, near, far
        self.rows = pair.shape[1]
        self.swaps, self.loads = {}, {}
        for k in range(4):
            mine = self.THEIRS[k]
            chip = plane.order[mine]
            source = part_of(2 * chip + 1 - c) if stage is None else stage.at[mine]
            self.swaps[k] = remote(
                source, near.at[k], sems.at[0, k], sems.at[1, k], plane.sibling()
            )
            if stage is None:
                self.loads[k] = pltpu.make_async_copy(
                    part_of(2 * plane.order[k] + c), pair.at[k], loc.at[k]
                )

        def out(i, k, chip):
            return remote(
                pair.at[k], far.at[i], sems.at[2, i], sems.at[3, i], plane.same(chip)
            )

        self.out = [out(0, 3, plane.to), out(1, 1, plane.to), out(2, 2, plane.fro)]

    def start(self):
        for k in (3, 1, 2, 0):
            self.swaps[k].start()
            self.loads[k].start()

    def landed(self, k):
        self.swaps[k].wait()
        if self.loads:
            self.loads[k].wait()

    def join(self, k):
        pair, near = self.pair, self.near
        self.landed(k)

        def add(at):
            both = pair[k, at, :].astype(f32) + near[k, at, :].astype(f32)
            pair[k, at, :] = both.astype(bf16)

        in_tiles(self.rows, add)

    def send_to(self):
        self.join(3)
        self.out[0].start()
        self.join(1)
        self.out[1].start()

    def ready(self):
        self.landed(2)

    def send_fro(self):
        pair, near, far = self.pair, self.near, self.far
        self.out[0].wait_recv()

        def add(at):
            both = pair[2, at, :].astype(f32) + near[2, at, :].astype(f32)
            pair[2, at, :] = (both + far[0, at, :].astype(f32)).astype(bf16)

        in_tiles(self.rows, add)
        self.out[2].start()

    def first(self, total):
        pair, near = self.pair, self.near
        self.landed(0)

        def add(at):
            total[at, :] = pair[0, at, :].astype(f32) + near[0, at, :].astype(f32)

        in_tiles(self.rows, add)

    def finish(self, total):
        far = self.far
        self.out[0].wait_send()
        self.out[1].wait()
        self.out[2].wait()

        def add(at):
            total[at, :] = (
                total[at, :] + far[1, at, :].astype(f32) + far[2, at, :].astype(f32)
            )

        in_tiles(self.rows, add)

    def run(self, total):
        self.start()
        self.send_to()
        self.ready()
        self.first(total)
        self.send_fro()
        self.finish(total)

    @staticmethod
    def scratch(rows, width):
        return [pltpu.VMEM((slots, rows, width), bf16) for slots in Reduce.SLOTS] + [
            pltpu.SemaphoreType.DMA((4, 4)),
            pltpu.SemaphoreType.DMA((4,)),
        ]


def last_body(
    n, m, parts, ffn, qkv, vec, total, ffn_out, qkv_out, vec_out,
    pair, near, far, sr, lr, got, summed, sems, st, loc,
):
    plane = Plane(n, m)
    enter_plane(plane, True)
    rows = ffn_out.shape[1]
    width = ffn.shape[2]
    across = fan(plane, lambda t: qkv.at[t], lambda t: got.at[t], st.at[0, 0], st.at[0, 1])
    across_vec = fan(plane, lambda t: vec.at[t], lambda t: vec_out.at[t], st.at[1, 0], st.at[1, 1])
    mine = [
        pltpu.make_async_copy(qkv.at[plane.t], got.at[plane.t], loc.at[0]),
        pltpu.make_async_copy(vec.at[plane.t], vec_out.at[plane.t], loc.at[1]),
    ]
    for copy in across + across_vec + mine:
        copy.start()
    reduce = Reduce(plane, lambda i: parts.at[i], pair, near, far, sr, lr)
    reduce.start()
    a = exchange(
        plane,
        lambda i: ffn.at[:, pl.ds(pl.multiple_of(i * rows, rows), rows), :],
        lambda i: ffn_out.at[:, :, pl.ds(pl.multiple_of(i * width, width), width)],
        sems.at[0, 0],
        sems.at[0, 1],
        loc.at[2],
    )
    for copy in a:
        copy.start()
    reduce.send_to()
    reduce.ready()
    reduce.first(total)
    for copy in across + across_vec + mine:
        copy.wait()
    groups, strip, _ = summed.shape

    for g in range(groups):

        def add(at, g=g):
            value = got[0, g, at, :].astype(f32)
            for t in range(1, m):
                value = value + got[t, g, at, :].astype(f32)
            summed[g, at, :] = value.astype(bf16)

        in_tiles(strip, add)
    b = exchange(
        plane,
        lambda i: summed.at[i],
        lambda i: qkv_out.at[i],
        sems.at[1, 0],
        sems.at[1, 1],
        loc.at[3],
    )
    for copy in b:
        copy.start()
    reduce.send_fro()
    reduce.finish(total)
    for copy in a + b:
        copy.wait()


def last(n, m, parts, ffn, qkv, vec, ident):
    rows, width = parts.shape[1:]
    return pl.pallas_call(
        functools.partial(last_body, n, m),
        out_shape=(
            jax.ShapeDtypeStruct((rows, width), f32),
            jax.ShapeDtypeStruct((3, ffn.shape[1] // n, ffn.shape[2] * n), ffn.dtype),
            jax.ShapeDtypeStruct(qkv.shape[1:], qkv.dtype),
            jax.ShapeDtypeStruct(vec.shape, vec.dtype),
        ),
        in_specs=[pl.BlockSpec(memory_space=ANY)] * 4,
        out_specs=[pl.BlockSpec(memory_space=pltpu.VMEM)]
        + [pl.BlockSpec(memory_space=ANY)] * 3,
        scratch_shapes=Reduce.scratch(rows, width)
        + [
            pltpu.VMEM(qkv.shape, bf16),
            pltpu.VMEM(qkv.shape[1:], bf16),
            pltpu.SemaphoreType.DMA((2, 2, n - 1)),
            pltpu.SemaphoreType.DMA((2, 2, m - 1)),
            pltpu.SemaphoreType.DMA((4,)),
        ],
        compiler_params=pltpu.CompilerParams(
            collective_id=ident, has_side_effects=True, vmem_limit_bytes=40 << 20
        ),
        cost_estimate=pl.CostEstimate(flops=0, transcendentals=0, bytes_accessed=150_000_000),
        name="last",
    )(parts, ffn, qkv, vec)


def column(row):
    return jnp.broadcast_to(row, (8, row.shape[1])).T[:, :1]


def project_body(
    n, m, heads, x, gain, w, places, inverse, wg, wu, wd, wo, norm, q, k, v, cosine, sine, ffn, wo_z,
    sems, loc, sz
):
    step = pl.program_id(0)
    plane = Plane(n, m)
    width, rows = wg.shape[1] // n, wg.shape[0]

    def moves():
        copies = []
        for j, weight in enumerate((wg, wu, wd)):
            copies += exchange(
                plane,
                lambda i, w=weight: w.at[:, pl.ds(pl.multiple_of(i * width, width), width)],
                lambda i, j=j: ffn.at[j, pl.ds(pl.multiple_of(i * rows, rows), rows), :],
                sems.at[j, 0],
                sems.at[j, 1],
                loc.at[j],
            )
        return copies

    def spread_wo():
        return fan(plane, lambda t: wo, lambda t: wo_z.at[t], sz.at[0], sz.at[1])

    def own_wo():
        return pltpu.make_async_copy(wo, wo_z.at[plane.t], loc.at[3])

    @pl.when(step == 0)
    def _():
        own_wo().start()
        enter_plane(plane, True)
        for copy in moves() + spread_wo():
            copy.start()

    value = x[0].astype(f32)
    scale = lax.rsqrt(jnp.mean(value * value, axis=1, keepdims=True) + norm_epsilon)
    low = (value * scale * gain[...]).astype(bf16)
    norm[...] = low
    out = jnp.dot(low, w[...], preferred_element_type=f32)
    angles = column(places[0, 1:2, :].astype(f32)) * inverse[...]
    cos = jnp.cos(angles)
    lanes = lax.broadcasted_iota(jnp.int32, angles.shape, 1)
    sin = jnp.sin(angles)
    sin = jnp.where(lanes < SLOT, -sin, sin)
    cosine[...] = cos
    sine[...] = sin
    for h in range(heads + 1):
        part = out[:, h * LANES : (h + 1) * LANES]
        turned = (part * cos + pltpu.roll(part, SLOT, 1) * sin).astype(bf16)
        if h < heads:
            q[h] = turned
        else:
            k[...] = turned
    v[...] = out[:, (heads + 1) * LANES :].astype(bf16)

    @pl.when(step == pl.num_programs(0) - 1)
    def _():
        own_wo().wait()
        for copy in moves() + spread_wo():
            copy.wait()


def project(n, m, heads, x_all, gain, w, places, inverse, wg, wu, wd, wo, ident):
    tiles, tile, width = x_all.shape
    length = tiles * tile
    wide = w.shape[1]
    rows, cols = wg.shape
    table = pl.BlockSpec((tile, LANES), lambda i: (i, 0))
    return pl.pallas_call(
        functools.partial(project_body, n, m, heads),
        grid=(tiles,),
        out_shape=(
            jax.ShapeDtypeStruct((length, width), bf16),
            jax.ShapeDtypeStruct((heads, length, LANES), bf16),
            jax.ShapeDtypeStruct((length, LANES), bf16),
            jax.ShapeDtypeStruct((length, LANES), bf16),
            jax.ShapeDtypeStruct((length, LANES), f32),
            jax.ShapeDtypeStruct((length, LANES), f32),
            jax.ShapeDtypeStruct((3, rows * n, cols // n), wg.dtype),
            jax.ShapeDtypeStruct((m,) + wo.shape, wo.dtype),
        ),
        in_specs=[
            pl.BlockSpec((1, tile, width), lambda i: (i, 0, 0)),
            pl.BlockSpec((1, width), lambda i: (0, 0)),
            pl.BlockSpec((width, wide), lambda i: (0, 0)),
            pl.BlockSpec((1,) + places.shape[1:], lambda i: (i, 0, 0)),
            pl.BlockSpec((1, LANES), lambda i: (0, 0)),
        ]
        + [pl.BlockSpec(memory_space=ANY)] * 4,
        out_specs=[
            pl.BlockSpec((tile, width), lambda i: (i, 0)),
            pl.BlockSpec((heads, tile, LANES), lambda i: (0, i, 0)),
            table,
            table,
            table,
            table,
            pl.BlockSpec(memory_space=ANY),
            pl.BlockSpec(memory_space=ANY),
        ],
        scratch_shapes=[
            pltpu.SemaphoreType.DMA((3, 2, n - 1)),
            pltpu.SemaphoreType.DMA((4,)),
            pltpu.SemaphoreType.DMA((2, m - 1)),
        ],
        compiler_params=pltpu.CompilerParams(collective_id=ident, has_side_effects=True),
        cost_estimate=pl.CostEstimate(
            flops=2 * length * width * wide * 3, transcendentals=0, bytes_accessed=30_000_000
        ),
        name="project",
    )(x_all, gain, w, places, inverse, wg, wu, wd, wo)


BLOCK = 512
NT = (((1,), (1,)), ((), ()))
LOG2E = 1.4426950408889634


def allowed_block(first_key, first_query, begin, causal):
    keys = first_key + lax.broadcasted_iota(jnp.int32, (BLOCK, BLOCK), 0)
    ok = keys >= begin
    if causal:
        queries = first_query + lax.broadcasted_iota(jnp.int32, (BLOCK, BLOCK), 1)
        ok = ok & (keys <= queries)
    return ok


def begins(docs):
    begin = jnp.zeros(docs.shape, jnp.int32)
    for d in range(3):
        count = jnp.sum((docs == d).astype(f32), axis=1, keepdims=True).astype(jnp.int32)
        begin = begin + jnp.where(docs > d, count, 0)
    return begin


def attend_body(
    n, m, factor, q, k, v, docs, wo, go, o, low, lse, start, wo_all, go_all,
    vt, top, total, acc, begin_row, sems, loc
):
    h, i = pl.program_id(0), pl.program_id(1)
    plane = Plane(n, m)
    first = Gather(plane, wo, wo_all, sems.at[0], sems.at[1], loc.at[0])
    second = Gather(plane, go, go_all, sems.at[2], sems.at[3], loc.at[1])
    at_step = h * pl.num_programs(1) + i

    @pl.when(at_step == 0)
    def _():
        enter_plane(plane, False)
        first.start()
        second.start()
        vt[...] = v[...].T
        begin_row[...] = begins(docs[...])
        start[...] = begin_row[...]

    @pl.when(at_step == 4)
    def _():
        first.relay_near()

    @pl.when(at_step == 6)
    def _():
        first.relay_far()

    top[...] = jnp.full_like(top, mask_fill_value)
    total[...] = jnp.zeros_like(total)
    acc[...] = jnp.zeros_like(acc)
    query = q[0]
    begin = begin_row[:, pl.ds(pl.multiple_of(i * BLOCK, BLOCK), BLOCK)]

    def step(j, causal):
        at = pl.ds(pl.multiple_of(j * BLOCK, BLOCK), BLOCK)
        raw = lax.dot_general(k[at, :], query, NT, preferred_element_type=f32)
        ok = allowed_block(j * BLOCK, i * BLOCK, begin, causal)
        scores = jnp.where(ok, raw * factor, mask_fill_value)
        new_top = jnp.maximum(top[...], jnp.max(scores, axis=0, keepdims=True))
        weights = jnp.exp2(scores - new_top)
        keep = jnp.exp2(top[...] - new_top)
        total[...] = total[...] * keep + jnp.sum(weights, axis=0, keepdims=True)
        acc[...] = acc[...] * keep + jnp.dot(
            vt[:, at], weights.astype(bf16), preferred_element_type=f32
        )
        top[...] = new_top

    def loop(j, carry):
        step(j, False)
        return carry

    lax.fori_loop(0, i, loop, 0)
    step(i, True)
    out = (acc[...] / total[...]).T
    o[0] = out
    low[...] = out.astype(bf16)
    lse[0] = top[...] + jnp.log2(total[...])

    @pl.when(at_step == pl.num_programs(0) * pl.num_programs(1) - 1)
    def _():
        second.relay_near()
        first.finish()
        second.relay_far()
        second.finish()


def attend(n, m, factor, q, k, v, docs, wo, go, ident):
    heads, length, _ = q.shape
    blocks = length // BLOCK
    pairs = heads * BLOCK * BLOCK * blocks * (blocks + 1) // 2
    return pl.pallas_call(
        functools.partial(attend_body, n, m, factor),
        grid=(heads, blocks),
        out_shape=(
            jax.ShapeDtypeStruct((heads, length, LANES), f32),
            jax.ShapeDtypeStruct((length, heads * LANES), bf16),
            jax.ShapeDtypeStruct((heads, 1, length), f32),
            jax.ShapeDtypeStruct((1, length), jnp.int32),
            jax.ShapeDtypeStruct((n,) + wo.shape, wo.dtype),
            jax.ShapeDtypeStruct((n,) + go.shape, go.dtype),
        ),
        in_specs=[
            pl.BlockSpec((1, BLOCK, LANES), lambda h, i: (h, i, 0)),
            pl.BlockSpec((length, LANES), lambda h, i: (0, 0)),
            pl.BlockSpec((length, LANES), lambda h, i: (0, 0)),
            pl.BlockSpec((1, length), lambda h, i: (0, 0)),
            pl.BlockSpec(memory_space=ANY),
            pl.BlockSpec(memory_space=ANY),
        ],
        out_specs=[
            pl.BlockSpec((1, BLOCK, LANES), lambda h, i: (h, i, 0)),
            pl.BlockSpec((BLOCK, LANES), lambda h, i: (i, h)),
            pl.BlockSpec((1, 1, BLOCK), lambda h, i: (h, 0, i)),
            pl.BlockSpec((1, length), lambda h, i: (0, 0)),
            pl.BlockSpec(memory_space=ANY),
            pl.BlockSpec(memory_space=ANY),
        ],
        scratch_shapes=[
            pltpu.VMEM((LANES, length), bf16),
            pltpu.VMEM((1, BLOCK), f32),
            pltpu.VMEM((1, BLOCK), f32),
            pltpu.VMEM((LANES, BLOCK), f32),
            pltpu.VMEM((1, length), jnp.int32),
            pltpu.SemaphoreType.DMA((4, Gather.COPIES)),
            pltpu.SemaphoreType.DMA((2,)),
        ],
        compiler_params=pltpu.CompilerParams(collective_id=ident, has_side_effects=True),
        cost_estimate=pl.CostEstimate(
            flops=pairs * 4 * LANES * 3, transcendentals=pairs, bytes_accessed=120_000_000
        ),
        name="attend",
    )(q, k, v, docs, wo, go)


def attend_back_body(
    n, m, factor, scale, heads, q, k, v, go, o, lse, begin, cosine, sine, mixed, terms,
    out, mixed_sum, term_sum, kt, dqt, dk, dv, delta,
    pair, near, far, sr, lr, pair2, near2, far2, sr2, lr2,
):
    h = pl.program_id(0)
    j = pl.program_id(1)
    blocks = pl.num_programs(1)
    plane = Plane(n, m)
    one = Reduce(plane, lambda i: mixed.at[i], pair, near, far, sr, lr)
    two = Reduce(plane, lambda i: terms.at[i], pair2, near2, far2, sr2, lr2)
    at_step = h * blocks + j

    @pl.when(at_step == 0)
    def _():
        enter_plane(plane, False)
        one.start()

    @pl.when(at_step == 1)
    def _():
        one.send_to()
        two.start()

    @pl.when(at_step == 2)
    def _():
        one.ready()
        one.first(mixed_sum)

    @pl.when(at_step == 4)
    def _():
        one.send_fro()
        two.send_to()

    @pl.when(at_step == 5)
    def _():
        two.ready()
        two.first(term_sum)

    @pl.when((h == 0) & (j == 0))
    def _():
        kt[...] = k[...].T
        dk[...] = jnp.zeros_like(dk)
        dv[...] = jnp.zeros_like(dv)

    @pl.when(j == 0)
    def _():
        dqt[...] = jnp.zeros_like(dqt)

        def deltas(i, carry):
            at = pl.ds(pl.multiple_of(i * BLOCK, BLOCK), BLOCK)
            both = (go[at, :].astype(f32) * o[0, at, :]).T
            delta[:, at] = jnp.sum(both, axis=0, keepdims=True)
            return carry

        lax.fori_loop(0, blocks, deltas, 0)

    keys_at = pl.ds(pl.multiple_of(j * BLOCK, BLOCK), BLOCK)
    key = k[keys_at, :]
    value = v[keys_at, :]

    def step(i, causal):
        at = pl.ds(pl.multiple_of(i * BLOCK, BLOCK), BLOCK)
        query = q[0, at, :]
        raw = lax.dot_general(key, query, NT, preferred_element_type=f32)
        ok = allowed_block(j * BLOCK, i * BLOCK, begin[:, at], causal)
        probs = jnp.where(ok, jnp.exp2(raw * factor - lse[0, :, at]), 0.0)
        grads = go[at, :]
        dprob = lax.dot_general(value, grads, NT, preferred_element_type=f32)
        dscore = (probs * (dprob - delta[:, at])).astype(bf16)
        dv[keys_at, :] += jnp.dot(probs.astype(bf16), grads, preferred_element_type=f32)
        dk[keys_at, :] += jnp.dot(dscore, query, preferred_element_type=f32)
        dqt[:, at] += jnp.dot(kt[:, keys_at], dscore, preferred_element_type=f32)

    step(j, True)

    def loop(i, carry):
        step(i, False)
        return carry

    lax.fori_loop(j + 1, blocks, loop, 0)

    def unturn(value, at):
        return value * cosine[at, :] - pltpu.roll(value, SLOT, 1) * sine[at, :]

    @pl.when(j == blocks - 1)
    def _():
        def write(i, carry):
            at = pl.ds(pl.multiple_of(i * BLOCK, BLOCK), BLOCK)
            got = unturn(dqt[:, at].T * scale, at).astype(bf16)
            for which in range(heads):

                @pl.when(h == which)
                def _(which=which):
                    out[at, which * LANES : (which + 1) * LANES] = got

            return carry

        lax.fori_loop(0, blocks, write, 0)

    @pl.when((h == heads - 1) & (j == blocks - 1))
    def _():
        def write(i, carry):
            at = pl.ds(pl.multiple_of(i * BLOCK, BLOCK), BLOCK)
            out[at, heads * LANES : (heads + 1) * LANES] = unturn(dk[at, :] * scale, at).astype(
                bf16
            )
            out[at, (heads + 1) * LANES :] = dv[at, :].astype(bf16)
            return carry

        lax.fori_loop(0, blocks, write, 0)
        one.finish(mixed_sum)
        two.send_fro()
        two.finish(term_sum)


def attend_back(n, m, factor, scale, q, k, v, go, o, lse, begin, cosine, sine, mixed, terms, ident):
    heads, length, _ = q.shape
    blocks = length // BLOCK
    pairs = heads * BLOCK * BLOCK * blocks * (blocks + 1) // 2
    whole = pl.BlockSpec((length, LANES), lambda h, j: (0, 0))
    one = pl.BlockSpec((1, length, LANES), lambda h, j: (h, 0, 0))
    return pl.pallas_call(
        functools.partial(attend_back_body, n, m, factor, scale, heads),
        grid=(heads, blocks),
        out_shape=(
            jax.ShapeDtypeStruct((length, (heads + 2) * LANES), bf16),
            jax.ShapeDtypeStruct(mixed.shape[1:], f32),
            jax.ShapeDtypeStruct(terms.shape[1:], f32),
        ),
        in_specs=[
            one,
            whole,
            whole,
            pl.BlockSpec((length, LANES), lambda h, j: (0, h)),
            one,
            pl.BlockSpec((1, 1, length), lambda h, j: (h, 0, 0)),
            pl.BlockSpec((1, length), lambda h, j: (0, 0)),
            whole,
            whole,
            pl.BlockSpec(memory_space=ANY),
            pl.BlockSpec(memory_space=ANY),
        ],
        out_specs=[
            pl.BlockSpec((length, (heads + 2) * LANES), lambda h, j: (0, 0)),
            pl.BlockSpec(mixed.shape[1:], lambda h, j: (0, 0)),
            pl.BlockSpec(terms.shape[1:], lambda h, j: (0, 0)),
        ],
        scratch_shapes=[
            pltpu.VMEM((LANES, length), bf16),
            pltpu.VMEM((LANES, length), f32),
            pltpu.VMEM((length, LANES), f32),
            pltpu.VMEM((length, LANES), f32),
            pltpu.VMEM((1, length), f32),
        ]
        + Reduce.scratch(*mixed.shape[1:])
        + Reduce.scratch(*terms.shape[1:]),
        compiler_params=pltpu.CompilerParams(
            collective_id=ident, has_side_effects=True, vmem_limit_bytes=56 << 20
        ),
        cost_estimate=pl.CostEstimate(
            flops=pairs * 10 * LANES * 2, transcendentals=pairs, bytes_accessed=150_000_000
        ),
        name="attend_back",
    )(q, k, v, go, o, lse, begin, cosine, sine, mixed, terms)


def feed_body(
    n, m, mine, go, w_in, dnorm, grads, mixed,
    rows, rows_t, go_t, go_two, w, h, mix_two, pair, near, far, stage,
    sg, sr, loc, sw, so, sm, sd,
):
    plane = Plane(n, m)
    c, q = plane.c, plane.q
    tokens = rows.shape[1]
    hid = w_in.shape[3]
    enter_plane(plane, False)
    gather = Gather(plane, mine, rows, sg.at[0], sg.at[1], loc.at[0])
    reduce = Reduce(plane, None, pair, near, far, sr, None, stage)
    gather.start()
    weights = [
        pltpu.make_async_copy(
            w_in.at[t, j], w.at[j, :, t * hid : (t + 1) * hid], sw.at[j, t]
        )
        for j in range(3)
        for t in range(m)
    ]
    for copy in weights:
        copy.start()

    def number(it):
        k, other = it // 2, lax.rem(it, 2)
        low, high = lax.rem(k, 2), k // 2
        dx = low * (1 - c) + high * c
        dy = high * (1 - c) + low * c
        x, y = lax.rem(q, 2), q // 2
        chip = 2 * (y + dy - 2 * y * dy) + x + dx - 2 * x * dx
        return 2 * chip + c + other * (1 - 2 * c)

    def load_go(it, slot):
        return pltpu.make_async_copy(go.at[number(it)], go_two.at[slot], so.at[slot])

    def store_mix(it, slot):
        return pltpu.make_async_copy(mix_two.at[slot], mixed.at[number(it)], sm.at[slot])

    load_go(0, 0).start()
    gather.own.wait()
    for copy in weights:
        copy.wait()

    def blocks(it, carry):
        slot = lax.rem(it, 2)
        k = it // 2
        b = number(it)

        @pl.when(it == 1)
        def _():
            gather.swap.wait_recv()

        @pl.when(it == 2)
        def _():
            gather.relay_near()

        @pl.when(it == 3)
        def _():
            gather.share[1].wait_recv()

        @pl.when(it == 5)
        def _():
            gather.share[0].wait_recv()

        @pl.when(it == 6)
        def _():
            reduce.join(1)
            reduce.out[1].start()
            gather.relay_far()

        @pl.when(it == 7)
        def _():
            gather.share[2].wait_recv()

        @pl.when(it < n - 1)
        def _():
            load_go(it + 1, 1 - slot).start()

        load_go(it, slot).wait()

        @pl.when(it >= 2)
        def _():
            store_mix(it - 2, slot).wait()

        here = pl.ds(pl.multiple_of(b * tokens, tokens), tokens)
        row = rows[b]
        gate = jnp.dot(row, w[0], preferred_element_type=f32)
        up = jnp.dot(row, w[1], preferred_element_type=f32)
        grad = go_two[slot]
        dhidden = jnp.dot(grad, w[2], preferred_element_type=f32)
        sig = jax.nn.sigmoid(gate)
        act = gate * sig
        hidden = (act * up).astype(bf16)
        dgate = (dhidden * up * sig * (1.0 + gate * (1.0 - sig))).astype(bf16)
        dup = (dhidden * act).astype(bf16)
        h[0, here, :] = dgate
        h[1, here, :] = dup
        h[2, here, :] = hidden
        part = lax.dot_general(dgate, w[0], NT, preferred_element_type=f32)
        part = part + lax.dot_general(dup, w[1], NT, preferred_element_type=f32)
        part = part.astype(bf16)

        @pl.when(lax.rem(it, 2) == 0)
        def _():
            pair[k] = part

        @pl.when(lax.rem(it, 2) == 1)
        def _():
            stage[k] = part

        for kk in range(4):

            @pl.when(it == 2 * kk + 1)
            def _(kk=kk):
                reduce.swaps[Reduce.THEIRS[kk]].start()

        mix_two[slot] = lax.dot_general(hidden, w[2], NT, preferred_element_type=f32).astype(bf16)
        store_mix(it, slot).start()
        rows_t[:, here] = row.T
        go_t[:, here] = grad.T
        return carry

    lax.fori_loop(0, n, blocks, 0)
    reduce.join(3)
    reduce.out[0].start()
    width = rows.shape[2]

    def weight_grad(j, left):
        def part(i, carry):
            at = pl.ds(pl.multiple_of(i * 256, 256), 256)
            value = jnp.dot(left[at, :], h[j], preferred_element_type=f32)
            w[j, at, :] = value.astype(bf16)
            return carry

        lax.fori_loop(0, width // 256, part, 0)
        outs = [
            pltpu.make_async_copy(
                w.at[j, :, t * hid : (t + 1) * hid], grads.at[t, j], sd.at[j, t]
            )
            for t in range(m)
        ]
        for copy in outs:
            copy.start()
        return outs

    outs = weight_grad(0, rows_t)
    reduce.ready()
    reduce.first(dnorm)
    reduce.send_fro()
    outs += weight_grad(1, rows_t)
    outs += weight_grad(2, go_t)
    gather.swap.wait_send()
    gather.ahead.wait_send()
    gather.back.wait_send()
    gather.relay.wait_send()
    for copy in gather.share:
        copy.wait_send()
    store_mix(n - 2, 0).wait()
    store_mix(n - 1, 1).wait()
    reduce.finish(dnorm)
    for copy in outs:
        copy.wait()


def feed(n, m, norm, go, w_in, ident):
    tokens, width = norm.shape
    hid = w_in.shape[3]
    length = n * tokens
    block = pltpu.VMEM((n, tokens, width), bf16)
    return pl.pallas_call(
        functools.partial(feed_body, n, m),
        out_shape=(
            jax.ShapeDtypeStruct((tokens, width), f32),
            jax.ShapeDtypeStruct(w_in.shape, bf16),
            jax.ShapeDtypeStruct((n, tokens, width), bf16),
        ),
        in_specs=[pl.BlockSpec(memory_space=ANY)] * 3,
        out_specs=[
            pl.BlockSpec(memory_space=pltpu.VMEM),
            pl.BlockSpec(memory_space=ANY),
            pl.BlockSpec(memory_space=ANY),
        ],
        scratch_shapes=[
            block,
            pltpu.VMEM((width, length), bf16),
            pltpu.VMEM((width, length), bf16),
            pltpu.VMEM((2, tokens, width), bf16),
            pltpu.VMEM((3, width, m * hid), bf16),
            pltpu.VMEM((3, length, m * hid), bf16),
            pltpu.VMEM((2, tokens, width), bf16),
        ]
        + [pltpu.VMEM((slots, tokens, width), bf16) for slots in Reduce.SLOTS]
        + [
            pltpu.VMEM((4, tokens, width), bf16),
            pltpu.SemaphoreType.DMA((2, Gather.COPIES)),
            pltpu.SemaphoreType.DMA((4, 4)),
            pltpu.SemaphoreType.DMA((1,)),
            pltpu.SemaphoreType.DMA((3, m)),
            pltpu.SemaphoreType.DMA((2,)),
            pltpu.SemaphoreType.DMA((2,)),
            pltpu.SemaphoreType.DMA((3, m)),
        ],
        compiler_params=pltpu.CompilerParams(
            collective_id=ident, has_side_effects=True, vmem_limit_bytes=60 << 20
        ),
        cost_estimate=pl.CostEstimate(
            flops=18 * length * width * m * hid,
            transcendentals=length * m * hid,
            bytes_accessed=60_000_000,
        ),
        name="feed",
    )(norm, go, w_in)


def split_heads(w, groups):
    rows = w.shape[0]
    return w.reshape(rows, groups, -1).transpose(1, 0, 2)


def spread(blocks):
    lead = blocks.shape[:-1]
    halves = blocks.reshape(lead + (-1, HALF))
    pad = [(0, 0)] * len(lead) + [(0, 0), (0, SLOT - HALF)]
    wide = jnp.pad(halves, pad)
    return wide.reshape(lead + (-1,))


def gathered(wide):
    lead = wide.shape[:-1]
    halves = wide.reshape(lead + (-1, SLOT))[..., :HALF]
    return halves.reshape(lead + (-1,))


def fast_layer(n, m):
    def on_plane(
        layer_input,
        doc_ids,
        positions,
        first_gain,
        query_weight,
        key_weight,
        value_weight,
        output_weight,
        second_gain,
        gate_weight,
        up_weight,
        down_weight,
        out_grad,
    ):
        x = layer_input[0]
        rows, width = x.shape
        length = rows * n
        heads = QUERY_HEADS // n
        scale = 1.0 / math.sqrt(HEAD_SIZE)
        factor = scale * LOG2E
        strip = query_weight.shape[0]
        hid = gate_weight.shape[1] // n

        packed = spread(
            jnp.concatenate(
                [split_heads(w, n) for w in (query_weight, key_weight, value_weight)], axis=2
            )
        )
        wide = packed.shape[2]
        gains = jnp.pad(
            jnp.stack([first_gain, second_gain]), ((0, 6), (0, LANES - strip))
        )
        places = jnp.concatenate([doc_ids, positions], axis=0)
        x_all, places_all, w_all, gains_all = entry(n, m, x, places, packed, gains)
        docs = places_all[:, 0].reshape(1, length)
        wqkv = w_all.reshape(width, wide)
        gain_one, gain_two = [
            gains_all[:, :, i, :strip].reshape(1, width).astype(f32) for i in range(2)
        ]
        lane = jnp.arange(LANES) % SLOT
        inverse = jnp.where(
            lane < HALF, rope_base ** (-(lane.astype(f32) * 2.0 / HEAD_SIZE)), 0.0
        )[None]

        norm_one, q, k, v, cosine, sine, ffn_mine, output_rows = project(
            n, m, heads, x_all, gain_one, wqkv, places_all, inverse,
            gate_weight, up_weight, down_weight, output_weight, 8,
        )
        ffn_all = lax.all_gather(ffn_mine, "tp", axis=0, tiled=False)
        o, low, lse, begin, output_full, grad_all = attend(
            n, m, factor, q, k, v, docs, output_rows.reshape(m * strip, width), out_grad[0], 9
        )
        output_full = output_full.reshape(-1, width)
        (mine,) = plane_swap(n, m, 1, low.reshape(n, rows, heads * LANES))
        attn_low = gathered(mine.transpose(1, 0, 2).reshape(rows, n * heads * LANES))

        x_f = x.astype(f32)
        resid = x_f + jnp.dot(attn_low, output_full, preferred_element_type=f32)
        scale_two = lax.rsqrt(jnp.mean(resid * resid, axis=1, keepdims=True) + norm_epsilon)
        norm_two = (resid * scale_two * gain_two).astype(bf16)
        grad_low = out_grad[0]
        dnorm_two, ffn_terms, mixed = feed(n, m, norm_two, grad_all, ffn_all, 2)
        ffn_sum = lax.psum_scatter(ffn_terms, "tp", scatter_dimension=0, tiled=False)

        inner = gain_two * dnorm_two
        moment = jnp.mean(resid * inner, axis=1, keepdims=True)
        dresid = (
            grad_low.astype(f32)
            + scale_two * inner
            - resid * scale_two * scale_two * scale_two * moment
        )
        dbranch = dresid.astype(bf16)
        output_term = outer_product(attn_low, dbranch).astype(bf16).reshape(n, m * strip, width)
        dheads = spread(times_transpose(dbranch, output_full).astype(bf16))
        dheads = dheads.reshape(rows, n, heads * LANES).transpose(1, 0, 2)
        gain_term = jnp.sum(dnorm_two * resid * scale_two, axis=0)
        go, gain_parts = plane_swap(n, m, 5, dheads, gain_term.reshape(n, 1, m * strip))
        go = go.reshape(length, heads * LANES)
        gain_part = jnp.sum(gain_parts, axis=(0, 1)).reshape(m, 1, strip)

        dqkv, mixed_sum, output_sum = attend_back(
            n, m, factor, scale, q, k, v, go, o, lse, begin, cosine, sine, mixed, output_term, 3
        )
        layer_output = (resid + mixed_sum).astype(bf16)[None]
        output_grad = lax.psum_scatter(
            output_sum.astype(bf16), "tp", scatter_dimension=0, tiled=True
        ).astype(f32)
        dnorm_one_part = times_transpose(dqkv, wqkv).astype(bf16)
        qkv_term = gathered(outer_product(norm_one, dqkv).astype(bf16))
        cols = qkv_term.shape[1]
        qkv_term = qkv_term.reshape(n, m, strip, cols).transpose(1, 0, 2, 3)
        dnorm_one, ffn_out, qkv_out, gain_sums = last(
            n, m, dnorm_one_part.reshape(n, rows, width), ffn_sum, qkv_term, gain_part, 6
        )

        scale_one = lax.rsqrt(jnp.mean(x_f * x_f, axis=1, keepdims=True) + norm_epsilon)
        inner = gain_one * dnorm_one
        moment = jnp.mean(x_f * inner, axis=1, keepdims=True)
        input_grad = (
            dresid + scale_one * inner - x_f * scale_one * scale_one * scale_one * moment
        )[None]

        gate_grad, up_grad, down_grad = [ffn_out[i].astype(f32) for i in range(3)]
        kv = HEAD_SIZE * KEY_VALUE_HEADS // n
        split = heads * HEAD_SIZE

        def columns(a, b):
            return qkv_out[:, :, a:b].transpose(1, 0, 2).reshape(strip, -1).astype(f32)

        query_grad = columns(0, split)
        key_grad = columns(split, split + kv)
        value_grad = columns(split + kv, cols)

        one = (
            jnp.sum(query_weight.astype(f32) * query_grad, axis=1)
            + jnp.sum(key_weight.astype(f32) * key_grad, axis=1)
            + jnp.sum(value_weight.astype(f32) * value_grad, axis=1)
        )
        first_gain_grad = one / first_gain.astype(f32)
        second_gain_grad = jnp.sum(gain_sums, axis=(0, 1))
        return (
            layer_output,
            input_grad,
            first_gain_grad,
            query_grad,
            key_grad,
            value_grad,
            output_grad,
            second_gain_grad,
            gate_grad,
            up_grad,
            down_grad,
        )

    return on_plane


def solution(mesh):
    n, m = mesh.shape["seq"], mesh.shape["tp"]
    fits = n == KEY_VALUE_HEADS == 8
    return jax.shard_map(
        fast_layer(n, m) if fits else on_device,
        mesh=mesh,
        in_specs=(
            P("tp", "seq", None),
            P("tp", "seq"),
            P("tp", "seq"),
            P(("seq", "tp")),
            P(("seq", "tp"), None),
            P(("seq", "tp"), None),
            P(("seq", "tp"), None),
            P(("seq", "tp"), None),
            P(("seq", "tp")),
            P("seq", "tp"),
            P("seq", "tp"),
            P("seq", "tp"),
            P("tp", "seq", None),
        ),
        out_specs=(
            P("tp", "seq", None),
            P("tp", "seq", None),
            P(("seq", "tp")),
            P(("seq", "tp"), None),
            P(("seq", "tp"), None),
            P(("seq", "tp"), None),
            P(("seq", "tp"), None),
            P(("seq", "tp")),
            P("seq", "tp"),
            P("seq", "tp"),
            P("seq", "tp"),
        ),
        check_vma=False,
    )
```

```python
import functools
import math

import jax
import jax.numpy as jnp
from jax import lax
from jax.experimental import pallas as pl
from jax.experimental.pallas import tpu as pltpu
from jax.sharding import PartitionSpec as P

QUERY_HEADS = 16
KEY_VALUE_HEADS = 8
HEAD_SIZE = 96


norm_epsilon = 1e-05
rope_base = 100000.0
mask_fill_value = -1e30


def rope_tables(places):
    half = HEAD_SIZE // 2
    inverse = rope_base ** (-(jnp.arange(half, dtype=jnp.float32) * 2.0 / HEAD_SIZE))
    angles = places.astype(jnp.float32)[:, None] * inverse[None, :]
    return (jnp.cos(angles), jnp.sin(angles))


def apply_rotary(value_rows, cosine_table, sine_table, heads, direction):
    sequence_length = value_rows.shape[0]
    split = value_rows.reshape(sequence_length, heads, 2, HEAD_SIZE // 2)
    first = split[:, :, 0]
    second = split[:, :, 1]
    cosine = cosine_table[:, None, :]
    sine = direction * sine_table[:, None, :]
    turned = jnp.stack([first * cosine - second * sine, second * cosine + first * sine], axis=2)
    return turned.reshape(sequence_length, heads * HEAD_SIZE)


def outer_product(left, right):
    return lax.dot_general(
        left, right, (((0,), (0,)), ((), ())), preferred_element_type=jnp.float32
    )


def times_transpose(left, right):
    return lax.dot_general(
        left, right, (((1,), (1,)), ((), ())), preferred_element_type=jnp.float32
    )


def norm_backward(inputs, scale, gain, upstream):
    inner = gain * upstream
    moment = jnp.mean(inputs * inner, axis=1, keepdims=True)
    return (
        scale * inner - inputs * scale * scale * scale * moment,
        jnp.sum(upstream * inputs * scale, axis=0),
    )


def on_device(
    layer_input,
    doc_ids,
    positions,
    first_gain,
    query_weight,
    key_weight,
    value_weight,
    output_weight,
    second_gain,
    gate_weight,
    up_weight,
    down_weight,
    out_grad,
):
    token_rows = layer_input.shape[1]
    query_groups = QUERY_HEADS // KEY_VALUE_HEADS
    scale_of_scores = 1.0 / math.sqrt(HEAD_SIZE)
    inputs_f = layer_input[0].astype(jnp.float32)
    my_docs = doc_ids[0]
    gain_one, query_full, complete_keys, value_full, output_full, gain_two = (
        lax.all_gather(first_gain, ("seq", "tp"), axis=0, tiled=True),
        lax.all_gather(query_weight, ("seq", "tp"), axis=0, tiled=True),
        lax.all_gather(key_weight, ("seq", "tp"), axis=0, tiled=True),
        lax.all_gather(value_weight, ("seq", "tp"), axis=0, tiled=True),
        lax.all_gather(output_weight, ("seq", "tp"), axis=0, tiled=True),
        lax.all_gather(second_gain, ("seq", "tp"), axis=0, tiled=True),
    )
    gain_one_f = gain_one.astype(jnp.float32)
    gain_two_f = gain_two.astype(jnp.float32)
    scale_one = lax.rsqrt(jnp.mean(inputs_f * inputs_f, axis=1, keepdims=True) + norm_epsilon)
    first_normalized = (inputs_f * scale_one * gain_one_f).astype(jnp.bfloat16)
    cosine_table, sine_table = rope_tables(positions[0])
    rotated_query = apply_rotary(
        jnp.dot(first_normalized, query_full, preferred_element_type=jnp.float32),
        cosine_table,
        sine_table,
        QUERY_HEADS,
        1.0,
    ).astype(jnp.bfloat16)
    key_rot = apply_rotary(
        jnp.dot(first_normalized, complete_keys, preferred_element_type=jnp.float32),
        cosine_table,
        sine_table,
        KEY_VALUE_HEADS,
        1.0,
    ).astype(jnp.bfloat16)
    value_low = jnp.dot(first_normalized, value_full, preferred_element_type=jnp.float32).astype(
        jnp.bfloat16
    )
    gathered_keys, gathered_values, doc_all = (
        lax.all_gather(key_rot, "seq", axis=0, tiled=True),
        lax.all_gather(value_low, "seq", axis=0, tiled=True),
        lax.all_gather(my_docs.astype(jnp.bfloat16), "seq", axis=0, tiled=True),
    )
    sequence_length = gathered_keys.shape[0]
    block_number = math.gcd(512, sequence_length)
    block_count = sequence_length // block_number
    query_index = lax.axis_index("seq") * token_rows + jnp.arange(token_rows, dtype=jnp.int32)
    my_doc_f = my_docs.astype(jnp.float32)
    heads_of_query = rotated_query.reshape(token_rows, KEY_VALUE_HEADS, query_groups, HEAD_SIZE)
    layer_entries = (
        gathered_keys.reshape(block_count, block_number, KEY_VALUE_HEADS, HEAD_SIZE),
        gathered_values.reshape(block_count, block_number, KEY_VALUE_HEADS, HEAD_SIZE),
        doc_all.astype(jnp.float32).reshape(block_count, block_number),
        jnp.arange(block_count, dtype=jnp.int32) * block_number,
    )

    def allowed_of(doc_piece, start):
        key_index = start + jnp.arange(block_number, dtype=jnp.int32)
        return (key_index[None, :] <= query_index[:, None]) & (
            doc_piece[None, :] == my_doc_f[:, None]
        )

    def scores_of(key_piece, allowed):
        raw = (
            jnp.einsum(
                "tgrd,kgd->tgrk", heads_of_query, key_piece, preferred_element_type=jnp.float32
            )
            * scale_of_scores
        )
        return jnp.where(allowed[:, None, None, :], raw, mask_fill_value)

    def total_step(carry, item):
        key_piece, value_piece, doc_piece, start = item
        allowed = allowed_of(doc_piece, start)

        def total_work(state):
            top, total = state
            scores = scores_of(key_piece, allowed)
            new_top = jnp.maximum(top, jnp.max(scores, axis=3))
            weights = jnp.where(
                allowed[:, None, None, :], jnp.exp(scores - new_top[..., None]), 0.0
            )
            return (new_top, total * jnp.exp(top - new_top) + jnp.sum(weights, axis=3))

        return (lax.cond(jnp.any(allowed), total_work, lambda state: state, carry), None)

    start_state = (
        jnp.full((token_rows, KEY_VALUE_HEADS, query_groups), mask_fill_value, jnp.float32),
        jnp.zeros((token_rows, KEY_VALUE_HEADS, query_groups), jnp.float32),
    )
    (top, total), unused_result = lax.scan(total_step, start_state, layer_entries)
    log_total = top + jnp.log(total)

    def probs_of(key_piece, allowed):
        scores = scores_of(key_piece, allowed)
        return jnp.where(allowed[:, None, None, :], jnp.exp(scores - log_total[..., None]), 0.0)

    def output_update(accum, item):
        key_piece, value_piece, doc_piece, start = item
        allowed = allowed_of(doc_piece, start)

        def output_work(state):
            probs = probs_of(key_piece, allowed).astype(jnp.bfloat16)
            return state + jnp.einsum(
                "tgrk,kgd->tgrd", probs, value_piece, preferred_element_type=jnp.float32
            )

        return (lax.cond(jnp.any(allowed), output_work, lambda state: state, accum), None)

    heads_output, unused_result = lax.scan(
        output_update,
        jnp.zeros((token_rows, KEY_VALUE_HEADS, query_groups, HEAD_SIZE), jnp.float32),
        layer_entries,
    )
    attn_low = heads_output.reshape(token_rows, QUERY_HEADS * HEAD_SIZE).astype(jnp.bfloat16)
    resid = inputs_f + jnp.dot(attn_low, output_full, preferred_element_type=jnp.float32)
    scale_two = lax.rsqrt(jnp.mean(resid * resid, axis=1, keepdims=True) + norm_epsilon)
    normed_two = (resid * scale_two * gain_two_f).astype(jnp.bfloat16)
    rows_all = lax.all_gather(normed_two, "tp", axis=0, tiled=True)
    gate_cols, up_cols, down_cols = (
        lax.all_gather(gate_weight, "seq", axis=0, tiled=True),
        lax.all_gather(up_weight, "seq", axis=0, tiled=True),
        lax.all_gather(down_weight, "seq", axis=0, tiled=True),
    )
    gate_pre = jnp.dot(rows_all, gate_cols, preferred_element_type=jnp.float32)
    up_pre = jnp.dot(rows_all, up_cols, preferred_element_type=jnp.float32)
    gate_sig = jax.nn.sigmoid(gate_pre)
    gate_act = gate_pre * gate_sig
    hidden = (gate_act * up_pre).astype(jnp.bfloat16)
    mixed = lax.psum_scatter(
        times_transpose(hidden, down_cols).astype(jnp.bfloat16),
        "tp",
        scatter_dimension=0,
        tiled=True,
    ).astype(jnp.float32)
    layer_output = (resid + mixed).astype(jnp.bfloat16)[None]
    grad_low = out_grad[0]
    grad_f = grad_low.astype(jnp.float32)
    grad_all = lax.all_gather(grad_low, "tp", axis=0, tiled=True)
    dhidden = jnp.dot(grad_all, down_cols, preferred_element_type=jnp.float32)
    dgate = (dhidden * up_pre * gate_sig * (1.0 + gate_pre * (1.0 - gate_sig))).astype(jnp.bfloat16)
    dup = (dhidden * gate_act).astype(jnp.bfloat16)
    gate_term = outer_product(rows_all, dgate)
    up_term = outer_product(rows_all, dup)
    down_term_grad = outer_product(grad_all, hidden)
    dnorm_two = lax.psum_scatter(
        (times_transpose(dgate, gate_cols) + times_transpose(dup, up_cols)).astype(jnp.bfloat16),
        "tp",
        scatter_dimension=0,
        tiled=True,
    ).astype(jnp.float32)
    gate_grad, up_grad, down_grad = (
        lax.psum_scatter(
            gate_term.astype(jnp.bfloat16), "seq", scatter_dimension=0, tiled=True
        ).astype(jnp.float32),
        lax.psum_scatter(
            up_term.astype(jnp.bfloat16), "seq", scatter_dimension=0, tiled=True
        ).astype(jnp.float32),
        lax.psum_scatter(
            down_term_grad.astype(jnp.bfloat16), "seq", scatter_dimension=0, tiled=True
        ).astype(jnp.float32),
    )
    resid_part, gain_two_term = norm_backward(resid, scale_two, gain_two_f, dnorm_two)
    dresid = grad_f + resid_part
    dbranch = dresid.astype(jnp.bfloat16)
    output_term = outer_product(attn_low, dbranch)
    heads_gradient = times_transpose(dbranch, output_full).astype(jnp.bfloat16)
    grouped_heads_gradient = heads_gradient.reshape(
        token_rows, KEY_VALUE_HEADS, query_groups, HEAD_SIZE
    )
    delta = jnp.sum(grouped_heads_gradient.astype(jnp.float32) * heads_output, axis=3)

    def gradient_update(dquery, item):
        key_piece, value_piece, doc_piece, start = item
        allowed = allowed_of(doc_piece, start)

        def gradient_work(state):
            probs = probs_of(key_piece, allowed)
            value_piece_grad = jnp.einsum(
                "tgrk,tgrd->kgd",
                probs.astype(jnp.bfloat16),
                grouped_heads_gradient,
                preferred_element_type=jnp.float32,
            )
            prob_grad = jnp.einsum(
                "tgrd,kgd->tgrk",
                grouped_heads_gradient,
                value_piece,
                preferred_element_type=jnp.float32,
            )
            score_grad = (probs * (prob_grad - delta[..., None])).astype(jnp.bfloat16)
            key_piece_grad = jnp.einsum(
                "tgrk,tgrd->kgd", score_grad, heads_of_query, preferred_element_type=jnp.float32
            )
            updated = state + jnp.einsum(
                "tgrk,kgd->tgrd", score_grad, key_piece, preferred_element_type=jnp.float32
            )
            return (updated, (key_piece_grad, value_piece_grad))

        def skip(state):
            blank_tensor = jnp.zeros((block_number, KEY_VALUE_HEADS, HEAD_SIZE), jnp.float32)
            return (state, (blank_tensor, blank_tensor))

        return lax.cond(jnp.any(allowed), gradient_work, skip, dquery)

    dquery, (key_contributions, value_contributions) = lax.scan(
        gradient_update,
        jnp.zeros((token_rows, KEY_VALUE_HEADS, query_groups, HEAD_SIZE), jnp.float32),
        layer_entries,
    )
    gathered_key_contributions = (
        key_contributions.reshape(sequence_length, KEY_VALUE_HEADS * HEAD_SIZE) * scale_of_scores
    )
    gathered_value_contributions = value_contributions.reshape(
        sequence_length, KEY_VALUE_HEADS * HEAD_SIZE
    )
    local_keys, value_mine = (
        lax.psum_scatter(
            gathered_key_contributions.astype(jnp.bfloat16), "seq", scatter_dimension=0, tiled=True
        ).astype(jnp.float32),
        lax.psum_scatter(
            gathered_value_contributions.astype(jnp.bfloat16),
            "seq",
            scatter_dimension=0,
            tiled=True,
        ).astype(jnp.float32),
    )
    dq_pre = apply_rotary(
        dquery.reshape(token_rows, QUERY_HEADS * HEAD_SIZE) * scale_of_scores,
        cosine_table,
        sine_table,
        QUERY_HEADS,
        -1.0,
    ).astype(jnp.bfloat16)
    key_gradient_unrotated = apply_rotary(
        local_keys, cosine_table, sine_table, KEY_VALUE_HEADS, -1.0
    ).astype(jnp.bfloat16)
    dv_pre = value_mine.astype(jnp.bfloat16)
    dnorm_one = (
        times_transpose(dq_pre, query_full)
        + times_transpose(key_gradient_unrotated, complete_keys)
        + times_transpose(dv_pre, value_full)
    )
    input_part, gain_one_term = norm_backward(inputs_f, scale_one, gain_one_f, dnorm_one)
    input_grad = (dresid + input_part)[None]
    query_term = outer_product(first_normalized, dq_pre)
    key_term = outer_product(first_normalized, key_gradient_unrotated)
    value_term = outer_product(first_normalized, dv_pre)
    first_gain_grad, query_grad, key_grad, value_grad, output_grad, second_gain_grad = (
        lax.psum_scatter(gain_one_term, ("seq", "tp"), scatter_dimension=0, tiled=True),
        lax.psum_scatter(query_term, ("seq", "tp"), scatter_dimension=0, tiled=True),
        lax.psum_scatter(key_term, ("seq", "tp"), scatter_dimension=0, tiled=True),
        lax.psum_scatter(value_term, ("seq", "tp"), scatter_dimension=0, tiled=True),
        lax.psum_scatter(output_term, ("seq", "tp"), scatter_dimension=0, tiled=True),
        lax.psum_scatter(gain_two_term, ("seq", "tp"), scatter_dimension=0, tiled=True),
    )
    return (
        layer_output,
        input_grad,
        first_gain_grad,
        query_grad,
        key_grad,
        value_grad,
        output_grad,
        second_gain_grad,
        gate_grad,
        up_grad,
        down_grad,
    )


MESH = pl.DeviceIdType.MESH
ANY = pl.ANY
HALF = HEAD_SIZE // 2
LANES = 128
SLOT = LANES // 2
f32 = jnp.float32
bf16 = jnp.bfloat16
COST = pl.CostEstimate(flops=1_000_000, transcendentals=0, bytes_accessed=100_000)


class Plane:
    def __init__(self, n, m):
        self.n, self.m, self.chips = n, m, n // 2
        self.s = lax.axis_index("seq")
        self.t = lax.axis_index("tp")
        self.q = self.s // 2
        self.c = lax.rem(self.s, 2)

        across = self.q + 1 - 2 * lax.rem(self.q, 2)
        along = lax.rem(self.q + 2, 4)
        self.to = across * (1 - self.c) + along * self.c
        self.fro = across * self.c + along * (1 - self.c)
        self.far = 3 - self.q
        self.order = (self.q, self.to, self.fro, self.far)

    def device(self, s):
        return (s, self.t)

    def same(self, chip):
        return (2 * chip + self.c, self.t)

    def number(self, k, other):
        c, q = self.c, self.q
        low, high = lax.rem(k, 2), k // 2
        dx = low * (1 - c) + high * c
        dy = high * (1 - c) + low * c
        x, y = lax.rem(q, 2), q // 2
        chip = 2 * (y + dy - 2 * y * dy) + x + dx - 2 * x * dx
        return 2 * chip + c + other * (1 - 2 * c)

    def sibling(self):
        return (2 * self.q + 1 - self.c, self.t)

    def ahead(self, k):
        return lax.rem(self.q + k, self.chips)

    def behind(self, k):
        return lax.rem(self.q + self.chips - k, self.chips)

    def seq_ahead(self, k):
        return lax.rem(self.s + k, self.n)

    def seq_behind(self, k):
        return lax.rem(self.s + self.n - k, self.n)

    def tp_ahead(self, k):
        return (self.s, lax.rem(self.t + k, self.m))

    def tp_behind(self, k):
        return lax.rem(self.t + self.m - k, self.m)


def enter_plane(plane, with_tp):
    barrier = pltpu.get_barrier_semaphore()
    for k in range(1, plane.n):
        pl.semaphore_signal(
            barrier, inc=1, device_id=plane.device(plane.seq_ahead(k)), device_id_type=MESH
        )
    count = plane.n - 1
    if with_tp:
        for k in range(1, plane.m):
            pl.semaphore_signal(barrier, inc=1, device_id=plane.tp_ahead(k), device_id_type=MESH)
        count += plane.m - 1
    pl.semaphore_wait(barrier, count)


def remote(src, dst, send, recv, device):
    return pltpu.make_async_remote_copy(
        src_ref=src,
        dst_ref=dst,
        send_sem=send,
        recv_sem=recv,
        device_id=device,
        device_id_type=MESH,
    )


class Gather:
    COPIES = 7

    def __init__(self, plane, src, dst, send, recv, local):
        to, fro, far, c = plane.to, plane.fro, plane.far, plane.c
        here = dst.at[plane.s]
        self.own = pltpu.make_async_copy(src, here, local)

        def block(chip):
            return dst.at[2 * chip + c]

        def copy(i, a, b, device):
            return remote(a, b, send.at[i], recv.at[i], device)

        sibling = plane.sibling()
        self.swap = copy(0, src, here, sibling)
        self.ahead = copy(1, src, here, plane.same(to))
        self.back = copy(2, src, here, plane.same(fro))
        self.relay = copy(3, block(fro), block(fro), plane.same(to))
        self.share = [
            copy(4, block(to), block(to), sibling),
            copy(5, block(fro), block(fro), sibling),
            copy(6, block(far), block(far), sibling),
        ]

    def start(self):
        self.back.start()
        self.ahead.start()
        self.swap.start()
        self.own.start()

    def relay_near(self):
        self.back.wait_recv()
        self.relay.start()
        self.share[1].start()
        self.ahead.wait_recv()
        self.share[0].start()

    def relay_far(self):
        self.relay.wait_recv()
        self.share[2].start()

    def finish(self):
        self.own.wait()
        self.swap.wait()
        self.ahead.wait_send()
        self.back.wait_send()
        self.relay.wait_send()
        for copy in self.share:
            copy.wait()

    def run(self):
        self.start()
        self.relay_near()
        self.relay_far()
        self.finish()


def fan(plane, src_of, dst_of, send, recv):
    copies = []
    for k in range(1, plane.m):
        device = plane.tp_ahead(k)
        copies.append(
            remote(src_of(device[1]), dst_of(plane.t), send.at[k - 1], recv.at[k - 1], device)
        )
    return copies


def exchange(plane, src_of, dst_of, send, recv, local):
    own = pltpu.make_async_copy(src_of(plane.s), dst_of(plane.s), local)
    copies = []
    for k in range(1, plane.n):
        peer = plane.seq_ahead(k)
        copies.append(
            remote(
                src_of(peer), dst_of(plane.s), send.at[k - 1], recv.at[k - 1], plane.device(peer)
            )
        )
    return [own] + copies


def swap_body(n, m, count, *refs):
    plane = Plane(n, m)
    enter_plane(plane, False)
    sems, loc = refs[2 * count :]
    copies = []
    for i in range(count):
        src, dst = refs[i], refs[count + i]
        copies += exchange(
            plane,
            lambda k, src=src: src.at[k],
            lambda k, dst=dst: dst.at[k],
            sems.at[i, 0],
            sems.at[i, 1],
            loc.at[i],
        )
    for copy in copies:
        copy.start()
    for copy in copies:
        copy.wait()


def plane_swap(n, m, ident, *arrays):
    count = len(arrays)
    return pl.pallas_call(
        functools.partial(swap_body, n, m, count),
        out_shape=tuple(jax.ShapeDtypeStruct(a.shape, a.dtype) for a in arrays),
        in_specs=[pl.BlockSpec(memory_space=ANY)] * count,
        out_specs=[pl.BlockSpec(memory_space=ANY)] * count,
        scratch_shapes=[
            pltpu.SemaphoreType.DMA((count, 2, n - 1)),
            pltpu.SemaphoreType.DMA((count,)),
        ],
        compiler_params=pltpu.CompilerParams(collective_id=ident, has_side_effects=True),
        cost_estimate=COST,
        name="plane_swap",
    )(*arrays)


TILE = 16


def in_tiles(rows, body):
    def one(i, carry):
        body(pl.ds(pl.multiple_of(i * TILE, TILE), TILE))
        return carry

    lax.fori_loop(0, rows // TILE, one, 0)


class Reduce:
    SLOTS = (4, 4, 3)

    THEIRS = (0, 2, 1, 3)

    def __init__(self, plane, part_of, pair, near, far, sems, loc, stage=None):
        c = plane.c
        self.pair, self.near, self.far = pair, near, far
        self.rows = pair.shape[1]
        self.swaps, self.loads = {}, {}
        for k in range(4):
            mine = self.THEIRS[k]
            chip = plane.order[mine]
            source = part_of(2 * chip + 1 - c) if stage is None else stage.at[mine]
            self.swaps[k] = remote(
                source, near.at[k], sems.at[0, k], sems.at[1, k], plane.sibling()
            )
            if stage is None:
                self.loads[k] = pltpu.make_async_copy(
                    part_of(2 * plane.order[k] + c), pair.at[k], loc.at[k]
                )

        def out(i, k, chip):
            return remote(
                pair.at[k], far.at[i], sems.at[2, i], sems.at[3, i], plane.same(chip)
            )

        self.out = [out(0, 3, plane.to), out(1, 1, plane.to), out(2, 2, plane.fro)]

    def start(self):
        for k in (3, 1, 2, 0):
            self.swaps[k].start()
            self.loads[k].start()

    def landed(self, k):
        self.swaps[k].wait()
        if self.loads:
            self.loads[k].wait()

    def join(self, k):
        pair, near = self.pair, self.near
        self.landed(k)

        def add(at):
            both = pair[k, at, :].astype(f32) + near[k, at, :].astype(f32)
            pair[k, at, :] = both.astype(bf16)

        in_tiles(self.rows, add)

    def send_to(self):
        self.join(3)
        self.out[0].start()
        self.join(1)
        self.out[1].start()

    def ready(self):
        self.landed(2)

    def send_fro(self):
        pair, near, far = self.pair, self.near, self.far
        self.out[0].wait_recv()

        def add(at):
            both = pair[2, at, :].astype(f32) + near[2, at, :].astype(f32)
            pair[2, at, :] = (both + far[0, at, :].astype(f32)).astype(bf16)

        in_tiles(self.rows, add)
        self.out[2].start()

    def first(self, total):
        pair, near = self.pair, self.near
        self.landed(0)

        def add(at):
            total[at, :] = pair[0, at, :].astype(f32) + near[0, at, :].astype(f32)

        in_tiles(self.rows, add)

    def finish(self, total, out=None):
        far = self.far
        out = total if out is None else out
        self.out[0].wait_send()
        self.out[1].wait()
        self.out[2].wait()

        def add(at):
            value = total[at, :] + far[1, at, :].astype(f32) + far[2, at, :].astype(f32)
            out[at, :] = value.astype(out.dtype)

        in_tiles(self.rows, add)

    def run(self, total):
        self.start()
        self.send_to()
        self.ready()
        self.first(total)
        self.send_fro()
        self.finish(total)

    @staticmethod
    def scratch(rows, width):
        return [pltpu.VMEM((slots, rows, width), bf16) for slots in Reduce.SLOTS] + [
            pltpu.SemaphoreType.DMA((4, 4)),
            pltpu.SemaphoreType.DMA((4,)),
        ]


def last_body(
    n, m, dqkv, w, narrow, norm_t, ffn, wo, vec, total, ffn_out, qkv_out, wo_out, vec_out,
    pair, near, far, sr, lr, stage, norms, mine, got, summed, sems, st, loc,
):
    plane = Plane(n, m)
    load = pltpu.make_async_copy(norm_t, norms, loc.at[0])
    load.start()
    enter_plane(plane, True)
    rows, width = ffn_out.shape[1], ffn.shape[2]
    across = fan(plane, lambda t: wo.at[t], lambda t: wo_out.at[t], st.at[1, 0], st.at[1, 1])
    across += fan(plane, lambda t: vec.at[t], lambda t: vec_out.at[t], st.at[2, 0], st.at[2, 1])
    across += [
        pltpu.make_async_copy(wo.at[plane.t], wo_out.at[plane.t], loc.at[1]),
        pltpu.make_async_copy(vec.at[plane.t], vec_out.at[plane.t], loc.at[2]),
    ]
    for copy in across:
        copy.start()
    a = exchange(
        plane,
        lambda i: ffn.at[:, pl.ds(pl.multiple_of(i * rows, rows), rows), :],
        lambda i: ffn_out.at[:, :, pl.ds(pl.multiple_of(i * width, width), width)],
        sems.at[0, 0],
        sems.at[0, 1],
        loc.at[3],
    )
    reduce = Reduce(plane, None, pair, near, far, sr, lr, stage)
    tokens = pair.shape[1]

    def blocks(it, carry):
        k = 3 - it // 2
        other = 1 - lax.rem(it, 2)
        b = plane.number(k, other)
        here = pl.ds(pl.multiple_of(b * tokens, tokens), tokens)
        part = lax.dot_general(dqkv[here, :], w[...], NT, preferred_element_type=f32).astype(bf16)

        @pl.when(other == 0)
        def _():
            pair[k] = part

        @pl.when(other == 1)
        def _():
            stage[k] = part

        for kk in range(4):

            @pl.when(it == 2 * (3 - kk))
            def _(kk=kk):
                reduce.swaps[Reduce.THEIRS[kk]].start()

        @pl.when(it == 2)
        def _():
            for copy in a:
                copy.start()

        return carry

    lax.fori_loop(0, n, blocks, 0)
    reduce.send_to()
    load.wait()
    strip = summed.shape[1]

    def weight_grads(s, carry):
        at = pl.ds(pl.multiple_of(s * m * strip, m * strip), m * strip)
        value = jnp.dot(norms[at, :], dqkv[...], preferred_element_type=f32).astype(bf16)
        value = jnp.dot(value, narrow[...], preferred_element_type=f32).astype(bf16)
        for t in range(m):
            mine[s, t] = value[t * strip : (t + 1) * strip]
        return carry

    lax.fori_loop(0, n, weight_grads, 0)
    over = fan(plane, lambda t: mine.at[:, t], lambda t: got.at[t], st.at[0, 0], st.at[0, 1])
    for copy in over:
        copy.start()
    reduce.ready()
    reduce.first(total)
    reduce.send_fro()
    for copy in over:
        copy.wait()

    def add(s, carry):
        value = mine[s, plane.t].astype(f32)
        for k in range(1, m):
            value = value + got[plane.tp_behind(k), s].astype(f32)
        summed[s] = value.astype(bf16)
        return carry

    lax.fori_loop(0, n, add, 0)
    b = exchange(
        plane,
        lambda i: summed.at[i],
        lambda i: qkv_out.at[i],
        sems.at[1, 0],
        sems.at[1, 1],
        loc.at[4],
    )
    for copy in b:
        copy.start()
    reduce.finish(total)
    for copy in a + b + across:
        copy.wait()


def last(n, m, dqkv, w, narrow, norm_t, ffn, wo, vec, ident):
    width, length = norm_t.shape
    tokens = length // n
    cols = narrow.shape[1]
    strip = width // (n * m)
    vmem = pl.BlockSpec(memory_space=pltpu.VMEM)
    hbm = pl.BlockSpec(memory_space=ANY)
    return pl.pallas_call(
        functools.partial(last_body, n, m),
        out_shape=(
            jax.ShapeDtypeStruct((tokens, width), f32),
            jax.ShapeDtypeStruct((3, ffn.shape[1] // n, ffn.shape[2] * n), ffn.dtype),
            jax.ShapeDtypeStruct((n, strip, cols), bf16),
            jax.ShapeDtypeStruct(wo.shape, wo.dtype),
            jax.ShapeDtypeStruct(vec.shape, vec.dtype),
        ),
        in_specs=[vmem] * 3 + [hbm] * 4,
        out_specs=[vmem] + [hbm] * 4,
        scratch_shapes=Reduce.scratch(tokens, width)
        + [
            pltpu.VMEM((4, tokens, width), bf16),
            pltpu.VMEM((width, length), bf16),
            pltpu.VMEM((n, m, strip, cols), bf16),
            pltpu.VMEM((m, n, strip, cols), bf16),
            pltpu.VMEM((n, strip, cols), bf16),
            pltpu.SemaphoreType.DMA((2, 2, n - 1)),
            pltpu.SemaphoreType.DMA((3, 2, m - 1)),
            pltpu.SemaphoreType.DMA((5,)),
        ],
        compiler_params=pltpu.CompilerParams(
            collective_id=ident, has_side_effects=True, vmem_limit_bytes=50 << 20
        ),
        cost_estimate=COST,
        name="last",
    )(dqkv, w, narrow, norm_t, ffn, wo, vec)


def column(row):
    return jnp.broadcast_to(row, (8, row.shape[1])).T[:, :1]


def gain_row(tiles, which, strip):
    stacked = tiles.reshape(-1, LANES).astype(bf16)
    count = stacked.shape[0] // 8
    shape = (LANES, count * strip)
    lane = lax.broadcasted_iota(jnp.int32, shape, 1).astype(f32)
    owner = jnp.floor((lane + 0.5) * (1.0 / strip))
    inside = lane - owner * strip
    pick = lax.broadcasted_iota(jnp.int32, shape, 0).astype(f32) == inside
    spread_out = jnp.dot(
        stacked, jnp.where(pick, 1.0, 0.0).astype(bf16), preferred_element_type=f32
    )
    shape = spread_out.shape
    lane = lax.broadcasted_iota(jnp.int32, shape, 1).astype(f32)
    owner = jnp.floor((lane + 0.5) * (1.0 / strip))
    row = lax.broadcasted_iota(jnp.int32, shape, 0).astype(f32)
    mine = row == owner * 8.0 + which
    return jnp.sum(jnp.where(mine, spread_out, 0.0), axis=0, keepdims=True)


def entry_body(
    n, m, heads, strip, x, places, wqkv, gains, wg, wu, wd, wo, widen, inverse,
    norm_t, q, k, v, cosine, sine, w, gain_rows, docs, ffn, wo_z,
    blocks, norms, turned, places_all, w_all, gains_all,
    sx, rem, sz, sn, loc,
):
    plane = Plane(n, m)
    enter_plane(plane, True)
    tokens = x.shape[0]
    gather = Gather(plane, x, blocks, sx.at[0], sx.at[1], loc.at[0])
    first = []
    for i, (src, dst) in enumerate(((gains, gains_all), (wqkv, w_all))):
        first += exchange(
            plane,
            lambda s, src=src, i=i: src.at[s] if i else src,
            lambda s, dst=dst: dst.at[s, plane.t],
            rem.at[i, 0],
            rem.at[i, 1],
            loc.at[1 + i],
        )
    few = exchange(
        plane, lambda i: places, lambda i: places_all.at[i], rem.at[2, 0], rem.at[2, 1], loc.at[3]
    )
    for copy in first + few:
        copy.start()
    gather.start()
    across = []
    for i, ref in enumerate((gains_all, w_all)):

        def slot(t, ref=ref):
            return ref.at[:, plane.t]

        across.append(fan(plane, slot, slot, sz.at[i, 0], sz.at[i, 1]))
    across.append(fan(plane, lambda t: wo, lambda t: wo_z.at[t], sz.at[2, 0], sz.at[2, 1]))
    own_wo = pltpu.make_async_copy(wo, wo_z.at[plane.t], loc.at[4])
    own_wo.start()
    for copy in first:
        copy.wait()
    for copy in across[0] + across[1] + across[2]:
        copy.start()
    moves = []
    width, rows = wg.shape[1] // n, wg.shape[0]
    for j, weight in enumerate((wg, wu, wd)):
        moves += exchange(
            plane,
            lambda i, weight=weight: weight.at[:, pl.ds(pl.multiple_of(i * width, width), width)],
            lambda i, j=j: ffn.at[j, pl.ds(pl.multiple_of(i * rows, rows), rows), :],
            rem.at[3 + j, 0],
            rem.at[3 + j, 1],
            loc.at[5 + j],
        )
    for copy in few + across[0]:
        copy.wait()
    tiles = gains_all[...]
    for i in range(2):
        gain_rows[i] = gain_row(tiles, i, strip)
    gather.own.wait()

    def number(it):
        return plane.number(it // 2, lax.rem(it, 2))

    def store(it, at):
        span = pl.ds(pl.multiple_of(number(it) * tokens, tokens), tokens)
        return pltpu.make_async_copy(turned.at[at], norm_t.at[:, span], sn.at[at])

    def normalize(it, carry):
        b = number(it)
        at = lax.rem(it, 2)

        @pl.when(it == 1)
        def _():
            gather.swap.wait_recv()

        @pl.when(it == 2)
        def _():
            gather.relay_near()

        @pl.when(it == 3)
        def _():
            gather.share[1].wait_recv()

        @pl.when(it == 5)
        def _():
            gather.share[0].wait_recv()

        @pl.when(it == 6)
        def _():
            gather.relay_far()
            for copy in moves:
                copy.start()

        @pl.when(it == 7)
        def _():
            gather.share[2].wait_recv()

        @pl.when(it >= 2)
        def _():
            store(it - 2, at).wait()

        value = blocks[b].astype(f32)
        scale = lax.rsqrt(jnp.mean(value * value, axis=1, keepdims=True) + norm_epsilon)
        low = (value * scale * gain_rows[0]).astype(bf16)
        norms[b] = low
        turned[at] = low.T
        store(it, at).start()
        here = pl.ds(pl.multiple_of(b * tokens, tokens), tokens)
        docs[:, here] = places_all[b, 0:1, :]
        angles = column(places_all[b, 1:2, :].astype(f32)) * inverse[...]
        lanes = lax.broadcasted_iota(jnp.int32, angles.shape, 1)
        sin = jnp.sin(angles)
        cosine[here, :] = jnp.cos(angles)
        sine[here, :] = jnp.where(lanes < SLOT, -sin, sin)
        return carry

    lax.fori_loop(0, n, normalize, 0)
    for copy in across[1]:
        copy.wait()

    def widened(s, carry):
        for t in range(m):
            at = pl.ds(pl.multiple_of((s * m + t) * strip, strip), strip)
            w[at, :] = jnp.dot(
                w_all[s, t], widen[...], preferred_element_type=f32
            ).astype(bf16)
        return carry

    lax.fori_loop(0, n, widened, 0)

    def project(b, carry):
        here = pl.ds(pl.multiple_of(b * tokens, tokens), tokens)
        out = jnp.dot(norms[b], w[...], preferred_element_type=f32)
        cos, sin = cosine[here, :], sine[here, :]
        for h in range(heads + 1):
            part = out[:, h * LANES : (h + 1) * LANES]
            rotated = (part * cos + pltpu.roll(part, SLOT, 1) * sin).astype(bf16)
            if h < heads:
                q[h, here, :] = rotated
            else:
                k[here, :] = rotated
        v[here, :] = out[:, (heads + 1) * LANES :].astype(bf16)
        return carry

    lax.fori_loop(0, n, project, 0)
    gather.swap.wait_send()
    gather.ahead.wait_send()
    gather.back.wait_send()
    gather.relay.wait_send()
    for copy in gather.share:
        copy.wait_send()
    store(n - 2, 0).wait()
    store(n - 1, 1).wait()
    own_wo.wait()
    for copy in across[2] + moves:
        copy.wait()


def entry(n, m, heads, x, places, wqkv, gains, wg, wu, wd, wo, widen, inverse, ident):
    tokens, width = x.shape
    length = n * tokens
    strip = wqkv.shape[1]
    wide = widen.shape[1]
    rows, cols = wg.shape
    vmem = pl.BlockSpec(memory_space=pltpu.VMEM)
    hbm = pl.BlockSpec(memory_space=ANY)
    return pl.pallas_call(
        functools.partial(entry_body, n, m, heads, strip),
        out_shape=(
            jax.ShapeDtypeStruct((width, length), bf16),
            jax.ShapeDtypeStruct((heads, length, LANES), bf16),
            jax.ShapeDtypeStruct((length, LANES), bf16),
            jax.ShapeDtypeStruct((length, LANES), bf16),
            jax.ShapeDtypeStruct((length, LANES), f32),
            jax.ShapeDtypeStruct((length, LANES), f32),
            jax.ShapeDtypeStruct((width, wide), bf16),
            jax.ShapeDtypeStruct((2, 1, width), f32),
            jax.ShapeDtypeStruct((1, length), jnp.int32),
            jax.ShapeDtypeStruct((3, rows * n, cols // n), wg.dtype),
            jax.ShapeDtypeStruct((m,) + wo.shape, wo.dtype),
        ),
        in_specs=[hbm] * 8 + [vmem] * 2,
        out_specs=[hbm] + [vmem] * 8 + [hbm] * 2,
        scratch_shapes=[
            pltpu.VMEM((n, tokens, width), bf16),
            pltpu.VMEM((n, tokens, width), bf16),
            pltpu.VMEM((2, width, tokens), bf16),
            pltpu.VMEM((n,) + places.shape, places.dtype),
            pltpu.VMEM((n, m) + wqkv.shape[1:], wqkv.dtype),
            pltpu.VMEM((n, m) + gains.shape, gains.dtype),
            pltpu.SemaphoreType.DMA((2, Gather.COPIES)),
            pltpu.SemaphoreType.DMA((6, 2, n - 1)),
            pltpu.SemaphoreType.DMA((3, 2, m - 1)),
            pltpu.SemaphoreType.DMA((2,)),
            pltpu.SemaphoreType.DMA((8,)),
        ],
        compiler_params=pltpu.CompilerParams(
            collective_id=ident, has_side_effects=True, vmem_limit_bytes=50 << 20
        ),
        cost_estimate=COST,
        name="entry",
    )(x, places, wqkv, gains, wg, wu, wd, wo, widen, inverse)


BLOCK = 512
NT = (((1,), (1,)), ((), ()))
LOG2E = 1.4426950408889634


def allowed_block(first_key, first_query, begin, causal):
    keys = first_key + lax.broadcasted_iota(jnp.int32, (BLOCK, BLOCK), 0)
    ok = keys >= begin
    if causal:
        queries = first_query + lax.broadcasted_iota(jnp.int32, (BLOCK, BLOCK), 1)
        ok = ok & (keys <= queries)
    return ok


def begins(docs):
    begin = jnp.zeros(docs.shape, jnp.int32)
    for d in range(3):
        count = jnp.sum((docs == d).astype(f32), axis=1, keepdims=True).astype(jnp.int32)
        begin = begin + jnp.where(docs > d, count, 0)
    return begin


def attend_body(
    n, m, factor, q, k, v, docs, wo, go, o, low, lse, start, wo_all, go_all,
    vt, top, total, acc, begin_row, sems, loc
):
    h, i = pl.program_id(0), pl.program_id(1)
    plane = Plane(n, m)
    first = Gather(plane, wo, wo_all, sems.at[0], sems.at[1], loc.at[0])
    second = Gather(plane, go, go_all, sems.at[2], sems.at[3], loc.at[1])
    at_step = h * pl.num_programs(1) + i

    @pl.when(at_step == 0)
    def _():
        enter_plane(plane, False)
        first.start()
        second.start()
        vt[...] = v[...].T
        begin_row[...] = begins(docs[...])
        start[...] = begin_row[...]

    @pl.when(at_step == 4)
    def _():
        first.relay_near()

    @pl.when(at_step == 6)
    def _():
        first.relay_far()

    top[...] = jnp.full_like(top, mask_fill_value)
    total[...] = jnp.zeros_like(total)
    acc[...] = jnp.zeros_like(acc)
    query = q[0]
    begin = begin_row[:, pl.ds(pl.multiple_of(i * BLOCK, BLOCK), BLOCK)]

    def step(j, causal):
        at = pl.ds(pl.multiple_of(j * BLOCK, BLOCK), BLOCK)
        raw = lax.dot_general(k[at, :], query, NT, preferred_element_type=f32)
        ok = allowed_block(j * BLOCK, i * BLOCK, begin, causal)
        scores = jnp.where(ok, raw * factor, mask_fill_value)
        new_top = jnp.maximum(top[...], jnp.max(scores, axis=0, keepdims=True))
        weights = jnp.exp2(scores - new_top)
        keep = jnp.exp2(top[...] - new_top)
        total[...] = total[...] * keep + jnp.sum(weights, axis=0, keepdims=True)
        acc[...] = acc[...] * keep + jnp.dot(
            vt[:, at], weights.astype(bf16), preferred_element_type=f32
        )
        top[...] = new_top

    def loop(j, carry):
        step(j, False)
        return carry

    lax.fori_loop(0, i, loop, 0)
    step(i, True)
    out = (acc[...] / total[...]).T
    o[0] = out
    low[...] = out.astype(bf16)
    lse[0] = top[...] + jnp.log2(total[...])

    @pl.when(at_step == pl.num_programs(0) * pl.num_programs(1) - 1)
    def _():
        second.relay_near()
        first.finish()
        second.relay_far()
        second.finish()


def attend(n, m, factor, q, k, v, docs, wo, go, ident):
    heads, length, _ = q.shape
    blocks = length // BLOCK
    pairs = heads * BLOCK * BLOCK * blocks * (blocks + 1) // 2
    return pl.pallas_call(
        functools.partial(attend_body, n, m, factor),
        grid=(heads, blocks),
        out_shape=(
            jax.ShapeDtypeStruct((heads, length, LANES), f32),
            jax.ShapeDtypeStruct((length, heads * LANES), bf16),
            jax.ShapeDtypeStruct((heads, 1, length), f32),
            jax.ShapeDtypeStruct((1, length), jnp.int32),
            jax.ShapeDtypeStruct((n,) + wo.shape, wo.dtype),
            jax.ShapeDtypeStruct((n,) + go.shape, go.dtype),
        ),
        in_specs=[
            pl.BlockSpec((1, BLOCK, LANES), lambda h, i: (h, i, 0)),
            pl.BlockSpec((length, LANES), lambda h, i: (0, 0)),
            pl.BlockSpec((length, LANES), lambda h, i: (0, 0)),
            pl.BlockSpec((1, length), lambda h, i: (0, 0)),
            pl.BlockSpec(memory_space=ANY),
            pl.BlockSpec(memory_space=ANY),
        ],
        out_specs=[
            pl.BlockSpec((1, BLOCK, LANES), lambda h, i: (h, i, 0)),
            pl.BlockSpec((BLOCK, LANES), lambda h, i: (i, h)),
            pl.BlockSpec((1, 1, BLOCK), lambda h, i: (h, 0, i)),
            pl.BlockSpec((1, length), lambda h, i: (0, 0)),
            pl.BlockSpec(memory_space=ANY),
            pl.BlockSpec(memory_space=ANY),
        ],
        scratch_shapes=[
            pltpu.VMEM((LANES, length), bf16),
            pltpu.VMEM((1, BLOCK), f32),
            pltpu.VMEM((1, BLOCK), f32),
            pltpu.VMEM((LANES, BLOCK), f32),
            pltpu.VMEM((1, length), jnp.int32),
            pltpu.SemaphoreType.DMA((4, Gather.COPIES)),
            pltpu.SemaphoreType.DMA((2,)),
        ],
        compiler_params=pltpu.CompilerParams(collective_id=ident, has_side_effects=True),
        cost_estimate=COST,
        name="attend",
    )(q, k, v, docs, wo, go)


def attend_back_body(
    n, m, factor, scale, heads, q, k, v, go, o, lse, begin, cosine, sine, mixed, terms,
    out, mixed_sum, term_sum, kt, dqt, dk, dv, delta,
    pair, near, far, sr, lr, pair2, near2, far2, sr2, lr2, held,
):
    h = pl.program_id(0)
    j = pl.program_id(1)
    blocks = pl.num_programs(1)
    plane = Plane(n, m)
    one = Reduce(plane, lambda i: mixed.at[i], pair, near, far, sr, lr)
    two = Reduce(plane, lambda i: terms.at[i], pair2, near2, far2, sr2, lr2)
    at_step = h * blocks + j

    @pl.when(at_step == 0)
    def _():
        enter_plane(plane, False)
        one.start()

    @pl.when(at_step == 1)
    def _():
        one.send_to()
        two.start()

    @pl.when(at_step == 2)
    def _():
        one.ready()
        one.first(mixed_sum)

    @pl.when(at_step == 4)
    def _():
        one.send_fro()
        two.send_to()

    @pl.when(at_step == 5)
    def _():
        two.ready()
        two.first(held)

    @pl.when((h == 0) & (j == 0))
    def _():
        kt[...] = k[...].T
        dk[...] = jnp.zeros_like(dk)
        dv[...] = jnp.zeros_like(dv)

    @pl.when(j == 0)
    def _():
        dqt[...] = jnp.zeros_like(dqt)

        def deltas(i, carry):
            at = pl.ds(pl.multiple_of(i * BLOCK, BLOCK), BLOCK)
            both = (go[at, :].astype(f32) * o[0, at, :]).T
            delta[:, at] = jnp.sum(both, axis=0, keepdims=True)
            return carry

        lax.fori_loop(0, blocks, deltas, 0)

    keys_at = pl.ds(pl.multiple_of(j * BLOCK, BLOCK), BLOCK)
    key = k[keys_at, :]
    value = v[keys_at, :]

    def step(i, causal):
        at = pl.ds(pl.multiple_of(i * BLOCK, BLOCK), BLOCK)
        query = q[0, at, :]
        raw = lax.dot_general(key, query, NT, preferred_element_type=f32)
        ok = allowed_block(j * BLOCK, i * BLOCK, begin[:, at], causal)
        probs = jnp.where(ok, jnp.exp2(raw * factor - lse[0, :, at]), 0.0)
        grads = go[at, :]
        dprob = lax.dot_general(value, grads, NT, preferred_element_type=f32)
        dscore = (probs * (dprob - delta[:, at])).astype(bf16)
        dv[keys_at, :] += jnp.dot(probs.astype(bf16), grads, preferred_element_type=f32)
        dk[keys_at, :] += jnp.dot(dscore, query, preferred_element_type=f32)
        dqt[:, at] += jnp.dot(kt[:, keys_at], dscore, preferred_element_type=f32)

    step(j, True)

    def loop(i, carry):
        step(i, False)
        return carry

    lax.fori_loop(j + 1, blocks, loop, 0)

    def unturn(value, at):
        return value * cosine[at, :] - pltpu.roll(value, SLOT, 1) * sine[at, :]

    @pl.when(j == blocks - 1)
    def _():
        def write(i, carry):
            at = pl.ds(pl.multiple_of(i * BLOCK, BLOCK), BLOCK)
            got = unturn(dqt[:, at].T * scale, at).astype(bf16)
            for which in range(heads):

                @pl.when(h == which)
                def _(which=which):
                    out[at, which * LANES : (which + 1) * LANES] = got

            return carry

        lax.fori_loop(0, blocks, write, 0)

    @pl.when((h == heads - 1) & (j == blocks - 1))
    def _():
        def write(i, carry):
            at = pl.ds(pl.multiple_of(i * BLOCK, BLOCK), BLOCK)
            out[at, heads * LANES : (heads + 1) * LANES] = unturn(dk[at, :] * scale, at).astype(
                bf16
            )
            out[at, (heads + 1) * LANES :] = dv[at, :].astype(bf16)
            return carry

        lax.fori_loop(0, blocks, write, 0)
        one.finish(mixed_sum)
        two.send_fro()
        two.finish(held, term_sum)


def attend_back(n, m, factor, scale, q, k, v, go, o, lse, begin, cosine, sine, mixed, terms, ident):
    heads, length, _ = q.shape
    blocks = length // BLOCK
    pairs = heads * BLOCK * BLOCK * blocks * (blocks + 1) // 2
    whole = pl.BlockSpec((length, LANES), lambda h, j: (0, 0))
    one = pl.BlockSpec((1, length, LANES), lambda h, j: (h, 0, 0))
    return pl.pallas_call(
        functools.partial(attend_back_body, n, m, factor, scale, heads),
        grid=(heads, blocks),
        out_shape=(
            jax.ShapeDtypeStruct((length, (heads + 2) * LANES), bf16),
            jax.ShapeDtypeStruct(mixed.shape[1:], f32),
            jax.ShapeDtypeStruct(terms.shape[1:], bf16),
        ),
        in_specs=[
            one,
            whole,
            whole,
            pl.BlockSpec((length, LANES), lambda h, j: (0, h)),
            one,
            pl.BlockSpec((1, 1, length), lambda h, j: (h, 0, 0)),
            pl.BlockSpec((1, length), lambda h, j: (0, 0)),
            whole,
            whole,
            pl.BlockSpec(memory_space=ANY),
            pl.BlockSpec(memory_space=ANY),
        ],
        out_specs=[
            pl.BlockSpec((length, (heads + 2) * LANES), lambda h, j: (0, 0)),
            pl.BlockSpec(mixed.shape[1:], lambda h, j: (0, 0)),
            pl.BlockSpec(terms.shape[1:], lambda h, j: (0, 0)),
        ],
        scratch_shapes=[
            pltpu.VMEM((LANES, length), bf16),
            pltpu.VMEM((LANES, length), f32),
            pltpu.VMEM((length, LANES), f32),
            pltpu.VMEM((length, LANES), f32),
            pltpu.VMEM((1, length), f32),
        ]
        + Reduce.scratch(*mixed.shape[1:])
        + Reduce.scratch(*terms.shape[1:])
        + [pltpu.VMEM(terms.shape[1:], f32)],
        compiler_params=pltpu.CompilerParams(
            collective_id=ident, has_side_effects=True, vmem_limit_bytes=56 << 20
        ),
        cost_estimate=COST,
        name="attend_back",
    )(q, k, v, go, o, lse, begin, cosine, sine, mixed, terms)


def feed_body(
    n, m, mine, go, w_in, dnorm, grads, mixed,
    rows, rows_t, go_t, go_two, w, h, mix_two, pair, near, far, stage,
    sg, sr, loc, sw, so, sm, sd,
):
    plane = Plane(n, m)
    tokens = rows.shape[1]
    hid = w_in.shape[3]
    enter_plane(plane, False)
    gather = Gather(plane, mine, rows, sg.at[0], sg.at[1], loc.at[0])
    reduce = Reduce(plane, None, pair, near, far, sr, None, stage)
    gather.start()
    weights = [
        pltpu.make_async_copy(
            w_in.at[t, j], w.at[j, :, t * hid : (t + 1) * hid], sw.at[j, t]
        )
        for j in range(3)
        for t in range(m)
    ]
    for copy in weights:
        copy.start()

    def number(it):
        return plane.number(it // 2, lax.rem(it, 2))

    def load_go(it, slot):
        return pltpu.make_async_copy(go.at[number(it)], go_two.at[slot], so.at[slot])

    def store_mix(it, slot):
        return pltpu.make_async_copy(mix_two.at[slot], mixed.at[number(it)], sm.at[slot])

    load_go(0, 0).start()
    gather.own.wait()
    for copy in weights:
        copy.wait()

    def blocks(it, carry):
        slot = lax.rem(it, 2)
        k = it // 2
        b = number(it)

        @pl.when(it == 1)
        def _():
            gather.swap.wait_recv()

        @pl.when(it == 2)
        def _():
            gather.relay_near()

        @pl.when(it == 3)
        def _():
            gather.share[1].wait_recv()

        @pl.when(it == 5)
        def _():
            gather.share[0].wait_recv()

        @pl.when(it == 6)
        def _():
            reduce.join(1)
            reduce.out[1].start()
            gather.relay_far()

        @pl.when(it == 7)
        def _():
            gather.share[2].wait_recv()

        @pl.when(it < n - 1)
        def _():
            load_go(it + 1, 1 - slot).start()

        load_go(it, slot).wait()

        @pl.when(it >= 2)
        def _():
            store_mix(it - 2, slot).wait()

        here = pl.ds(pl.multiple_of(b * tokens, tokens), tokens)
        row = rows[b]
        gate = jnp.dot(row, w[0], preferred_element_type=f32)
        up = jnp.dot(row, w[1], preferred_element_type=f32)
        grad = go_two[slot]
        dhidden = jnp.dot(grad, w[2], preferred_element_type=f32)
        sig = jax.nn.sigmoid(gate)
        act = gate * sig
        hidden = (act * up).astype(bf16)
        dgate = (dhidden * up * sig * (1.0 + gate * (1.0 - sig))).astype(bf16)
        dup = (dhidden * act).astype(bf16)
        h[0, here, :] = dgate
        h[1, here, :] = dup
        h[2, here, :] = hidden
        part = lax.dot_general(dgate, w[0], NT, preferred_element_type=f32)
        part = part + lax.dot_general(dup, w[1], NT, preferred_element_type=f32)
        part = part.astype(bf16)

        @pl.when(lax.rem(it, 2) == 0)
        def _():
            pair[k] = part

        @pl.when(lax.rem(it, 2) == 1)
        def _():
            stage[k] = part

        for kk in range(4):

            @pl.when(it == 2 * kk + 1)
            def _(kk=kk):
                reduce.swaps[Reduce.THEIRS[kk]].start()

        mix_two[slot] = lax.dot_general(hidden, w[2], NT, preferred_element_type=f32).astype(bf16)
        store_mix(it, slot).start()
        rows_t[:, here] = row.T
        go_t[:, here] = grad.T
        return carry

    lax.fori_loop(0, n, blocks, 0)
    reduce.join(3)
    reduce.out[0].start()
    width = rows.shape[2]

    def weight_grad(j, left):
        def part(i, carry):
            at = pl.ds(pl.multiple_of(i * 256, 256), 256)
            value = jnp.dot(left[at, :], h[j], preferred_element_type=f32)
            w[j, at, :] = value.astype(bf16)
            return carry

        lax.fori_loop(0, width // 256, part, 0)
        outs = [
            pltpu.make_async_copy(
                w.at[j, :, t * hid : (t + 1) * hid], grads.at[t, j], sd.at[j, t]
            )
            for t in range(m)
        ]
        for copy in outs:
            copy.start()
        return outs

    outs = weight_grad(0, rows_t)
    reduce.ready()
    reduce.first(dnorm)
    reduce.send_fro()
    outs += weight_grad(1, rows_t)
    outs += weight_grad(2, go_t)
    gather.swap.wait_send()
    gather.ahead.wait_send()
    gather.back.wait_send()
    gather.relay.wait_send()
    for copy in gather.share:
        copy.wait_send()
    store_mix(n - 2, 0).wait()
    store_mix(n - 1, 1).wait()
    reduce.finish(dnorm)
    for copy in outs:
        copy.wait()


def feed(n, m, norm, go, w_in, ident):
    tokens, width = norm.shape
    hid = w_in.shape[3]
    length = n * tokens
    block = pltpu.VMEM((n, tokens, width), bf16)
    return pl.pallas_call(
        functools.partial(feed_body, n, m),
        out_shape=(
            jax.ShapeDtypeStruct((tokens, width), f32),
            jax.ShapeDtypeStruct(w_in.shape, bf16),
            jax.ShapeDtypeStruct((n, tokens, width), bf16),
        ),
        in_specs=[pl.BlockSpec(memory_space=ANY)] * 3,
        out_specs=[
            pl.BlockSpec(memory_space=pltpu.VMEM),
            pl.BlockSpec(memory_space=ANY),
            pl.BlockSpec(memory_space=ANY),
        ],
        scratch_shapes=[
            block,
            pltpu.VMEM((width, length), bf16),
            pltpu.VMEM((width, length), bf16),
            pltpu.VMEM((2, tokens, width), bf16),
            pltpu.VMEM((3, width, m * hid), bf16),
            pltpu.VMEM((3, length, m * hid), bf16),
            pltpu.VMEM((2, tokens, width), bf16),
        ]
        + [pltpu.VMEM((slots, tokens, width), bf16) for slots in Reduce.SLOTS]
        + [
            pltpu.VMEM((4, tokens, width), bf16),
            pltpu.SemaphoreType.DMA((2, Gather.COPIES)),
            pltpu.SemaphoreType.DMA((4, 4)),
            pltpu.SemaphoreType.DMA((1,)),
            pltpu.SemaphoreType.DMA((3, m)),
            pltpu.SemaphoreType.DMA((2,)),
            pltpu.SemaphoreType.DMA((2,)),
            pltpu.SemaphoreType.DMA((3, m)),
        ],
        compiler_params=pltpu.CompilerParams(
            collective_id=ident, has_side_effects=True, vmem_limit_bytes=60 << 20
        ),
        cost_estimate=COST,
        name="feed",
    )(norm, go, w_in)


def split_heads(w, groups):
    rows = w.shape[0]
    return w.reshape(rows, groups, -1).transpose(1, 0, 2)


def spread(blocks):
    lead = blocks.shape[:-1]
    halves = blocks.reshape(lead + (-1, HALF))
    pad = [(0, 0)] * len(lead) + [(0, 0), (0, SLOT - HALF)]
    wide = jnp.pad(halves, pad)
    return wide.reshape(lead + (-1,))


def gathered(wide):
    lead = wide.shape[:-1]
    halves = wide.reshape(lead + (-1, SLOT))[..., :HALF]
    return halves.reshape(lead + (-1,))


def fast_layer(n, m):
    def on_plane(
        layer_input,
        doc_ids,
        positions,
        first_gain,
        query_weight,
        key_weight,
        value_weight,
        output_weight,
        second_gain,
        gate_weight,
        up_weight,
        down_weight,
        out_grad,
    ):
        x = layer_input[0]
        rows, width = x.shape
        length = rows * n
        heads = QUERY_HEADS // n
        scale = 1.0 / math.sqrt(HEAD_SIZE)
        factor = scale * LOG2E
        strip = query_weight.shape[0]
        hid = gate_weight.shape[1] // n

        packed = jnp.concatenate(
            [split_heads(w, n) for w in (query_weight, key_weight, value_weight)], axis=2
        )
        cols = packed.shape[2]
        gains = jnp.pad(
            jnp.stack([first_gain, second_gain]).astype(f32), ((0, 6), (0, LANES - strip))
        )
        places = jnp.concatenate([doc_ids, positions], axis=0)
        lane = jnp.arange(LANES) % SLOT
        inverse = jnp.where(
            lane < HALF, rope_base ** (-(lane.astype(f32) * 2.0 / HEAD_SIZE)), 0.0
        )[None]
        from_col = jnp.arange(cols)
        to_lane = from_col // HALF * SLOT + from_col % HALF
        widen = (to_lane[:, None] == jnp.arange(cols // HALF * SLOT)[None, :]).astype(bf16)

        norm_t, q, k, v, cosine, sine, wqkv, gain_rows, docs, ffn_mine, output_rows = entry(
            n, m, heads, x, places, packed, gains,
            gate_weight, up_weight, down_weight, output_weight, widen, inverse, 0,
        )
        gain_one, gain_two = gain_rows[0], gain_rows[1]
        ffn_all = lax.all_gather(ffn_mine, "tp", axis=0, tiled=False)
        o, low, lse, begin, output_full, grad_all = attend(
            n, m, factor, q, k, v, docs, output_rows.reshape(m * strip, width), out_grad[0], 9
        )
        output_full = output_full.reshape(-1, width)
        (mine,) = plane_swap(n, m, 1, low.reshape(n, rows, heads * LANES))
        attn_low = gathered(mine.transpose(1, 0, 2).reshape(rows, n * heads * LANES))

        x_f = x.astype(f32)
        resid = x_f + jnp.dot(attn_low, output_full, preferred_element_type=f32)
        scale_two = lax.rsqrt(jnp.mean(resid * resid, axis=1, keepdims=True) + norm_epsilon)
        norm_two = (resid * scale_two * gain_two).astype(bf16)
        grad_low = out_grad[0]
        dnorm_two, ffn_terms, mixed = feed(n, m, norm_two, grad_all, ffn_all, 2)
        ffn_sum = lax.psum_scatter(ffn_terms, "tp", scatter_dimension=0, tiled=False)

        inner = gain_two * dnorm_two
        moment = jnp.mean(resid * inner, axis=1, keepdims=True)
        dresid = (
            grad_low.astype(f32)
            + scale_two * inner
            - resid * scale_two * scale_two * scale_two * moment
        )
        dbranch = dresid.astype(bf16)
        output_term = outer_product(attn_low, dbranch).astype(bf16).reshape(n, m * strip, width)
        dheads = spread(times_transpose(dbranch, output_full).astype(bf16))
        dheads = dheads.reshape(rows, n, heads * LANES).transpose(1, 0, 2)
        gain_term = jnp.sum(dnorm_two * resid * scale_two, axis=0)
        go, gain_parts = plane_swap(n, m, 5, dheads, gain_term.reshape(n, 1, m * strip))
        go = go.reshape(length, heads * LANES)
        gain_part = jnp.sum(gain_parts, axis=(0, 1)).reshape(m, 1, strip)

        dqkv, mixed_sum, output_sum = attend_back(
            n, m, factor, scale, q, k, v, go, o, lse, begin, cosine, sine, mixed, output_term, 3
        )
        layer_output = (resid + mixed_sum).astype(bf16)[None]
        dnorm_one, ffn_out, qkv_out, output_parts, gain_sums = last(
            n, m, dqkv, wqkv, widen.T, norm_t, ffn_sum,
            output_sum.reshape(m, strip, width), gain_part, 6,
        )
        output_grad = jnp.sum(output_parts.astype(f32), axis=0)

        scale_one = lax.rsqrt(jnp.mean(x_f * x_f, axis=1, keepdims=True) + norm_epsilon)
        inner = gain_one * dnorm_one
        moment = jnp.mean(x_f * inner, axis=1, keepdims=True)
        input_grad = (
            dresid + scale_one * inner - x_f * scale_one * scale_one * scale_one * moment
        )[None]

        gate_grad, up_grad, down_grad = [ffn_out[i].astype(f32) for i in range(3)]
        kv = HEAD_SIZE * KEY_VALUE_HEADS // n
        split = heads * HEAD_SIZE

        def columns(a, b):
            return qkv_out[:, :, a:b].transpose(1, 0, 2).reshape(strip, -1).astype(f32)

        query_grad = columns(0, split)
        key_grad = columns(split, split + kv)
        value_grad = columns(split + kv, cols)

        one = (
            jnp.sum(query_weight.astype(f32) * query_grad, axis=1)
            + jnp.sum(key_weight.astype(f32) * key_grad, axis=1)
            + jnp.sum(value_weight.astype(f32) * value_grad, axis=1)
        )
        first_gain_grad = one / first_gain.astype(f32)
        second_gain_grad = jnp.sum(gain_sums, axis=(0, 1))
        return (
            layer_output,
            input_grad,
            first_gain_grad,
            query_grad,
            key_grad,
            value_grad,
            output_grad,
            second_gain_grad,
            gate_grad,
            up_grad,
            down_grad,
        )

    return on_plane


def solution(mesh):
    n, m = mesh.shape["seq"], mesh.shape["tp"]
    fits = n == KEY_VALUE_HEADS == 8
    return jax.shard_map(
        fast_layer(n, m) if fits else on_device,
        mesh=mesh,
        in_specs=(
            P("tp", "seq", None),
            P("tp", "seq"),
            P("tp", "seq"),
            P(("seq", "tp")),
            P(("seq", "tp"), None),
            P(("seq", "tp"), None),
            P(("seq", "tp"), None),
            P(("seq", "tp"), None),
            P(("seq", "tp")),
            P("seq", "tp"),
            P("seq", "tp"),
            P("seq", "tp"),
            P("tp", "seq", None),
        ),
        out_specs=(
            P("tp", "seq", None),
            P("tp", "seq", None),
            P(("seq", "tp")),
            P(("seq", "tp"), None),
            P(("seq", "tp"), None),
            P(("seq", "tp"), None),
            P(("seq", "tp"), None),
            P(("seq", "tp")),
            P("seq", "tp"),
            P("seq", "tp"),
            P("seq", "tp"),
        ),
        check_vma=False,
    )
```

```python
import functools
import math

import jax
import jax.numpy as jnp
from jax import lax
from jax.experimental import pallas as pl
from jax.experimental.pallas import tpu as pltpu
from jax.sharding import PartitionSpec as P

QUERY_HEADS = 16
KEY_VALUE_HEADS = 8
HEAD_SIZE = 96


norm_epsilon = 1e-05
rope_base = 100000.0
mask_fill_value = -1e30


def rope_tables(places):
    half = HEAD_SIZE // 2
    inverse = rope_base ** (-(jnp.arange(half, dtype=jnp.float32) * 2.0 / HEAD_SIZE))
    angles = places.astype(jnp.float32)[:, None] * inverse[None, :]
    return (jnp.cos(angles), jnp.sin(angles))


def apply_rotary(value_rows, cosine_table, sine_table, heads, direction):
    sequence_length = value_rows.shape[0]
    split = value_rows.reshape(sequence_length, heads, 2, HEAD_SIZE // 2)
    first = split[:, :, 0]
    second = split[:, :, 1]
    cosine = cosine_table[:, None, :]
    sine = direction * sine_table[:, None, :]
    turned = jnp.stack([first * cosine - second * sine, second * cosine + first * sine], axis=2)
    return turned.reshape(sequence_length, heads * HEAD_SIZE)


def outer_product(left, right):
    return lax.dot_general(
        left, right, (((0,), (0,)), ((), ())), preferred_element_type=jnp.float32
    )


def times_transpose(left, right):
    return lax.dot_general(
        left, right, (((1,), (1,)), ((), ())), preferred_element_type=jnp.float32
    )


def norm_backward(inputs, scale, gain, upstream):
    inner = gain * upstream
    moment = jnp.mean(inputs * inner, axis=1, keepdims=True)
    return (
        scale * inner - inputs * scale * scale * scale * moment,
        jnp.sum(upstream * inputs * scale, axis=0),
    )


def on_device(
    layer_input,
    doc_ids,
    positions,
    first_gain,
    query_weight,
    key_weight,
    value_weight,
    output_weight,
    second_gain,
    gate_weight,
    up_weight,
    down_weight,
    out_grad,
):
    token_rows = layer_input.shape[1]
    query_groups = QUERY_HEADS // KEY_VALUE_HEADS
    scale_of_scores = 1.0 / math.sqrt(HEAD_SIZE)
    inputs_f = layer_input[0].astype(jnp.float32)
    my_docs = doc_ids[0]
    gain_one, query_full, complete_keys, value_full, output_full, gain_two = (
        lax.all_gather(first_gain, ("seq", "tp"), axis=0, tiled=True),
        lax.all_gather(query_weight, ("seq", "tp"), axis=0, tiled=True),
        lax.all_gather(key_weight, ("seq", "tp"), axis=0, tiled=True),
        lax.all_gather(value_weight, ("seq", "tp"), axis=0, tiled=True),
        lax.all_gather(output_weight, ("seq", "tp"), axis=0, tiled=True),
        lax.all_gather(second_gain, ("seq", "tp"), axis=0, tiled=True),
    )
    gain_one_f = gain_one.astype(jnp.float32)
    gain_two_f = gain_two.astype(jnp.float32)
    scale_one = lax.rsqrt(jnp.mean(inputs_f * inputs_f, axis=1, keepdims=True) + norm_epsilon)
    first_normalized = (inputs_f * scale_one * gain_one_f).astype(jnp.bfloat16)
    cosine_table, sine_table = rope_tables(positions[0])
    rotated_query = apply_rotary(
        jnp.dot(first_normalized, query_full, preferred_element_type=jnp.float32),
        cosine_table,
        sine_table,
        QUERY_HEADS,
        1.0,
    ).astype(jnp.bfloat16)
    key_rot = apply_rotary(
        jnp.dot(first_normalized, complete_keys, preferred_element_type=jnp.float32),
        cosine_table,
        sine_table,
        KEY_VALUE_HEADS,
        1.0,
    ).astype(jnp.bfloat16)
    value_low = jnp.dot(first_normalized, value_full, preferred_element_type=jnp.float32).astype(
        jnp.bfloat16
    )
    gathered_keys, gathered_values, doc_all = (
        lax.all_gather(key_rot, "seq", axis=0, tiled=True),
        lax.all_gather(value_low, "seq", axis=0, tiled=True),
        lax.all_gather(my_docs.astype(jnp.bfloat16), "seq", axis=0, tiled=True),
    )
    sequence_length = gathered_keys.shape[0]
    block_number = math.gcd(512, sequence_length)
    block_count = sequence_length // block_number
    query_index = lax.axis_index("seq") * token_rows + jnp.arange(token_rows, dtype=jnp.int32)
    my_doc_f = my_docs.astype(jnp.float32)
    heads_of_query = rotated_query.reshape(token_rows, KEY_VALUE_HEADS, query_groups, HEAD_SIZE)
    layer_entries = (
        gathered_keys.reshape(block_count, block_number, KEY_VALUE_HEADS, HEAD_SIZE),
        gathered_values.reshape(block_count, block_number, KEY_VALUE_HEADS, HEAD_SIZE),
        doc_all.astype(jnp.float32).reshape(block_count, block_number),
        jnp.arange(block_count, dtype=jnp.int32) * block_number,
    )

    def allowed_of(doc_piece, start):
        key_index = start + jnp.arange(block_number, dtype=jnp.int32)
        return (key_index[None, :] <= query_index[:, None]) & (
            doc_piece[None, :] == my_doc_f[:, None]
        )

    def scores_of(key_piece, allowed):
        raw = (
            jnp.einsum(
                "tgrd,kgd->tgrk", heads_of_query, key_piece, preferred_element_type=jnp.float32
            )
            * scale_of_scores
        )
        return jnp.where(allowed[:, None, None, :], raw, mask_fill_value)

    def total_step(carry, item):
        key_piece, value_piece, doc_piece, start = item
        allowed = allowed_of(doc_piece, start)

        def total_work(state):
            top, total = state
            scores = scores_of(key_piece, allowed)
            new_top = jnp.maximum(top, jnp.max(scores, axis=3))
            weights = jnp.where(
                allowed[:, None, None, :], jnp.exp(scores - new_top[..., None]), 0.0
            )
            return (new_top, total * jnp.exp(top - new_top) + jnp.sum(weights, axis=3))

        return (lax.cond(jnp.any(allowed), total_work, lambda state: state, carry), None)

    start_state = (
        jnp.full((token_rows, KEY_VALUE_HEADS, query_groups), mask_fill_value, jnp.float32),
        jnp.zeros((token_rows, KEY_VALUE_HEADS, query_groups), jnp.float32),
    )
    (top, total), unused_result = lax.scan(total_step, start_state, layer_entries)
    log_total = top + jnp.log(total)

    def probs_of(key_piece, allowed):
        scores = scores_of(key_piece, allowed)
        return jnp.where(allowed[:, None, None, :], jnp.exp(scores - log_total[..., None]), 0.0)

    def output_update(accum, item):
        key_piece, value_piece, doc_piece, start = item
        allowed = allowed_of(doc_piece, start)

        def output_work(state):
            probs = probs_of(key_piece, allowed).astype(jnp.bfloat16)
            return state + jnp.einsum(
                "tgrk,kgd->tgrd", probs, value_piece, preferred_element_type=jnp.float32
            )

        return (lax.cond(jnp.any(allowed), output_work, lambda state: state, accum), None)

    heads_output, unused_result = lax.scan(
        output_update,
        jnp.zeros((token_rows, KEY_VALUE_HEADS, query_groups, HEAD_SIZE), jnp.float32),
        layer_entries,
    )
    attn_low = heads_output.reshape(token_rows, QUERY_HEADS * HEAD_SIZE).astype(jnp.bfloat16)
    resid = inputs_f + jnp.dot(attn_low, output_full, preferred_element_type=jnp.float32)
    scale_two = lax.rsqrt(jnp.mean(resid * resid, axis=1, keepdims=True) + norm_epsilon)
    normed_two = (resid * scale_two * gain_two_f).astype(jnp.bfloat16)
    rows_all = lax.all_gather(normed_two, "tp", axis=0, tiled=True)
    gate_cols, up_cols, down_cols = (
        lax.all_gather(gate_weight, "seq", axis=0, tiled=True),
        lax.all_gather(up_weight, "seq", axis=0, tiled=True),
        lax.all_gather(down_weight, "seq", axis=0, tiled=True),
    )
    gate_pre = jnp.dot(rows_all, gate_cols, preferred_element_type=jnp.float32)
    up_pre = jnp.dot(rows_all, up_cols, preferred_element_type=jnp.float32)
    gate_sig = jax.nn.sigmoid(gate_pre)
    gate_act = gate_pre * gate_sig
    hidden = (gate_act * up_pre).astype(jnp.bfloat16)
    mixed = lax.psum_scatter(
        times_transpose(hidden, down_cols).astype(jnp.bfloat16),
        "tp",
        scatter_dimension=0,
        tiled=True,
    ).astype(jnp.float32)
    layer_output = (resid + mixed).astype(jnp.bfloat16)[None]
    grad_low = out_grad[0]
    grad_f = grad_low.astype(jnp.float32)
    grad_all = lax.all_gather(grad_low, "tp", axis=0, tiled=True)
    dhidden = jnp.dot(grad_all, down_cols, preferred_element_type=jnp.float32)
    dgate = (dhidden * up_pre * gate_sig * (1.0 + gate_pre * (1.0 - gate_sig))).astype(jnp.bfloat16)
    dup = (dhidden * gate_act).astype(jnp.bfloat16)
    gate_term = outer_product(rows_all, dgate)
    up_term = outer_product(rows_all, dup)
    down_term_grad = outer_product(grad_all, hidden)
    dnorm_two = lax.psum_scatter(
        (times_transpose(dgate, gate_cols) + times_transpose(dup, up_cols)).astype(jnp.bfloat16),
        "tp",
        scatter_dimension=0,
        tiled=True,
    ).astype(jnp.float32)
    gate_grad, up_grad, down_grad = (
        lax.psum_scatter(
            gate_term.astype(jnp.bfloat16), "seq", scatter_dimension=0, tiled=True
        ).astype(jnp.float32),
        lax.psum_scatter(
            up_term.astype(jnp.bfloat16), "seq", scatter_dimension=0, tiled=True
        ).astype(jnp.float32),
        lax.psum_scatter(
            down_term_grad.astype(jnp.bfloat16), "seq", scatter_dimension=0, tiled=True
        ).astype(jnp.float32),
    )
    resid_part, gain_two_term = norm_backward(resid, scale_two, gain_two_f, dnorm_two)
    dresid = grad_f + resid_part
    dbranch = dresid.astype(jnp.bfloat16)
    output_term = outer_product(attn_low, dbranch)
    heads_gradient = times_transpose(dbranch, output_full).astype(jnp.bfloat16)
    grouped_heads_gradient = heads_gradient.reshape(
        token_rows, KEY_VALUE_HEADS, query_groups, HEAD_SIZE
    )
    delta = jnp.sum(grouped_heads_gradient.astype(jnp.float32) * heads_output, axis=3)

    def gradient_update(dquery, item):
        key_piece, value_piece, doc_piece, start = item
        allowed = allowed_of(doc_piece, start)

        def gradient_work(state):
            probs = probs_of(key_piece, allowed)
            value_piece_grad = jnp.einsum(
                "tgrk,tgrd->kgd",
                probs.astype(jnp.bfloat16),
                grouped_heads_gradient,
                preferred_element_type=jnp.float32,
            )
            prob_grad = jnp.einsum(
                "tgrd,kgd->tgrk",
                grouped_heads_gradient,
                value_piece,
                preferred_element_type=jnp.float32,
            )
            score_grad = (probs * (prob_grad - delta[..., None])).astype(jnp.bfloat16)
            key_piece_grad = jnp.einsum(
                "tgrk,tgrd->kgd", score_grad, heads_of_query, preferred_element_type=jnp.float32
            )
            updated = state + jnp.einsum(
                "tgrk,kgd->tgrd", score_grad, key_piece, preferred_element_type=jnp.float32
            )
            return (updated, (key_piece_grad, value_piece_grad))

        def skip(state):
            blank_tensor = jnp.zeros((block_number, KEY_VALUE_HEADS, HEAD_SIZE), jnp.float32)
            return (state, (blank_tensor, blank_tensor))

        return lax.cond(jnp.any(allowed), gradient_work, skip, dquery)

    dquery, (key_contributions, value_contributions) = lax.scan(
        gradient_update,
        jnp.zeros((token_rows, KEY_VALUE_HEADS, query_groups, HEAD_SIZE), jnp.float32),
        layer_entries,
    )
    gathered_key_contributions = (
        key_contributions.reshape(sequence_length, KEY_VALUE_HEADS * HEAD_SIZE) * scale_of_scores
    )
    gathered_value_contributions = value_contributions.reshape(
        sequence_length, KEY_VALUE_HEADS * HEAD_SIZE
    )
    local_keys, value_mine = (
        lax.psum_scatter(
            gathered_key_contributions.astype(jnp.bfloat16), "seq", scatter_dimension=0, tiled=True
        ).astype(jnp.float32),
        lax.psum_scatter(
            gathered_value_contributions.astype(jnp.bfloat16),
            "seq",
            scatter_dimension=0,
            tiled=True,
        ).astype(jnp.float32),
    )
    dq_pre = apply_rotary(
        dquery.reshape(token_rows, QUERY_HEADS * HEAD_SIZE) * scale_of_scores,
        cosine_table,
        sine_table,
        QUERY_HEADS,
        -1.0,
    ).astype(jnp.bfloat16)
    key_gradient_unrotated = apply_rotary(
        local_keys, cosine_table, sine_table, KEY_VALUE_HEADS, -1.0
    ).astype(jnp.bfloat16)
    dv_pre = value_mine.astype(jnp.bfloat16)
    dnorm_one = (
        times_transpose(dq_pre, query_full)
        + times_transpose(key_gradient_unrotated, complete_keys)
        + times_transpose(dv_pre, value_full)
    )
    input_part, gain_one_term = norm_backward(inputs_f, scale_one, gain_one_f, dnorm_one)
    input_grad = (dresid + input_part)[None]
    query_term = outer_product(first_normalized, dq_pre)
    key_term = outer_product(first_normalized, key_gradient_unrotated)
    value_term = outer_product(first_normalized, dv_pre)
    first_gain_grad, query_grad, key_grad, value_grad, output_grad, second_gain_grad = (
        lax.psum_scatter(gain_one_term, ("seq", "tp"), scatter_dimension=0, tiled=True),
        lax.psum_scatter(query_term, ("seq", "tp"), scatter_dimension=0, tiled=True),
        lax.psum_scatter(key_term, ("seq", "tp"), scatter_dimension=0, tiled=True),
        lax.psum_scatter(value_term, ("seq", "tp"), scatter_dimension=0, tiled=True),
        lax.psum_scatter(output_term, ("seq", "tp"), scatter_dimension=0, tiled=True),
        lax.psum_scatter(gain_two_term, ("seq", "tp"), scatter_dimension=0, tiled=True),
    )
    return (
        layer_output,
        input_grad,
        first_gain_grad,
        query_grad,
        key_grad,
        value_grad,
        output_grad,
        second_gain_grad,
        gate_grad,
        up_grad,
        down_grad,
    )


MESH = pl.DeviceIdType.MESH
ANY = pl.ANY
HALF = HEAD_SIZE // 2
LANES = 128
SLOT = LANES // 2
f32 = jnp.float32
bf16 = jnp.bfloat16
VMEM_LIMIT = 62 << 20
COST = pl.CostEstimate(flops=1_000_000, transcendentals=0, bytes_accessed=100_000)


class Plane:
    def __init__(self, n, m):
        self.n, self.m, self.chips = n, m, n // 2
        self.s = lax.axis_index("seq")
        self.t = lax.axis_index("tp")
        self.q = self.s // 2
        self.c = lax.rem(self.s, 2)

        across = self.q + 1 - 2 * lax.rem(self.q, 2)
        along = lax.rem(self.q + 2, 4)
        self.to = across * (1 - self.c) + along * self.c
        self.fro = across * self.c + along * (1 - self.c)
        self.far = 3 - self.q
        self.order = (self.q, self.to, self.fro, self.far)

    def device(self, s):
        return (s, self.t)

    def same(self, chip):
        return (2 * chip + self.c, self.t)

    def number(self, k, other):
        c, q = self.c, self.q
        low, high = lax.rem(k, 2), k // 2
        dx = low * (1 - c) + high * c
        dy = high * (1 - c) + low * c
        x, y = lax.rem(q, 2), q // 2
        chip = 2 * (y + dy - 2 * y * dy) + x + dx - 2 * x * dx
        return 2 * chip + c + other * (1 - 2 * c)

    def sibling(self):
        return (2 * self.q + 1 - self.c, self.t)

    def ahead(self, k):
        return lax.rem(self.q + k, self.chips)

    def behind(self, k):
        return lax.rem(self.q + self.chips - k, self.chips)

    def seq_ahead(self, k):
        return lax.rem(self.s + k, self.n)

    def seq_behind(self, k):
        return lax.rem(self.s + self.n - k, self.n)

    def tp_ahead(self, k):
        return (self.s, lax.rem(self.t + k, self.m))

    def tp_behind(self, k):
        return lax.rem(self.t + self.m - k, self.m)


def enter_plane(plane, with_tp):
    barrier = pltpu.get_barrier_semaphore()
    for k in range(1, plane.n):
        pl.semaphore_signal(
            barrier, inc=1, device_id=plane.device(plane.seq_ahead(k)), device_id_type=MESH
        )
    count = plane.n - 1
    if with_tp:
        for k in range(1, plane.m):
            pl.semaphore_signal(barrier, inc=1, device_id=plane.tp_ahead(k), device_id_type=MESH)
        count += plane.m - 1
    pl.semaphore_wait(barrier, count)


def remote(src, dst, send, recv, device):
    return pltpu.make_async_remote_copy(
        src_ref=src,
        dst_ref=dst,
        send_sem=send,
        recv_sem=recv,
        device_id=device,
        device_id_type=MESH,
    )


class Gather:
    COPIES = 7

    def __init__(self, plane, src, dst_of, send, recv, local):
        to, fro, far, c = plane.to, plane.fro, plane.far, plane.c
        here = dst_of(plane.s)
        self.own = pltpu.make_async_copy(src, here, local)

        def block(chip):
            return dst_of(2 * chip + c)

        def copy(i, a, b, device):
            return remote(a, b, send.at[i], recv.at[i], device)

        sibling = plane.sibling()
        self.swap = copy(0, src, here, sibling)
        self.ahead = copy(1, src, here, plane.same(to))
        self.back = copy(2, src, here, plane.same(fro))
        self.relay = copy(3, block(fro), block(fro), plane.same(to))
        self.share = [
            copy(4, block(to), block(to), sibling),
            copy(5, block(fro), block(fro), sibling),
            copy(6, block(far), block(far), sibling),
        ]

    def start(self):
        self.back.start()
        self.ahead.start()

    def start_here(self):
        self.swap.start()
        self.own.start()

    def relay_near(self):
        self.back.wait_recv()
        self.relay.start()
        self.share[1].start()
        self.ahead.wait_recv()
        self.share[0].start()

    def relay_far(self):
        self.relay.wait_recv()
        self.share[2].start()

    def wait_sends(self):
        for copy in [self.swap, self.ahead, self.back, self.relay] + self.share:
            copy.wait_send()


class Gathers:
    def __init__(self, plane, src, dst_of, sems, local, pieces):
        rows = src.shape[0] // pieces
        self.parts = []
        for i in range(pieces):
            at = pl.ds(i * rows, rows)
            self.parts.append(
                Gather(
                    plane,
                    src.at[at],
                    lambda d, at=at: dst_of(d).at[at],
                    sems.at[i, 0],
                    sems.at[i, 1],
                    local.at[i],
                )
            )

    def start(self):
        for part in self.parts:
            part.start()
        for part in self.parts:
            part.start_here()

    def relay_near(self):
        for part in self.parts:
            part.relay_near()

    def relay_far(self):
        for part in self.parts:
            part.relay_far()

    def wait_own(self):
        for part in self.parts:
            part.own.wait()

    def wait_swap(self):
        for part in self.parts:
            part.swap.wait_recv()

    def wait_share(self, i):
        for part in self.parts:
            part.share[i].wait_recv()

    def wait_sends(self):
        for part in self.parts:
            part.wait_sends()

    def finish(self):
        self.wait_own()
        self.wait_swap()
        for i in range(3):
            self.wait_share(i)
        self.wait_sends()

    @staticmethod
    def scratch(pieces):
        return [
            pltpu.SemaphoreType.DMA((pieces, 2, Gather.COPIES)),
            pltpu.SemaphoreType.DMA((pieces,)),
        ]


class Chain:
    def __init__(self, plane, mine, slot_of, sems):
        self.plane, self.mine, self.slot_of, self.sems = plane, mine, slot_of, sems

    def copy(self, way, hop, to):
        plane, row = self.plane, 0 if way > 0 else 2
        slot = self.slot_of(plane.t - way * hop)
        return remote(
            self.mine if hop == 0 else slot,
            slot,
            self.sems.at[row, hop],
            self.sems.at[row + 1, hop],
            (plane.s, to),
        )

    def inside(self, way, hop):
        t, m = self.plane.t, self.plane.m
        holds = t >= hop if way > 0 else t < m - hop
        passes = t < m - 1 if way > 0 else t > 0
        return holds, passes

    def start(self):
        self.pass_on(0)

    def pass_on(self, hop):
        for way in (1, -1):
            holds, passes = self.inside(way, hop)

            @pl.when(holds & passes)
            def _(way=way):
                self.copy(way, hop, self.plane.t + way).start()

    def step(self, hop):
        plane = self.plane
        for way in (1, -1):
            holds, _ = self.inside(way, hop)

            @pl.when(holds)
            def _(way=way):
                row = 0 if way > 0 else 2
                slot = self.slot_of(plane.t - way * hop)
                remote(
                    slot,
                    slot,
                    self.sems.at[row, hop - 1],
                    self.sems.at[row + 1, hop - 1],
                    (plane.s, plane.t - way),
                ).wait_recv()

        if hop < plane.m - 1:
            self.pass_on(hop)

    def wait_sends(self):
        for hop in range(self.plane.m - 1):
            for way in (1, -1):
                holds, passes = self.inside(way, hop)

                @pl.when(holds & passes)
                def _(way=way, hop=hop):
                    self.copy(way, hop, self.plane.t + way).wait_send()


def fan(plane, src_of, dst_of, send, recv):
    copies = []
    for k in range(1, plane.m):
        device = plane.tp_ahead(k)
        copies.append(
            remote(src_of(device[1]), dst_of(plane.t), send.at[k - 1], recv.at[k - 1], device)
        )
    return copies


def exchange(plane, src_of, dst_of, send, recv, local):
    own = pltpu.make_async_copy(src_of(plane.s), dst_of(plane.s), local)
    copies = []
    for k in range(1, plane.n):
        peer = plane.seq_ahead(k)
        copies.append(
            remote(
                src_of(peer), dst_of(plane.s), send.at[k - 1], recv.at[k - 1], plane.device(peer)
            )
        )
    return [own] + copies


TILE = 16


def in_tiles(rows, body):
    def one(i, carry):
        body(pl.ds(pl.multiple_of(i * TILE, TILE), TILE))
        return carry

    lax.fori_loop(0, rows // TILE, one, 0)


class Reduce:
    SLOTS = (4, 4, 3)

    THEIRS = (0, 2, 1, 3)

    def __init__(self, plane, part_of, pair, near, far, sems, loc, stage=None):
        c = plane.c
        self.pair, self.near, self.far = pair, near, far
        self.rows = pair.shape[1]
        self.swaps, self.loads = {}, {}
        for k in range(4):
            mine = self.THEIRS[k]
            chip = plane.order[mine]
            source = part_of(2 * chip + 1 - c) if stage is None else stage.at[mine]
            self.swaps[k] = remote(
                source, near.at[k], sems.at[0, k], sems.at[1, k], plane.sibling()
            )
            if stage is None:
                self.loads[k] = pltpu.make_async_copy(
                    part_of(2 * plane.order[k] + c), pair.at[k], loc.at[k]
                )

        def out(i, k, chip):
            return remote(
                pair.at[k], far.at[i], sems.at[2, i], sems.at[3, i], plane.same(chip)
            )

        self.out = [out(0, 3, plane.to), out(1, 1, plane.to), out(2, 2, plane.fro)]

    def start(self, *which):
        for k in which:
            self.swaps[k].start()
            self.loads[k].start()

    def landed(self, k):
        self.swaps[k].wait()
        if self.loads:
            self.loads[k].wait()

    def join(self, k):
        pair, near = self.pair, self.near
        self.landed(k)

        def add(at):
            both = pair[k, at, :].astype(f32) + near[k, at, :].astype(f32)
            pair[k, at, :] = both.astype(bf16)

        in_tiles(self.rows, add)

    def send_to(self):
        self.join(3)
        self.out[0].start()
        self.join(1)
        self.out[1].start()

    def ready(self):
        self.landed(2)

    def send_fro(self):
        pair, near, far = self.pair, self.near, self.far
        self.out[0].wait_recv()

        def add(at):
            both = pair[2, at, :].astype(f32) + near[2, at, :].astype(f32)
            pair[2, at, :] = (both + far[0, at, :].astype(f32)).astype(bf16)

        in_tiles(self.rows, add)
        self.out[2].start()

    def first(self, total, more=None):
        pair, near = self.pair, self.near
        self.landed(0)

        def add(at):
            value = pair[0, at, :].astype(f32) + near[0, at, :].astype(f32)
            total[at, :] = value if more is None else value + more[at, :]

        in_tiles(self.rows, add)

    def finish(self, total, out=None):
        far = self.far
        out = total if out is None else out
        self.out[0].wait_send()
        self.out[1].wait()
        self.out[2].wait()

        def add(at):
            value = total[at, :] + far[1, at, :].astype(f32) + far[2, at, :].astype(f32)
            out[at, :] = value.astype(out.dtype)

        in_tiles(self.rows, add)

    @staticmethod
    def scratch(rows, width):
        return [pltpu.VMEM((slots, rows, width), bf16) for slots in Reduce.SLOTS] + [
            pltpu.SemaphoreType.DMA((4, 4)),
            pltpu.SemaphoreType.DMA((4,)),
        ]


def last_body(
    n, m, dqkv_in, w_in, narrow, x_in, dresid_in, gain, norm_t, ffn, wo, vec,
    input_grad, ffn_out, qkv_out, wo_out, vec_out,
    dqkv, w, x, dresid, pair, near, far, sr, lr, total, stage, norms, mine, got, summed, sems, st, loc,
):
    plane = Plane(n, m)
    loads = [
        pltpu.make_async_copy(a, b, loc.at[5 + i])
        for i, (a, b) in enumerate(
            ((dqkv_in, dqkv), (w_in, w), (x_in, x), (dresid_in, dresid))
        )
    ]
    load = pltpu.make_async_copy(norm_t, norms, loc.at[0])
    for copy in loads + [load]:
        copy.start()
    enter_plane(plane, True)
    rows, width = ffn_out.shape[1], ffn.shape[2]
    across = fan(plane, lambda t: wo.at[t], lambda t: wo_out.at[t], st.at[1, 0], st.at[1, 1])
    across += fan(plane, lambda t: vec.at[t], lambda t: vec_out.at[t], st.at[2, 0], st.at[2, 1])
    across += [
        pltpu.make_async_copy(wo.at[plane.t], wo_out.at[plane.t], loc.at[1]),
        pltpu.make_async_copy(vec.at[plane.t], vec_out.at[plane.t], loc.at[2]),
    ]
    for copy in across:
        copy.start()
    a = exchange(
        plane,
        lambda i: ffn.at[:, pl.ds(pl.multiple_of(i * rows, rows), rows), :],
        lambda i: ffn_out.at[:, :, pl.ds(pl.multiple_of(i * width, width), width)],
        sems.at[0, 0],
        sems.at[0, 1],
        loc.at[3],
    )
    reduce = Reduce(plane, None, pair, near, far, sr, lr, stage)
    tokens = pair.shape[1]
    for copy in loads[:2]:
        copy.wait()

    def blocks(it, carry):
        k = 3 - it // 2
        other = 1 - lax.rem(it, 2)
        b = plane.number(k, other)
        here = pl.ds(pl.multiple_of(b * tokens, tokens), tokens)
        part = lax.dot_general(dqkv[here, :], w[...], NT, preferred_element_type=f32).astype(bf16)

        @pl.when(other == 0)
        def _():
            pair[k] = part

        @pl.when(other == 1)
        def _():
            stage[k] = part

        for kk in range(4):

            @pl.when(it == 2 * (3 - kk))
            def _(kk=kk):
                reduce.swaps[Reduce.THEIRS[kk]].start()

        @pl.when(it == 2)
        def _():
            for copy in a:
                copy.start()

        return carry

    lax.fori_loop(0, n, blocks, 0)
    reduce.send_to()
    load.wait()
    strip = summed.shape[1]

    def weight_grads(s, carry):
        at = pl.ds(pl.multiple_of(s * m * strip, m * strip), m * strip)
        value = jnp.dot(norms[at, :], dqkv[...], preferred_element_type=f32).astype(bf16)
        value = jnp.dot(value, narrow[...], preferred_element_type=f32).astype(bf16)
        for t in range(m):
            mine[s, t] = value[t * strip : (t + 1) * strip]
        return carry

    lax.fori_loop(0, n, weight_grads, 0)
    over = fan(plane, lambda t: mine.at[:, t], lambda t: got.at[t], st.at[0, 0], st.at[0, 1])
    for copy in over:
        copy.start()
    reduce.ready()
    reduce.first(total)
    reduce.send_fro()
    for copy in over:
        copy.wait()

    def add(s, carry):
        value = mine[s, plane.t].astype(f32)
        for k in range(1, m):
            value = value + got[plane.tp_behind(k), s].astype(f32)
        summed[s] = value.astype(bf16)
        return carry

    lax.fori_loop(0, n, add, 0)
    b = exchange(
        plane,
        lambda i: summed.at[i],
        lambda i: qkv_out.at[i],
        sems.at[1, 0],
        sems.at[1, 1],
        loc.at[4],
    )
    for copy in b:
        copy.start()
    for copy in loads[2:]:
        copy.wait()
    reduce.finish(total)

    def into_input(at):
        value = x[at, :].astype(f32)
        scale = lax.rsqrt(jnp.mean(value * value, axis=1, keepdims=True) + norm_epsilon)
        inner = gain[...] * total[at, :]
        moment = jnp.mean(value * inner, axis=1, keepdims=True)
        input_grad[at, :] = (
            dresid[at, :] + scale * inner - value * scale * (scale * scale * moment)
        )

    in_tiles(tokens, into_input)
    for copy in a + b + across:
        copy.wait()


def last(n, m, dqkv, w, narrow, x, dresid, gain, norm_t, ffn, wo, vec, ident):
    width, length = norm_t.shape
    tokens = length // n
    cols = narrow.shape[1]
    strip = width // (n * m)
    vmem = pl.BlockSpec(memory_space=pltpu.VMEM)
    hbm = pl.BlockSpec(memory_space=ANY)
    return pl.pallas_call(
        functools.partial(last_body, n, m),
        out_shape=(
            jax.ShapeDtypeStruct((tokens, width), f32),
            jax.ShapeDtypeStruct((3, ffn.shape[1] // n, ffn.shape[2] * n), ffn.dtype),
            jax.ShapeDtypeStruct((n, strip, cols), bf16),
            jax.ShapeDtypeStruct(wo.shape, wo.dtype),
            jax.ShapeDtypeStruct(vec.shape, vec.dtype),
        ),
        in_specs=[hbm, hbm, vmem, hbm, hbm, vmem] + [hbm] * 4,
        out_specs=[vmem] + [hbm] * 4,
        scratch_shapes=[
            pltpu.VMEM(dqkv.shape, bf16),
            pltpu.VMEM(w.shape, bf16),
            pltpu.VMEM(x.shape, bf16),
            pltpu.VMEM(dresid.shape, f32),
        ]
        + Reduce.scratch(tokens, width)
        + [
            pltpu.VMEM((tokens, width), f32),
            pltpu.VMEM((4, tokens, width), bf16),
            pltpu.VMEM((width, length), bf16),
            pltpu.VMEM((n, m, strip, cols), bf16),
            pltpu.VMEM((m, n, strip, cols), bf16),
            pltpu.VMEM((n, strip, cols), bf16),
            pltpu.SemaphoreType.DMA((2, 2, n - 1)),
            pltpu.SemaphoreType.DMA((3, 2, m - 1)),
            pltpu.SemaphoreType.DMA((9,)),
        ],
        compiler_params=pltpu.CompilerParams(
            collective_id=ident, has_side_effects=True, vmem_limit_bytes=VMEM_LIMIT
        ),
        cost_estimate=COST,
        name="last",
    )(dqkv, w, narrow, x, dresid, gain, norm_t, ffn, wo, vec)


def column(row):
    return jnp.broadcast_to(row, (8, row.shape[1])).T[:, :1]


def gain_row(tiles, which, strip):
    stacked = tiles.reshape(-1, LANES).astype(bf16)
    count = stacked.shape[0] // 8
    shape = (LANES, count * strip)
    lane = lax.broadcasted_iota(jnp.int32, shape, 1).astype(f32)
    owner = jnp.floor((lane + 0.5) * (1.0 / strip))
    inside = lane - owner * strip
    pick = lax.broadcasted_iota(jnp.int32, shape, 0).astype(f32) == inside
    spread_out = jnp.dot(
        stacked, jnp.where(pick, 1.0, 0.0).astype(bf16), preferred_element_type=f32
    )
    shape = spread_out.shape
    lane = lax.broadcasted_iota(jnp.int32, shape, 1).astype(f32)
    owner = jnp.floor((lane + 0.5) * (1.0 / strip))
    row = lax.broadcasted_iota(jnp.int32, shape, 0).astype(f32)
    mine = row == owner * 8.0 + which
    return jnp.sum(jnp.where(mine, spread_out, 0.0), axis=0, keepdims=True)


def entry_body(
    n, m, heads, strip, x, places, wqkv, gains, wg, wu, wd, wo, widen, inverse,
    norm_t, q, k, v, cosine, sine, w, gain_rows, docs, ffn, down, wo_z,
    blocks, norms, turned, places_all, w_all, gains_all, q_here, k_here, v_here, cos_here, sin_here,
    sx, lx, rem, sz, sn, loc,
):
    plane = Plane(n, m)
    enter_plane(plane, True)
    tokens = x.shape[0]
    gather = Gathers(plane, x, lambda i: blocks.at[i], sx, lx, 2)
    first = []
    for i, (src, dst) in enumerate(((gains, gains_all), (wqkv, w_all))):
        first += exchange(
            plane,
            lambda s, src=src, i=i: src.at[s] if i else src,
            lambda s, dst=dst: dst.at[s, plane.t],
            rem.at[i, 0],
            rem.at[i, 1],
            loc.at[1 + i],
        )
    few = exchange(
        plane, lambda i: places, lambda i: places_all.at[i], rem.at[2, 0], rem.at[2, 1], loc.at[3]
    )
    for copy in first + few:
        copy.start()
    gather.start()
    across = []
    for i, ref in enumerate((gains_all, w_all)):

        def slot(t, ref=ref):
            return ref.at[:, plane.t]

        across.append(fan(plane, slot, slot, sz.at[i, 0], sz.at[i, 1]))
    across.append(fan(plane, lambda t: wo, lambda t: wo_z.at[t], sz.at[2, 0], sz.at[2, 1]))
    own_wo = pltpu.make_async_copy(wo, wo_z.at[plane.t], loc.at[4])
    own_wo.start()
    for copy in first:
        copy.wait()
    for copy in across[0] + across[1]:
        copy.start()
    moves = []
    width, rows = wg.shape[1] // n, wg.shape[0]
    for j, weight in enumerate((wg, wu, wd)):
        moves += exchange(
            plane,
            lambda i, weight=weight: weight.at[:, pl.ds(pl.multiple_of(i * width, width), width)],
            lambda i, dst=ffn.at[j] if j < 2 else down: dst.at[
                pl.ds(pl.multiple_of(i * rows, rows), rows), :
            ],
            rem.at[3 + j, 0],
            rem.at[3 + j, 1],
            loc.at[5 + j],
        )
    for copy in few + across[0]:
        copy.wait()
    tiles = gains_all[...]
    for i in range(2):
        gain_rows[i] = gain_row(tiles, i, strip)
    gather.wait_own()

    def number(it):
        return plane.number(it // 2, lax.rem(it, 2))

    def store(it, at):
        span = pl.ds(pl.multiple_of(number(it) * tokens, tokens), tokens)
        return pltpu.make_async_copy(turned.at[at], norm_t.at[:, span], sn.at[at])

    def normalize(it, carry):
        b = number(it)
        at = lax.rem(it, 2)

        @pl.when(it == 1)
        def _():
            gather.wait_swap()

        @pl.when(it == 2)
        def _():
            gather.relay_near()

        @pl.when(it == 3)
        def _():
            gather.wait_share(1)

        @pl.when(it == 5)
        def _():
            gather.wait_share(0)

        @pl.when(it == 6)
        def _():
            gather.relay_far()
            for copy in moves + across[2]:
                copy.start()

        @pl.when(it == 7)
        def _():
            gather.wait_share(2)

        @pl.when(it >= 2)
        def _():
            store(it - 2, at).wait()

        value = blocks[b].astype(f32)
        scale = lax.rsqrt(jnp.mean(value * value, axis=1, keepdims=True) + norm_epsilon)
        low = (value * scale * gain_rows[0]).astype(bf16)
        norms[b] = low
        turned[at] = low.T
        store(it, at).start()
        here = pl.ds(pl.multiple_of(b * tokens, tokens), tokens)
        docs[:, here] = places_all[b, 0:1, :]
        angles = column(places_all[b, 1:2, :].astype(f32)) * inverse[...]
        lanes = lax.broadcasted_iota(jnp.int32, angles.shape, 1)
        sin = jnp.sin(angles)
        cos_here[here, :] = jnp.cos(angles)
        sin_here[here, :] = jnp.where(lanes < SLOT, -sin, sin)
        return carry

    lax.fori_loop(0, n, normalize, 0)
    outs = [
        pltpu.make_async_copy(cos_here, cosine, loc.at[8]),
        pltpu.make_async_copy(sin_here, sine, loc.at[9]),
        pltpu.make_async_copy(q_here, q, loc.at[10]),
        pltpu.make_async_copy(k_here, k, loc.at[11]),
        pltpu.make_async_copy(v_here, v, loc.at[12]),
    ]
    for copy in outs[:2]:
        copy.start()
    for copy in across[1]:
        copy.wait()

    def widened(s, carry):
        at = pl.ds(pl.multiple_of(s * m * strip, m * strip), m * strip)
        narrow = w_all[s].reshape(m * strip, w_all.shape[3])
        w[at, :] = jnp.dot(narrow, widen[...], preferred_element_type=f32).astype(bf16)
        return carry

    lax.fori_loop(0, n, widened, 0)

    def project(b, carry):
        here = pl.ds(pl.multiple_of(b * tokens, tokens), tokens)
        out = jnp.dot(norms[b], w[...], preferred_element_type=f32)
        cos, sin = cos_here[here, :], sin_here[here, :]
        for h in range(heads + 1):
            part = out[:, h * LANES : (h + 1) * LANES]
            rotated = (part * cos + pltpu.roll(part, SLOT, 1) * sin).astype(bf16)
            if h < heads:
                q_here[h, here, :] = rotated
            else:
                k_here[here, :] = rotated
        v_here[here, :] = out[:, (heads + 1) * LANES :].astype(bf16)
        return carry

    lax.fori_loop(0, n, project, 0)
    for copy in outs[2:]:
        copy.start()
    gather.wait_sends()
    store(n - 2, 0).wait()
    store(n - 1, 1).wait()
    own_wo.wait()
    for copy in across[2] + moves + outs:
        copy.wait()


def entry(n, m, heads, x, places, wqkv, gains, wg, wu, wd, wo, widen, inverse, ident):
    tokens, width = x.shape
    length = n * tokens
    strip = wqkv.shape[1]
    wide = widen.shape[1]
    rows, cols = wg.shape
    vmem = pl.BlockSpec(memory_space=pltpu.VMEM)
    hbm = pl.BlockSpec(memory_space=ANY)
    return pl.pallas_call(
        functools.partial(entry_body, n, m, heads, strip),
        out_shape=(
            jax.ShapeDtypeStruct((width, length), bf16),
            jax.ShapeDtypeStruct((heads, length, LANES), bf16),
            jax.ShapeDtypeStruct((length, LANES), bf16),
            jax.ShapeDtypeStruct((length, LANES), bf16),
            jax.ShapeDtypeStruct((length, LANES), f32),
            jax.ShapeDtypeStruct((length, LANES), f32),
            jax.ShapeDtypeStruct((width, wide), bf16),
            jax.ShapeDtypeStruct((2, 1, width), f32),
            jax.ShapeDtypeStruct((1, length), jnp.int32),
            jax.ShapeDtypeStruct((2, rows * n, cols // n), wg.dtype),
            jax.ShapeDtypeStruct((rows * n, cols // n), wg.dtype),
            jax.ShapeDtypeStruct((m,) + wo.shape, wo.dtype),
        ),
        in_specs=[hbm] * 8 + [vmem] * 2,
        out_specs=[hbm] * 6 + [vmem] * 3 + [hbm] * 3,
        scratch_shapes=[
            pltpu.VMEM((n, tokens, width), bf16),
            pltpu.VMEM((n, tokens, width), bf16),
            pltpu.VMEM((2, width, tokens), bf16),
            pltpu.VMEM((n,) + places.shape, places.dtype),
            pltpu.VMEM((n, m) + wqkv.shape[1:], wqkv.dtype),
            pltpu.VMEM((n, m) + gains.shape, gains.dtype),
            pltpu.VMEM((heads, length, LANES), bf16),
            pltpu.VMEM((length, LANES), bf16),
            pltpu.VMEM((length, LANES), bf16),
            pltpu.VMEM((length, LANES), f32),
            pltpu.VMEM((length, LANES), f32),
            *Gathers.scratch(2),
            pltpu.SemaphoreType.DMA((6, 2, n - 1)),
            pltpu.SemaphoreType.DMA((3, 2, m - 1)),
            pltpu.SemaphoreType.DMA((2,)),
            pltpu.SemaphoreType.DMA((13,)),
        ],
        compiler_params=pltpu.CompilerParams(
            collective_id=ident, has_side_effects=True, vmem_limit_bytes=VMEM_LIMIT
        ),
        cost_estimate=COST,
        name="entry",
    )(x, places, wqkv, gains, wg, wu, wd, wo, widen, inverse)


BLOCK = 512
NT = (((1,), (1,)), ((), ()))
LOG2E = 1.4426950408889634


def allowed_block(first_key, first_query, begin, causal):
    keys = first_key + lax.broadcasted_iota(jnp.int32, (BLOCK, BLOCK), 0)
    ok = keys >= begin
    if causal:
        queries = first_query + lax.broadcasted_iota(jnp.int32, (BLOCK, BLOCK), 1)
        ok = ok & (keys <= queries)
    return ok


def begins(docs):
    begin = jnp.zeros(docs.shape, jnp.int32)
    for d in range(3):
        count = jnp.sum((docs == d).astype(f32), axis=1, keepdims=True).astype(jnp.int32)
        begin = begin + jnp.where(docs > d, count, 0)
    return begin


def attend_body(
    n, m, factor, q, k, v, docs, wo, go, x, gain,
    o, lse, start, mine_all, wo_all, go_all, resid, norm,
    mine, vt, top, total, acc, begin_row, low, wo_here, go_here, sems, so, sl, loc,
):
    h, i = pl.program_id(0), pl.program_id(1)
    heads, blocks = pl.num_programs(0), pl.num_programs(1)
    plane = Plane(n, m)
    filled = wo.shape[1]

    def wo_at(i):
        return wo_here.at[i, :, pl.ds(0, filled), :]

    first = Gathers(plane, wo, wo_at, sems.at[0], loc.at[0], 2)
    second = Gathers(plane, go, lambda i: go_here.at[i], sems.at[1], loc.at[1], 2)
    at_step = h * blocks + i
    rows = go.shape[0]
    each = BLOCK // rows

    @pl.when(at_step == 0)
    def _():
        enter_plane(plane, False)
        first.start()
        gap = (n, wo_here.shape[1], SLOT - filled, wo_here.shape[3])
        wo_here[:, :, filled:, :] = jnp.zeros(gap, bf16)
        vt[...] = v[...].T
        begin_row[...] = begins(docs[...])
        start[...] = begin_row[...]

    @pl.when(at_step == 6)
    def _():
        second.start()
        first.relay_near()

    top[...] = jnp.full_like(top, mask_fill_value)
    total[...] = jnp.zeros_like(total)
    acc[...] = jnp.zeros_like(acc)
    query = q[0]
    begin = begin_row[:, pl.ds(pl.multiple_of(i * BLOCK, BLOCK), BLOCK)]

    def step(j, causal):
        at = pl.ds(pl.multiple_of(j * BLOCK, BLOCK), BLOCK)
        raw = lax.dot_general(k[at, :], query, NT, preferred_element_type=f32)
        ok = allowed_block(j * BLOCK, i * BLOCK, begin, causal)
        scores = jnp.where(ok, raw * factor, mask_fill_value)
        new_top = jnp.maximum(top[...], jnp.max(scores, axis=0, keepdims=True))
        weights = jnp.exp2(scores - new_top)
        keep = jnp.exp2(top[...] - new_top)
        total[...] = total[...] * keep + jnp.sum(weights, axis=0, keepdims=True)
        acc[...] = acc[...] * keep + jnp.dot(
            vt[:, at], weights.astype(bf16), preferred_element_type=f32
        )
        top[...] = new_top

    def loop(j, carry):
        step(j, False)
        return carry

    lax.fori_loop(0, i, loop, 0)
    step(i, True)
    out = (acc[...] / total[...]).T
    o[0] = out
    low[h, pl.ds(pl.multiple_of(i * BLOCK, BLOCK), BLOCK), :] = out.astype(bf16)
    lse[0] = top[...] + jnp.log2(total[...])

    def part(hh, owner):
        return low.at[hh, pl.ds(pl.multiple_of(owner * rows, rows), rows), :]

    def place(hh, source):
        return mine.at[source, :, pl.ds(pl.multiple_of(hh * LANES, LANES), LANES)]

    def send(hh, owner):
        return remote(
            part(hh, owner),
            place(hh, plane.s),
            so.at[0, hh, owner],
            so.at[1, hh, plane.s],
            plane.device(owner),
        )

    def keep_own(hh):
        return pltpu.make_async_copy(part(hh, plane.s), place(hh, plane.s), sl.at[hh])

    for r in range(each):
        owner = i * each + r

        @pl.when(owner != plane.s)
        def _(owner=owner):
            send(h, owner).start()

        @pl.when(owner == plane.s)
        def _():
            keep_own(h).start()

    @pl.when(at_step == heads * blocks - 1)
    def _():
        first.relay_far()
        second.relay_near()
        for hh in range(low.shape[0]):
            keep_own(hh).wait()
            for owner in range(n):

                @pl.when(owner != plane.s)
                def _(hh=hh, owner=owner):
                    send(hh, owner).wait_send()
                    remote(
                        part(hh, owner),
                        place(hh, owner),
                        so.at[0, hh, owner],
                        so.at[1, hh, owner],
                        plane.device(owner),
                    ).wait_recv()

        first.finish()
        whole = [
            pltpu.make_async_copy(wo_here, wo_all, loc.at[2, 0]),
            pltpu.make_async_copy(mine, mine_all, loc.at[2, 1]),
        ]
        for copy in whole:
            copy.start()
        resid[...] = x[...].astype(f32)
        width = resid.shape[1]

        def branch(s, carry):
            rhs = wo_here[s].reshape(-1, width)
            resid[...] += jnp.dot(mine[s], rhs, preferred_element_type=f32)
            return carry

        lax.fori_loop(0, n, branch, 0)
        second.relay_far()

        def normalize(at):
            value = resid[at, :]
            scale = lax.rsqrt(jnp.mean(value * value, axis=1, keepdims=True) + norm_epsilon)
            norm[at, :] = (value * scale * gain[...]).astype(bf16)

        in_tiles(rows, normalize)
        second.finish()
        rest = pltpu.make_async_copy(go_here, go_all, loc.at[3, 0])
        rest.start()
        for copy in whole + [rest]:
            copy.wait()


def attend(n, m, factor, q, k, v, docs, wo, go, x, gain, ident):
    heads, length, _ = q.shape
    blocks = length // BLOCK
    rows, width = x.shape
    hbm = pl.BlockSpec(memory_space=ANY)

    def fixed(*shape):
        return pl.BlockSpec(
            shape, lambda h, i: (0,) * len(shape), pipeline_mode=pl.Buffered(buffer_count=1)
        )

    return pl.pallas_call(
        functools.partial(attend_body, n, m, factor),
        grid=(heads, blocks),
        out_shape=(
            jax.ShapeDtypeStruct((heads, length, LANES), f32),
            jax.ShapeDtypeStruct((heads, 1, length), f32),
            jax.ShapeDtypeStruct((1, length), jnp.int32),
            jax.ShapeDtypeStruct((n, rows, heads * LANES), bf16),
            jax.ShapeDtypeStruct((n, wo.shape[0], SLOT, width), wo.dtype),
            jax.ShapeDtypeStruct((n,) + go.shape, go.dtype),
            jax.ShapeDtypeStruct((rows, width), f32),
            jax.ShapeDtypeStruct((rows, width), bf16),
        ),
        in_specs=[
            pl.BlockSpec((1, BLOCK, LANES), lambda h, i: (h, i, 0)),
            fixed(length, LANES),
            fixed(length, LANES),
            fixed(1, length),
            hbm,
            hbm,
            fixed(rows, width),
            fixed(1, width),
        ],
        out_specs=[
            pl.BlockSpec((1, BLOCK, LANES), lambda h, i: (h, i, 0)),
            pl.BlockSpec((1, 1, BLOCK), lambda h, i: (h, 0, i)),
            fixed(1, length),
            hbm,
            hbm,
            hbm,
            fixed(rows, width),
            fixed(rows, width),
        ],
        scratch_shapes=[
            pltpu.VMEM((n, rows, heads * LANES), bf16),
            pltpu.VMEM((LANES, length), bf16),
            pltpu.VMEM((1, BLOCK), f32),
            pltpu.VMEM((1, BLOCK), f32),
            pltpu.VMEM((LANES, BLOCK), f32),
            pltpu.VMEM((1, length), jnp.int32),
            pltpu.VMEM((heads, length, LANES), bf16),
            pltpu.VMEM((n, wo.shape[0], SLOT, width), wo.dtype),
            pltpu.VMEM((n,) + go.shape, go.dtype),
            pltpu.SemaphoreType.DMA((2, 2, 2, Gather.COPIES)),
            pltpu.SemaphoreType.DMA((2, heads, n)),
            pltpu.SemaphoreType.DMA((heads,)),
            pltpu.SemaphoreType.DMA((4, 2)),
        ],
        compiler_params=pltpu.CompilerParams(
            collective_id=ident, has_side_effects=True, vmem_limit_bytes=VMEM_LIMIT
        ),
        cost_estimate=COST,
        name="attend",
    )(q, k, v, docs, wo, go, x, gain)


def attend_back_body(
    n, m, factor, scale, heads, q, k, v, o, lse, begin, cosine, sine,
    mixed, wo, mine, dnorm, resid, grad, gain,
    out, layer, term_sum, dresid, gain_out,
    kt, dqt, dk, dv, delta, pair, near, far, sr, lr, pair2, near2, far2, sr2, lr2, stage2,
    held, held2, wo_here, dbranch, go_out, go, gain_sum, gain_cut, gain_got, sg, sv, loc,
):
    h = pl.program_id(0)
    j = pl.program_id(1)
    blocks = pl.num_programs(1)
    plane = Plane(n, m)
    one = Reduce(plane, lambda i: mixed.at[i], pair, near, far, sr, lr)
    two = Reduce(plane, None, pair2, near2, far2, sr2, lr2, stage2)
    at_step = h * blocks + j
    rows, width = dnorm.shape
    strip = gain_out.shape[2]
    gain_copies = exchange(
        plane, lambda i: gain_cut.at[i], lambda i: gain_got.at[i], sv.at[0], sv.at[1], loc.at[1]
    )

    def own_heads():
        return pltpu.make_async_copy(go_out.at[plane.s], go.at[plane.s], loc.at[2])

    def send_heads(r):
        peer = plane.seq_ahead(r)
        return remote(
            go_out.at[peer], go.at[plane.s], sg.at[0, r], sg.at[1, r], plane.device(peer)
        )

    @pl.when(at_step == 0)
    def _():
        load = pltpu.make_async_copy(wo, wo_here, loc.at[0])
        load.start()
        enter_plane(plane, False)
        one.start(3, 1)
        gain_sum[...] = jnp.zeros_like(gain_sum)

        def into_branch(at):
            value, up = resid[at, :], dnorm[at, :]
            scale_two = lax.rsqrt(jnp.mean(value * value, axis=1, keepdims=True) + norm_epsilon)
            inner = gain[...] * up
            moment = jnp.mean(value * inner, axis=1, keepdims=True)
            turned = value * scale_two
            got = (
                grad[at, :].astype(f32)
                + scale_two * inner
                - turned * (scale_two * scale_two * moment)
            )
            dresid[at, :] = got
            dbranch[at, :] = got.astype(bf16)
            gain_sum[...] += up * turned

        in_tiles(rows, into_branch)
        one.send_to()
        one.start(2, 0)
        total_gain = jnp.sum(gain_sum[...], axis=0, keepdims=True)
        for i in range(n):
            gain_cut[i] = total_gain[:, i * (width // n) : (i + 1) * (width // n)]
        for copy in gain_copies:
            copy.start()
        load.wait()

        def into_heads(r, carry):
            peer = plane.seq_ahead(r)
            value = lax.dot_general(
                dbranch[...], wo_here[peer], NT, preferred_element_type=f32
            ).astype(bf16)
            for hh in range(heads):
                go_out[peer, hh] = value[:, hh * LANES : (hh + 1) * LANES]

            @pl.when(r == 0)
            def _():
                own_heads().start()

            @pl.when(r > 0)
            def _():
                send_heads(r).start()

            return carry

        lax.fori_loop(0, n, into_heads, 0)

        def into_terms(it, carry):
            kk = 3 - it // 2
            other = 1 - lax.rem(it, 2)
            b = plane.number(kk, other)
            value = lax.dot_general(
                mine[b], dbranch[...], (((0,), (0,)), ((), ())), preferred_element_type=f32
            ).astype(bf16)
            for half in range(2 * heads):
                cut = value[half * SLOT : half * SLOT + HALF]
                at = slice(half * HALF, (half + 1) * HALF)

                @pl.when(other == 0)
                def _(cut=cut, at=at):
                    pair2[kk, at, :] = cut

                @pl.when(other == 1)
                def _(cut=cut, at=at):
                    stage2[kk, at, :] = cut

            for which in range(4):

                @pl.when(it == 2 * (3 - which))
                def _(which=which):
                    two.swaps[Reduce.THEIRS[which]].start()

            return carry

        lax.fori_loop(0, n, into_terms, 0)
        own_heads().wait()
        for r in range(1, n):
            send_heads(r).wait()

    @pl.when(at_step == 1)
    def _():
        two.send_to()
        one.ready()
        one.first(held, resid)

    @pl.when(at_step == 3)
    def _():
        one.send_fro()

    @pl.when(at_step == 4)
    def _():
        two.ready()
        two.first(held2)

    def heads_grad(i):
        each = BLOCK // rows
        return go[pl.ds(i * each, each), h].reshape(BLOCK, LANES)

    @pl.when((h == 0) & (j == 0))
    def _():
        kt[...] = k[...].T
        dk[...] = jnp.zeros_like(dk)
        dv[...] = jnp.zeros_like(dv)

    @pl.when(j == 0)
    def _():
        dqt[...] = jnp.zeros_like(dqt)

        def deltas(i, carry):
            at = pl.ds(pl.multiple_of(i * BLOCK, BLOCK), BLOCK)
            both = (heads_grad(i).astype(f32) * o[0, at, :]).T
            delta[:, at] = jnp.sum(both, axis=0, keepdims=True)
            return carry

        lax.fori_loop(0, blocks, deltas, 0)

    keys_at = pl.ds(pl.multiple_of(j * BLOCK, BLOCK), BLOCK)
    key = k[keys_at, :]
    value = v[keys_at, :]

    def step(i, causal):
        at = pl.ds(pl.multiple_of(i * BLOCK, BLOCK), BLOCK)
        query = q[0, at, :]
        raw = lax.dot_general(key, query, NT, preferred_element_type=f32)
        ok = allowed_block(j * BLOCK, i * BLOCK, begin[:, at], causal)
        probs = jnp.where(ok, jnp.exp2(raw * factor - lse[0, :, at]), 0.0)
        grads = heads_grad(i)
        dprob = lax.dot_general(value, grads, NT, preferred_element_type=f32)
        dscore = (probs * (dprob - delta[:, at])).astype(bf16)
        dv[keys_at, :] += jnp.dot(probs.astype(bf16), grads, preferred_element_type=f32)
        dk[keys_at, :] += jnp.dot(dscore, query, preferred_element_type=f32)
        dqt[:, at] += jnp.dot(kt[:, keys_at], dscore, preferred_element_type=f32)

    step(j, True)

    def loop(i, carry):
        step(i, False)
        return carry

    lax.fori_loop(j + 1, blocks, loop, 0)

    def unturn(value, at):
        return value * cosine[at, :] - pltpu.roll(value, SLOT, 1) * sine[at, :]

    @pl.when(j == blocks - 1)
    def _():
        def write(i, carry):
            at = pl.ds(pl.multiple_of(i * BLOCK, BLOCK), BLOCK)
            got = unturn(dqt[:, at].T * scale, at).astype(bf16)
            for which in range(heads):

                @pl.when(h == which)
                def _(which=which):
                    out[at, which * LANES : (which + 1) * LANES] = got

            return carry

        lax.fori_loop(0, blocks, write, 0)

    @pl.when((h == heads - 1) & (j == blocks - 1))
    def _():
        def write(i, carry):
            at = pl.ds(pl.multiple_of(i * BLOCK, BLOCK), BLOCK)
            out[at, heads * LANES : (heads + 1) * LANES] = unturn(dk[at, :] * scale, at).astype(
                bf16
            )
            out[at, (heads + 1) * LANES :] = dv[at, :].astype(bf16)
            return carry

        lax.fori_loop(0, blocks, write, 0)
        two.send_fro()
        one.finish(held, layer)
        for copy in gain_copies:
            copy.wait()
        got = gain_got[0]
        for i in range(1, n):
            got = got + gain_got[i]
        for t in range(m):
            gain_out[t] = got[:, t * strip : (t + 1) * strip]
        two.finish(held2, term_sum)


def attend_back(
    n, m, factor, scale, q, k, v, o, lse, begin, cosine, sine,
    mixed, wo, mine, dnorm, resid, grad, gain, ident,
):
    heads, length, _ = q.shape
    blocks = length // BLOCK
    rows, width = dnorm.shape
    strip = width // (n * m)

    def fixed(*shape):
        return pl.BlockSpec(
            shape, lambda h, j: (0,) * len(shape), pipeline_mode=pl.Buffered(buffer_count=1)
        )

    hbm = pl.BlockSpec(memory_space=ANY)
    one = pl.BlockSpec((1, length, LANES), lambda h, j: (h, 0, 0))
    return pl.pallas_call(
        functools.partial(attend_back_body, n, m, factor, scale, heads),
        grid=(heads, blocks),
        out_shape=(
            jax.ShapeDtypeStruct((length, (heads + 2) * LANES), bf16),
            jax.ShapeDtypeStruct((rows, width), bf16),
            jax.ShapeDtypeStruct((width // n, width), bf16),
            jax.ShapeDtypeStruct((rows, width), f32),
            jax.ShapeDtypeStruct((m, 1, strip), f32),
        ),
        in_specs=[
            one,
            fixed(length, LANES),
            fixed(length, LANES),
            one,
            pl.BlockSpec((1, 1, length), lambda h, j: (h, 0, 0)),
            fixed(1, length),
            fixed(length, LANES),
            fixed(length, LANES),
            hbm,
            hbm,
            fixed(*mine.shape),
            fixed(rows, width),
            fixed(rows, width),
            fixed(rows, width),
            fixed(1, width),
        ],
        out_specs=[
            fixed(length, (heads + 2) * LANES),
            fixed(rows, width),
            fixed(width // n, width),
            fixed(rows, width),
            fixed(m, 1, strip),
        ],
        scratch_shapes=[
            pltpu.VMEM((LANES, length), bf16),
            pltpu.VMEM((LANES, length), f32),
            pltpu.VMEM((length, LANES), f32),
            pltpu.VMEM((length, LANES), f32),
            pltpu.VMEM((1, length), f32),
        ]
        + Reduce.scratch(rows, width)
        + Reduce.scratch(width // n, width)
        + [
            pltpu.VMEM((4, width // n, width), bf16),
            pltpu.VMEM((rows, width), f32),
            pltpu.VMEM((width // n, width), f32),
            pltpu.VMEM(wo.shape, bf16),
            pltpu.VMEM((rows, width), bf16),
            pltpu.VMEM((n, heads, rows, LANES), bf16),
            pltpu.VMEM((n, heads, rows, LANES), bf16),
            pltpu.VMEM((TILE, width), f32),
            pltpu.VMEM((n, 1, width // n), f32),
            pltpu.VMEM((n, 1, width // n), f32),
            pltpu.SemaphoreType.DMA((2, n)),
            pltpu.SemaphoreType.DMA((2, n - 1)),
            pltpu.SemaphoreType.DMA((3,)),
        ],
        compiler_params=pltpu.CompilerParams(
            collective_id=ident, has_side_effects=True, vmem_limit_bytes=VMEM_LIMIT
        ),
        cost_estimate=COST,
        name="attend_back",
    )(q, k, v, o, lse, begin, cosine, sine, mixed, wo, mine, dnorm, resid, grad, gain)


def feed_body(
    n, m, mine, go, w_in, down, dnorm, grads, mixed,
    rows, rows_t, go_t, go_two, w, gates, h, mix_two, down_held, pair, near, far, stage,
    sg, lg, sr, loc, sw, so, sm, sd, sz,
):
    plane = Plane(n, m)
    tokens = rows.shape[1]
    hid = down.shape[1]
    enter_plane(plane, True)
    gather = Gathers(plane, mine, lambda i: rows.at[i], sg, lg, 2)
    reduce = Reduce(plane, None, pair, near, far, sr, None, stage)
    gather.start()

    def down_at(t):
        return w.at[2, :, pl.ds(pl.multiple_of(t * hid, hid), hid)]

    chain = Chain(plane, down, down_at, sz)
    chain.start()
    own_down = pltpu.make_async_copy(down, down_at(plane.t), loc.at[0])
    own_down.start()
    weights = [
        pltpu.make_async_copy(
            w_in.at[t, j], w.at[j, :, t * hid : (t + 1) * hid], sw.at[j, t]
        )
        for j in range(2)
        for t in range(m)
    ]
    for copy in weights:
        copy.start()

    gather.wait_own()
    for copy in weights:
        copy.wait()

    def span(b):
        return pl.ds(pl.multiple_of(b * tokens, tokens), tokens)

    def forward(it, carry):
        b = plane.number(it // 2, lax.rem(it, 2))

        @pl.when(it == 1)
        def _():
            gather.wait_swap()

        @pl.when(it == 2)
        def _():
            chain.step(1)
            gather.relay_near()

        @pl.when(it == 3)
        def _():
            gather.wait_share(1)

        @pl.when(it == 4)
        def _():
            chain.step(2)

        @pl.when(it == 5)
        def _():
            gather.wait_share(0)

        @pl.when(it == 6)
        def _():
            gather.relay_far()

        @pl.when(it == 7)
        def _():
            gather.wait_share(2)

        slot = lax.rem(it, 2)

        @pl.when(it < n - 1)
        def _():
            early_go(it + 1, 1 - slot).start()

        row = rows[b]
        gate = jnp.dot(row, w[0], preferred_element_type=f32)
        up = jnp.dot(row, w[1], preferred_element_type=f32)
        gates[0, span(b), :] = gate
        gates[1, span(b), :] = up
        h[2, span(b), :] = (gate * jax.nn.sigmoid(gate) * up).astype(bf16)
        rows_t[:, span(b)] = row.T
        early_go(it, slot).wait()
        go_t[:, span(b)] = go_two[slot].T
        return carry

    def early_go(it, slot):
        b = plane.number(it // 2, lax.rem(it, 2))
        return pltpu.make_async_copy(go.at[b], go_two.at[slot], so.at[slot])

    early_go(0, 0).start()
    lax.fori_loop(0, n, forward, 0)

    def number(it):
        return plane.number(3 - it // 2, 1 - lax.rem(it, 2))

    def load_go(it, slot):
        return pltpu.make_async_copy(go.at[number(it)], go_two.at[slot], so.at[slot])

    def store_mix(it, slot):
        return pltpu.make_async_copy(mix_two.at[slot], mixed.at[number(it)], sm.at[slot])

    width = rows.shape[2]

    def weight_grad(j, left, held):
        def part(i, carry):
            at = pl.ds(pl.multiple_of(i * 256, 256), 256)
            value = jnp.dot(left[at, :], h[j], preferred_element_type=f32)
            held[at, :] = value.astype(bf16)
            return carry

        lax.fori_loop(0, width // 256, part, 0)
        outs = [
            pltpu.make_async_copy(
                held.at[:, t * hid : (t + 1) * hid], grads.at[t, j], sd.at[j, t]
            )
            for t in range(m)
        ]
        for copy in outs:
            copy.start()
        return outs

    load_go(0, 0).start()
    outs = weight_grad(2, go_t, down_held)
    for hop in range(3, m):
        chain.step(hop)
    own_down.wait()

    def backward(it, carry):
        slot = lax.rem(it, 2)
        k = 3 - it // 2
        b = number(it)

        @pl.when(it == 3)
        def _():
            reduce.join(3)
            reduce.out[0].start()

        @pl.when(it == 6)
        def _():
            reduce.join(1)
            reduce.out[1].start()

        @pl.when(it < n - 1)
        def _():
            load_go(it + 1, 1 - slot).start()

        load_go(it, slot).wait()

        @pl.when(it >= 2)
        def _():
            store_mix(it - 2, slot).wait()

        gate = gates[0, span(b), :]
        up = gates[1, span(b), :]
        grad = go_two[slot]
        dhidden = jnp.dot(grad, w[2], preferred_element_type=f32)
        sig = jax.nn.sigmoid(gate)
        hidden = h[2, span(b), :]
        dgate = (dhidden * up * sig * (1.0 + gate * (1.0 - sig))).astype(bf16)
        dup = (dhidden * gate * sig).astype(bf16)
        h[0, span(b), :] = dgate
        h[1, span(b), :] = dup
        part = lax.dot_general(dgate, w[0], NT, preferred_element_type=f32)
        part = part + lax.dot_general(dup, w[1], NT, preferred_element_type=f32)
        part = part.astype(bf16)

        @pl.when(lax.rem(it, 2) == 1)
        def _():
            pair[k] = part

        @pl.when(lax.rem(it, 2) == 0)
        def _():
            stage[k] = part

        for kk in range(4):

            @pl.when(it == 2 * (3 - kk))
            def _(kk=kk):
                reduce.swaps[Reduce.THEIRS[kk]].start()

        mix_two[slot] = lax.dot_general(hidden, w[2], NT, preferred_element_type=f32).astype(bf16)
        store_mix(it, slot).start()
        return carry

    lax.fori_loop(0, n, backward, 0)
    store_mix(n - 2, 0).wait()
    store_mix(n - 1, 1).wait()
    reduce.ready()
    reduce.send_fro()
    outs += weight_grad(0, rows_t, w.at[0])
    reduce.first(dnorm)
    outs += weight_grad(1, rows_t, w.at[1])
    gather.wait_sends()
    chain.wait_sends()
    reduce.finish(dnorm)
    for copy in outs:
        copy.wait()


def feed(n, m, norm, go, w_in, down, ident):
    tokens, width = norm.shape
    hid = down.shape[1]
    length = n * tokens
    return pl.pallas_call(
        functools.partial(feed_body, n, m),
        out_shape=(
            jax.ShapeDtypeStruct((tokens, width), f32),
            jax.ShapeDtypeStruct((m, 3, width, hid), bf16),
            jax.ShapeDtypeStruct((n, tokens, width), bf16),
        ),
        in_specs=[pl.BlockSpec(memory_space=ANY)] * 4,
        out_specs=[
            pl.BlockSpec(memory_space=pltpu.VMEM),
            pl.BlockSpec(memory_space=ANY),
            pl.BlockSpec(memory_space=ANY),
        ],
        scratch_shapes=[
            pltpu.VMEM((n, tokens, width), bf16),
            pltpu.VMEM((width, length), bf16),
            pltpu.VMEM((width, length), bf16),
            pltpu.VMEM((2, tokens, width), bf16),
            pltpu.VMEM((3, width, m * hid), bf16),
            pltpu.VMEM((2, length, m * hid), f32),
            pltpu.VMEM((3, length, m * hid), bf16),
            pltpu.VMEM((2, tokens, width), bf16),
            pltpu.VMEM((width, m * hid), bf16),
        ]
        + [pltpu.VMEM((slots, tokens, width), bf16) for slots in Reduce.SLOTS]
        + [
            pltpu.VMEM((4, tokens, width), bf16),
            *Gathers.scratch(2),
            pltpu.SemaphoreType.DMA((4, 4)),
            pltpu.SemaphoreType.DMA((1,)),
            pltpu.SemaphoreType.DMA((2, m)),
            pltpu.SemaphoreType.DMA((2,)),
            pltpu.SemaphoreType.DMA((2,)),
            pltpu.SemaphoreType.DMA((3, m)),
            pltpu.SemaphoreType.DMA((4, m)),
        ],
        compiler_params=pltpu.CompilerParams(
            collective_id=ident, has_side_effects=True, vmem_limit_bytes=VMEM_LIMIT
        ),
        cost_estimate=COST,
        name="feed",
    )(norm, go, w_in, down)


def split_heads(w, groups):
    rows = w.shape[0]
    return w.reshape(rows, groups, -1).transpose(1, 0, 2)


def fast_layer(n, m):
    def on_plane(
        layer_input,
        doc_ids,
        positions,
        first_gain,
        query_weight,
        key_weight,
        value_weight,
        output_weight,
        second_gain,
        gate_weight,
        up_weight,
        down_weight,
        out_grad,
    ):
        x = layer_input[0]
        rows, width = x.shape
        length = rows * n
        heads = QUERY_HEADS // n
        scale = 1.0 / math.sqrt(HEAD_SIZE)
        factor = scale * LOG2E
        strip = query_weight.shape[0]
        hid = gate_weight.shape[1] // n

        packed = jnp.concatenate(
            [split_heads(w, n) for w in (query_weight, key_weight, value_weight)], axis=2
        )
        cols = packed.shape[2]
        gains = jnp.pad(
            jnp.stack([first_gain, second_gain]).astype(f32), ((0, 6), (0, LANES - strip))
        )
        places = jnp.concatenate([doc_ids, positions], axis=0)
        lane = jnp.arange(LANES) % SLOT
        inverse = jnp.where(
            lane < HALF, rope_base ** (-(lane.astype(f32) * 2.0 / HEAD_SIZE)), 0.0
        )[None]
        from_col = jnp.arange(cols)
        to_lane = from_col // HALF * SLOT + from_col % HALF
        widen = (to_lane[:, None] == jnp.arange(cols // HALF * SLOT)[None, :]).astype(bf16)

        norm_t, q, k, v, cosine, sine, wqkv, gain_rows, docs, ffn_mine, down_mine, output_rows = entry(
            n, m, heads, x, places, packed, gains,
            gate_weight, up_weight, down_weight, output_weight, widen, inverse, 0,
        )
        gain_one, gain_two = gain_rows[0], gain_rows[1]
        ffn_all = lax.all_gather(ffn_mine, "tp", axis=0, tiled=False)
        o, lse, begin, mine, output_full, grad_all, resid, norm_two = attend(
            n, m, factor, q, k, v, docs,
            output_rows.reshape(-1, HALF, width), out_grad[0], x, gain_two, 9,
        )
        dnorm_two, ffn_terms, mixed = feed(n, m, norm_two, grad_all, ffn_all, down_mine, 2)
        ffn_sum = lax.psum_scatter(ffn_terms, "tp", scatter_dimension=0, tiled=False)
        dqkv, layer_output, output_sum, dresid, gain_part = attend_back(
            n, m, factor, scale, q, k, v, o, lse, begin, cosine, sine, mixed,
            output_full.reshape(n, -1, width), mine, dnorm_two, resid, out_grad[0], gain_two, 3,
        )
        input_grad, ffn_out, qkv_out, output_parts, gain_sums = last(
            n, m, dqkv, wqkv, widen.T, x, dresid, gain_one, norm_t, ffn_sum,
            output_sum.reshape(m, strip, width), gain_part, 6,
        )
        output_grad = jnp.sum(output_parts.astype(f32), axis=0)

        gate_grad, up_grad, down_grad = [ffn_out[i].astype(f32) for i in range(3)]
        kv = HEAD_SIZE * KEY_VALUE_HEADS // n
        split = heads * HEAD_SIZE

        def columns(a, b):
            return qkv_out[:, :, a:b].transpose(1, 0, 2).reshape(strip, -1).astype(f32)

        query_grad = columns(0, split)
        key_grad = columns(split, split + kv)
        value_grad = columns(split + kv, cols)

        one = (
            jnp.sum(query_weight.astype(f32) * query_grad, axis=1)
            + jnp.sum(key_weight.astype(f32) * key_grad, axis=1)
            + jnp.sum(value_weight.astype(f32) * value_grad, axis=1)
        )
        first_gain_grad = one / first_gain.astype(f32)
        second_gain_grad = jnp.sum(gain_sums, axis=(0, 1))
        return (
            layer_output[None],
            input_grad[None],
            first_gain_grad,
            query_grad,
            key_grad,
            value_grad,
            output_grad,
            second_gain_grad,
            gate_grad,
            up_grad,
            down_grad,
        )

    return on_plane


def solution(mesh):
    n, m = mesh.shape["seq"], mesh.shape["tp"]
    fits = n == KEY_VALUE_HEADS == 8
    return jax.shard_map(
        fast_layer(n, m) if fits else on_device,
        mesh=mesh,
        in_specs=(
            P("tp", "seq", None),
            P("tp", "seq"),
            P("tp", "seq"),
            P(("seq", "tp")),
            P(("seq", "tp"), None),
            P(("seq", "tp"), None),
            P(("seq", "tp"), None),
            P(("seq", "tp"), None),
            P(("seq", "tp")),
            P("seq", "tp"),
            P("seq", "tp"),
            P("seq", "tp"),
            P("tp", "seq", None),
        ),
        out_specs=(
            P("tp", "seq", None),
            P("tp", "seq", None),
            P(("seq", "tp")),
            P(("seq", "tp"), None),
            P(("seq", "tp"), None),
            P(("seq", "tp"), None),
            P(("seq", "tp"), None),
            P(("seq", "tp")),
            P("seq", "tp"),
            P("seq", "tp"),
            P("seq", "tp"),
        ),
        check_vma=False,
    )
```

```python
import functools
import math

import jax
import jax.numpy as jnp
from jax import lax
from jax.experimental import pallas as pl
from jax.experimental.pallas import tpu as pltpu
from jax.sharding import PartitionSpec as P

QUERY_HEADS = 16
KEY_VALUE_HEADS = 8
HEAD_SIZE = 96


norm_epsilon = 1e-05
rope_base = 100000.0
mask_fill_value = -1e30


def rope_tables(places):
    half = HEAD_SIZE // 2
    inverse = rope_base ** (-(jnp.arange(half, dtype=jnp.float32) * 2.0 / HEAD_SIZE))
    angles = places.astype(jnp.float32)[:, None] * inverse[None, :]
    return (jnp.cos(angles), jnp.sin(angles))


def apply_rotary(value_rows, cosine_table, sine_table, heads, direction):
    sequence_length = value_rows.shape[0]
    split = value_rows.reshape(sequence_length, heads, 2, HEAD_SIZE // 2)
    first = split[:, :, 0]
    second = split[:, :, 1]
    cosine = cosine_table[:, None, :]
    sine = direction * sine_table[:, None, :]
    turned = jnp.stack([first * cosine - second * sine, second * cosine + first * sine], axis=2)
    return turned.reshape(sequence_length, heads * HEAD_SIZE)


def outer_product(left, right):
    return lax.dot_general(
        left, right, (((0,), (0,)), ((), ())), preferred_element_type=jnp.float32
    )


def times_transpose(left, right):
    return lax.dot_general(
        left, right, (((1,), (1,)), ((), ())), preferred_element_type=jnp.float32
    )


def norm_backward(inputs, scale, gain, upstream):
    inner = gain * upstream
    moment = jnp.mean(inputs * inner, axis=1, keepdims=True)
    return (
        scale * inner - inputs * scale * scale * scale * moment,
        jnp.sum(upstream * inputs * scale, axis=0),
    )


def on_device(
    layer_input,
    doc_ids,
    positions,
    first_gain,
    query_weight,
    key_weight,
    value_weight,
    output_weight,
    second_gain,
    gate_weight,
    up_weight,
    down_weight,
    out_grad,
):
    token_rows = layer_input.shape[1]
    query_groups = QUERY_HEADS // KEY_VALUE_HEADS
    scale_of_scores = 1.0 / math.sqrt(HEAD_SIZE)
    inputs_f = layer_input[0].astype(jnp.float32)
    my_docs = doc_ids[0]
    gain_one, query_full, complete_keys, value_full, output_full, gain_two = (
        lax.all_gather(first_gain, ("seq", "tp"), axis=0, tiled=True),
        lax.all_gather(query_weight, ("seq", "tp"), axis=0, tiled=True),
        lax.all_gather(key_weight, ("seq", "tp"), axis=0, tiled=True),
        lax.all_gather(value_weight, ("seq", "tp"), axis=0, tiled=True),
        lax.all_gather(output_weight, ("seq", "tp"), axis=0, tiled=True),
        lax.all_gather(second_gain, ("seq", "tp"), axis=0, tiled=True),
    )
    gain_one_f = gain_one.astype(jnp.float32)
    gain_two_f = gain_two.astype(jnp.float32)
    scale_one = lax.rsqrt(jnp.mean(inputs_f * inputs_f, axis=1, keepdims=True) + norm_epsilon)
    first_normalized = (inputs_f * scale_one * gain_one_f).astype(jnp.bfloat16)
    cosine_table, sine_table = rope_tables(positions[0])
    rotated_query = apply_rotary(
        jnp.dot(first_normalized, query_full, preferred_element_type=jnp.float32),
        cosine_table,
        sine_table,
        QUERY_HEADS,
        1.0,
    ).astype(jnp.bfloat16)
    key_rot = apply_rotary(
        jnp.dot(first_normalized, complete_keys, preferred_element_type=jnp.float32),
        cosine_table,
        sine_table,
        KEY_VALUE_HEADS,
        1.0,
    ).astype(jnp.bfloat16)
    value_low = jnp.dot(first_normalized, value_full, preferred_element_type=jnp.float32).astype(
        jnp.bfloat16
    )
    gathered_keys, gathered_values, doc_all = (
        lax.all_gather(key_rot, "seq", axis=0, tiled=True),
        lax.all_gather(value_low, "seq", axis=0, tiled=True),
        lax.all_gather(my_docs.astype(jnp.bfloat16), "seq", axis=0, tiled=True),
    )
    sequence_length = gathered_keys.shape[0]
    block_number = math.gcd(512, sequence_length)
    block_count = sequence_length // block_number
    query_index = lax.axis_index("seq") * token_rows + jnp.arange(token_rows, dtype=jnp.int32)
    my_doc_f = my_docs.astype(jnp.float32)
    heads_of_query = rotated_query.reshape(token_rows, KEY_VALUE_HEADS, query_groups, HEAD_SIZE)
    layer_entries = (
        gathered_keys.reshape(block_count, block_number, KEY_VALUE_HEADS, HEAD_SIZE),
        gathered_values.reshape(block_count, block_number, KEY_VALUE_HEADS, HEAD_SIZE),
        doc_all.astype(jnp.float32).reshape(block_count, block_number),
        jnp.arange(block_count, dtype=jnp.int32) * block_number,
    )

    def allowed_of(doc_piece, start):
        key_index = start + jnp.arange(block_number, dtype=jnp.int32)
        return (key_index[None, :] <= query_index[:, None]) & (
            doc_piece[None, :] == my_doc_f[:, None]
        )

    def scores_of(key_piece, allowed):
        raw = (
            jnp.einsum(
                "tgrd,kgd->tgrk", heads_of_query, key_piece, preferred_element_type=jnp.float32
            )
            * scale_of_scores
        )
        return jnp.where(allowed[:, None, None, :], raw, mask_fill_value)

    def total_step(carry, item):
        key_piece, value_piece, doc_piece, start = item
        allowed = allowed_of(doc_piece, start)

        def total_work(state):
            top, total = state
            scores = scores_of(key_piece, allowed)
            new_top = jnp.maximum(top, jnp.max(scores, axis=3))
            weights = jnp.where(
                allowed[:, None, None, :], jnp.exp(scores - new_top[..., None]), 0.0
            )
            return (new_top, total * jnp.exp(top - new_top) + jnp.sum(weights, axis=3))

        return (lax.cond(jnp.any(allowed), total_work, lambda state: state, carry), None)

    start_state = (
        jnp.full((token_rows, KEY_VALUE_HEADS, query_groups), mask_fill_value, jnp.float32),
        jnp.zeros((token_rows, KEY_VALUE_HEADS, query_groups), jnp.float32),
    )
    (top, total), unused_result = lax.scan(total_step, start_state, layer_entries)
    log_total = top + jnp.log(total)

    def probs_of(key_piece, allowed):
        scores = scores_of(key_piece, allowed)
        return jnp.where(allowed[:, None, None, :], jnp.exp(scores - log_total[..., None]), 0.0)

    def output_update(accum, item):
        key_piece, value_piece, doc_piece, start = item
        allowed = allowed_of(doc_piece, start)

        def output_work(state):
            probs = probs_of(key_piece, allowed).astype(jnp.bfloat16)
            return state + jnp.einsum(
                "tgrk,kgd->tgrd", probs, value_piece, preferred_element_type=jnp.float32
            )

        return (lax.cond(jnp.any(allowed), output_work, lambda state: state, accum), None)

    heads_output, unused_result = lax.scan(
        output_update,
        jnp.zeros((token_rows, KEY_VALUE_HEADS, query_groups, HEAD_SIZE), jnp.float32),
        layer_entries,
    )
    attn_low = heads_output.reshape(token_rows, QUERY_HEADS * HEAD_SIZE).astype(jnp.bfloat16)
    resid = inputs_f + jnp.dot(attn_low, output_full, preferred_element_type=jnp.float32)
    scale_two = lax.rsqrt(jnp.mean(resid * resid, axis=1, keepdims=True) + norm_epsilon)
    normed_two = (resid * scale_two * gain_two_f).astype(jnp.bfloat16)
    rows_all = lax.all_gather(normed_two, "tp", axis=0, tiled=True)
    gate_cols, up_cols, down_cols = (
        lax.all_gather(gate_weight, "seq", axis=0, tiled=True),
        lax.all_gather(up_weight, "seq", axis=0, tiled=True),
        lax.all_gather(down_weight, "seq", axis=0, tiled=True),
    )
    gate_pre = jnp.dot(rows_all, gate_cols, preferred_element_type=jnp.float32)
    up_pre = jnp.dot(rows_all, up_cols, preferred_element_type=jnp.float32)
    gate_sig = jax.nn.sigmoid(gate_pre)
    gate_act = gate_pre * gate_sig
    hidden = (gate_act * up_pre).astype(jnp.bfloat16)
    mixed = lax.psum_scatter(
        times_transpose(hidden, down_cols).astype(jnp.bfloat16),
        "tp",
        scatter_dimension=0,
        tiled=True,
    ).astype(jnp.float32)
    layer_output = (resid + mixed).astype(jnp.bfloat16)[None]
    grad_low = out_grad[0]
    grad_f = grad_low.astype(jnp.float32)
    grad_all = lax.all_gather(grad_low, "tp", axis=0, tiled=True)
    dhidden = jnp.dot(grad_all, down_cols, preferred_element_type=jnp.float32)
    dgate = (dhidden * up_pre * gate_sig * (1.0 + gate_pre * (1.0 - gate_sig))).astype(jnp.bfloat16)
    dup = (dhidden * gate_act).astype(jnp.bfloat16)
    gate_term = outer_product(rows_all, dgate)
    up_term = outer_product(rows_all, dup)
    down_term_grad = outer_product(grad_all, hidden)
    dnorm_two = lax.psum_scatter(
        (times_transpose(dgate, gate_cols) + times_transpose(dup, up_cols)).astype(jnp.bfloat16),
        "tp",
        scatter_dimension=0,
        tiled=True,
    ).astype(jnp.float32)
    gate_grad, up_grad, down_grad = (
        lax.psum_scatter(
            gate_term.astype(jnp.bfloat16), "seq", scatter_dimension=0, tiled=True
        ).astype(jnp.float32),
        lax.psum_scatter(
            up_term.astype(jnp.bfloat16), "seq", scatter_dimension=0, tiled=True
        ).astype(jnp.float32),
        lax.psum_scatter(
            down_term_grad.astype(jnp.bfloat16), "seq", scatter_dimension=0, tiled=True
        ).astype(jnp.float32),
    )
    resid_part, gain_two_term = norm_backward(resid, scale_two, gain_two_f, dnorm_two)
    dresid = grad_f + resid_part
    dbranch = dresid.astype(jnp.bfloat16)
    output_term = outer_product(attn_low, dbranch)
    heads_gradient = times_transpose(dbranch, output_full).astype(jnp.bfloat16)
    grouped_heads_gradient = heads_gradient.reshape(
        token_rows, KEY_VALUE_HEADS, query_groups, HEAD_SIZE
    )
    delta = jnp.sum(grouped_heads_gradient.astype(jnp.float32) * heads_output, axis=3)

    def gradient_update(dquery, item):
        key_piece, value_piece, doc_piece, start = item
        allowed = allowed_of(doc_piece, start)

        def gradient_work(state):
            probs = probs_of(key_piece, allowed)
            value_piece_grad = jnp.einsum(
                "tgrk,tgrd->kgd",
                probs.astype(jnp.bfloat16),
                grouped_heads_gradient,
                preferred_element_type=jnp.float32,
            )
            prob_grad = jnp.einsum(
                "tgrd,kgd->tgrk",
                grouped_heads_gradient,
                value_piece,
                preferred_element_type=jnp.float32,
            )
            score_grad = (probs * (prob_grad - delta[..., None])).astype(jnp.bfloat16)
            key_piece_grad = jnp.einsum(
                "tgrk,tgrd->kgd", score_grad, heads_of_query, preferred_element_type=jnp.float32
            )
            updated = state + jnp.einsum(
                "tgrk,kgd->tgrd", score_grad, key_piece, preferred_element_type=jnp.float32
            )
            return (updated, (key_piece_grad, value_piece_grad))

        def skip(state):
            blank_tensor = jnp.zeros((block_number, KEY_VALUE_HEADS, HEAD_SIZE), jnp.float32)
            return (state, (blank_tensor, blank_tensor))

        return lax.cond(jnp.any(allowed), gradient_work, skip, dquery)

    dquery, (key_contributions, value_contributions) = lax.scan(
        gradient_update,
        jnp.zeros((token_rows, KEY_VALUE_HEADS, query_groups, HEAD_SIZE), jnp.float32),
        layer_entries,
    )
    gathered_key_contributions = (
        key_contributions.reshape(sequence_length, KEY_VALUE_HEADS * HEAD_SIZE) * scale_of_scores
    )
    gathered_value_contributions = value_contributions.reshape(
        sequence_length, KEY_VALUE_HEADS * HEAD_SIZE
    )
    local_keys, value_mine = (
        lax.psum_scatter(
            gathered_key_contributions.astype(jnp.bfloat16), "seq", scatter_dimension=0, tiled=True
        ).astype(jnp.float32),
        lax.psum_scatter(
            gathered_value_contributions.astype(jnp.bfloat16),
            "seq",
            scatter_dimension=0,
            tiled=True,
        ).astype(jnp.float32),
    )
    dq_pre = apply_rotary(
        dquery.reshape(token_rows, QUERY_HEADS * HEAD_SIZE) * scale_of_scores,
        cosine_table,
        sine_table,
        QUERY_HEADS,
        -1.0,
    ).astype(jnp.bfloat16)
    key_gradient_unrotated = apply_rotary(
        local_keys, cosine_table, sine_table, KEY_VALUE_HEADS, -1.0
    ).astype(jnp.bfloat16)
    dv_pre = value_mine.astype(jnp.bfloat16)
    dnorm_one = (
        times_transpose(dq_pre, query_full)
        + times_transpose(key_gradient_unrotated, complete_keys)
        + times_transpose(dv_pre, value_full)
    )
    input_part, gain_one_term = norm_backward(inputs_f, scale_one, gain_one_f, dnorm_one)
    input_grad = (dresid + input_part)[None]
    query_term = outer_product(first_normalized, dq_pre)
    key_term = outer_product(first_normalized, key_gradient_unrotated)
    value_term = outer_product(first_normalized, dv_pre)
    first_gain_grad, query_grad, key_grad, value_grad, output_grad, second_gain_grad = (
        lax.psum_scatter(gain_one_term, ("seq", "tp"), scatter_dimension=0, tiled=True),
        lax.psum_scatter(query_term, ("seq", "tp"), scatter_dimension=0, tiled=True),
        lax.psum_scatter(key_term, ("seq", "tp"), scatter_dimension=0, tiled=True),
        lax.psum_scatter(value_term, ("seq", "tp"), scatter_dimension=0, tiled=True),
        lax.psum_scatter(output_term, ("seq", "tp"), scatter_dimension=0, tiled=True),
        lax.psum_scatter(gain_two_term, ("seq", "tp"), scatter_dimension=0, tiled=True),
    )
    return (
        layer_output,
        input_grad,
        first_gain_grad,
        query_grad,
        key_grad,
        value_grad,
        output_grad,
        second_gain_grad,
        gate_grad,
        up_grad,
        down_grad,
    )


MESH = pl.DeviceIdType.MESH
ANY = pl.ANY
HALF = HEAD_SIZE // 2
LANES = 128
SLOT = LANES // 2
f32 = jnp.float32
bf16 = jnp.bfloat16
VMEM_LIMIT = 62 << 20
COST = pl.CostEstimate(flops=1_000_000, transcendentals=0, bytes_accessed=100_000)


class Plane:
    def __init__(self, n, m):
        self.n, self.m, self.chips = n, m, n // 2
        self.s = lax.axis_index("seq")
        self.t = lax.axis_index("tp")
        self.q = self.s // 2
        self.c = lax.rem(self.s, 2)

        across = self.q + 1 - 2 * lax.rem(self.q, 2)
        along = lax.rem(self.q + 2, 4)
        self.to = across * (1 - self.c) + along * self.c
        self.fro = across * self.c + along * (1 - self.c)
        self.far = 3 - self.q
        self.order = (self.q, self.to, self.fro, self.far)

    def device(self, s):
        return (s, self.t)

    def same(self, chip):
        return (2 * chip + self.c, self.t)

    def number(self, k, other):
        c, q = self.c, self.q
        low, high = lax.rem(k, 2), k // 2
        dx = low * (1 - c) + high * c
        dy = high * (1 - c) + low * c
        x, y = lax.rem(q, 2), q // 2
        chip = 2 * (y + dy - 2 * y * dy) + x + dx - 2 * x * dx
        return 2 * chip + c + other * (1 - 2 * c)

    def sibling(self):
        return (2 * self.q + 1 - self.c, self.t)

    def ahead(self, k):
        return lax.rem(self.q + k, self.chips)

    def behind(self, k):
        return lax.rem(self.q + self.chips - k, self.chips)

    def seq_ahead(self, k):
        return lax.rem(self.s + k, self.n)

    def seq_behind(self, k):
        return lax.rem(self.s + self.n - k, self.n)

    def tp_ahead(self, k):
        return (self.s, lax.rem(self.t + k, self.m))

    def tp_behind(self, k):
        return lax.rem(self.t + self.m - k, self.m)


def enter_plane(plane, with_tp):
    barrier = pltpu.get_barrier_semaphore()
    for k in range(1, plane.n):
        pl.semaphore_signal(
            barrier, inc=1, device_id=plane.device(plane.seq_ahead(k)), device_id_type=MESH
        )
    count = plane.n - 1
    if with_tp:
        for k in range(1, plane.m):
            pl.semaphore_signal(barrier, inc=1, device_id=plane.tp_ahead(k), device_id_type=MESH)
        count += plane.m - 1
    pl.semaphore_wait(barrier, count)


def remote(src, dst, send, recv, device):
    return pltpu.make_async_remote_copy(
        src_ref=src,
        dst_ref=dst,
        send_sem=send,
        recv_sem=recv,
        device_id=device,
        device_id_type=MESH,
    )


class Gather:
    COPIES = 7

    def __init__(self, plane, src, dst_of, send, recv, local):
        to, fro, far, c = plane.to, plane.fro, plane.far, plane.c
        here = dst_of(plane.s)
        self.own = pltpu.make_async_copy(src, here, local)

        def block(chip):
            return dst_of(2 * chip + c)

        def copy(i, a, b, device):
            return remote(a, b, send.at[i], recv.at[i], device)

        sibling = plane.sibling()
        self.swap = copy(0, src, here, sibling)
        self.ahead = copy(1, src, here, plane.same(to))
        self.back = copy(2, src, here, plane.same(fro))
        self.relay = copy(3, block(fro), block(fro), plane.same(to))
        self.share = [
            copy(4, block(to), block(to), sibling),
            copy(5, block(fro), block(fro), sibling),
            copy(6, block(far), block(far), sibling),
        ]

    def start(self):
        self.back.start()
        self.ahead.start()

    def start_here(self):
        self.swap.start()
        self.own.start()

    def relay_near(self):
        self.back.wait_recv()
        self.relay.start()
        self.share[1].start()
        self.ahead.wait_recv()
        self.share[0].start()

    def relay_far(self):
        self.relay.wait_recv()
        self.share[2].start()

    def wait_sends(self):
        for copy in [self.swap, self.ahead, self.back, self.relay] + self.share:
            copy.wait_send()


class Gathers:
    def __init__(self, plane, src, dst_of, sems, local, pieces):
        rows = src.shape[0] // pieces
        self.parts = []
        for i in range(pieces):
            at = pl.ds(i * rows, rows)
            self.parts.append(
                Gather(
                    plane,
                    src.at[at],
                    lambda d, at=at: dst_of(d).at[at],
                    sems.at[i, 0],
                    sems.at[i, 1],
                    local.at[i],
                )
            )

    def start(self):
        for part in self.parts:
            part.start()
        for part in self.parts:
            part.start_here()

    def relay_near(self):
        for part in self.parts:
            part.relay_near()

    def relay_far(self):
        for part in self.parts:
            part.relay_far()

    def wait_own(self):
        for part in self.parts:
            part.own.wait()

    def wait_swap(self):
        for part in self.parts:
            part.swap.wait_recv()

    def wait_share(self, i):
        for part in self.parts:
            part.share[i].wait_recv()

    def wait_sends(self):
        for part in self.parts:
            part.wait_sends()

    def finish(self):
        self.wait_own()
        self.wait_swap()
        for i in range(3):
            self.wait_share(i)
        self.wait_sends()

    @staticmethod
    def scratch(pieces):
        return [
            pltpu.SemaphoreType.DMA((pieces, 2, Gather.COPIES)),
            pltpu.SemaphoreType.DMA((pieces,)),
        ]


class Chain:
    def __init__(self, plane, mine, slot_of, sems):
        self.plane, self.mine, self.slot_of, self.sems = plane, mine, slot_of, sems

    def copy(self, way, hop, to):
        plane, row = self.plane, 0 if way > 0 else 2
        slot = self.slot_of(plane.t - way * hop)
        return remote(
            self.mine if hop == 0 else slot,
            slot,
            self.sems.at[row, hop],
            self.sems.at[row + 1, hop],
            (plane.s, to),
        )

    def inside(self, way, hop):
        t, m = self.plane.t, self.plane.m
        holds = t >= hop if way > 0 else t < m - hop
        passes = t < m - 1 if way > 0 else t > 0
        return holds, passes

    def start(self):
        self.pass_on(0)

    def pass_on(self, hop):
        for way in (1, -1):
            holds, passes = self.inside(way, hop)

            @pl.when(holds & passes)
            def _(way=way):
                self.copy(way, hop, self.plane.t + way).start()

    def step(self, hop):
        plane = self.plane
        for way in (1, -1):
            holds, _ = self.inside(way, hop)

            @pl.when(holds)
            def _(way=way):
                row = 0 if way > 0 else 2
                slot = self.slot_of(plane.t - way * hop)
                remote(
                    slot,
                    slot,
                    self.sems.at[row, hop - 1],
                    self.sems.at[row + 1, hop - 1],
                    (plane.s, plane.t - way),
                ).wait_recv()

        if hop < plane.m - 1:
            self.pass_on(hop)

    def wait_sends(self):
        for hop in range(self.plane.m - 1):
            for way in (1, -1):
                holds, passes = self.inside(way, hop)

                @pl.when(holds & passes)
                def _(way=way, hop=hop):
                    self.copy(way, hop, self.plane.t + way).wait_send()


def fan(plane, src_of, dst_of, send, recv):
    copies = []
    for k in range(1, plane.m):
        device = plane.tp_ahead(k)
        copies.append(
            remote(src_of(device[1]), dst_of(plane.t), send.at[k - 1], recv.at[k - 1], device)
        )
    return copies


def exchange(plane, src_of, dst_of, send, recv, local):
    own = pltpu.make_async_copy(src_of(plane.s), dst_of(plane.s), local)
    copies = []
    for k in range(1, plane.n):
        peer = plane.seq_ahead(k)
        copies.append(
            remote(
                src_of(peer), dst_of(plane.s), send.at[k - 1], recv.at[k - 1], plane.device(peer)
            )
        )
    return [own] + copies


TILE = 16


def in_tiles(rows, body):
    def one(i, carry):
        body(pl.ds(pl.multiple_of(i * TILE, TILE), TILE))
        return carry

    lax.fori_loop(0, rows // TILE, one, 0)


class Reduce:
    SLOTS = (4, 4, 3)

    THEIRS = (0, 2, 1, 3)

    def __init__(self, plane, part_of, pair, near, far, sems, loc, stage=None):
        c = plane.c
        self.pair, self.near, self.far = pair, near, far
        self.rows = pair.shape[1]
        self.swaps, self.loads = {}, {}
        for k in range(4):
            mine = self.THEIRS[k]
            chip = plane.order[mine]
            source = part_of(2 * chip + 1 - c) if stage is None else stage.at[mine]
            self.swaps[k] = remote(
                source, near.at[k], sems.at[0, k], sems.at[1, k], plane.sibling()
            )
            if stage is None:
                self.loads[k] = pltpu.make_async_copy(
                    part_of(2 * plane.order[k] + c), pair.at[k], loc.at[k]
                )

        def out(i, k, chip):
            return remote(
                pair.at[k], far.at[i], sems.at[2, i], sems.at[3, i], plane.same(chip)
            )

        self.out = [out(0, 3, plane.to), out(1, 1, plane.to), out(2, 2, plane.fro)]

    def start(self, *which):
        for k in which:
            self.swaps[k].start()
            self.loads[k].start()

    def landed(self, k):
        self.swaps[k].wait()
        if self.loads:
            self.loads[k].wait()

    def join(self, k):
        pair, near = self.pair, self.near
        self.landed(k)

        def add(at):
            both = pair[k, at, :].astype(f32) + near[k, at, :].astype(f32)
            pair[k, at, :] = both.astype(bf16)

        in_tiles(self.rows, add)

    def send_to(self):
        self.join(3)
        self.out[0].start()
        self.join(1)
        self.out[1].start()

    def ready(self):
        self.landed(2)

    def send_fro(self):
        pair, near, far = self.pair, self.near, self.far
        self.out[0].wait_recv()

        def add(at):
            both = pair[2, at, :].astype(f32) + near[2, at, :].astype(f32)
            pair[2, at, :] = (both + far[0, at, :].astype(f32)).astype(bf16)

        in_tiles(self.rows, add)
        self.out[2].start()

    def first(self, total, more=None):
        pair, near = self.pair, self.near
        self.landed(0)

        def add(at):
            value = pair[0, at, :].astype(f32) + near[0, at, :].astype(f32)
            total[at, :] = value if more is None else value + more[at, :].astype(f32)

        in_tiles(self.rows, add)

    def finish(self, total, out=None):
        far = self.far
        out = total if out is None else out
        self.out[0].wait_send()
        self.out[1].wait()
        self.out[2].wait()

        def add(at):
            value = total[at, :] + far[1, at, :].astype(f32) + far[2, at, :].astype(f32)
            out[at, :] = value.astype(out.dtype)

        in_tiles(self.rows, add)

    @staticmethod
    def scratch(rows, width):
        return [pltpu.VMEM((slots, rows, width), bf16) for slots in Reduce.SLOTS] + [
            pltpu.SemaphoreType.DMA((4, 4)),
            pltpu.SemaphoreType.DMA((4,)),
        ]


def last_body(
    n, m, dqkv_in, w_in, narrow, x_in, dresid_in, gain, norm_t, ffn, downs, wo, vec,
    input_grad, ffn_out, qkv_out, wo_out, vec_out,
    dqkv, w, x, dresid, down_here, down_sum, pair, near, far, sr, lr, total, stage, norms, mine, got, summed, sems, st, loc,
):
    plane = Plane(n, m)
    loads = [
        pltpu.make_async_copy(a, b, loc.at[5 + i])
        for i, (a, b) in enumerate(
            ((dqkv_in, dqkv), (w_in, w), (downs, down_here), (x_in, x), (dresid_in, dresid))
        )
    ]
    load = pltpu.make_async_copy(norm_t, norms, loc.at[0])
    for copy in loads + [load]:
        copy.start()
    enter_plane(plane, True)
    rows, width = ffn_out.shape[1], ffn.shape[2]
    across = fan(plane, lambda t: wo.at[t], lambda t: wo_out.at[t], st.at[1, 0], st.at[1, 1])
    across += fan(plane, lambda t: vec.at[t], lambda t: vec_out.at[t], st.at[2, 0], st.at[2, 1])
    across += [
        pltpu.make_async_copy(wo.at[plane.t], wo_out.at[plane.t], loc.at[1]),
        pltpu.make_async_copy(vec.at[plane.t], vec_out.at[plane.t], loc.at[2]),
    ]
    for copy in across:
        copy.start()
    a = exchange(
        plane,
        lambda i: ffn.at[:, pl.ds(pl.multiple_of(i * rows, rows), rows), :],
        lambda i: ffn_out.at[
            pl.ds(0, 2), :, pl.ds(pl.multiple_of(i * width, width), width)
        ],
        sems.at[0, 0],
        sems.at[0, 1],
        loc.at[3],
    )
    a_down = exchange(
        plane,
        lambda i: down_sum.at[pl.ds(pl.multiple_of(i * rows, rows), rows), :],
        lambda i: ffn_out.at[2, :, pl.ds(pl.multiple_of(i * width, width), width)],
        sems.at[2, 0],
        sems.at[2, 1],
        loc.at[10],
    )
    reduce = Reduce(plane, None, pair, near, far, sr, lr, stage)
    tokens = pair.shape[1]
    for copy in loads[:2]:
        copy.wait()

    def blocks(it, carry):
        k = 3 - it // 2
        other = 1 - lax.rem(it, 2)
        b = plane.number(k, other)
        here = pl.ds(pl.multiple_of(b * tokens, tokens), tokens)
        part = lax.dot_general(dqkv[here, :], w[...], NT, preferred_element_type=f32).astype(bf16)

        @pl.when(other == 0)
        def _():
            pair[k] = part

        @pl.when(other == 1)
        def _():
            stage[k] = part

        for kk in range(4):

            @pl.when(it == 2 * (3 - kk))
            def _(kk=kk):
                reduce.swaps[Reduce.THEIRS[kk]].start()

        @pl.when(it == 2)
        def _():
            for copy in a:
                copy.start()

        return carry

    lax.fori_loop(0, n, blocks, 0)
    reduce.send_to()
    loads[2].wait()

    def add_down(at):
        value = down_here[0, at, :].astype(f32)
        for t in range(1, m):
            value = value + down_here[t, at, :].astype(f32)
        down_sum[at, :] = value.astype(bf16)

    in_tiles(down_sum.shape[0], add_down)
    for copy in a_down:
        copy.start()
    load.wait()
    strip = summed.shape[1]

    def weight_grads(s, carry):
        at = pl.ds(pl.multiple_of(s * m * strip, m * strip), m * strip)
        value = jnp.dot(norms[at, :], dqkv[...], preferred_element_type=f32).astype(bf16)
        value = jnp.dot(value, narrow[...], preferred_element_type=f32).astype(bf16)
        for t in range(m):
            mine[s, t] = value[t * strip : (t + 1) * strip]
        return carry

    lax.fori_loop(0, n, weight_grads, 0)
    over = fan(plane, lambda t: mine.at[:, t], lambda t: got.at[t], st.at[0, 0], st.at[0, 1])
    for copy in over:
        copy.start()
    reduce.ready()
    reduce.first(total)
    reduce.send_fro()
    for copy in over:
        copy.wait()

    def add(s, carry):
        value = mine[s, plane.t].astype(f32)
        for k in range(1, m):
            value = value + got[plane.tp_behind(k), s].astype(f32)
        summed[s] = value.astype(bf16)
        return carry

    lax.fori_loop(0, n, add, 0)
    b = exchange(
        plane,
        lambda i: summed.at[i],
        lambda i: qkv_out.at[i],
        sems.at[1, 0],
        sems.at[1, 1],
        loc.at[4],
    )
    for copy in b:
        copy.start()
    for copy in loads[3:]:
        copy.wait()
    reduce.finish(total)

    def into_input(at):
        value = x[at, :].astype(f32)
        scale = lax.rsqrt(jnp.mean(value * value, axis=1, keepdims=True) + norm_epsilon)
        inner = gain[...] * total[at, :]
        moment = jnp.mean(value * inner, axis=1, keepdims=True)
        input_grad[at, :] = (
            dresid[at, :] + scale * inner - value * scale * (scale * scale * moment)
        )

    in_tiles(tokens, into_input)
    for copy in a + a_down + b + across:
        copy.wait()


def last(n, m, dqkv, w, narrow, x, dresid, gain, norm_t, ffn, downs, wo, vec, ident):
    width, length = norm_t.shape
    tokens = length // n
    cols = narrow.shape[1]
    strip = width // (n * m)
    vmem = pl.BlockSpec(memory_space=pltpu.VMEM)
    hbm = pl.BlockSpec(memory_space=ANY)
    return pl.pallas_call(
        functools.partial(last_body, n, m),
        out_shape=(
            jax.ShapeDtypeStruct((tokens, width), f32),
            jax.ShapeDtypeStruct((3, ffn.shape[1] // n, ffn.shape[2] * n), ffn.dtype),
            jax.ShapeDtypeStruct((n, strip, cols), bf16),
            jax.ShapeDtypeStruct(wo.shape, wo.dtype),
            jax.ShapeDtypeStruct(vec.shape, vec.dtype),
        ),
        in_specs=[hbm, hbm, vmem, hbm, hbm, vmem] + [hbm] * 5,
        out_specs=[vmem] + [hbm] * 4,
        scratch_shapes=[
            pltpu.VMEM(dqkv.shape, bf16),
            pltpu.VMEM(w.shape, bf16),
            pltpu.VMEM(x.shape, bf16),
            pltpu.VMEM(dresid.shape, f32),
            pltpu.VMEM(downs.shape, bf16),
            pltpu.VMEM(downs.shape[1:], bf16),
        ]
        + Reduce.scratch(tokens, width)
        + [
            pltpu.VMEM((tokens, width), f32),
            pltpu.VMEM((4, tokens, width), bf16),
            pltpu.VMEM((width, length), bf16),
            pltpu.VMEM((n, m, strip, cols), bf16),
            pltpu.VMEM((m, n, strip, cols), bf16),
            pltpu.VMEM((n, strip, cols), bf16),
            pltpu.SemaphoreType.DMA((3, 2, n - 1)),
            pltpu.SemaphoreType.DMA((3, 2, m - 1)),
            pltpu.SemaphoreType.DMA((11,)),
        ],
        compiler_params=pltpu.CompilerParams(
            collective_id=ident, has_side_effects=True, vmem_limit_bytes=VMEM_LIMIT
        ),
        cost_estimate=COST,
        name="last",
    )(dqkv, w, narrow, x, dresid, gain, norm_t, ffn, downs, wo, vec)


def column(row):
    return jnp.broadcast_to(row, (8, row.shape[1])).T[:, :1]


def gain_row(tiles, which, strip):
    stacked = tiles.reshape(-1, LANES).astype(bf16)
    count = stacked.shape[0] // 8
    shape = (LANES, count * strip)
    lane = lax.broadcasted_iota(jnp.int32, shape, 1).astype(f32)
    owner = jnp.floor((lane + 0.5) * (1.0 / strip))
    inside = lane - owner * strip
    pick = lax.broadcasted_iota(jnp.int32, shape, 0).astype(f32) == inside
    spread_out = jnp.dot(
        stacked, jnp.where(pick, 1.0, 0.0).astype(bf16), preferred_element_type=f32
    )
    shape = spread_out.shape
    lane = lax.broadcasted_iota(jnp.int32, shape, 1).astype(f32)
    owner = jnp.floor((lane + 0.5) * (1.0 / strip))
    row = lax.broadcasted_iota(jnp.int32, shape, 0).astype(f32)
    mine = row == owner * 8.0 + which
    return jnp.sum(jnp.where(mine, spread_out, 0.0), axis=0, keepdims=True)


def entry_body(
    n, m, heads, strip, x, places, wqkv, gains, wg, wu, wd, wo, widen, inverse,
    norm_t, q, k, v, cosine, sine, w, gain_rows, docs, ffn, down, wo_z,
    blocks, norms, turned, places_all, w_all, gains_all, q_here, k_here, v_here, cos_here, sin_here,
    sx, lx, rem, sz, sn, loc,
):
    plane = Plane(n, m)
    enter_plane(plane, True)
    tokens = x.shape[0]
    gather = Gathers(plane, x, lambda i: blocks.at[i], sx, lx, 2)
    first = []
    for i, (src, dst) in enumerate(((gains, gains_all), (wqkv, w_all))):
        first += exchange(
            plane,
            lambda s, src=src, i=i: src.at[s] if i else src,
            lambda s, dst=dst: dst.at[s, plane.t],
            rem.at[i, 0],
            rem.at[i, 1],
            loc.at[1 + i],
        )
    few = exchange(
        plane, lambda i: places, lambda i: places_all.at[i], rem.at[2, 0], rem.at[2, 1], loc.at[3]
    )
    for copy in first + few:
        copy.start()
    gather.start()
    across = []
    for i, ref in enumerate((gains_all, w_all)):

        def slot(t, ref=ref):
            return ref.at[:, plane.t]

        across.append(fan(plane, slot, slot, sz.at[i, 0], sz.at[i, 1]))
    across.append(fan(plane, lambda t: wo, lambda t: wo_z.at[t], sz.at[2, 0], sz.at[2, 1]))
    own_wo = pltpu.make_async_copy(wo, wo_z.at[plane.t], loc.at[4])
    own_wo.start()
    for copy in first:
        copy.wait()
    for copy in across[0] + across[1]:
        copy.start()
    moves = []
    width, rows = wg.shape[1] // n, wg.shape[0]
    for j, weight in enumerate((wg, wu, wd)):
        moves += exchange(
            plane,
            lambda i, weight=weight: weight.at[:, pl.ds(pl.multiple_of(i * width, width), width)],
            lambda i, dst=ffn.at[j] if j < 2 else down: dst.at[
                pl.ds(pl.multiple_of(i * rows, rows), rows), :
            ],
            rem.at[3 + j, 0],
            rem.at[3 + j, 1],
            loc.at[5 + j],
        )
    for copy in few + across[0]:
        copy.wait()
    tiles = gains_all[...]
    for i in range(2):
        gain_rows[i] = gain_row(tiles, i, strip)
    gather.wait_own()

    def number(it):
        return plane.number(it // 2, lax.rem(it, 2))

    def store(it, at):
        span = pl.ds(pl.multiple_of(number(it) * tokens, tokens), tokens)
        return pltpu.make_async_copy(turned.at[at], norm_t.at[:, span], sn.at[at])

    def normalize(it, carry):
        b = number(it)
        at = lax.rem(it, 2)

        @pl.when(it == 1)
        def _():
            gather.wait_swap()

        @pl.when(it == 2)
        def _():
            gather.relay_near()

        @pl.when(it == 3)
        def _():
            gather.wait_share(1)

        @pl.when(it == 5)
        def _():
            gather.wait_share(0)

        @pl.when(it == 6)
        def _():
            gather.relay_far()
            for copy in moves + across[2]:
                copy.start()

        @pl.when(it == 7)
        def _():
            gather.wait_share(2)

        @pl.when(it >= 2)
        def _():
            store(it - 2, at).wait()

        value = blocks[b].astype(f32)
        scale = lax.rsqrt(jnp.mean(value * value, axis=1, keepdims=True) + norm_epsilon)
        low = (value * scale * gain_rows[0]).astype(bf16)
        norms[b] = low
        turned[at] = low.T
        store(it, at).start()
        here = pl.ds(pl.multiple_of(b * tokens, tokens), tokens)
        docs[:, here] = places_all[b, 0:1, :]
        angles = column(places_all[b, 1:2, :].astype(f32)) * inverse[...]
        lanes = lax.broadcasted_iota(jnp.int32, angles.shape, 1)
        sin = jnp.sin(angles)
        cos_here[here, :] = jnp.cos(angles)
        sin_here[here, :] = jnp.where(lanes < SLOT, -sin, sin)
        return carry

    lax.fori_loop(0, n, normalize, 0)
    outs = [
        pltpu.make_async_copy(cos_here, cosine, loc.at[8]),
        pltpu.make_async_copy(sin_here, sine, loc.at[9]),
        pltpu.make_async_copy(q_here, q, loc.at[10]),
        pltpu.make_async_copy(k_here, k, loc.at[11]),
        pltpu.make_async_copy(v_here, v, loc.at[12]),
    ]
    for copy in outs[:2]:
        copy.start()
    for copy in across[1]:
        copy.wait()

    def widened(s, carry):
        at = pl.ds(pl.multiple_of(s * m * strip, m * strip), m * strip)
        narrow = w_all[s].reshape(m * strip, w_all.shape[3])
        w[at, :] = jnp.dot(narrow, widen[...], preferred_element_type=f32).astype(bf16)
        return carry

    lax.fori_loop(0, n, widened, 0)

    def project(b, carry):
        here = pl.ds(pl.multiple_of(b * tokens, tokens), tokens)
        out = jnp.dot(norms[b], w[...], preferred_element_type=f32)
        cos, sin = cos_here[here, :], sin_here[here, :]
        for h in range(heads + 1):
            part = out[:, h * LANES : (h + 1) * LANES]
            rotated = (part * cos + pltpu.roll(part, SLOT, 1) * sin).astype(bf16)
            if h < heads:
                q_here[h, here, :] = rotated
            else:
                k_here[here, :] = rotated
        v_here[here, :] = out[:, (heads + 1) * LANES :].astype(bf16)
        return carry

    lax.fori_loop(0, n, project, 0)
    for copy in outs[2:]:
        copy.start()
    gather.wait_sends()
    store(n - 2, 0).wait()
    store(n - 1, 1).wait()
    own_wo.wait()
    for copy in across[2] + moves + outs:
        copy.wait()


def entry(n, m, heads, x, places, wqkv, gains, wg, wu, wd, wo, widen, inverse, ident):
    tokens, width = x.shape
    length = n * tokens
    strip = wqkv.shape[1]
    wide = widen.shape[1]
    rows, cols = wg.shape
    vmem = pl.BlockSpec(memory_space=pltpu.VMEM)
    hbm = pl.BlockSpec(memory_space=ANY)
    return pl.pallas_call(
        functools.partial(entry_body, n, m, heads, strip),
        out_shape=(
            jax.ShapeDtypeStruct((width, length), bf16),
            jax.ShapeDtypeStruct((heads, length, LANES), bf16),
            jax.ShapeDtypeStruct((length, LANES), bf16),
            jax.ShapeDtypeStruct((length, LANES), bf16),
            jax.ShapeDtypeStruct((length, LANES), f32),
            jax.ShapeDtypeStruct((length, LANES), f32),
            jax.ShapeDtypeStruct((width, wide), bf16),
            jax.ShapeDtypeStruct((2, 1, width), f32),
            jax.ShapeDtypeStruct((1, length), jnp.int32),
            jax.ShapeDtypeStruct((2, rows * n, cols // n), wg.dtype),
            jax.ShapeDtypeStruct((rows * n, cols // n), wg.dtype),
            jax.ShapeDtypeStruct((m,) + wo.shape, wo.dtype),
        ),
        in_specs=[hbm] * 8 + [vmem] * 2,
        out_specs=[hbm] * 6 + [vmem] * 3 + [hbm] * 3,
        scratch_shapes=[
            pltpu.VMEM((n, tokens, width), bf16),
            pltpu.VMEM((n, tokens, width), bf16),
            pltpu.VMEM((2, width, tokens), bf16),
            pltpu.VMEM((n,) + places.shape, places.dtype),
            pltpu.VMEM((n, m) + wqkv.shape[1:], wqkv.dtype),
            pltpu.VMEM((n, m) + gains.shape, gains.dtype),
            pltpu.VMEM((heads, length, LANES), bf16),
            pltpu.VMEM((length, LANES), bf16),
            pltpu.VMEM((length, LANES), bf16),
            pltpu.VMEM((length, LANES), f32),
            pltpu.VMEM((length, LANES), f32),
            *Gathers.scratch(2),
            pltpu.SemaphoreType.DMA((6, 2, n - 1)),
            pltpu.SemaphoreType.DMA((3, 2, m - 1)),
            pltpu.SemaphoreType.DMA((2,)),
            pltpu.SemaphoreType.DMA((13,)),
        ],
        compiler_params=pltpu.CompilerParams(
            collective_id=ident, has_side_effects=True, vmem_limit_bytes=VMEM_LIMIT
        ),
        cost_estimate=COST,
        name="entry",
    )(x, places, wqkv, gains, wg, wu, wd, wo, widen, inverse)


BLOCK = 512
NT = (((1,), (1,)), ((), ()))
LOG2E = 1.4426950408889634


def allowed_block(first_key, first_query, begin, causal):
    keys = first_key + lax.broadcasted_iota(jnp.int32, (BLOCK, BLOCK), 0)
    ok = keys >= begin
    if causal:
        queries = first_query + lax.broadcasted_iota(jnp.int32, (BLOCK, BLOCK), 1)
        ok = ok & (keys <= queries)
    return ok


def begins(docs):
    begin = jnp.zeros(docs.shape, jnp.int32)
    for d in range(3):
        count = jnp.sum((docs == d).astype(f32), axis=1, keepdims=True).astype(jnp.int32)
        begin = begin + jnp.where(docs > d, count, 0)
    return begin


def spread_rows(wo, wo_here):
    halves, filled, width = wo.shape
    for i in range(halves):
        wo_here[i * SLOT : i * SLOT + filled, :] = wo[i]
        wo_here[i * SLOT + filled : (i + 1) * SLOT, :] = jnp.zeros((SLOT - filled, width), bf16)


def attend_body(
    n, m, factor, q, k, v, docs, wo, go, x, gain,
    o_out, lse, start, low_out, go_all, resid, norm,
    o, low, vt, top, total, acc, wo_here, go_here,
    pair, near, far, sr, lr, stage, sg, lg, loc,
):
    plane = Plane(n, m)
    rows = x.shape[0]
    heads = q.shape[0]
    enter_plane(plane, False)
    gather = Gathers(plane, go, lambda i: go_here.at[i], sg, lg, 2)
    reduce = Reduce(plane, None, pair, near, far, sr, None, stage)
    gather.start()
    spread_rows(wo, wo_here)
    vt[...] = v[...].T
    start[...] = begins(docs[...])

    def chips(step, carry):
        kk = 3 - step
        i = plane.number(kk, 0) // 2
        here = pl.ds(pl.multiple_of(i * BLOCK, BLOCK), BLOCK)
        begin = start[:, here]

        def head(h, carry):
            query = q[h, here, :]
            top[...] = jnp.full_like(top, mask_fill_value)
            total[...] = jnp.zeros_like(total)
            acc[...] = jnp.zeros_like(acc)

            def keys(j, causal):
                at = pl.ds(pl.multiple_of(j * BLOCK, BLOCK), BLOCK)
                raw = lax.dot_general(k[at, :], query, NT, preferred_element_type=f32)
                ok = allowed_block(j * BLOCK, i * BLOCK, begin, causal)
                scores = jnp.where(ok, raw * factor, mask_fill_value)
                new_top = jnp.maximum(top[...], jnp.max(scores, axis=0, keepdims=True))
                weights = jnp.exp2(scores - new_top)
                keep = jnp.exp2(top[...] - new_top)
                total[...] = total[...] * keep + jnp.sum(weights, axis=0, keepdims=True)
                acc[...] = acc[...] * keep + jnp.dot(
                    vt[:, at], weights.astype(bf16), preferred_element_type=f32
                )
                top[...] = new_top

            def loop(j, carry):
                keys(j, False)
                return carry

            lax.fori_loop(0, i, loop, 0)
            keys(i, True)
            out = (acc[...] / total[...]).T
            o[h, here, :] = out
            low[here, pl.ds(pl.multiple_of(h * LANES, LANES), LANES)] = out.astype(bf16)
            lse[h, :, here] = top[...] + jnp.log2(total[...])
            return carry

        lax.fori_loop(0, heads, head, 0)

        @pl.when(step == 1)
        def _():
            reduce.join(3)
            reduce.out[0].start()

        @pl.when(step == 3)
        def _():
            reduce.join(1)
            reduce.out[1].start()

        for other in (1, 0):
            b = plane.number(kk, other)
            at = pl.ds(pl.multiple_of(b * rows, rows), rows)
            part = jnp.dot(low[at, :], wo_here[...], preferred_element_type=f32).astype(bf16)
            if other:
                stage[kk] = part
                for which in range(4):

                    @pl.when(kk == which)
                    def _(which=which):
                        reduce.swaps[Reduce.THEIRS[which]].start()

            else:
                pair[kk] = part
        return carry

    lax.fori_loop(0, 4, chips, 0)
    outs = [
        pltpu.make_async_copy(o, o_out, loc.at[0]),
        pltpu.make_async_copy(low, low_out, loc.at[1]),
    ]
    for copy in outs:
        copy.start()
    gather.relay_near()
    reduce.ready()
    reduce.first(resid, x)
    reduce.send_fro()
    gather.relay_far()
    reduce.finish(resid)

    def normalize(at):
        value = resid[at, :]
        scale = lax.rsqrt(jnp.mean(value * value, axis=1, keepdims=True) + norm_epsilon)
        norm[at, :] = (value * scale * gain[...]).astype(bf16)

    in_tiles(rows, normalize)
    gather.finish()
    outs.append(pltpu.make_async_copy(go_here, go_all, loc.at[2]))
    outs[-1].start()
    for copy in outs:
        copy.wait()


def attend(n, m, factor, q, k, v, docs, wo, go, x, gain, ident):
    heads, length, _ = q.shape
    rows, width = x.shape
    hbm = pl.BlockSpec(memory_space=ANY)
    vmem = pl.BlockSpec(memory_space=pltpu.VMEM)
    return pl.pallas_call(
        functools.partial(attend_body, n, m, factor),
        out_shape=(
            jax.ShapeDtypeStruct((heads, length, LANES), f32),
            jax.ShapeDtypeStruct((heads, 1, length), f32),
            jax.ShapeDtypeStruct((1, length), jnp.int32),
            jax.ShapeDtypeStruct((length, heads * LANES), bf16),
            jax.ShapeDtypeStruct((n,) + go.shape, go.dtype),
            jax.ShapeDtypeStruct((rows, width), f32),
            jax.ShapeDtypeStruct((rows, width), bf16),
        ),
        in_specs=[vmem] * 5 + [hbm] + [vmem] * 2,
        out_specs=[hbm, vmem, vmem, hbm, hbm, vmem, vmem],
        scratch_shapes=[
            pltpu.VMEM((heads, length, LANES), f32),
            pltpu.VMEM((length, heads * LANES), bf16),
            pltpu.VMEM((LANES, length), bf16),
            pltpu.VMEM((1, BLOCK), f32),
            pltpu.VMEM((1, BLOCK), f32),
            pltpu.VMEM((LANES, BLOCK), f32),
            pltpu.VMEM((heads * LANES, width), bf16),
            pltpu.VMEM((n,) + go.shape, go.dtype),
        ]
        + Reduce.scratch(rows, width)
        + [pltpu.VMEM((4, rows, width), bf16)]
        + Gathers.scratch(2)
        + [pltpu.SemaphoreType.DMA((3,))],
        compiler_params=pltpu.CompilerParams(
            collective_id=ident, has_side_effects=True, vmem_limit_bytes=VMEM_LIMIT
        ),
        cost_estimate=COST,
        name="attend",
    )(q, k, v, docs, wo, go, x, gain)


def attend_back_body(
    n, m, factor, scale, q_in, k_in, v_in, o_in, lse, begin, cos_in, sin_in, low_in,
    mixed, wo, dnorm, resid, grad, gain,
    out, layer, terms, dresid, gain_out,
    q, k, v, o, cosine, sine, low, kt, dqt, dk, dv, delta, go, every, dbranch, wo_here,
    pair, near, far, sr, lr, held, gain_sum, gain_cut, gain_got, sg, lg, sv, loc,
):
    plane = Plane(n, m)
    heads, length, _ = q.shape
    rows, width = dnorm.shape
    strip = gain_out.shape[2]
    loads = [
        pltpu.make_async_copy(a, b, loc.at[i])
        for i, (a, b) in enumerate(
            (
                (q_in, q), (k_in, k), (v_in, v), (o_in, o),
                (cos_in, cosine), (sin_in, sine), (low_in, low),
            )
        )
    ]
    for copy in loads:
        copy.start()
    enter_plane(plane, False)
    one = Reduce(plane, lambda i: mixed.at[i], pair, near, far, sr, lr)
    one.start(3, 1)
    gather = Gathers(plane, dbranch, lambda i: every.at[i], sg, lg, 2)
    gain_copies = exchange(
        plane, lambda i: gain_cut.at[i], lambda i: gain_got.at[i], sv.at[0], sv.at[1], loc.at[7]
    )
    gain_sum[...] = jnp.zeros_like(gain_sum)

    def into_branch(at):
        value, up = resid[at, :], dnorm[at, :]
        scale_two = lax.rsqrt(jnp.mean(value * value, axis=1, keepdims=True) + norm_epsilon)
        inner = gain[...] * up
        moment = jnp.mean(value * inner, axis=1, keepdims=True)
        turned = value * scale_two
        got = (
            grad[at, :].astype(f32) + scale_two * inner - turned * (scale_two * scale_two * moment)
        )
        dresid[at, :] = got
        dbranch[at, :] = got.astype(bf16)
        gain_sum[...] += up * turned

    in_tiles(rows, into_branch)
    gather.start()
    one.start(2, 0)
    total_gain = jnp.sum(gain_sum[...], axis=0, keepdims=True)
    for i in range(n):
        gain_cut[i] = total_gain[:, i * (width // n) : (i + 1) * (width // n)]
    for copy in gain_copies:
        copy.start()
    spread_rows(wo, wo_here)
    for copy in loads:
        copy.wait()
    kt[...] = k[...].T
    dk[...] = jnp.zeros_like(dk)
    dv[...] = jnp.zeros_like(dv)

    def unturn(value, at):
        return value * cosine[at, :] - pltpu.roll(value, SLOT, 1) * sine[at, :]

    def chips(kk, carry):
        @pl.when(kk == 0)
        def _():
            gather.wait_own()
            gather.wait_swap()

        @pl.when(kk == 1)
        def _():
            gather.relay_near()
            gather.wait_share(1)

        @pl.when(kk == 2)
        def _():
            one.send_to()
            gather.wait_share(0)

        @pl.when(kk == 3)
        def _():
            one.ready()
            one.first(held, resid)
            gather.relay_far()
            gather.wait_share(2)

        i = plane.number(kk, 0) // 2
        here = pl.ds(pl.multiple_of(i * BLOCK, BLOCK), BLOCK)
        for other in range(2):
            b = plane.number(kk, other)
            at = pl.ds(pl.multiple_of(b * rows, rows), rows)
            value = lax.dot_general(every[b], wo_here[...], NT, preferred_element_type=f32)
            for h in range(heads):
                go[h, at, :] = value[:, h * LANES : (h + 1) * LANES].astype(bf16)

        def head(h, carry):
            query = q[h, here, :]
            grads = go[h, here, :]
            delta[...] = jnp.sum((grads.astype(f32) * o[h, here, :]).T, axis=0, keepdims=True)
            dqt[...] = jnp.zeros_like(dqt)

            def keys(j, causal):
                at = pl.ds(pl.multiple_of(j * BLOCK, BLOCK), BLOCK)
                raw = lax.dot_general(k[at, :], query, NT, preferred_element_type=f32)
                ok = allowed_block(j * BLOCK, i * BLOCK, begin[:, here], causal)
                probs = jnp.where(ok, jnp.exp2(raw * factor - lse[h, :, here]), 0.0)
                dprob = lax.dot_general(v[at, :], grads, NT, preferred_element_type=f32)
                dscore = (probs * (dprob - delta[...])).astype(bf16)
                dv[at, :] += jnp.dot(probs.astype(bf16), grads, preferred_element_type=f32)
                dk[at, :] += jnp.dot(dscore, query, preferred_element_type=f32)
                dqt[...] += jnp.dot(kt[:, at], dscore, preferred_element_type=f32)

            def loop(j, carry):
                keys(j, False)
                return carry

            lax.fori_loop(0, i, loop, 0)
            keys(i, True)
            got = unturn(dqt[...].T * scale, here).astype(bf16)
            out[here, pl.ds(pl.multiple_of(h * LANES, LANES), LANES)] = got
            return carry

        lax.fori_loop(0, heads, head, 0)
        return carry

    lax.fori_loop(0, 4, chips, 0)

    def write(i, carry):
        at = pl.ds(pl.multiple_of(i * BLOCK, BLOCK), BLOCK)
        turned = unturn(dk[at, :] * scale, at).astype(bf16)
        out[at, heads * LANES : (heads + 1) * LANES] = turned
        out[at, (heads + 1) * LANES :] = dv[at, :].astype(bf16)
        return carry

    lax.fori_loop(0, length // BLOCK, write, 0)
    one.send_fro()
    across = every.reshape(length, width)
    part = 512

    def into_terms(i, carry):
        at = pl.ds(pl.multiple_of(i * part, part), part)
        value = lax.dot_general(
            low[...], across[:, at], (((0,), (0,)), ((), ())), preferred_element_type=f32
        ).astype(bf16)
        for half in range(terms.shape[0]):
            terms[half, :, at] = value[half * SLOT : half * SLOT + HALF]
        return carry

    lax.fori_loop(0, width // part, into_terms, 0)
    for copy in gain_copies:
        copy.wait()
    got = gain_got[0]
    for i in range(1, n):
        got = got + gain_got[i]
    for t in range(m):
        gain_out[t] = got[:, t * strip : (t + 1) * strip]
    gather.wait_sends()
    one.finish(held, layer)


def attend_back(
    n, m, factor, scale, q, k, v, o, lse, begin, cosine, sine, low,
    mixed, wo, dnorm, resid, grad, gain, ident,
):
    heads, length, _ = q.shape
    rows, width = dnorm.shape
    strip = width // (n * m)
    hbm = pl.BlockSpec(memory_space=ANY)
    vmem = pl.BlockSpec(memory_space=pltpu.VMEM)
    return pl.pallas_call(
        functools.partial(attend_back_body, n, m, factor, scale),
        out_shape=(
            jax.ShapeDtypeStruct((length, (heads + 2) * LANES), bf16),
            jax.ShapeDtypeStruct((rows, width), bf16),
            jax.ShapeDtypeStruct(wo.shape, bf16),
            jax.ShapeDtypeStruct((rows, width), f32),
            jax.ShapeDtypeStruct((m, 1, strip), f32),
        ),
        in_specs=[hbm] * 4 + [vmem] * 2 + [hbm] * 4 + [vmem] * 5,
        out_specs=[vmem] * 5,
        scratch_shapes=[
            pltpu.VMEM(q.shape, bf16),
            pltpu.VMEM(k.shape, bf16),
            pltpu.VMEM(v.shape, bf16),
            pltpu.VMEM(o.shape, f32),
            pltpu.VMEM(cosine.shape, f32),
            pltpu.VMEM(sine.shape, f32),
            pltpu.VMEM(low.shape, bf16),
            pltpu.VMEM((LANES, length), bf16),
            pltpu.VMEM((LANES, BLOCK), f32),
            pltpu.VMEM((length, LANES), f32),
            pltpu.VMEM((length, LANES), f32),
            pltpu.VMEM((1, BLOCK), f32),
            pltpu.VMEM((heads, length, LANES), bf16),
            pltpu.VMEM((n, rows, width), bf16),
            pltpu.VMEM((rows, width), bf16),
            pltpu.VMEM((heads * LANES, width), bf16),
        ]
        + Reduce.scratch(rows, width)
        + [
            pltpu.VMEM((rows, width), f32),
            pltpu.VMEM((TILE, width), f32),
            pltpu.VMEM((n, 1, width // n), f32),
            pltpu.VMEM((n, 1, width // n), f32),
        ]
        + Gathers.scratch(2)
        + [pltpu.SemaphoreType.DMA((2, n - 1)), pltpu.SemaphoreType.DMA((8,))],
        compiler_params=pltpu.CompilerParams(
            collective_id=ident, has_side_effects=True, vmem_limit_bytes=VMEM_LIMIT
        ),
        cost_estimate=COST,
        name="attend_back",
    )(q, k, v, o, lse, begin, cosine, sine, low, mixed, wo, dnorm, resid, grad, gain)


def feed_body(
    n, m, mine, go, w_in, down, dnorm, grads, mixed, down_parts,
    rows, rows_t, go_t, go_two, w, gates, h, mix_two, down_held, pair, near, far, stage,
    sg, lg, sr, loc, sw, so, sm, sd, sz, sf,
):
    plane = Plane(n, m)
    tokens = rows.shape[1]
    hid = down.shape[1]
    enter_plane(plane, True)
    gather = Gathers(plane, mine, lambda i: rows.at[i], sg, lg, 2)
    reduce = Reduce(plane, None, pair, near, far, sr, None, stage)
    gather.start()

    def down_at(t):
        return w.at[2, :, pl.ds(pl.multiple_of(t * hid, hid), hid)]

    chain = Chain(plane, down, down_at, sz)
    chain.start()
    own_down = pltpu.make_async_copy(down, down_at(plane.t), loc.at[0])
    own_down.start()
    weights = [
        pltpu.make_async_copy(
            w_in.at[t, j], w.at[j, :, t * hid : (t + 1) * hid], sw.at[j, t]
        )
        for j in range(2)
        for t in range(m)
    ]
    for copy in weights:
        copy.start()

    gather.wait_own()
    for copy in weights:
        copy.wait()

    def span(b):
        return pl.ds(pl.multiple_of(b * tokens, tokens), tokens)

    def forward(it, carry):
        b = plane.number(it // 2, lax.rem(it, 2))

        @pl.when(it == 1)
        def _():
            gather.wait_swap()

        @pl.when(it == 2)
        def _():
            chain.step(1)
            gather.relay_near()

        @pl.when(it == 3)
        def _():
            gather.wait_share(1)

        @pl.when(it == 4)
        def _():
            chain.step(2)

        @pl.when(it == 5)
        def _():
            gather.wait_share(0)

        @pl.when(it == 6)
        def _():
            gather.relay_far()

        @pl.when(it == 7)
        def _():
            gather.wait_share(2)

        slot = lax.rem(it, 2)

        @pl.when(it < n - 1)
        def _():
            early_go(it + 1, 1 - slot).start()

        row = rows[b]
        gate = jnp.dot(row, w[0], preferred_element_type=f32)
        up = jnp.dot(row, w[1], preferred_element_type=f32)
        gates[0, span(b), :] = gate
        gates[1, span(b), :] = up
        h[2, span(b), :] = (gate * jax.nn.sigmoid(gate) * up).astype(bf16)
        rows_t[:, span(b)] = row.T
        early_go(it, slot).wait()
        go_t[:, span(b)] = go_two[slot].T
        return carry

    def early_go(it, slot):
        b = plane.number(it // 2, lax.rem(it, 2))
        return pltpu.make_async_copy(go.at[b], go_two.at[slot], so.at[slot])

    early_go(0, 0).start()
    lax.fori_loop(0, n, forward, 0)

    def number(it):
        return plane.number(3 - it // 2, 1 - lax.rem(it, 2))

    def load_go(it, slot):
        return pltpu.make_async_copy(go.at[number(it)], go_two.at[slot], so.at[slot])

    def store_mix(it, slot):
        return pltpu.make_async_copy(mix_two.at[slot], mixed.at[number(it)], sm.at[slot])

    width = rows.shape[2]

    def weight_grad(j, left, held):
        def part(i, carry):
            at = pl.ds(pl.multiple_of(i * 256, 256), 256)
            value = jnp.dot(left[at, :], h[j], preferred_element_type=f32)
            held[at, :] = value.astype(bf16)
            return carry

        lax.fori_loop(0, width // 256, part, 0)
        if j == 2:
            return []
        outs = [
            pltpu.make_async_copy(
                held.at[:, t * hid : (t + 1) * hid], grads.at[t, j], sd.at[j, t]
            )
            for t in range(m)
        ]
        for copy in outs:
            copy.start()
        return outs

    load_go(0, 0).start()
    outs = weight_grad(2, go_t, down_held)

    def down_part(t):
        return down_held.at[:, pl.ds(pl.multiple_of(t * hid, hid), hid)]

    outs += fan(plane, down_part, lambda t: down_parts.at[t], sf.at[0], sf.at[1])
    outs.append(
        pltpu.make_async_copy(down_part(plane.t), down_parts.at[plane.t], loc.at[1])
    )
    for copy in outs:
        copy.start()
    for hop in range(3, m):
        chain.step(hop)
    own_down.wait()

    def backward(it, carry):
        slot = lax.rem(it, 2)
        k = 3 - it // 2
        b = number(it)

        @pl.when(it == 3)
        def _():
            reduce.join(3)
            reduce.out[0].start()

        @pl.when(it == 6)
        def _():
            reduce.join(1)
            reduce.out[1].start()

        @pl.when(it < n - 1)
        def _():
            load_go(it + 1, 1 - slot).start()

        load_go(it, slot).wait()

        @pl.when(it >= 2)
        def _():
            store_mix(it - 2, slot).wait()

        gate = gates[0, span(b), :]
        up = gates[1, span(b), :]
        grad = go_two[slot]
        dhidden = jnp.dot(grad, w[2], preferred_element_type=f32)
        sig = jax.nn.sigmoid(gate)
        hidden = h[2, span(b), :]
        dgate = (dhidden * up * sig * (1.0 + gate * (1.0 - sig))).astype(bf16)
        dup = (dhidden * gate * sig).astype(bf16)
        h[0, span(b), :] = dgate
        h[1, span(b), :] = dup
        part = lax.dot_general(dgate, w[0], NT, preferred_element_type=f32)
        part = part + lax.dot_general(dup, w[1], NT, preferred_element_type=f32)
        part = part.astype(bf16)

        @pl.when(lax.rem(it, 2) == 1)
        def _():
            pair[k] = part

        @pl.when(lax.rem(it, 2) == 0)
        def _():
            stage[k] = part

        for kk in range(4):

            @pl.when(it == 2 * (3 - kk))
            def _(kk=kk):
                reduce.swaps[Reduce.THEIRS[kk]].start()

        mix_two[slot] = lax.dot_general(hidden, w[2], NT, preferred_element_type=f32).astype(bf16)
        store_mix(it, slot).start()
        return carry

    lax.fori_loop(0, n, backward, 0)
    store_mix(n - 2, 0).wait()
    store_mix(n - 1, 1).wait()
    reduce.ready()
    reduce.send_fro()
    outs += weight_grad(0, rows_t, w.at[0])
    reduce.first(dnorm)
    outs += weight_grad(1, rows_t, w.at[1])
    gather.wait_sends()
    chain.wait_sends()
    reduce.finish(dnorm)
    for copy in outs:
        copy.wait()


def feed(n, m, norm, go, w_in, down, ident):
    tokens, width = norm.shape
    hid = down.shape[1]
    length = n * tokens
    return pl.pallas_call(
        functools.partial(feed_body, n, m),
        out_shape=(
            jax.ShapeDtypeStruct((tokens, width), f32),
            jax.ShapeDtypeStruct((m, 2, width, hid), bf16),
            jax.ShapeDtypeStruct((n, tokens, width), bf16),
            jax.ShapeDtypeStruct((m, width, hid), bf16),
        ),
        in_specs=[pl.BlockSpec(memory_space=ANY)] * 4,
        out_specs=[
            pl.BlockSpec(memory_space=pltpu.VMEM),
            pl.BlockSpec(memory_space=ANY),
            pl.BlockSpec(memory_space=ANY),
            pl.BlockSpec(memory_space=ANY),
        ],
        scratch_shapes=[
            pltpu.VMEM((n, tokens, width), bf16),
            pltpu.VMEM((width, length), bf16),
            pltpu.VMEM((width, length), bf16),
            pltpu.VMEM((2, tokens, width), bf16),
            pltpu.VMEM((3, width, m * hid), bf16),
            pltpu.VMEM((2, length, m * hid), f32),
            pltpu.VMEM((3, length, m * hid), bf16),
            pltpu.VMEM((2, tokens, width), bf16),
            pltpu.VMEM((width, m * hid), bf16),
        ]
        + [pltpu.VMEM((slots, tokens, width), bf16) for slots in Reduce.SLOTS]
        + [
            pltpu.VMEM((4, tokens, width), bf16),
            *Gathers.scratch(2),
            pltpu.SemaphoreType.DMA((4, 4)),
            pltpu.SemaphoreType.DMA((2,)),
            pltpu.SemaphoreType.DMA((2, m)),
            pltpu.SemaphoreType.DMA((2,)),
            pltpu.SemaphoreType.DMA((2,)),
            pltpu.SemaphoreType.DMA((3, m)),
            pltpu.SemaphoreType.DMA((4, m)),
            pltpu.SemaphoreType.DMA((2, m - 1)),
        ],
        compiler_params=pltpu.CompilerParams(
            collective_id=ident, has_side_effects=True, vmem_limit_bytes=VMEM_LIMIT
        ),
        cost_estimate=COST,
        name="feed",
    )(norm, go, w_in, down)


def split_heads(w, groups):
    rows = w.shape[0]
    return w.reshape(rows, groups, -1).transpose(1, 0, 2)


def fast_layer(n, m):
    def on_plane(
        layer_input,
        doc_ids,
        positions,
        first_gain,
        query_weight,
        key_weight,
        value_weight,
        output_weight,
        second_gain,
        gate_weight,
        up_weight,
        down_weight,
        out_grad,
    ):
        x = layer_input[0]
        rows, width = x.shape
        length = rows * n
        heads = QUERY_HEADS // n
        scale = 1.0 / math.sqrt(HEAD_SIZE)
        factor = scale * LOG2E
        strip = query_weight.shape[0]
        hid = gate_weight.shape[1] // n

        packed = jnp.concatenate(
            [split_heads(w, n) for w in (query_weight, key_weight, value_weight)], axis=2
        )
        cols = packed.shape[2]
        gains = jnp.pad(
            jnp.stack([first_gain, second_gain]).astype(f32), ((0, 6), (0, LANES - strip))
        )
        places = jnp.concatenate([doc_ids, positions], axis=0)
        lane = jnp.arange(LANES) % SLOT
        inverse = jnp.where(
            lane < HALF, rope_base ** (-(lane.astype(f32) * 2.0 / HEAD_SIZE)), 0.0
        )[None]
        from_col = jnp.arange(cols)
        to_lane = from_col // HALF * SLOT + from_col % HALF
        widen = (to_lane[:, None] == jnp.arange(cols // HALF * SLOT)[None, :]).astype(bf16)

        norm_t, q, k, v, cosine, sine, wqkv, gain_rows, docs, ffn_mine, down_mine, output_rows = entry(
            n, m, heads, x, places, packed, gains,
            gate_weight, up_weight, down_weight, output_weight, widen, inverse, 0,
        )
        gain_one, gain_two = gain_rows[0], gain_rows[1]
        ffn_all = lax.all_gather(ffn_mine, "tp", axis=0, tiled=False)
        o, lse, begin, low, grad_all, resid, norm_two = attend(
            n, m, factor, q, k, v, docs, output_rows, out_grad[0], x, gain_two, 9
        )
        dnorm_two, ffn_terms, mixed, down_parts = feed(
            n, m, norm_two, grad_all, ffn_all, down_mine, 2
        )
        ffn_sum = lax.psum_scatter(ffn_terms, "tp", scatter_dimension=0, tiled=False)
        dqkv, layer_output, output_terms, dresid, gain_part = attend_back(
            n, m, factor, scale, q, k, v, o, lse, begin, cosine, sine, low, mixed,
            output_rows, dnorm_two, resid, out_grad[0], gain_two, 3,
        )
        input_grad, ffn_out, qkv_out, output_parts, gain_sums = last(
            n, m, dqkv, wqkv, widen.T, x, dresid, gain_one, norm_t, ffn_sum, down_parts,
            output_terms, gain_part, 6,
        )
        output_grad = jnp.sum(output_parts.astype(f32), axis=0)

        gate_grad, up_grad, down_grad = [ffn_out[i].astype(f32) for i in range(3)]
        kv = HEAD_SIZE * KEY_VALUE_HEADS // n
        split = heads * HEAD_SIZE

        def columns(a, b):
            return qkv_out[:, :, a:b].transpose(1, 0, 2).reshape(strip, -1).astype(f32)

        query_grad = columns(0, split)
        key_grad = columns(split, split + kv)
        value_grad = columns(split + kv, cols)

        one = (
            jnp.sum(query_weight.astype(f32) * query_grad, axis=1)
            + jnp.sum(key_weight.astype(f32) * key_grad, axis=1)
            + jnp.sum(value_weight.astype(f32) * value_grad, axis=1)
        )
        first_gain_grad = one / first_gain.astype(f32)
        second_gain_grad = jnp.sum(gain_sums, axis=(0, 1))
        return (
            layer_output[None],
            input_grad[None],
            first_gain_grad,
            query_grad,
            key_grad,
            value_grad,
            output_grad,
            second_gain_grad,
            gate_grad,
            up_grad,
            down_grad,
        )

    return on_plane


def solution(mesh):
    n, m = mesh.shape["seq"], mesh.shape["tp"]
    fits = n == KEY_VALUE_HEADS == 8
    return jax.shard_map(
        fast_layer(n, m) if fits else on_device,
        mesh=mesh,
        in_specs=(
            P("tp", "seq", None),
            P("tp", "seq"),
            P("tp", "seq"),
            P(("seq", "tp")),
            P(("seq", "tp"), None),
            P(("seq", "tp"), None),
            P(("seq", "tp"), None),
            P(("seq", "tp"), None),
            P(("seq", "tp")),
            P("seq", "tp"),
            P("seq", "tp"),
            P("seq", "tp"),
            P("tp", "seq", None),
        ),
        out_specs=(
            P("tp", "seq", None),
            P("tp", "seq", None),
            P(("seq", "tp")),
            P(("seq", "tp"), None),
            P(("seq", "tp"), None),
            P(("seq", "tp"), None),
            P(("seq", "tp"), None),
            P(("seq", "tp")),
            P("seq", "tp"),
            P("seq", "tp"),
            P("seq", "tp"),
        ),
        check_vma=False,
    )
```

```python
import functools
import math

import jax
import jax.numpy as jnp
import numpy as np
from jax import lax
from jax.experimental import pallas as pl
from jax.experimental.pallas import tpu as pltpu
from jax.sharding import PartitionSpec as P

QUERY_HEADS = 16
KEY_VALUE_HEADS = 8
HEAD_SIZE = 96


norm_epsilon = 1e-05
rope_base = 100000.0
mask_fill_value = -1e30


def rope_tables(places):
    half = HEAD_SIZE // 2
    inverse = rope_base ** (-(jnp.arange(half, dtype=jnp.float32) * 2.0 / HEAD_SIZE))
    angles = places.astype(jnp.float32)[:, None] * inverse[None, :]
    return (jnp.cos(angles), jnp.sin(angles))


def apply_rotary(value_rows, cosine_table, sine_table, heads, direction):
    sequence_length = value_rows.shape[0]
    split = value_rows.reshape(sequence_length, heads, 2, HEAD_SIZE // 2)
    first = split[:, :, 0]
    second = split[:, :, 1]
    cosine = cosine_table[:, None, :]
    sine = direction * sine_table[:, None, :]
    turned = jnp.stack([first * cosine - second * sine, second * cosine + first * sine], axis=2)
    return turned.reshape(sequence_length, heads * HEAD_SIZE)


def outer_product(left, right):
    return lax.dot_general(
        left, right, (((0,), (0,)), ((), ())), preferred_element_type=jnp.float32
    )


def times_transpose(left, right):
    return lax.dot_general(
        left, right, (((1,), (1,)), ((), ())), preferred_element_type=jnp.float32
    )


def norm_backward(inputs, scale, gain, upstream):
    inner = gain * upstream
    moment = jnp.mean(inputs * inner, axis=1, keepdims=True)
    return (
        scale * inner - inputs * scale * scale * scale * moment,
        jnp.sum(upstream * inputs * scale, axis=0),
    )


def on_device(
    layer_input,
    doc_ids,
    positions,
    first_gain,
    query_weight,
    key_weight,
    value_weight,
    output_weight,
    second_gain,
    gate_weight,
    up_weight,
    down_weight,
    out_grad,
):
    token_rows = layer_input.shape[1]
    query_groups = QUERY_HEADS // KEY_VALUE_HEADS
    scale_of_scores = 1.0 / math.sqrt(HEAD_SIZE)
    inputs_f = layer_input[0].astype(jnp.float32)
    my_docs = doc_ids[0]
    gain_one, query_full, complete_keys, value_full, output_full, gain_two = (
        lax.all_gather(first_gain, ("seq", "tp"), axis=0, tiled=True),
        lax.all_gather(query_weight, ("seq", "tp"), axis=0, tiled=True),
        lax.all_gather(key_weight, ("seq", "tp"), axis=0, tiled=True),
        lax.all_gather(value_weight, ("seq", "tp"), axis=0, tiled=True),
        lax.all_gather(output_weight, ("seq", "tp"), axis=0, tiled=True),
        lax.all_gather(second_gain, ("seq", "tp"), axis=0, tiled=True),
    )
    gain_one_f = gain_one.astype(jnp.float32)
    gain_two_f = gain_two.astype(jnp.float32)
    scale_one = lax.rsqrt(jnp.mean(inputs_f * inputs_f, axis=1, keepdims=True) + norm_epsilon)
    first_normalized = (inputs_f * scale_one * gain_one_f).astype(jnp.bfloat16)
    cosine_table, sine_table = rope_tables(positions[0])
    rotated_query = apply_rotary(
        jnp.dot(first_normalized, query_full, preferred_element_type=jnp.float32),
        cosine_table,
        sine_table,
        QUERY_HEADS,
        1.0,
    ).astype(jnp.bfloat16)
    key_rot = apply_rotary(
        jnp.dot(first_normalized, complete_keys, preferred_element_type=jnp.float32),
        cosine_table,
        sine_table,
        KEY_VALUE_HEADS,
        1.0,
    ).astype(jnp.bfloat16)
    value_low = jnp.dot(first_normalized, value_full, preferred_element_type=jnp.float32).astype(
        jnp.bfloat16
    )
    gathered_keys, gathered_values, doc_all = (
        lax.all_gather(key_rot, "seq", axis=0, tiled=True),
        lax.all_gather(value_low, "seq", axis=0, tiled=True),
        lax.all_gather(my_docs.astype(jnp.bfloat16), "seq", axis=0, tiled=True),
    )
    sequence_length = gathered_keys.shape[0]
    block_number = math.gcd(512, sequence_length)
    block_count = sequence_length // block_number
    query_index = lax.axis_index("seq") * token_rows + jnp.arange(token_rows, dtype=jnp.int32)
    my_doc_f = my_docs.astype(jnp.float32)
    heads_of_query = rotated_query.reshape(token_rows, KEY_VALUE_HEADS, query_groups, HEAD_SIZE)
    layer_entries = (
        gathered_keys.reshape(block_count, block_number, KEY_VALUE_HEADS, HEAD_SIZE),
        gathered_values.reshape(block_count, block_number, KEY_VALUE_HEADS, HEAD_SIZE),
        doc_all.astype(jnp.float32).reshape(block_count, block_number),
        jnp.arange(block_count, dtype=jnp.int32) * block_number,
    )

    def allowed_of(doc_piece, start):
        key_index = start + jnp.arange(block_number, dtype=jnp.int32)
        return (key_index[None, :] <= query_index[:, None]) & (
            doc_piece[None, :] == my_doc_f[:, None]
        )

    def scores_of(key_piece, allowed):
        raw = (
            jnp.einsum(
                "tgrd,kgd->tgrk", heads_of_query, key_piece, preferred_element_type=jnp.float32
            )
            * scale_of_scores
        )
        return jnp.where(allowed[:, None, None, :], raw, mask_fill_value)

    def total_step(carry, item):
        key_piece, value_piece, doc_piece, start = item
        allowed = allowed_of(doc_piece, start)

        def total_work(state):
            top, total = state
            scores = scores_of(key_piece, allowed)
            new_top = jnp.maximum(top, jnp.max(scores, axis=3))
            weights = jnp.where(
                allowed[:, None, None, :], jnp.exp(scores - new_top[..., None]), 0.0
            )
            return (new_top, total * jnp.exp(top - new_top) + jnp.sum(weights, axis=3))

        return (lax.cond(jnp.any(allowed), total_work, lambda state: state, carry), None)

    start_state = (
        jnp.full((token_rows, KEY_VALUE_HEADS, query_groups), mask_fill_value, jnp.float32),
        jnp.zeros((token_rows, KEY_VALUE_HEADS, query_groups), jnp.float32),
    )
    (top, total), unused_result = lax.scan(total_step, start_state, layer_entries)
    log_total = top + jnp.log(total)

    def probs_of(key_piece, allowed):
        scores = scores_of(key_piece, allowed)
        return jnp.where(allowed[:, None, None, :], jnp.exp(scores - log_total[..., None]), 0.0)

    def output_update(accum, item):
        key_piece, value_piece, doc_piece, start = item
        allowed = allowed_of(doc_piece, start)

        def output_work(state):
            probs = probs_of(key_piece, allowed).astype(jnp.bfloat16)
            return state + jnp.einsum(
                "tgrk,kgd->tgrd", probs, value_piece, preferred_element_type=jnp.float32
            )

        return (lax.cond(jnp.any(allowed), output_work, lambda state: state, accum), None)

    heads_output, unused_result = lax.scan(
        output_update,
        jnp.zeros((token_rows, KEY_VALUE_HEADS, query_groups, HEAD_SIZE), jnp.float32),
        layer_entries,
    )
    attn_low = heads_output.reshape(token_rows, QUERY_HEADS * HEAD_SIZE).astype(jnp.bfloat16)
    resid = inputs_f + jnp.dot(attn_low, output_full, preferred_element_type=jnp.float32)
    scale_two = lax.rsqrt(jnp.mean(resid * resid, axis=1, keepdims=True) + norm_epsilon)
    normed_two = (resid * scale_two * gain_two_f).astype(jnp.bfloat16)
    rows_all = lax.all_gather(normed_two, "tp", axis=0, tiled=True)
    gate_cols, up_cols, down_cols = (
        lax.all_gather(gate_weight, "seq", axis=0, tiled=True),
        lax.all_gather(up_weight, "seq", axis=0, tiled=True),
        lax.all_gather(down_weight, "seq", axis=0, tiled=True),
    )
    gate_pre = jnp.dot(rows_all, gate_cols, preferred_element_type=jnp.float32)
    up_pre = jnp.dot(rows_all, up_cols, preferred_element_type=jnp.float32)
    gate_sig = jax.nn.sigmoid(gate_pre)
    gate_act = gate_pre * gate_sig
    hidden = (gate_act * up_pre).astype(jnp.bfloat16)
    mixed = lax.psum_scatter(
        times_transpose(hidden, down_cols).astype(jnp.bfloat16),
        "tp",
        scatter_dimension=0,
        tiled=True,
    ).astype(jnp.float32)
    layer_output = (resid + mixed).astype(jnp.bfloat16)[None]
    grad_low = out_grad[0]
    grad_f = grad_low.astype(jnp.float32)
    grad_all = lax.all_gather(grad_low, "tp", axis=0, tiled=True)
    dhidden = jnp.dot(grad_all, down_cols, preferred_element_type=jnp.float32)
    dgate = (dhidden * up_pre * gate_sig * (1.0 + gate_pre * (1.0 - gate_sig))).astype(jnp.bfloat16)
    dup = (dhidden * gate_act).astype(jnp.bfloat16)
    gate_term = outer_product(rows_all, dgate)
    up_term = outer_product(rows_all, dup)
    down_term_grad = outer_product(grad_all, hidden)
    dnorm_two = lax.psum_scatter(
        (times_transpose(dgate, gate_cols) + times_transpose(dup, up_cols)).astype(jnp.bfloat16),
        "tp",
        scatter_dimension=0,
        tiled=True,
    ).astype(jnp.float32)
    gate_grad, up_grad, down_grad = (
        lax.psum_scatter(
            gate_term.astype(jnp.bfloat16), "seq", scatter_dimension=0, tiled=True
        ).astype(jnp.float32),
        lax.psum_scatter(
            up_term.astype(jnp.bfloat16), "seq", scatter_dimension=0, tiled=True
        ).astype(jnp.float32),
        lax.psum_scatter(
            down_term_grad.astype(jnp.bfloat16), "seq", scatter_dimension=0, tiled=True
        ).astype(jnp.float32),
    )
    resid_part, gain_two_term = norm_backward(resid, scale_two, gain_two_f, dnorm_two)
    dresid = grad_f + resid_part
    dbranch = dresid.astype(jnp.bfloat16)
    output_term = outer_product(attn_low, dbranch)
    heads_gradient = times_transpose(dbranch, output_full).astype(jnp.bfloat16)
    grouped_heads_gradient = heads_gradient.reshape(
        token_rows, KEY_VALUE_HEADS, query_groups, HEAD_SIZE
    )
    delta = jnp.sum(grouped_heads_gradient.astype(jnp.float32) * heads_output, axis=3)

    def gradient_update(dquery, item):
        key_piece, value_piece, doc_piece, start = item
        allowed = allowed_of(doc_piece, start)

        def gradient_work(state):
            probs = probs_of(key_piece, allowed)
            value_piece_grad = jnp.einsum(
                "tgrk,tgrd->kgd",
                probs.astype(jnp.bfloat16),
                grouped_heads_gradient,
                preferred_element_type=jnp.float32,
            )
            prob_grad = jnp.einsum(
                "tgrd,kgd->tgrk",
                grouped_heads_gradient,
                value_piece,
                preferred_element_type=jnp.float32,
            )
            score_grad = (probs * (prob_grad - delta[..., None])).astype(jnp.bfloat16)
            key_piece_grad = jnp.einsum(
                "tgrk,tgrd->kgd", score_grad, heads_of_query, preferred_element_type=jnp.float32
            )
            updated = state + jnp.einsum(
                "tgrk,kgd->tgrd", score_grad, key_piece, preferred_element_type=jnp.float32
            )
            return (updated, (key_piece_grad, value_piece_grad))

        def skip(state):
            blank_tensor = jnp.zeros((block_number, KEY_VALUE_HEADS, HEAD_SIZE), jnp.float32)
            return (state, (blank_tensor, blank_tensor))

        return lax.cond(jnp.any(allowed), gradient_work, skip, dquery)

    dquery, (key_contributions, value_contributions) = lax.scan(
        gradient_update,
        jnp.zeros((token_rows, KEY_VALUE_HEADS, query_groups, HEAD_SIZE), jnp.float32),
        layer_entries,
    )
    gathered_key_contributions = (
        key_contributions.reshape(sequence_length, KEY_VALUE_HEADS * HEAD_SIZE) * scale_of_scores
    )
    gathered_value_contributions = value_contributions.reshape(
        sequence_length, KEY_VALUE_HEADS * HEAD_SIZE
    )
    local_keys, value_mine = (
        lax.psum_scatter(
            gathered_key_contributions.astype(jnp.bfloat16), "seq", scatter_dimension=0, tiled=True
        ).astype(jnp.float32),
        lax.psum_scatter(
            gathered_value_contributions.astype(jnp.bfloat16),
            "seq",
            scatter_dimension=0,
            tiled=True,
        ).astype(jnp.float32),
    )
    dq_pre = apply_rotary(
        dquery.reshape(token_rows, QUERY_HEADS * HEAD_SIZE) * scale_of_scores,
        cosine_table,
        sine_table,
        QUERY_HEADS,
        -1.0,
    ).astype(jnp.bfloat16)
    key_gradient_unrotated = apply_rotary(
        local_keys, cosine_table, sine_table, KEY_VALUE_HEADS, -1.0
    ).astype(jnp.bfloat16)
    dv_pre = value_mine.astype(jnp.bfloat16)
    dnorm_one = (
        times_transpose(dq_pre, query_full)
        + times_transpose(key_gradient_unrotated, complete_keys)
        + times_transpose(dv_pre, value_full)
    )
    input_part, gain_one_term = norm_backward(inputs_f, scale_one, gain_one_f, dnorm_one)
    input_grad = (dresid + input_part)[None]
    query_term = outer_product(first_normalized, dq_pre)
    key_term = outer_product(first_normalized, key_gradient_unrotated)
    value_term = outer_product(first_normalized, dv_pre)
    first_gain_grad, query_grad, key_grad, value_grad, output_grad, second_gain_grad = (
        lax.psum_scatter(gain_one_term, ("seq", "tp"), scatter_dimension=0, tiled=True),
        lax.psum_scatter(query_term, ("seq", "tp"), scatter_dimension=0, tiled=True),
        lax.psum_scatter(key_term, ("seq", "tp"), scatter_dimension=0, tiled=True),
        lax.psum_scatter(value_term, ("seq", "tp"), scatter_dimension=0, tiled=True),
        lax.psum_scatter(output_term, ("seq", "tp"), scatter_dimension=0, tiled=True),
        lax.psum_scatter(gain_two_term, ("seq", "tp"), scatter_dimension=0, tiled=True),
    )
    return (
        layer_output,
        input_grad,
        first_gain_grad,
        query_grad,
        key_grad,
        value_grad,
        output_grad,
        second_gain_grad,
        gate_grad,
        up_grad,
        down_grad,
    )


MESH = pl.DeviceIdType.MESH
ANY = pl.ANY
HALF = HEAD_SIZE // 2
LANES = 128
SLOT = LANES // 2
f32 = jnp.float32
bf16 = jnp.bfloat16
VMEM_LIMIT = 62 << 20
COST = pl.CostEstimate(flops=1_000_000, transcendentals=0, bytes_accessed=100_000)


class Plane:
    def __init__(self, n, m):
        self.n, self.m, self.chips = n, m, n // 2
        self.s = lax.axis_index("seq")
        self.t = lax.axis_index("tp")
        self.q = self.s // 2
        self.c = lax.rem(self.s, 2)

        across = self.q + 1 - 2 * lax.rem(self.q, 2)
        along = lax.rem(self.q + 2, 4)
        self.to = across * (1 - self.c) + along * self.c
        self.fro = across * self.c + along * (1 - self.c)
        self.far = 3 - self.q
        self.order = (self.q, self.to, self.fro, self.far)

    def device(self, s):
        return (s, self.t)

    def same(self, chip):
        return (2 * chip + self.c, self.t)

    def number(self, k, other):
        c, q = self.c, self.q
        low, high = lax.rem(k, 2), k // 2
        dx = low * (1 - c) + high * c
        dy = high * (1 - c) + low * c
        x, y = lax.rem(q, 2), q // 2
        chip = 2 * (y + dy - 2 * y * dy) + x + dx - 2 * x * dx
        return 2 * chip + c + other * (1 - 2 * c)

    def sibling(self):
        return (2 * self.q + 1 - self.c, self.t)

    def ahead(self, k):
        return lax.rem(self.q + k, self.chips)

    def behind(self, k):
        return lax.rem(self.q + self.chips - k, self.chips)

    def seq_ahead(self, k):
        return lax.rem(self.s + k, self.n)

    def seq_behind(self, k):
        return lax.rem(self.s + self.n - k, self.n)

    def tp_ahead(self, k):
        return (self.s, lax.rem(self.t + k, self.m))

    def tp_behind(self, k):
        return lax.rem(self.t + self.m - k, self.m)


def greet(plane, with_tp):
    barrier = pltpu.get_barrier_semaphore()
    for k in range(1, plane.n):
        pl.semaphore_signal(
            barrier, inc=1, device_id=plane.device(plane.seq_ahead(k)), device_id_type=MESH
        )
    if with_tp:
        for k in range(1, plane.m):
            pl.semaphore_signal(barrier, inc=1, device_id=plane.tp_ahead(k), device_id_type=MESH)


def meet(plane, with_tp):
    count = plane.n - 1 + (plane.m - 1 if with_tp else 0)
    pl.semaphore_wait(pltpu.get_barrier_semaphore(), count)


def remote(src, dst, send, recv, device):
    return pltpu.make_async_remote_copy(
        src_ref=src,
        dst_ref=dst,
        send_sem=send,
        recv_sem=recv,
        device_id=device,
        device_id_type=MESH,
    )


class Gather:
    COPIES = 7

    def __init__(self, plane, src, dst_of, send, recv, local):
        to, fro, far, c = plane.to, plane.fro, plane.far, plane.c
        here = dst_of(plane.s)
        self.own = pltpu.make_async_copy(src, here, local)

        def block(chip):
            return dst_of(2 * chip + c)

        def copy(i, a, b, device):
            return remote(a, b, send.at[i], recv.at[i], device)

        sibling = plane.sibling()
        self.swap = copy(0, src, here, sibling)
        self.ahead = copy(1, src, here, plane.same(to))
        self.back = copy(2, src, here, plane.same(fro))
        self.relay = copy(3, block(fro), block(fro), plane.same(to))
        self.share = [
            copy(4, block(to), block(to), sibling),
            copy(5, block(fro), block(fro), sibling),
            copy(6, block(far), block(far), sibling),
        ]

    def start(self):
        self.back.start()
        self.ahead.start()

    def start_here(self):
        self.swap.start()
        self.own.start()

    def relay_near(self):
        self.back.wait_recv()
        self.relay.start()
        self.share[1].start()
        self.ahead.wait_recv()
        self.share[0].start()

    def relay_far(self):
        self.relay.wait_recv()
        self.share[2].start()

    def wait_sends(self):
        for copy in [self.swap, self.ahead, self.back, self.relay] + self.share:
            copy.wait_send()


class Gathers:
    def __init__(self, plane, src, dst_of, sems, local, pieces):
        rows = src.shape[0] // pieces
        self.parts = []
        for i in range(pieces):
            at = pl.ds(i * rows, rows)
            self.parts.append(
                Gather(
                    plane,
                    src.at[at],
                    lambda d, at=at: dst_of(d).at[at],
                    sems.at[i, 0],
                    sems.at[i, 1],
                    local.at[i],
                )
            )

    def start(self):
        for part in self.parts:
            part.start()
        for part in self.parts:
            part.start_here()

    def relay_near(self):
        for part in self.parts:
            part.relay_near()

    def relay_far(self):
        for part in self.parts:
            part.relay_far()

    def wait_own(self):
        for part in self.parts:
            part.own.wait()

    def wait_swap(self):
        for part in self.parts:
            part.swap.wait_recv()

    def wait_share(self, i):
        for part in self.parts:
            part.share[i].wait_recv()

    def wait_sends(self):
        for part in self.parts:
            part.wait_sends()

    def finish(self):
        self.wait_own()
        self.wait_swap()
        for i in range(3):
            self.wait_share(i)
        self.wait_sends()

    @staticmethod
    def scratch(pieces):
        return [
            pltpu.SemaphoreType.DMA((pieces, 2, Gather.COPIES)),
            pltpu.SemaphoreType.DMA((pieces,)),
        ]


class Chain:
    def __init__(self, plane, mine, slot_of, sems):
        self.plane, self.mine, self.slot_of, self.sems = plane, mine, slot_of, sems

    def copy(self, way, hop, to):
        plane, row = self.plane, 0 if way > 0 else 2
        slot = self.slot_of(plane.t - way * hop)
        return remote(
            self.mine if hop == 0 else slot,
            slot,
            self.sems.at[row, hop],
            self.sems.at[row + 1, hop],
            (plane.s, to),
        )

    def inside(self, way, hop):
        t, m = self.plane.t, self.plane.m
        holds = t >= hop if way > 0 else t < m - hop
        passes = t < m - 1 if way > 0 else t > 0
        return holds, passes

    def start(self):
        self.pass_on(0)

    def pass_on(self, hop):
        for way in (1, -1):
            holds, passes = self.inside(way, hop)

            @pl.when(holds & passes)
            def _(way=way):
                self.copy(way, hop, self.plane.t + way).start()

    def step(self, hop):
        plane = self.plane
        for way in (1, -1):
            holds, _ = self.inside(way, hop)

            @pl.when(holds)
            def _(way=way):
                row = 0 if way > 0 else 2
                slot = self.slot_of(plane.t - way * hop)
                remote(
                    slot,
                    slot,
                    self.sems.at[row, hop - 1],
                    self.sems.at[row + 1, hop - 1],
                    (plane.s, plane.t - way),
                ).wait_recv()

        if hop < plane.m - 1:
            self.pass_on(hop)

    def wait_sends(self):
        for hop in range(self.plane.m - 1):
            for way in (1, -1):
                holds, passes = self.inside(way, hop)

                @pl.when(holds & passes)
                def _(way=way, hop=hop):
                    self.copy(way, hop, self.plane.t + way).wait_send()


def fan(plane, src_of, dst_of, send, recv):
    copies = []
    for k in range(1, plane.m):
        device = plane.tp_ahead(k)
        copies.append(
            remote(src_of(device[1]), dst_of(plane.t), send.at[k - 1], recv.at[k - 1], device)
        )
    return copies


def exchange(plane, src_of, dst_of, send, recv, local):
    own = pltpu.make_async_copy(src_of(plane.s), dst_of(plane.s), local)
    copies = []
    for k in range(1, plane.n):
        peer = plane.seq_ahead(k)
        copies.append(
            remote(
                src_of(peer), dst_of(plane.s), send.at[k - 1], recv.at[k - 1], plane.device(peer)
            )
        )
    return [own] + copies


TILE = 16


def in_tiles(rows, body):
    def one(i, carry):
        body(pl.ds(pl.multiple_of(i * TILE, TILE), TILE))
        return carry

    lax.fori_loop(0, rows // TILE, one, 0)


class Reduce:
    SLOTS = (4, 4, 3)

    THEIRS = (0, 2, 1, 3)

    def __init__(self, plane, part_of, pair, near, far, sems, loc, stage=None):
        c = plane.c
        self.pair, self.near, self.far = pair, near, far
        self.rows = pair.shape[1]
        self.swaps, self.loads = {}, {}
        for k in range(4):
            mine = self.THEIRS[k]
            chip = plane.order[mine]
            source = part_of(2 * chip + 1 - c) if stage is None else stage.at[mine]
            self.swaps[k] = remote(
                source, near.at[k], sems.at[0, k], sems.at[1, k], plane.sibling()
            )
            if stage is None:
                self.loads[k] = pltpu.make_async_copy(
                    part_of(2 * plane.order[k] + c), pair.at[k], loc.at[k]
                )

        def out(i, k, chip):
            return remote(
                pair.at[k], far.at[i], sems.at[2, i], sems.at[3, i], plane.same(chip)
            )

        self.out = [out(0, 3, plane.to), out(1, 1, plane.to), out(2, 2, plane.fro)]

    def start(self, *which):
        for k in which:
            self.swaps[k].start()
            self.loads[k].start()

    def landed(self, k):
        self.swaps[k].wait()
        if self.loads:
            self.loads[k].wait()

    def join(self, k):
        pair, near = self.pair, self.near
        self.landed(k)

        def add(at):
            both = pair[k, at, :].astype(f32) + near[k, at, :].astype(f32)
            pair[k, at, :] = both.astype(bf16)

        in_tiles(self.rows, add)

    def send_to(self):
        self.join(3)
        self.out[0].start()
        self.join(1)
        self.out[1].start()

    def ready(self):
        self.landed(2)

    def send_fro(self):
        pair, near, far = self.pair, self.near, self.far
        self.out[0].wait_recv()

        def add(at):
            both = pair[2, at, :].astype(f32) + near[2, at, :].astype(f32)
            pair[2, at, :] = (both + far[0, at, :].astype(f32)).astype(bf16)

        in_tiles(self.rows, add)
        self.out[2].start()

    def first(self, total, more=None):
        pair, near = self.pair, self.near
        self.landed(0)

        def add(at):
            value = pair[0, at, :].astype(f32) + near[0, at, :].astype(f32)
            total[at, :] = value if more is None else value + more[at, :].astype(f32)

        in_tiles(self.rows, add)

    def finish(self, total, out=None):
        far = self.far
        out = total if out is None else out
        self.out[0].wait_send()
        self.out[1].wait()
        self.out[2].wait()

        def add(at):
            value = total[at, :] + far[1, at, :].astype(f32) + far[2, at, :].astype(f32)
            out[at, :] = value.astype(out.dtype)

        in_tiles(self.rows, add)

    @staticmethod
    def scratch(rows, width):
        return [pltpu.VMEM((slots, rows, width), bf16) for slots in Reduce.SLOTS] + [
            pltpu.SemaphoreType.DMA((4, 4)),
            pltpu.SemaphoreType.DMA((4,)),
        ]


def last_body(
    n, m, dqkv_in, w_in, x_in, dresid_in, gain, norm_t, ffn, downs, wo, vec,
    input_grad, ffn_out, qkv_out, wo_out, vec_out,
    dqkv, w, x, dresid, down_here, down_sum, narrow, pair, near, far, sr, lr, total, stage, norms, mine, got, summed, sems, st, loc,
):
    plane = Plane(n, m)
    greet(plane, True)
    loads = [
        pltpu.make_async_copy(a, b, loc.at[5 + i])
        for i, (a, b) in enumerate(
            ((dqkv_in, dqkv), (w_in, w), (downs, down_here), (x_in, x), (dresid_in, dresid))
        )
    ]
    load = pltpu.make_async_copy(norm_t, norms, loc.at[0])
    for copy in loads + [load]:
        copy.start()
    narrow[...] = lanes_of_columns(narrow.shape, 1)
    meet(plane, True)
    rows, width = ffn_out.shape[1], ffn.shape[2]
    across = fan(plane, lambda t: wo.at[t], lambda t: wo_out.at[t], st.at[1, 0], st.at[1, 1])
    across += fan(plane, lambda t: vec.at[t], lambda t: vec_out.at[t], st.at[2, 0], st.at[2, 1])
    across += [
        pltpu.make_async_copy(wo.at[plane.t], wo_out.at[plane.t], loc.at[1]),
        pltpu.make_async_copy(vec.at[plane.t], vec_out.at[plane.t], loc.at[2]),
    ]
    for copy in across:
        copy.start()
    a = exchange(
        plane,
        lambda i: ffn.at[:, pl.ds(pl.multiple_of(i * rows, rows), rows), :],
        lambda i: ffn_out.at[
            pl.ds(0, 2), :, pl.ds(pl.multiple_of(i * width, width), width)
        ],
        sems.at[0, 0],
        sems.at[0, 1],
        loc.at[3],
    )
    a_down = exchange(
        plane,
        lambda i: down_sum.at[pl.ds(pl.multiple_of(i * rows, rows), rows), :],
        lambda i: ffn_out.at[2, :, pl.ds(pl.multiple_of(i * width, width), width)],
        sems.at[2, 0],
        sems.at[2, 1],
        loc.at[10],
    )
    for copy in a:
        copy.start()
    reduce = Reduce(plane, None, pair, near, far, sr, lr, stage)
    tokens = pair.shape[1]
    for copy in loads[:2]:
        copy.wait()

    def blocks(it, carry):
        k = 3 - it // 2
        other = 1 - lax.rem(it, 2)
        b = plane.number(k, other)
        here = pl.ds(pl.multiple_of(b * tokens, tokens), tokens)
        part = lax.dot_general(dqkv[here, :], w[...], NT, preferred_element_type=f32).astype(bf16)

        @pl.when(other == 0)
        def _():
            pair[k] = part

        @pl.when(other == 1)
        def _():
            stage[k] = part

        for kk in range(4):

            @pl.when(it == 2 * (3 - kk))
            def _(kk=kk):
                reduce.swaps[Reduce.THEIRS[kk]].start()

        return carry

    lax.fori_loop(0, n, blocks, 0)
    reduce.send_to()
    loads[2].wait()

    def add_down(at):
        value = down_here[0, at, :].astype(f32)
        for t in range(1, m):
            value = value + down_here[t, at, :].astype(f32)
        down_sum[at, :] = value.astype(bf16)

    in_tiles(down_sum.shape[0], add_down)
    for copy in a_down:
        copy.start()
    load.wait()
    strip = summed.shape[1]

    def weight_grads(s, carry):
        at = pl.ds(pl.multiple_of(s * m * strip, m * strip), m * strip)
        value = jnp.dot(norms[at, :], dqkv[...], preferred_element_type=f32).astype(bf16)
        value = jnp.dot(value, narrow[...], preferred_element_type=f32).astype(bf16)
        for t in range(m):
            mine[s, t] = value[t * strip : (t + 1) * strip]
        return carry

    lax.fori_loop(0, n, weight_grads, 0)
    over = fan(plane, lambda t: mine.at[:, t], lambda t: got.at[t], st.at[0, 0], st.at[0, 1])
    for copy in over:
        copy.start()
    reduce.ready()
    reduce.first(total)
    reduce.send_fro()
    for copy in over:
        copy.wait()

    def add(s, carry):
        value = mine[s, plane.t].astype(f32)
        for k in range(1, m):
            value = value + got[plane.tp_behind(k), s].astype(f32)
        summed[s] = value.astype(bf16)
        return carry

    lax.fori_loop(0, n, add, 0)
    b = exchange(
        plane,
        lambda i: summed.at[i],
        lambda i: qkv_out.at[i],
        sems.at[1, 0],
        sems.at[1, 1],
        loc.at[4],
    )
    for copy in b:
        copy.start()
    for copy in loads[3:]:
        copy.wait()
    reduce.finish(total)

    def into_input(at):
        value = x[at, :].astype(f32)
        scale = lax.rsqrt(jnp.mean(value * value, axis=1, keepdims=True) + norm_epsilon)
        inner = gain[...] * total[at, :]
        moment = jnp.mean(value * inner, axis=1, keepdims=True)
        input_grad[at, :] = (
            dresid[at, :] + scale * inner - value * scale * (scale * scale * moment)
        )

    in_tiles(tokens, into_input)
    for copy in a + a_down + b + across:
        copy.wait()


def last(n, m, dqkv, w, x, dresid, gain, norm_t, ffn, downs, wo, vec, ident):
    width, length = norm_t.shape
    tokens = length // n
    cols = w.shape[1] // SLOT * HALF
    strip = width // (n * m)
    vmem = pl.BlockSpec(memory_space=pltpu.VMEM)
    hbm = pl.BlockSpec(memory_space=ANY)
    return pl.pallas_call(
        functools.partial(last_body, n, m),
        out_shape=(
            jax.ShapeDtypeStruct((tokens, width), f32),
            jax.ShapeDtypeStruct((3, ffn.shape[1] // n, ffn.shape[2] * n), ffn.dtype),
            jax.ShapeDtypeStruct((n, strip, cols), bf16),
            jax.ShapeDtypeStruct(wo.shape, wo.dtype),
            jax.ShapeDtypeStruct(vec.shape, vec.dtype),
        ),
        in_specs=[hbm] * 4 + [vmem] + [hbm] * 5,
        out_specs=[vmem] + [hbm] * 4,
        scratch_shapes=[
            pltpu.VMEM(dqkv.shape, bf16),
            pltpu.VMEM(w.shape, bf16),
            pltpu.VMEM(x.shape, bf16),
            pltpu.VMEM(dresid.shape, f32),
            pltpu.VMEM(downs.shape, bf16),
            pltpu.VMEM(downs.shape[1:], bf16),
            pltpu.VMEM((w.shape[1], cols), bf16),
        ]
        + Reduce.scratch(tokens, width)
        + [
            pltpu.VMEM((tokens, width), f32),
            pltpu.VMEM((4, tokens, width), bf16),
            pltpu.VMEM((width, length), bf16),
            pltpu.VMEM((n, m, strip, cols), bf16),
            pltpu.VMEM((m, n, strip, cols), bf16),
            pltpu.VMEM((n, strip, cols), bf16),
            pltpu.SemaphoreType.DMA((3, 2, n - 1)),
            pltpu.SemaphoreType.DMA((3, 2, m - 1)),
            pltpu.SemaphoreType.DMA((11,)),
        ],
        compiler_params=pltpu.CompilerParams(
            collective_id=ident, has_side_effects=True, vmem_limit_bytes=VMEM_LIMIT
        ),
        cost_estimate=COST,
        name="last",
    )(dqkv, w, x, dresid, gain, norm_t, ffn, downs, wo, vec)


def column(row):
    return jnp.broadcast_to(row, (8, row.shape[1])).T[:, :1]


def lanes_of_columns(shape, of):
    column = lax.broadcasted_iota(jnp.int32, shape, of).astype(f32)
    lane = lax.broadcasted_iota(jnp.int32, shape, 1 - of).astype(f32)
    half = jnp.floor((column + 0.5) * (1.0 / HALF))
    return jnp.where(lane == column + half * (SLOT - HALF), 1.0, 0.0).astype(bf16)


def gain_row(tiles, which, strip):
    stacked = tiles.reshape(-1, LANES).astype(bf16)
    count = stacked.shape[0] // 8
    shape = (LANES, count * strip)
    lane = lax.broadcasted_iota(jnp.int32, shape, 1).astype(f32)
    owner = jnp.floor((lane + 0.5) * (1.0 / strip))
    inside = lane - owner * strip
    pick = lax.broadcasted_iota(jnp.int32, shape, 0).astype(f32) == inside
    spread_out = jnp.dot(
        stacked, jnp.where(pick, 1.0, 0.0).astype(bf16), preferred_element_type=f32
    )
    shape = spread_out.shape
    lane = lax.broadcasted_iota(jnp.int32, shape, 1).astype(f32)
    owner = jnp.floor((lane + 0.5) * (1.0 / strip))
    row = lax.broadcasted_iota(jnp.int32, shape, 0).astype(f32)
    mine = row == owner * 8.0 + which
    return jnp.sum(jnp.where(mine, spread_out, 0.0), axis=0, keepdims=True)


def entry_body(
    n, m, heads, strip, x, doc_ids, positions, wq, wk, wv, one, two, wg, wu, wd, wo, inverse,
    norm_t, q, k, v, cosine, sine, w, gain_one, gain_two, docs, ffn, down, wo_z,
    blocks, norms, turned, places_all, w_all, gains_all, q_here, k_here, v_here, cos_here, sin_here,
    places, wqkv, gains, widen, sx, lx, rem, sz, sn, loc,
):
    plane = Plane(n, m)
    greet(plane, True)
    tokens = x.shape[0]
    start = 0
    for weight in (wq, wk, wv):
        each = weight.shape[1] // n
        for i in range(n):
            wqkv[i, :, start : start + each] = weight[:, i * each : (i + 1) * each]
        start += each
    gains[...] = jnp.zeros_like(gains)
    gains[0:1, :strip] = one[...].astype(f32)
    gains[1:2, :strip] = two[...].astype(f32)
    places[0:1, :] = doc_ids[...]
    places[1:2, :] = positions[...]
    meet(plane, True)
    gather = Gathers(plane, x, lambda i: blocks.at[i], sx, lx, 2)
    first = []
    for i, (src, dst) in enumerate(((gains, gains_all), (wqkv, w_all))):
        first += exchange(
            plane,
            lambda s, src=src, i=i: src.at[s] if i else src,
            lambda s, dst=dst: dst.at[s, plane.t],
            rem.at[i, 0],
            rem.at[i, 1],
            loc.at[1 + i],
        )
    few = exchange(
        plane, lambda i: places, lambda i: places_all.at[i], rem.at[2, 0], rem.at[2, 1], loc.at[3]
    )
    for copy in first + few:
        copy.start()
    gather.start()
    across = []
    for i, ref in enumerate((gains_all, w_all)):

        def slot(t, ref=ref):
            return ref.at[:, plane.t]

        across.append(fan(plane, slot, slot, sz.at[i, 0], sz.at[i, 1]))
    across.append(fan(plane, lambda t: wo, lambda t: wo_z.at[t], sz.at[2, 0], sz.at[2, 1]))
    own_wo = pltpu.make_async_copy(wo, wo_z.at[plane.t], loc.at[4])
    own_wo.start()
    for copy in first:
        copy.wait()
    for copy in across[0] + across[1]:
        copy.start()
    widen[...] = lanes_of_columns(widen.shape, 0)
    moves = []
    width, rows = wg.shape[1] // n, wg.shape[0]
    for j, weight in enumerate((wg, wu, wd)):
        moves += exchange(
            plane,
            lambda i, weight=weight: weight.at[:, pl.ds(pl.multiple_of(i * width, width), width)],
            lambda i, dst=ffn.at[j] if j < 2 else down: dst.at[
                pl.ds(pl.multiple_of(i * rows, rows), rows), :
            ],
            rem.at[3 + j, 0],
            rem.at[3 + j, 1],
            loc.at[5 + j],
        )
    for copy in few + across[0]:
        copy.wait()
    tiles = gains_all[...]
    gain_one[...] = gain_row(tiles, 0, strip)
    gain_two[...] = gain_row(tiles, 1, strip)
    gather.wait_own()

    def number(it):
        return plane.number(it // 2, lax.rem(it, 2))

    def store(it, at):
        span = pl.ds(pl.multiple_of(number(it) * tokens, tokens), tokens)
        return pltpu.make_async_copy(turned.at[at], norm_t.at[:, span], sn.at[at])

    def normalize(it, carry):
        b = number(it)
        at = lax.rem(it, 2)

        @pl.when(it == 1)
        def _():
            gather.wait_swap()

        @pl.when(it == 2)
        def _():
            gather.relay_near()

        @pl.when(it == 3)
        def _():
            gather.wait_share(1)

        @pl.when(it == 5)
        def _():
            gather.wait_share(0)

        @pl.when(it == 6)
        def _():
            gather.relay_far()
            for copy in moves + across[2]:
                copy.start()

        @pl.when(it == 7)
        def _():
            gather.wait_share(2)

        @pl.when(it >= 2)
        def _():
            store(it - 2, at).wait()

        value = blocks[b].astype(f32)
        scale = lax.rsqrt(jnp.mean(value * value, axis=1, keepdims=True) + norm_epsilon)
        low = (value * scale * gain_one[...]).astype(bf16)
        norms[b] = low
        turned[at] = low.T
        store(it, at).start()
        here = pl.ds(pl.multiple_of(b * tokens, tokens), tokens)
        docs[:, here] = places_all[b, 0:1, :]
        angles = column(places_all[b, 1:2, :].astype(f32)) * inverse[...]
        lanes = lax.broadcasted_iota(jnp.int32, angles.shape, 1)
        sin = jnp.sin(angles)
        cos_here[here, :] = jnp.cos(angles)
        sin_here[here, :] = jnp.where(lanes < SLOT, -sin, sin)
        return carry

    lax.fori_loop(0, n, normalize, 0)
    outs = [
        pltpu.make_async_copy(cos_here, cosine, loc.at[8]),
        pltpu.make_async_copy(sin_here, sine, loc.at[9]),
        pltpu.make_async_copy(q_here, q, loc.at[10]),
        pltpu.make_async_copy(k_here, k, loc.at[11]),
        pltpu.make_async_copy(v_here, v, loc.at[12]),
    ]
    for copy in outs[:2]:
        copy.start()
    for copy in across[1]:
        copy.wait()

    def widened(s, carry):
        at = pl.ds(pl.multiple_of(s * m * strip, m * strip), m * strip)
        narrow = w_all[s].reshape(m * strip, w_all.shape[3])
        w[at, :] = jnp.dot(narrow, widen[...], preferred_element_type=f32).astype(bf16)
        return carry

    lax.fori_loop(0, n, widened, 0)

    def project(b, carry):
        here = pl.ds(pl.multiple_of(b * tokens, tokens), tokens)
        out = jnp.dot(norms[b], w[...], preferred_element_type=f32)
        cos, sin = cos_here[here, :], sin_here[here, :]
        for h in range(heads + 1):
            part = out[:, h * LANES : (h + 1) * LANES]
            rotated = (part * cos + pltpu.roll(part, SLOT, 1) * sin).astype(bf16)
            if h < heads:
                q_here[h, here, :] = rotated
            else:
                k_here[here, :] = rotated
        v_here[here, :] = out[:, (heads + 1) * LANES :].astype(bf16)
        return carry

    lax.fori_loop(0, n, project, 0)
    for copy in outs[2:]:
        copy.start()
    gather.wait_sends()
    store(n - 2, 0).wait()
    store(n - 1, 1).wait()
    own_wo.wait()
    for copy in across[2] + moves + outs:
        copy.wait()


def entry(n, m, heads, x, docs, positions, wq, wk, wv, one, two, wg, wu, wd, wo, inverse, ident):
    tokens, width = x.shape
    length = n * tokens
    strip = wq.shape[0]
    each = (wq.shape[1] + wk.shape[1] + wv.shape[1]) // n
    wide = each // HALF * SLOT
    rows, cols = wg.shape
    vmem = pl.BlockSpec(memory_space=pltpu.VMEM)
    hbm = pl.BlockSpec(memory_space=ANY)
    return pl.pallas_call(
        functools.partial(entry_body, n, m, heads, strip),
        out_shape=(
            jax.ShapeDtypeStruct((width, length), bf16),
            jax.ShapeDtypeStruct((heads, length, LANES), bf16),
            jax.ShapeDtypeStruct((length, LANES), bf16),
            jax.ShapeDtypeStruct((length, LANES), bf16),
            jax.ShapeDtypeStruct((length, LANES), f32),
            jax.ShapeDtypeStruct((length, LANES), f32),
            jax.ShapeDtypeStruct((width, wide), bf16),
            jax.ShapeDtypeStruct((1, width), f32),
            jax.ShapeDtypeStruct((1, width), f32),
            jax.ShapeDtypeStruct((1, length), jnp.int32),
            jax.ShapeDtypeStruct((2, rows * n, cols // n), wg.dtype),
            jax.ShapeDtypeStruct((rows * n, cols // n), wg.dtype),
            jax.ShapeDtypeStruct((m,) + wo.shape, wo.dtype),
        ),
        in_specs=[hbm] + [vmem] * 7 + [hbm] * 4 + [vmem],
        out_specs=[hbm] * 6 + [vmem] * 4 + [hbm] * 3,
        scratch_shapes=[
            pltpu.VMEM((n, tokens, width), bf16),
            pltpu.VMEM((n, tokens, width), bf16),
            pltpu.VMEM((2, width, tokens), bf16),
            pltpu.VMEM((n, 2, tokens), jnp.int32),
            pltpu.VMEM((n, m, strip, each), bf16),
            pltpu.VMEM((n, m, 8, LANES), f32),
            pltpu.VMEM((heads, length, LANES), bf16),
            pltpu.VMEM((length, LANES), bf16),
            pltpu.VMEM((length, LANES), bf16),
            pltpu.VMEM((length, LANES), f32),
            pltpu.VMEM((length, LANES), f32),
            pltpu.VMEM((2, tokens), jnp.int32),
            pltpu.VMEM((n, strip, each), bf16),
            pltpu.VMEM((8, LANES), f32),
            pltpu.VMEM((each, wide), bf16),
            *Gathers.scratch(2),
            pltpu.SemaphoreType.DMA((6, 2, n - 1)),
            pltpu.SemaphoreType.DMA((3, 2, m - 1)),
            pltpu.SemaphoreType.DMA((2,)),
            pltpu.SemaphoreType.DMA((13,)),
        ],
        compiler_params=pltpu.CompilerParams(
            collective_id=ident, has_side_effects=True, vmem_limit_bytes=VMEM_LIMIT
        ),
        cost_estimate=COST,
        name="entry",
    )(x, docs, positions, wq, wk, wv, one, two, wg, wu, wd, wo, inverse)


BLOCK = 512
NT = (((1,), (1,)), ((), ()))
LOG2E = 1.4426950408889634


def allowed_block(first_key, first_query, begin, causal):
    keys = first_key + lax.broadcasted_iota(jnp.int32, (BLOCK, BLOCK), 0)
    ok = keys >= begin
    if causal:
        queries = first_query + lax.broadcasted_iota(jnp.int32, (BLOCK, BLOCK), 1)
        ok = ok & (keys <= queries)
    return ok


def begins(docs):
    begin = jnp.zeros(docs.shape, jnp.int32)
    for d in range(3):
        count = jnp.sum((docs == d).astype(f32), axis=1, keepdims=True).astype(jnp.int32)
        begin = begin + jnp.where(docs > d, count, 0)
    return begin


def spread_rows(wo, wo_here):
    halves, filled, width = wo.shape
    for i in range(halves):
        wo_here[i * SLOT : i * SLOT + filled, :] = wo[i]
        wo_here[i * SLOT + filled : (i + 1) * SLOT, :] = jnp.zeros((SLOT - filled, width), bf16)


def attend_body(
    n, m, factor, q, k, v, docs, wo, go, x, gain, ffn,
    o_out, lse, start, low_out, go_all, resid, norm, ffn_all,
    o, low, vt, top, total, acc, wo_here, go_here,
    pair, near, far, sr, lr, stage, sg, lg, sz, loc,
):
    plane = Plane(n, m)
    rows = x.shape[0]
    heads = q.shape[0]
    greet(plane, True)
    gather = Gathers(plane, go, lambda i: go_here.at[i], sg, lg, 2)
    reduce = Reduce(plane, None, pair, near, far, sr, None, stage)
    spread_rows(wo, wo_here)
    vt[...] = v[...].T
    start[...] = begins(docs[...])
    meet(plane, True)
    gather.start()
    chain = Chain(plane, ffn, lambda t: ffn_all.at[t], sz)
    chain.start()
    own_ffn = pltpu.make_async_copy(ffn, ffn_all.at[plane.t], loc.at[3])
    own_ffn.start()

    def chips(step, carry):
        kk = 3 - step
        i = plane.number(kk, 0) // 2
        here = pl.ds(pl.multiple_of(i * BLOCK, BLOCK), BLOCK)
        begin = start[:, here]

        def head(h, carry):
            query = q[h, here, :]
            top[...] = jnp.full_like(top, mask_fill_value)
            total[...] = jnp.zeros_like(total)
            acc[...] = jnp.zeros_like(acc)

            def keys(j, causal):
                at = pl.ds(pl.multiple_of(j * BLOCK, BLOCK), BLOCK)
                raw = lax.dot_general(k[at, :], query, NT, preferred_element_type=f32)
                ok = allowed_block(j * BLOCK, i * BLOCK, begin, causal)
                scores = jnp.where(ok, raw * factor, mask_fill_value)
                new_top = jnp.maximum(top[...], jnp.max(scores, axis=0, keepdims=True))
                weights = jnp.exp2(scores - new_top)
                keep = jnp.exp2(top[...] - new_top)
                total[...] = total[...] * keep + jnp.sum(weights, axis=0, keepdims=True)
                acc[...] = acc[...] * keep + jnp.dot(
                    vt[:, at], weights.astype(bf16), preferred_element_type=f32
                )
                top[...] = new_top

            def loop(j, carry):
                keys(j, False)
                return carry

            lax.fori_loop(0, i, loop, 0)
            keys(i, True)
            out = (acc[...] / total[...]).T
            o[h, here, :] = out
            low[here, pl.ds(pl.multiple_of(h * LANES, LANES), LANES)] = out.astype(bf16)
            lse[h, :, here] = top[...] + jnp.log2(total[...])
            return carry

        lax.fori_loop(0, heads, head, 0)

        @pl.when(step == 1)
        def _():
            reduce.join(3)
            reduce.out[0].start()

        @pl.when(step == 3)
        def _():
            reduce.join(1)
            reduce.out[1].start()

        for other in (1, 0):
            b = plane.number(kk, other)
            at = pl.ds(pl.multiple_of(b * rows, rows), rows)
            part = jnp.dot(low[at, :], wo_here[...], preferred_element_type=f32).astype(bf16)
            if other:
                stage[kk] = part
                for which in range(4):

                    @pl.when(kk == which)
                    def _(which=which):
                        reduce.swaps[Reduce.THEIRS[which]].start()

            else:
                pair[kk] = part
        return carry

    lax.fori_loop(0, 4, chips, 0)
    outs = [
        pltpu.make_async_copy(o, o_out, loc.at[0]),
        pltpu.make_async_copy(low, low_out, loc.at[1]),
    ]
    for copy in outs:
        copy.start()
    gather.relay_near()
    chain.step(1)
    reduce.ready()
    reduce.first(resid, x)
    reduce.send_fro()
    for hop in range(2, m - 1):
        chain.step(hop)
    gather.relay_far()
    reduce.finish(resid)

    def normalize(at):
        value = resid[at, :]
        scale = lax.rsqrt(jnp.mean(value * value, axis=1, keepdims=True) + norm_epsilon)
        norm[at, :] = (value * scale * gain[...]).astype(bf16)

    in_tiles(rows, normalize)
    gather.finish()
    outs.append(pltpu.make_async_copy(go_here, go_all, loc.at[2]))
    outs[-1].start()
    chain.step(m - 1)
    chain.wait_sends()
    own_ffn.wait()
    for copy in outs:
        copy.wait()


def attend(n, m, factor, q, k, v, docs, wo, go, x, gain, ffn, ident):
    heads, length, _ = q.shape
    rows, width = x.shape
    hbm = pl.BlockSpec(memory_space=ANY)
    vmem = pl.BlockSpec(memory_space=pltpu.VMEM)
    return pl.pallas_call(
        functools.partial(attend_body, n, m, factor),
        out_shape=(
            jax.ShapeDtypeStruct((heads, length, LANES), f32),
            jax.ShapeDtypeStruct((heads, 1, length), f32),
            jax.ShapeDtypeStruct((1, length), jnp.int32),
            jax.ShapeDtypeStruct((length, heads * LANES), bf16),
            jax.ShapeDtypeStruct((n,) + go.shape, go.dtype),
            jax.ShapeDtypeStruct((rows, width), f32),
            jax.ShapeDtypeStruct((rows, width), bf16),
            jax.ShapeDtypeStruct((m,) + ffn.shape, bf16),
        ),
        in_specs=[vmem] * 5 + [hbm] + [vmem] * 2 + [hbm],
        out_specs=[hbm, vmem, vmem, hbm, hbm, vmem, vmem, hbm],
        scratch_shapes=[
            pltpu.VMEM((heads, length, LANES), f32),
            pltpu.VMEM((length, heads * LANES), bf16),
            pltpu.VMEM((LANES, length), bf16),
            pltpu.VMEM((1, BLOCK), f32),
            pltpu.VMEM((1, BLOCK), f32),
            pltpu.VMEM((LANES, BLOCK), f32),
            pltpu.VMEM((heads * LANES, width), bf16),
            pltpu.VMEM((n,) + go.shape, go.dtype),
        ]
        + Reduce.scratch(rows, width)
        + [pltpu.VMEM((4, rows, width), bf16)]
        + Gathers.scratch(2)
        + [pltpu.SemaphoreType.DMA((4, m)), pltpu.SemaphoreType.DMA((4,))],
        compiler_params=pltpu.CompilerParams(
            collective_id=ident, has_side_effects=True, vmem_limit_bytes=VMEM_LIMIT
        ),
        cost_estimate=COST,
        name="attend",
    )(q, k, v, docs, wo, go, x, gain, ffn)


def attend_back_body(
    n, m, factor, scale, q_in, k_in, v_in, o_in, lse, begin, cos_in, sin_in, low_in,
    hid_in, down_in, wo, dnorm, resid, grad, gain,
    out, layer, terms, dresid, gain_out,
    q, k, v, o, cosine, sine, low, kt, dqt, dk, dv, delta, go, every, dbranch, wo_here,
    hid_low, w_down, stage, pair, near, far, sr, lr, held, gain_sum, gain_cut, gain_got, sg, lg, sv, loc,
):
    plane = Plane(n, m)
    heads, length, _ = q.shape
    rows, width = dnorm.shape
    strip = gain_out.shape[2]
    loads = [
        pltpu.make_async_copy(a, b, loc.at[i])
        for i, (a, b) in enumerate(
            (
                (q_in, q), (k_in, k), (v_in, v), (o_in, o),
                (cos_in, cosine), (sin_in, sine), (low_in, low),
            )
        )
    ]
    for copy in loads:
        copy.start()
    greet(plane, False)
    moves = [
        pltpu.make_async_copy(hid_in, hid_low, loc.at[8]),
        pltpu.make_async_copy(down_in, w_down, loc.at[9]),
    ]
    for copy in moves:
        copy.start()
    one = Reduce(plane, None, pair, near, far, sr, None, stage)
    gather = Gathers(plane, dbranch, lambda i: every.at[i], sg, lg, 2)
    gain_copies = exchange(
        plane, lambda i: gain_cut.at[i], lambda i: gain_got.at[i], sv.at[0], sv.at[1], loc.at[7]
    )
    gain_sum[...] = jnp.zeros_like(gain_sum)

    def into_branch(at):
        value, up = resid[at, :], dnorm[at, :]
        scale_two = lax.rsqrt(jnp.mean(value * value, axis=1, keepdims=True) + norm_epsilon)
        inner = gain[...] * up
        moment = jnp.mean(value * inner, axis=1, keepdims=True)
        turned = value * scale_two
        got = (
            grad[at, :].astype(f32) + scale_two * inner - turned * (scale_two * scale_two * moment)
        )
        dresid[at, :] = got
        dbranch[at, :] = got.astype(bf16)
        gain_sum[...] += up * turned

    in_tiles(rows, into_branch)
    meet(plane, False)
    gather.start()
    total_gain = jnp.sum(gain_sum[...], axis=0, keepdims=True)
    for i in range(n):
        gain_cut[i] = total_gain[:, i * (width // n) : (i + 1) * (width // n)]
    for copy in gain_copies:
        copy.start()
    spread_rows(wo, wo_here)
    for copy in moves:
        copy.wait()

    def mix(it, carry):
        kk = 3 - it // 2
        other = 1 - lax.rem(it, 2)
        b = plane.number(kk, other)
        at = pl.ds(pl.multiple_of(b * rows, rows), rows)
        part = lax.dot_general(
            hid_low[at, :], w_down[...], NT, preferred_element_type=f32
        ).astype(bf16)

        @pl.when(other == 0)
        def _():
            pair[kk] = part

        @pl.when(other == 1)
        def _():
            stage[kk] = part

        for which in range(4):

            @pl.when(it == 2 * (3 - which))
            def _(which=which):
                one.swaps[Reduce.THEIRS[which]].start()

        return carry

    lax.fori_loop(0, n, mix, 0)
    for copy in loads:
        copy.wait()
    kt[...] = k[...].T
    dk[...] = jnp.zeros_like(dk)
    dv[...] = jnp.zeros_like(dv)

    def unturn(value, at):
        return value * cosine[at, :] - pltpu.roll(value, SLOT, 1) * sine[at, :]

    def chips(kk, carry):
        @pl.when(kk == 0)
        def _():
            gather.wait_own()
            gather.wait_swap()

        @pl.when(kk == 1)
        def _():
            gather.relay_near()
            gather.wait_share(1)

        @pl.when(kk == 2)
        def _():
            one.send_to()
            gather.wait_share(0)

        @pl.when(kk == 3)
        def _():
            one.ready()
            one.first(held, resid)
            gather.relay_far()
            gather.wait_share(2)

        i = plane.number(kk, 0) // 2
        here = pl.ds(pl.multiple_of(i * BLOCK, BLOCK), BLOCK)
        for other in range(2):
            b = plane.number(kk, other)
            at = pl.ds(pl.multiple_of(b * rows, rows), rows)
            value = lax.dot_general(every[b], wo_here[...], NT, preferred_element_type=f32)
            for h in range(heads):
                go[h, at, :] = value[:, h * LANES : (h + 1) * LANES].astype(bf16)

        def head(h, carry):
            query = q[h, here, :]
            grads = go[h, here, :]
            delta[...] = jnp.sum((grads.astype(f32) * o[h, here, :]).T, axis=0, keepdims=True)
            dqt[...] = jnp.zeros_like(dqt)

            def keys(j, causal):
                at = pl.ds(pl.multiple_of(j * BLOCK, BLOCK), BLOCK)
                raw = lax.dot_general(k[at, :], query, NT, preferred_element_type=f32)
                ok = allowed_block(j * BLOCK, i * BLOCK, begin[:, here], causal)
                probs = jnp.where(ok, jnp.exp2(raw * factor - lse[h, :, here]), 0.0)
                dprob = lax.dot_general(v[at, :], grads, NT, preferred_element_type=f32)
                dscore = (probs * (dprob - delta[...])).astype(bf16)
                dv[at, :] += jnp.dot(probs.astype(bf16), grads, preferred_element_type=f32)
                dk[at, :] += jnp.dot(dscore, query, preferred_element_type=f32)
                dqt[...] += jnp.dot(kt[:, at], dscore, preferred_element_type=f32)

            def loop(j, carry):
                keys(j, False)
                return carry

            lax.fori_loop(0, i, loop, 0)
            keys(i, True)
            got = unturn(dqt[...].T * scale, here).astype(bf16)
            out[here, pl.ds(pl.multiple_of(h * LANES, LANES), LANES)] = got
            return carry

        lax.fori_loop(0, heads, head, 0)
        return carry

    lax.fori_loop(0, 4, chips, 0)

    def write(i, carry):
        at = pl.ds(pl.multiple_of(i * BLOCK, BLOCK), BLOCK)
        turned = unturn(dk[at, :] * scale, at).astype(bf16)
        out[at, heads * LANES : (heads + 1) * LANES] = turned
        out[at, (heads + 1) * LANES :] = dv[at, :].astype(bf16)
        return carry

    lax.fori_loop(0, length // BLOCK, write, 0)
    one.send_fro()
    across = every.reshape(length, width)
    part = 512

    def into_terms(i, carry):
        at = pl.ds(pl.multiple_of(i * part, part), part)
        value = lax.dot_general(
            low[...], across[:, at], (((0,), (0,)), ((), ())), preferred_element_type=f32
        ).astype(bf16)
        for half in range(terms.shape[0]):
            terms[half, :, at] = value[half * SLOT : half * SLOT + HALF]
        return carry

    lax.fori_loop(0, width // part, into_terms, 0)
    for copy in gain_copies:
        copy.wait()
    got = gain_got[0]
    for i in range(1, n):
        got = got + gain_got[i]
    for t in range(m):
        gain_out[t] = got[:, t * strip : (t + 1) * strip]
    gather.wait_sends()
    one.finish(held, layer)


def attend_back(
    n, m, factor, scale, q, k, v, o, lse, begin, cosine, sine, low,
    hid_low, w_down, wo, dnorm, resid, grad, gain, ident,
):
    heads, length, _ = q.shape
    rows, width = dnorm.shape
    strip = width // (n * m)
    hbm = pl.BlockSpec(memory_space=ANY)
    vmem = pl.BlockSpec(memory_space=pltpu.VMEM)
    return pl.pallas_call(
        functools.partial(attend_back_body, n, m, factor, scale),
        out_shape=(
            jax.ShapeDtypeStruct((length, (heads + 2) * LANES), bf16),
            jax.ShapeDtypeStruct((rows, width), bf16),
            jax.ShapeDtypeStruct(wo.shape, bf16),
            jax.ShapeDtypeStruct((rows, width), f32),
            jax.ShapeDtypeStruct((m, 1, strip), f32),
        ),
        in_specs=[hbm] * 4 + [vmem] * 2 + [hbm] * 5 + [vmem] * 5,
        out_specs=[vmem] * 5,
        scratch_shapes=[
            pltpu.VMEM(q.shape, bf16),
            pltpu.VMEM(k.shape, bf16),
            pltpu.VMEM(v.shape, bf16),
            pltpu.VMEM(o.shape, f32),
            pltpu.VMEM(cosine.shape, f32),
            pltpu.VMEM(sine.shape, f32),
            pltpu.VMEM(low.shape, bf16),
            pltpu.VMEM((LANES, length), bf16),
            pltpu.VMEM((LANES, BLOCK), f32),
            pltpu.VMEM((length, LANES), f32),
            pltpu.VMEM((length, LANES), f32),
            pltpu.VMEM((1, BLOCK), f32),
            pltpu.VMEM((heads, length, LANES), bf16),
            pltpu.VMEM((n, rows, width), bf16),
            pltpu.VMEM((rows, width), bf16),
            pltpu.VMEM((heads * LANES, width), bf16),
            pltpu.VMEM(hid_low.shape, bf16),
            pltpu.VMEM(w_down.shape, bf16),
            pltpu.VMEM((4, rows, width), bf16),
        ]
        + Reduce.scratch(rows, width)
        + [
            pltpu.VMEM((rows, width), f32),
            pltpu.VMEM((TILE, width), f32),
            pltpu.VMEM((n, 1, width // n), f32),
            pltpu.VMEM((n, 1, width // n), f32),
        ]
        + Gathers.scratch(2)
        + [pltpu.SemaphoreType.DMA((2, n - 1)), pltpu.SemaphoreType.DMA((10,))],
        compiler_params=pltpu.CompilerParams(
            collective_id=ident, has_side_effects=True, vmem_limit_bytes=VMEM_LIMIT
        ),
        cost_estimate=COST,
        name="attend_back",
    )(q, k, v, o, lse, begin, cosine, sine, low, hid_low, w_down, wo, dnorm, resid, grad, gain)


def feed_body(
    n, m, mine, go, w_in, down, dnorm, grads, hid_out, down_out, down_parts,
    rows, rows_t, go_t, go_two, w, w_down, gates, h, hid_low, down_held, down_sum,
    pair, near, far, stage,
    sg, lg, sr, loc, sw, so, sd, sz, sf,
):
    plane = Plane(n, m)
    tokens, width = rows.shape[1:]
    hid = down.shape[1]
    half = m * hid
    greet(plane, True)
    gather = Gathers(plane, mine, lambda i: rows.at[i], sg, lg, 2)
    reduce = Reduce(plane, None, pair, near, far, sr, None, stage)

    def columns(ref, j, t):
        return ref.at[:, j * half + t * hid : j * half + (t + 1) * hid]

    weights = [
        pltpu.make_async_copy(w_in.at[t, j], columns(w, j, t), sw.at[j, t])
        for j in range(2)
        for t in range(m)
    ]
    for copy in weights:
        copy.start()
    meet(plane, True)
    gather.start()

    def down_at(ref, t):
        return ref.at[:, pl.ds(pl.multiple_of(t * hid, hid), hid)]

    chain = Chain(plane, down, lambda t: down_at(w_down, t), sz)
    chain.start()
    own_down = pltpu.make_async_copy(down, down_at(w_down, plane.t), loc.at[0])
    own_down.start()
    gather.wait_own()
    for copy in weights:
        copy.wait()

    def span(b):
        return pl.ds(pl.multiple_of(b * tokens, tokens), tokens)

    def down_grad(kk, keep):
        chip = plane.number(kk, 0) // 2
        at = pl.ds(pl.multiple_of(chip * 2 * tokens, 2 * tokens), 2 * tokens)

        def part(i, carry):
            line = pl.ds(pl.multiple_of(i * 256, 256), 256)
            value = jnp.dot(go_t[line, at], hid_low[at, :], preferred_element_type=f32)
            keep(line, value)
            return carry

        lax.fori_loop(0, width // 256, part, 0)

    def set_down(line, value):
        down_sum[line, :] = value

    def add_down(line, value):
        down_sum[line, :] += value

    def hold_down(line, value):
        down_held[line, :] = (down_sum[line, :] + value).astype(bf16)

    def early_go(it, slot):
        b = plane.number(it // 2, lax.rem(it, 2))
        return pltpu.make_async_copy(go.at[b], go_two.at[slot], so.at[slot])

    def forward(it, carry):
        b = plane.number(it // 2, lax.rem(it, 2))

        @pl.when(it == 1)
        def _():
            gather.wait_swap()

        @pl.when(it == 2)
        def _():
            down_grad(0, set_down)
            chain.step(1)
            gather.relay_near()

        @pl.when(it == 3)
        def _():
            gather.wait_share(1)

        @pl.when(it == 4)
        def _():
            chain.step(2)

        @pl.when(it == 5)
        def _():
            gather.wait_share(0)

        @pl.when(it == 6)
        def _():
            down_grad(1, add_down)
            down_grad(2, add_down)
            gather.relay_far()

        @pl.when(it == 7)
        def _():
            gather.wait_share(2)

        slot = lax.rem(it, 2)

        @pl.when(it < n - 1)
        def _():
            early_go(it + 1, 1 - slot).start()

        row = rows[b]
        both = jnp.dot(row, w[...], preferred_element_type=f32)
        gates[span(b), :] = both
        gate, up = both[:, :half], both[:, half:]
        hid_low[span(b), :] = (gate * jax.nn.sigmoid(gate) * up).astype(bf16)
        rows_t[:, span(b)] = row.T
        early_go(it, slot).wait()
        go_t[:, span(b)] = go_two[slot].T
        return carry

    early_go(0, 0).start()
    lax.fori_loop(0, n, forward, 0)

    def number(it):
        return plane.number(3 - it // 2, 1 - lax.rem(it, 2))

    def load_go(it, slot):
        return pltpu.make_async_copy(go.at[number(it)], go_two.at[slot], so.at[slot])

    load_go(0, 0).start()
    down_grad(3, hold_down)
    outs = fan(
        plane, lambda t: down_at(down_held, t), lambda t: down_parts.at[t], sf.at[0], sf.at[1]
    )
    outs.append(
        pltpu.make_async_copy(down_at(down_held, plane.t), down_parts.at[plane.t], loc.at[1])
    )
    outs.append(pltpu.make_async_copy(hid_low, hid_out, loc.at[2]))
    for copy in outs:
        copy.start()
    for hop in range(3, m):
        chain.step(hop)
    own_down.wait()
    outs.append(pltpu.make_async_copy(w_down, down_out, loc.at[3]))
    outs[-1].start()

    def backward(it, carry):
        slot = lax.rem(it, 2)
        k = 3 - it // 2
        b = number(it)

        @pl.when(it == 3)
        def _():
            reduce.join(3)
            reduce.out[0].start()

        @pl.when(it == 6)
        def _():
            reduce.join(1)
            reduce.out[1].start()

        @pl.when(it == 7)
        def _():
            reduce.ready()
            reduce.send_fro()

        @pl.when(it < n - 1)
        def _():
            load_go(it + 1, 1 - slot).start()

        load_go(it, slot).wait()

        gate = gates[span(b), :half]
        up = gates[span(b), half:]
        dhidden = jnp.dot(go_two[slot], w_down[...], preferred_element_type=f32)
        sig = jax.nn.sigmoid(gate)
        dgate = (dhidden * up * sig * (1.0 + gate * (1.0 - sig))).astype(bf16)
        dup = (dhidden * gate * sig).astype(bf16)
        h[span(b), :half] = dgate
        h[span(b), half:] = dup
        part = lax.dot_general(h[span(b), :], w[...], NT, preferred_element_type=f32)
        part = part.astype(bf16)

        @pl.when(lax.rem(it, 2) == 1)
        def _():
            pair[k] = part

        @pl.when(lax.rem(it, 2) == 0)
        def _():
            stage[k] = part

        for kk in range(4):

            @pl.when(it == 2 * (3 - kk))
            def _(kk=kk):
                reduce.swaps[Reduce.THEIRS[kk]].start()

        return carry

    lax.fori_loop(0, n, backward, 0)

    def weight_grad(i, carry):
        at = pl.ds(pl.multiple_of(i * 256, 256), 256)
        value = jnp.dot(rows_t[at, :], h[...], preferred_element_type=f32)
        w[at, :] = value.astype(bf16)
        return carry

    lax.fori_loop(0, width // 256, weight_grad, 0)
    ends = [
        pltpu.make_async_copy(columns(w, j, t), grads.at[t, j], sd.at[j, t])
        for j in range(2)
        for t in range(m)
    ]
    for copy in ends:
        copy.start()
    reduce.first(dnorm)
    gather.wait_sends()
    chain.wait_sends()
    reduce.finish(dnorm)
    for copy in outs + ends:
        copy.wait()


def feed(n, m, norm, go, w_in, down, ident):
    tokens, width = norm.shape
    hid = down.shape[1]
    length = n * tokens
    half = m * hid
    hbm = pl.BlockSpec(memory_space=ANY)
    return pl.pallas_call(
        functools.partial(feed_body, n, m),
        out_shape=(
            jax.ShapeDtypeStruct((tokens, width), f32),
            jax.ShapeDtypeStruct((m, 2, width, hid), bf16),
            jax.ShapeDtypeStruct((length, half), bf16),
            jax.ShapeDtypeStruct((width, half), bf16),
            jax.ShapeDtypeStruct((m, width, hid), bf16),
        ),
        in_specs=[hbm] * 4,
        out_specs=[pl.BlockSpec(memory_space=pltpu.VMEM)] + [hbm] * 4,
        scratch_shapes=[
            pltpu.VMEM((n, tokens, width), bf16),
            pltpu.VMEM((width, length), bf16),
            pltpu.VMEM((width, length), bf16),
            pltpu.VMEM((2, tokens, width), bf16),
            pltpu.VMEM((width, 2 * half), bf16),
            pltpu.VMEM((width, half), bf16),
            pltpu.VMEM((length, 2 * half), f32),
            pltpu.VMEM((length, 2 * half), bf16),
            pltpu.VMEM((length, half), bf16),
            pltpu.VMEM((width, half), bf16),
            pltpu.VMEM((width, half), f32),
        ]
        + [pltpu.VMEM((slots, tokens, width), bf16) for slots in Reduce.SLOTS]
        + [
            pltpu.VMEM((4, tokens, width), bf16),
            *Gathers.scratch(2),
            pltpu.SemaphoreType.DMA((4, 4)),
            pltpu.SemaphoreType.DMA((4,)),
            pltpu.SemaphoreType.DMA((2, m)),
            pltpu.SemaphoreType.DMA((2,)),
            pltpu.SemaphoreType.DMA((2, m)),
            pltpu.SemaphoreType.DMA((4, m)),
            pltpu.SemaphoreType.DMA((2, m - 1)),
        ],
        compiler_params=pltpu.CompilerParams(
            collective_id=ident, has_side_effects=True, vmem_limit_bytes=VMEM_LIMIT
        ),
        cost_estimate=COST,
        name="feed",
    )(norm, go, w_in, down)


def fast_layer(n, m):
    def on_plane(
        layer_input,
        doc_ids,
        positions,
        first_gain,
        query_weight,
        key_weight,
        value_weight,
        output_weight,
        second_gain,
        gate_weight,
        up_weight,
        down_weight,
        out_grad,
    ):
        x = layer_input[0]
        width = x.shape[1]
        heads = QUERY_HEADS // n
        scale = 1.0 / math.sqrt(HEAD_SIZE)
        factor = scale * LOG2E
        strip = query_weight.shape[0]

        lane = np.arange(LANES) % SLOT
        inverse = np.where(lane < HALF, rope_base ** (-(lane * 2.0 / HEAD_SIZE)), 0.0)
        (
            norm_t, q, k, v, cosine, sine, wqkv, gain_one, gain_two, docs,
            ffn_mine, down_mine, output_rows,
        ) = entry(
            n, m, heads, x, doc_ids, positions, query_weight, key_weight, value_weight,
            first_gain.reshape(1, strip), second_gain.reshape(1, strip),
            gate_weight, up_weight, down_weight, output_weight,
            jnp.asarray(inverse[None], f32), 0,
        )
        o, lse, begin, low, grad_all, resid, norm_two, ffn_all = attend(
            n, m, factor, q, k, v, docs, output_rows, out_grad[0], x, gain_two, ffn_mine, 9
        )
        dnorm_two, ffn_terms, hid_low, w_down, down_parts = feed(
            n, m, norm_two, grad_all, ffn_all, down_mine, 2
        )
        ffn_sum = lax.psum_scatter(ffn_terms, "tp", scatter_dimension=0, tiled=False)
        dqkv, layer_output, output_terms, dresid, gain_part = attend_back(
            n, m, factor, scale, q, k, v, o, lse, begin, cosine, sine, low, hid_low, w_down,
            output_rows, dnorm_two, resid, out_grad[0], gain_two, 3,
        )
        input_grad, ffn_out, qkv_out, output_parts, gain_sums = last(
            n, m, dqkv, wqkv, x, dresid, gain_one, norm_t, ffn_sum, down_parts,
            output_terms, gain_part, 6,
        )
        output_grad = jnp.sum(output_parts.astype(f32), axis=0)

        gate_grad, up_grad, down_grad = [ffn_out[i].astype(f32) for i in range(3)]
        kv = HEAD_SIZE * KEY_VALUE_HEADS // n
        split = heads * HEAD_SIZE

        def columns(a, b):
            return qkv_out[:, :, a:b].transpose(1, 0, 2).reshape(strip, -1).astype(f32)

        query_grad = columns(0, split)
        key_grad = columns(split, split + kv)
        value_grad = columns(split + kv, split + 2 * kv)

        one = (
            jnp.sum(query_weight.astype(f32) * query_grad, axis=1)
            + jnp.sum(key_weight.astype(f32) * key_grad, axis=1)
            + jnp.sum(value_weight.astype(f32) * value_grad, axis=1)
        )
        first_gain_grad = one / first_gain.astype(f32)
        second_gain_grad = jnp.sum(gain_sums, axis=(0, 1))
        return (
            layer_output[None],
            input_grad[None],
            first_gain_grad,
            query_grad,
            key_grad,
            value_grad,
            output_grad,
            second_gain_grad,
            gate_grad,
            up_grad,
            down_grad,
        )

    return on_plane


def solution(mesh):
    n, m = mesh.shape["seq"], mesh.shape["tp"]
    fits = n == KEY_VALUE_HEADS == 8
    return jax.shard_map(
        fast_layer(n, m) if fits else on_device,
        mesh=mesh,
        in_specs=(
            P("tp", "seq", None),
            P("tp", "seq"),
            P("tp", "seq"),
            P(("seq", "tp")),
            P(("seq", "tp"), None),
            P(("seq", "tp"), None),
            P(("seq", "tp"), None),
            P(("seq", "tp"), None),
            P(("seq", "tp")),
            P("seq", "tp"),
            P("seq", "tp"),
            P("seq", "tp"),
            P("tp", "seq", None),
        ),
        out_specs=(
            P("tp", "seq", None),
            P("tp", "seq", None),
            P(("seq", "tp")),
            P(("seq", "tp"), None),
            P(("seq", "tp"), None),
            P(("seq", "tp"), None),
            P(("seq", "tp"), None),
            P(("seq", "tp")),
            P("seq", "tp"),
            P("seq", "tp"),
            P("seq", "tp"),
        ),
        check_vma=False,
    )
```

```python
import functools
import math

import jax
import jax.numpy as jnp
import numpy as np
from jax import lax
from jax.experimental import pallas as pl
from jax.experimental.pallas import tpu as pltpu
from jax.sharding import PartitionSpec as P

QUERY_HEADS = 16
KEY_VALUE_HEADS = 8
HEAD_SIZE = 96


norm_epsilon = 1e-05
rope_base = 100000.0
mask_fill_value = -1e30


def rope_tables(places):
    half = HEAD_SIZE // 2
    inverse = rope_base ** (-(jnp.arange(half, dtype=jnp.float32) * 2.0 / HEAD_SIZE))
    angles = places.astype(jnp.float32)[:, None] * inverse[None, :]
    return (jnp.cos(angles), jnp.sin(angles))


def apply_rotary(value_rows, cosine_table, sine_table, heads, direction):
    sequence_length = value_rows.shape[0]
    split = value_rows.reshape(sequence_length, heads, 2, HEAD_SIZE // 2)
    first = split[:, :, 0]
    second = split[:, :, 1]
    cosine = cosine_table[:, None, :]
    sine = direction * sine_table[:, None, :]
    turned = jnp.stack([first * cosine - second * sine, second * cosine + first * sine], axis=2)
    return turned.reshape(sequence_length, heads * HEAD_SIZE)


def outer_product(left, right):
    return lax.dot_general(
        left, right, (((0,), (0,)), ((), ())), preferred_element_type=jnp.float32
    )


def times_transpose(left, right):
    return lax.dot_general(
        left, right, (((1,), (1,)), ((), ())), preferred_element_type=jnp.float32
    )


def norm_backward(inputs, scale, gain, upstream):
    inner = gain * upstream
    moment = jnp.mean(inputs * inner, axis=1, keepdims=True)
    return (
        scale * inner - inputs * scale * scale * scale * moment,
        jnp.sum(upstream * inputs * scale, axis=0),
    )


def on_device(
    layer_input,
    doc_ids,
    positions,
    first_gain,
    query_weight,
    key_weight,
    value_weight,
    output_weight,
    second_gain,
    gate_weight,
    up_weight,
    down_weight,
    out_grad,
):
    token_rows = layer_input.shape[1]
    query_groups = QUERY_HEADS // KEY_VALUE_HEADS
    scale_of_scores = 1.0 / math.sqrt(HEAD_SIZE)
    inputs_f = layer_input[0].astype(jnp.float32)
    my_docs = doc_ids[0]
    gain_one, query_full, complete_keys, value_full, output_full, gain_two = (
        lax.all_gather(first_gain, ("seq", "tp"), axis=0, tiled=True),
        lax.all_gather(query_weight, ("seq", "tp"), axis=0, tiled=True),
        lax.all_gather(key_weight, ("seq", "tp"), axis=0, tiled=True),
        lax.all_gather(value_weight, ("seq", "tp"), axis=0, tiled=True),
        lax.all_gather(output_weight, ("seq", "tp"), axis=0, tiled=True),
        lax.all_gather(second_gain, ("seq", "tp"), axis=0, tiled=True),
    )
    gain_one_f = gain_one.astype(jnp.float32)
    gain_two_f = gain_two.astype(jnp.float32)
    scale_one = lax.rsqrt(jnp.mean(inputs_f * inputs_f, axis=1, keepdims=True) + norm_epsilon)
    first_normalized = (inputs_f * scale_one * gain_one_f).astype(jnp.bfloat16)
    cosine_table, sine_table = rope_tables(positions[0])
    rotated_query = apply_rotary(
        jnp.dot(first_normalized, query_full, preferred_element_type=jnp.float32),
        cosine_table,
        sine_table,
        QUERY_HEADS,
        1.0,
    ).astype(jnp.bfloat16)
    key_rot = apply_rotary(
        jnp.dot(first_normalized, complete_keys, preferred_element_type=jnp.float32),
        cosine_table,
        sine_table,
        KEY_VALUE_HEADS,
        1.0,
    ).astype(jnp.bfloat16)
    value_low = jnp.dot(first_normalized, value_full, preferred_element_type=jnp.float32).astype(
        jnp.bfloat16
    )
    gathered_keys, gathered_values, doc_all = (
        lax.all_gather(key_rot, "seq", axis=0, tiled=True),
        lax.all_gather(value_low, "seq", axis=0, tiled=True),
        lax.all_gather(my_docs.astype(jnp.bfloat16), "seq", axis=0, tiled=True),
    )
    sequence_length = gathered_keys.shape[0]
    block_number = math.gcd(512, sequence_length)
    block_count = sequence_length // block_number
    query_index = lax.axis_index("seq") * token_rows + jnp.arange(token_rows, dtype=jnp.int32)
    my_doc_f = my_docs.astype(jnp.float32)
    heads_of_query = rotated_query.reshape(token_rows, KEY_VALUE_HEADS, query_groups, HEAD_SIZE)
    layer_entries = (
        gathered_keys.reshape(block_count, block_number, KEY_VALUE_HEADS, HEAD_SIZE),
        gathered_values.reshape(block_count, block_number, KEY_VALUE_HEADS, HEAD_SIZE),
        doc_all.astype(jnp.float32).reshape(block_count, block_number),
        jnp.arange(block_count, dtype=jnp.int32) * block_number,
    )

    def allowed_of(doc_piece, start):
        key_index = start + jnp.arange(block_number, dtype=jnp.int32)
        return (key_index[None, :] <= query_index[:, None]) & (
            doc_piece[None, :] == my_doc_f[:, None]
        )

    def scores_of(key_piece, allowed):
        raw = (
            jnp.einsum(
                "tgrd,kgd->tgrk", heads_of_query, key_piece, preferred_element_type=jnp.float32
            )
            * scale_of_scores
        )
        return jnp.where(allowed[:, None, None, :], raw, mask_fill_value)

    def total_step(carry, item):
        key_piece, value_piece, doc_piece, start = item
        allowed = allowed_of(doc_piece, start)

        def total_work(state):
            top, total = state
            scores = scores_of(key_piece, allowed)
            new_top = jnp.maximum(top, jnp.max(scores, axis=3))
            weights = jnp.where(
                allowed[:, None, None, :], jnp.exp(scores - new_top[..., None]), 0.0
            )
            return (new_top, total * jnp.exp(top - new_top) + jnp.sum(weights, axis=3))

        return (lax.cond(jnp.any(allowed), total_work, lambda state: state, carry), None)

    start_state = (
        jnp.full((token_rows, KEY_VALUE_HEADS, query_groups), mask_fill_value, jnp.float32),
        jnp.zeros((token_rows, KEY_VALUE_HEADS, query_groups), jnp.float32),
    )
    (top, total), unused_result = lax.scan(total_step, start_state, layer_entries)
    log_total = top + jnp.log(total)

    def probs_of(key_piece, allowed):
        scores = scores_of(key_piece, allowed)
        return jnp.where(allowed[:, None, None, :], jnp.exp(scores - log_total[..., None]), 0.0)

    def output_update(accum, item):
        key_piece, value_piece, doc_piece, start = item
        allowed = allowed_of(doc_piece, start)

        def output_work(state):
            probs = probs_of(key_piece, allowed).astype(jnp.bfloat16)
            return state + jnp.einsum(
                "tgrk,kgd->tgrd", probs, value_piece, preferred_element_type=jnp.float32
            )

        return (lax.cond(jnp.any(allowed), output_work, lambda state: state, accum), None)

    heads_output, unused_result = lax.scan(
        output_update,
        jnp.zeros((token_rows, KEY_VALUE_HEADS, query_groups, HEAD_SIZE), jnp.float32),
        layer_entries,
    )
    attn_low = heads_output.reshape(token_rows, QUERY_HEADS * HEAD_SIZE).astype(jnp.bfloat16)
    resid = inputs_f + jnp.dot(attn_low, output_full, preferred_element_type=jnp.float32)
    scale_two = lax.rsqrt(jnp.mean(resid * resid, axis=1, keepdims=True) + norm_epsilon)
    normed_two = (resid * scale_two * gain_two_f).astype(jnp.bfloat16)
    rows_all = lax.all_gather(normed_two, "tp", axis=0, tiled=True)
    gate_cols, up_cols, down_cols = (
        lax.all_gather(gate_weight, "seq", axis=0, tiled=True),
        lax.all_gather(up_weight, "seq", axis=0, tiled=True),
        lax.all_gather(down_weight, "seq", axis=0, tiled=True),
    )
    gate_pre = jnp.dot(rows_all, gate_cols, preferred_element_type=jnp.float32)
    up_pre = jnp.dot(rows_all, up_cols, preferred_element_type=jnp.float32)
    gate_sig = jax.nn.sigmoid(gate_pre)
    gate_act = gate_pre * gate_sig
    hidden = (gate_act * up_pre).astype(jnp.bfloat16)
    mixed = lax.psum_scatter(
        times_transpose(hidden, down_cols).astype(jnp.bfloat16),
        "tp",
        scatter_dimension=0,
        tiled=True,
    ).astype(jnp.float32)
    layer_output = (resid + mixed).astype(jnp.bfloat16)[None]
    grad_low = out_grad[0]
    grad_f = grad_low.astype(jnp.float32)
    grad_all = lax.all_gather(grad_low, "tp", axis=0, tiled=True)
    dhidden = jnp.dot(grad_all, down_cols, preferred_element_type=jnp.float32)
    dgate = (dhidden * up_pre * gate_sig * (1.0 + gate_pre * (1.0 - gate_sig))).astype(jnp.bfloat16)
    dup = (dhidden * gate_act).astype(jnp.bfloat16)
    gate_term = outer_product(rows_all, dgate)
    up_term = outer_product(rows_all, dup)
    down_term_grad = outer_product(grad_all, hidden)
    dnorm_two = lax.psum_scatter(
        (times_transpose(dgate, gate_cols) + times_transpose(dup, up_cols)).astype(jnp.bfloat16),
        "tp",
        scatter_dimension=0,
        tiled=True,
    ).astype(jnp.float32)
    gate_grad, up_grad, down_grad = (
        lax.psum_scatter(
            gate_term.astype(jnp.bfloat16), "seq", scatter_dimension=0, tiled=True
        ).astype(jnp.float32),
        lax.psum_scatter(
            up_term.astype(jnp.bfloat16), "seq", scatter_dimension=0, tiled=True
        ).astype(jnp.float32),
        lax.psum_scatter(
            down_term_grad.astype(jnp.bfloat16), "seq", scatter_dimension=0, tiled=True
        ).astype(jnp.float32),
    )
    resid_part, gain_two_term = norm_backward(resid, scale_two, gain_two_f, dnorm_two)
    dresid = grad_f + resid_part
    dbranch = dresid.astype(jnp.bfloat16)
    output_term = outer_product(attn_low, dbranch)
    heads_gradient = times_transpose(dbranch, output_full).astype(jnp.bfloat16)
    grouped_heads_gradient = heads_gradient.reshape(
        token_rows, KEY_VALUE_HEADS, query_groups, HEAD_SIZE
    )
    delta = jnp.sum(grouped_heads_gradient.astype(jnp.float32) * heads_output, axis=3)

    def gradient_update(dquery, item):
        key_piece, value_piece, doc_piece, start = item
        allowed = allowed_of(doc_piece, start)

        def gradient_work(state):
            probs = probs_of(key_piece, allowed)
            value_piece_grad = jnp.einsum(
                "tgrk,tgrd->kgd",
                probs.astype(jnp.bfloat16),
                grouped_heads_gradient,
                preferred_element_type=jnp.float32,
            )
            prob_grad = jnp.einsum(
                "tgrd,kgd->tgrk",
                grouped_heads_gradient,
                value_piece,
                preferred_element_type=jnp.float32,
            )
            score_grad = (probs * (prob_grad - delta[..., None])).astype(jnp.bfloat16)
            key_piece_grad = jnp.einsum(
                "tgrk,tgrd->kgd", score_grad, heads_of_query, preferred_element_type=jnp.float32
            )
            updated = state + jnp.einsum(
                "tgrk,kgd->tgrd", score_grad, key_piece, preferred_element_type=jnp.float32
            )
            return (updated, (key_piece_grad, value_piece_grad))

        def skip(state):
            blank_tensor = jnp.zeros((block_number, KEY_VALUE_HEADS, HEAD_SIZE), jnp.float32)
            return (state, (blank_tensor, blank_tensor))

        return lax.cond(jnp.any(allowed), gradient_work, skip, dquery)

    dquery, (key_contributions, value_contributions) = lax.scan(
        gradient_update,
        jnp.zeros((token_rows, KEY_VALUE_HEADS, query_groups, HEAD_SIZE), jnp.float32),
        layer_entries,
    )
    gathered_key_contributions = (
        key_contributions.reshape(sequence_length, KEY_VALUE_HEADS * HEAD_SIZE) * scale_of_scores
    )
    gathered_value_contributions = value_contributions.reshape(
        sequence_length, KEY_VALUE_HEADS * HEAD_SIZE
    )
    local_keys, value_mine = (
        lax.psum_scatter(
            gathered_key_contributions.astype(jnp.bfloat16), "seq", scatter_dimension=0, tiled=True
        ).astype(jnp.float32),
        lax.psum_scatter(
            gathered_value_contributions.astype(jnp.bfloat16),
            "seq",
            scatter_dimension=0,
            tiled=True,
        ).astype(jnp.float32),
    )
    dq_pre = apply_rotary(
        dquery.reshape(token_rows, QUERY_HEADS * HEAD_SIZE) * scale_of_scores,
        cosine_table,
        sine_table,
        QUERY_HEADS,
        -1.0,
    ).astype(jnp.bfloat16)
    key_gradient_unrotated = apply_rotary(
        local_keys, cosine_table, sine_table, KEY_VALUE_HEADS, -1.0
    ).astype(jnp.bfloat16)
    dv_pre = value_mine.astype(jnp.bfloat16)
    dnorm_one = (
        times_transpose(dq_pre, query_full)
        + times_transpose(key_gradient_unrotated, complete_keys)
        + times_transpose(dv_pre, value_full)
    )
    input_part, gain_one_term = norm_backward(inputs_f, scale_one, gain_one_f, dnorm_one)
    input_grad = (dresid + input_part)[None]
    query_term = outer_product(first_normalized, dq_pre)
    key_term = outer_product(first_normalized, key_gradient_unrotated)
    value_term = outer_product(first_normalized, dv_pre)
    first_gain_grad, query_grad, key_grad, value_grad, output_grad, second_gain_grad = (
        lax.psum_scatter(gain_one_term, ("seq", "tp"), scatter_dimension=0, tiled=True),
        lax.psum_scatter(query_term, ("seq", "tp"), scatter_dimension=0, tiled=True),
        lax.psum_scatter(key_term, ("seq", "tp"), scatter_dimension=0, tiled=True),
        lax.psum_scatter(value_term, ("seq", "tp"), scatter_dimension=0, tiled=True),
        lax.psum_scatter(output_term, ("seq", "tp"), scatter_dimension=0, tiled=True),
        lax.psum_scatter(gain_two_term, ("seq", "tp"), scatter_dimension=0, tiled=True),
    )
    return (
        layer_output,
        input_grad,
        first_gain_grad,
        query_grad,
        key_grad,
        value_grad,
        output_grad,
        second_gain_grad,
        gate_grad,
        up_grad,
        down_grad,
    )


MESH = pl.DeviceIdType.MESH
ANY = pl.ANY
HALF = HEAD_SIZE // 2
LANES = 128
SLOT = LANES // 2
f32 = jnp.float32
bf16 = jnp.bfloat16
VMEM_LIMIT = 62 << 20
COST = pl.CostEstimate(flops=1_000_000, transcendentals=0, bytes_accessed=100_000)


class Plane:
    def __init__(self, n, m):
        self.n, self.m, self.chips = n, m, n // 2
        self.s = lax.axis_index("seq")
        self.t = lax.axis_index("tp")
        self.q = self.s // 2
        self.c = lax.rem(self.s, 2)

        across = self.q + 1 - 2 * lax.rem(self.q, 2)
        along = lax.rem(self.q + 2, 4)
        self.to = across * (1 - self.c) + along * self.c
        self.fro = across * self.c + along * (1 - self.c)
        self.far = 3 - self.q
        self.order = (self.q, self.to, self.fro, self.far)

    def device(self, s):
        return (s, self.t)

    def same(self, chip):
        return (2 * chip + self.c, self.t)

    def number(self, k, other):
        c, q = self.c, self.q
        low, high = lax.rem(k, 2), k // 2
        dx = low * (1 - c) + high * c
        dy = high * (1 - c) + low * c
        x, y = lax.rem(q, 2), q // 2
        chip = 2 * (y + dy - 2 * y * dy) + x + dx - 2 * x * dx
        return 2 * chip + c + other * (1 - 2 * c)

    def sibling(self):
        return (2 * self.q + 1 - self.c, self.t)

    def ahead(self, k):
        return lax.rem(self.q + k, self.chips)

    def behind(self, k):
        return lax.rem(self.q + self.chips - k, self.chips)

    def seq_ahead(self, k):
        return lax.rem(self.s + k, self.n)

    def seq_behind(self, k):
        return lax.rem(self.s + self.n - k, self.n)

    def tp_ahead(self, k):
        return (self.s, lax.rem(self.t + k, self.m))

    def tp_behind(self, k):
        return lax.rem(self.t + self.m - k, self.m)


def greet(plane, with_tp):
    barrier = pltpu.get_barrier_semaphore()
    for k in range(1, plane.n):
        pl.semaphore_signal(
            barrier, inc=1, device_id=plane.device(plane.seq_ahead(k)), device_id_type=MESH
        )
    if with_tp:
        for k in range(1, plane.m):
            pl.semaphore_signal(barrier, inc=1, device_id=plane.tp_ahead(k), device_id_type=MESH)


def meet(plane, with_tp):
    count = plane.n - 1 + (plane.m - 1 if with_tp else 0)
    pl.semaphore_wait(pltpu.get_barrier_semaphore(), count)


def remote(src, dst, send, recv, device):
    return pltpu.make_async_remote_copy(
        src_ref=src,
        dst_ref=dst,
        send_sem=send,
        recv_sem=recv,
        device_id=device,
        device_id_type=MESH,
    )


class Gather:
    COPIES = 7

    def __init__(self, plane, src, dst_of, send, recv, local):
        to, fro, far, c = plane.to, plane.fro, plane.far, plane.c
        here = dst_of(plane.s)
        self.own = pltpu.make_async_copy(src, here, local)

        def block(chip):
            return dst_of(2 * chip + c)

        def copy(i, a, b, device):
            return remote(a, b, send.at[i], recv.at[i], device)

        sibling = plane.sibling()
        self.swap = copy(0, src, here, sibling)
        self.ahead = copy(1, src, here, plane.same(to))
        self.back = copy(2, src, here, plane.same(fro))
        self.relay = copy(3, block(fro), block(fro), plane.same(to))
        self.share = [
            copy(4, block(to), block(to), sibling),
            copy(5, block(fro), block(fro), sibling),
            copy(6, block(far), block(far), sibling),
        ]

    def start(self):
        self.back.start()
        self.ahead.start()

    def start_here(self):
        self.swap.start()
        self.own.start()

    def relay_near(self):
        self.back.wait_recv()
        self.relay.start()
        self.share[1].start()
        self.ahead.wait_recv()
        self.share[0].start()

    def relay_far(self):
        self.relay.wait_recv()
        self.share[2].start()

    def wait_sends(self):
        for copy in [self.swap, self.ahead, self.back, self.relay] + self.share:
            copy.wait_send()


class Gathers:
    def __init__(self, plane, src, dst_of, sems, local, pieces):
        rows = src.shape[0] // pieces
        self.parts = []
        for i in range(pieces):
            at = pl.ds(i * rows, rows)
            self.parts.append(
                Gather(
                    plane,
                    src.at[at],
                    lambda d, at=at: dst_of(d).at[at],
                    sems.at[i, 0],
                    sems.at[i, 1],
                    local.at[i],
                )
            )

    def start(self):
        for part in self.parts:
            part.start()
        for part in self.parts:
            part.start_here()

    def relay_near(self):
        for part in self.parts:
            part.relay_near()

    def relay_far(self):
        for part in self.parts:
            part.relay_far()

    def wait_own(self):
        for part in self.parts:
            part.own.wait()

    def wait_swap(self):
        for part in self.parts:
            part.swap.wait_recv()

    def wait_share(self, i):
        for part in self.parts:
            part.share[i].wait_recv()

    def wait_sends(self):
        for part in self.parts:
            part.wait_sends()

    def finish(self):
        self.wait_own()
        self.wait_swap()
        for i in range(3):
            self.wait_share(i)
        self.wait_sends()

    @staticmethod
    def scratch(pieces):
        return [
            pltpu.SemaphoreType.DMA((pieces, 2, Gather.COPIES)),
            pltpu.SemaphoreType.DMA((pieces,)),
        ]


class Chain:
    def __init__(self, plane, mine, slot_of, sems):
        self.plane, self.mine, self.slot_of, self.sems = plane, mine, slot_of, sems

    def copy(self, way, hop, to):
        plane, row = self.plane, 0 if way > 0 else 2
        slot = self.slot_of(plane.t - way * hop)
        return remote(
            self.mine if hop == 0 else slot,
            slot,
            self.sems.at[row, hop],
            self.sems.at[row + 1, hop],
            (plane.s, to),
        )

    def inside(self, way, hop):
        t, m = self.plane.t, self.plane.m
        holds = t >= hop if way > 0 else t < m - hop
        passes = t < m - 1 if way > 0 else t > 0
        return holds, passes

    def start(self):
        self.pass_on(0)

    def pass_on(self, hop):
        for way in (1, -1):
            holds, passes = self.inside(way, hop)

            @pl.when(holds & passes)
            def _(way=way):
                self.copy(way, hop, self.plane.t + way).start()

    def step(self, hop):
        plane = self.plane
        for way in (1, -1):
            holds, _ = self.inside(way, hop)

            @pl.when(holds)
            def _(way=way):
                row = 0 if way > 0 else 2
                slot = self.slot_of(plane.t - way * hop)
                remote(
                    slot,
                    slot,
                    self.sems.at[row, hop - 1],
                    self.sems.at[row + 1, hop - 1],
                    (plane.s, plane.t - way),
                ).wait_recv()

        if hop < plane.m - 1:
            self.pass_on(hop)

    def wait_sends(self):
        for hop in range(self.plane.m - 1):
            for way in (1, -1):
                holds, passes = self.inside(way, hop)

                @pl.when(holds & passes)
                def _(way=way, hop=hop):
                    self.copy(way, hop, self.plane.t + way).wait_send()


class Scatter:
    def __init__(self, plane, parts, total, add, own, got, sems, loc):
        t = plane.t
        self.plane, self.total = plane, total
        self.add, self.own, self.got, self.loc = add, own, got, loc
        self.inner = (t == 1) | (t == 2)
        self.outer = (t == 0) | (t == 3)
        up = t // 2
        self.near = t + 1 - 2 * lax.rem(t, 2)
        self.far_outer = 3 - 3 * up
        self.far_inner = 2 - up
        self.parts, self.sems = parts, sems

    def copy(self, i, j, src, dst, to):
        return remote(
            src, dst, self.sems.at[0, i, j], self.sems.at[1, i, j], (self.plane.s, to)
        )

    def first(self, i, j):
        chunk = (self.far_outer, self.far_inner, self.near)[i]
        dst = self.got.at[0, j] if i == 2 else self.add.at[i, j]
        return self.copy(i, j, self.parts.at[chunk, j], dst, self.near)

    def back(self, j):
        return self.copy(2, j, self.parts.at[self.near, j], self.got.at[0, j], self.near)

    def sent(self, i, j):
        to = self.far_inner if i else self.far_outer
        return remote(
            self.add.at[i, j],
            self.got.at[1, j],
            self.sems.at[0, 3 + i, j],
            self.sems.at[1, 3, j],
            (self.plane.s, to),
        )

    def load(self, i, j):
        chunk = (self.far_outer, self.far_inner, self.plane.t)[i]
        dst = self.total.at[j] if i == 2 else self.own.at[i, j]
        return pltpu.make_async_copy(self.parts.at[chunk, j], dst, self.loc.at[i, j])

    def start(self):
        for j in range(2):
            self.load(2, j).start()

        @pl.when(self.outer)
        def _():
            for i in range(3):
                for j in range(2):
                    self.first(i, j).start()

        @pl.when(self.inner)
        def _():
            for j in range(2):
                self.back(j).start()
            for i in range(2):
                for j in range(2):
                    self.load(i, j).start()

    def relay(self, i, j):
        @pl.when(self.inner)
        def _():
            self.first(i, j).wait_recv()
            self.load(i, j).wait()
            add, own = self.add, self.own

            def both(at):
                value = add[i, j, at, :].astype(f32) + own[i, j, at, :].astype(f32)
                add[i, j, at, :] = value.astype(bf16)

            in_tiles(add.shape[2], both, 256)
            self.sent(i, j).start()

    def finish(self):
        total, got = self.total, self.got
        for j in range(2):
            self.load(2, j).wait()
            self.back(j).wait_recv()
            self.sent(0, j).wait_recv()

            def sums(at, j=j):
                value = total[j, at, :].astype(f32) + got[0, j, at, :].astype(f32)
                total[j, at, :] = (value + got[1, j, at, :].astype(f32)).astype(bf16)

            in_tiles(total.shape[1], sums, 256)

        @pl.when(self.outer)
        def _():
            for i in range(3):
                for j in range(2):
                    self.first(i, j).wait_send()

        @pl.when(self.inner)
        def _():
            for j in range(2):
                self.back(j).wait_send()
                for i in range(2):
                    self.sent(i, j).wait_send()

    @staticmethod
    def scratch(shape):
        return [
            pltpu.VMEM((2,) + shape, bf16),
            pltpu.VMEM((2,) + shape, bf16),
            pltpu.VMEM((2,) + shape, bf16),
            pltpu.SemaphoreType.DMA((2, 5, 2)),
            pltpu.SemaphoreType.DMA((3, 2)),
        ]


def fan(plane, src_of, dst_of, send, recv):
    copies = []
    for k in range(1, plane.m):
        device = plane.tp_ahead(k)
        copies.append(
            remote(src_of(device[1]), dst_of(plane.t), send.at[k - 1], recv.at[k - 1], device)
        )
    return copies


def exchange(plane, src_of, dst_of, send, recv, local):
    own = pltpu.make_async_copy(src_of(plane.s), dst_of(plane.s), local)
    copies = []
    for k in range(1, plane.n):
        peer = plane.seq_ahead(k)
        copies.append(
            remote(
                src_of(peer), dst_of(plane.s), send.at[k - 1], recv.at[k - 1], plane.device(peer)
            )
        )
    return [own] + copies


TILE = 16


def in_tiles(rows, body, tile=TILE):
    def one(i, carry):
        body(pl.ds(pl.multiple_of(i * tile, tile), tile))
        return carry

    lax.fori_loop(0, rows // tile, one, 0)


class Reduce:
    SLOTS = (4, 4, 3)

    THEIRS = (0, 2, 1, 3)

    def __init__(self, plane, part_of, pair, near, far, sems, loc, stage=None):
        c = plane.c
        self.pair, self.near, self.far = pair, near, far
        self.rows = pair.shape[1]
        self.swaps, self.loads = {}, {}
        for k in range(4):
            mine = self.THEIRS[k]
            chip = plane.order[mine]
            source = part_of(2 * chip + 1 - c) if stage is None else stage.at[mine]
            self.swaps[k] = remote(
                source, near.at[k], sems.at[0, k], sems.at[1, k], plane.sibling()
            )
            if stage is None:
                self.loads[k] = pltpu.make_async_copy(
                    part_of(2 * plane.order[k] + c), pair.at[k], loc.at[k]
                )

        def out(i, k, chip):
            return remote(
                pair.at[k], far.at[i], sems.at[2, i], sems.at[3, i], plane.same(chip)
            )

        self.out = [out(0, 3, plane.to), out(1, 1, plane.to), out(2, 2, plane.fro)]

    def start(self, *which):
        for k in which:
            self.swaps[k].start()
            self.loads[k].start()

    def landed(self, k):
        self.swaps[k].wait()
        if self.loads:
            self.loads[k].wait()

    def join(self, k):
        pair, near = self.pair, self.near
        self.landed(k)

        def add(at):
            both = pair[k, at, :].astype(f32) + near[k, at, :].astype(f32)
            pair[k, at, :] = both.astype(bf16)

        in_tiles(self.rows, add)

    def send_to(self):
        self.join(3)
        self.out[0].start()
        self.join(1)
        self.out[1].start()

    def ready(self):
        self.landed(2)

    def send_fro(self):
        pair, near, far = self.pair, self.near, self.far
        self.out[0].wait_recv()

        def add(at):
            both = pair[2, at, :].astype(f32) + near[2, at, :].astype(f32)
            pair[2, at, :] = (both + far[0, at, :].astype(f32)).astype(bf16)

        in_tiles(self.rows, add)
        self.out[2].start()

    def first(self, total, more=None):
        pair, near = self.pair, self.near
        self.landed(0)

        def add(at):
            value = pair[0, at, :].astype(f32) + near[0, at, :].astype(f32)
            total[at, :] = value if more is None else value + more[at, :].astype(f32)

        in_tiles(self.rows, add)

    def finish(self, total, out=None):
        far = self.far
        out = total if out is None else out
        self.out[0].wait_send()
        self.out[1].wait()
        self.out[2].wait()

        def add(at):
            value = total[at, :] + far[1, at, :].astype(f32) + far[2, at, :].astype(f32)
            out[at, :] = value.astype(out.dtype)

        in_tiles(self.rows, add)

    @staticmethod
    def scratch(rows, width):
        return [pltpu.VMEM((slots, rows, width), bf16) for slots in Reduce.SLOTS] + [
            pltpu.SemaphoreType.DMA((4, 4)),
            pltpu.SemaphoreType.DMA((4,)),
        ]


def last_body(
    n, m, dqkv_in, w_in, x_in, dresid_in, gain, norm_t, ffn, downs, wo, vec,
    input_grad, ffn_out, qkv_out, wo_out, vec_out,
    dqkv, w, x, dresid, down_here, down_sum, narrow, pair, near, far, sr, lr, total, stage, norms, mine, got, summed, sems, st, loc,
):
    plane = Plane(n, m)
    greet(plane, True)
    loads = [
        pltpu.make_async_copy(a, b, loc.at[5 + i])
        for i, (a, b) in enumerate(
            ((dqkv_in, dqkv), (w_in, w), (downs, down_here), (x_in, x), (dresid_in, dresid))
        )
    ]
    load = pltpu.make_async_copy(norm_t, norms, loc.at[0])
    for copy in loads + [load]:
        copy.start()
    narrow[...] = lanes_of_columns(narrow.shape, 1)
    meet(plane, True)
    rows, width = ffn_out.shape[1], ffn.shape[2]
    across = fan(plane, lambda t: wo.at[t], lambda t: wo_out.at[t], st.at[1, 0], st.at[1, 1])
    across += fan(plane, lambda t: vec.at[t], lambda t: vec_out.at[t], st.at[2, 0], st.at[2, 1])
    across += [
        pltpu.make_async_copy(wo.at[plane.t], wo_out.at[plane.t], loc.at[1]),
        pltpu.make_async_copy(vec.at[plane.t], vec_out.at[plane.t], loc.at[2]),
    ]
    for copy in across:
        copy.start()
    a = exchange(
        plane,
        lambda i: ffn.at[:, pl.ds(pl.multiple_of(i * rows, rows), rows), :],
        lambda i: ffn_out.at[
            pl.ds(0, 2), :, pl.ds(pl.multiple_of(i * width, width), width)
        ],
        sems.at[0, 0],
        sems.at[0, 1],
        loc.at[3],
    )
    a_down = exchange(
        plane,
        lambda i: down_sum.at[pl.ds(pl.multiple_of(i * rows, rows), rows), :],
        lambda i: ffn_out.at[2, :, pl.ds(pl.multiple_of(i * width, width), width)],
        sems.at[2, 0],
        sems.at[2, 1],
        loc.at[10],
    )
    for copy in a:
        copy.start()
    reduce = Reduce(plane, None, pair, near, far, sr, lr, stage)
    tokens = pair.shape[1]
    for copy in loads[:2]:
        copy.wait()

    def blocks(it, carry):
        k = 3 - it // 2
        other = 1 - lax.rem(it, 2)
        b = plane.number(k, other)
        here = pl.ds(pl.multiple_of(b * tokens, tokens), tokens)
        part = lax.dot_general(dqkv[here, :], w[...], NT, preferred_element_type=f32).astype(bf16)

        @pl.when(other == 0)
        def _():
            pair[k] = part

        @pl.when(other == 1)
        def _():
            stage[k] = part

        for kk in range(4):

            @pl.when(it == 2 * (3 - kk))
            def _(kk=kk):
                reduce.swaps[Reduce.THEIRS[kk]].start()

        return carry

    lax.fori_loop(0, n, blocks, 0)
    reduce.send_to()
    loads[2].wait()

    def add_down(at):
        value = down_here[0, at, :].astype(f32)
        for t in range(1, m):
            value = value + down_here[t, at, :].astype(f32)
        down_sum[at, :] = value.astype(bf16)

    in_tiles(down_sum.shape[0], add_down)
    for copy in a_down:
        copy.start()
    load.wait()
    strip = summed.shape[1]

    def weight_grads(s, carry):
        at = pl.ds(pl.multiple_of(s * m * strip, m * strip), m * strip)
        value = jnp.dot(norms[at, :], dqkv[...], preferred_element_type=f32).astype(bf16)
        value = jnp.dot(value, narrow[...], preferred_element_type=f32).astype(bf16)
        for t in range(m):
            mine[s, t] = value[t * strip : (t + 1) * strip]
        return carry

    lax.fori_loop(0, n, weight_grads, 0)
    over = fan(plane, lambda t: mine.at[:, t], lambda t: got.at[t], st.at[0, 0], st.at[0, 1])
    for copy in over:
        copy.start()
    reduce.ready()
    reduce.first(total)
    reduce.send_fro()
    for copy in over:
        copy.wait()

    def add(s, carry):
        value = mine[s, plane.t].astype(f32)
        for k in range(1, m):
            value = value + got[plane.tp_behind(k), s].astype(f32)
        summed[s] = value.astype(bf16)
        return carry

    lax.fori_loop(0, n, add, 0)
    b = exchange(
        plane,
        lambda i: summed.at[i],
        lambda i: qkv_out.at[i],
        sems.at[1, 0],
        sems.at[1, 1],
        loc.at[4],
    )
    for copy in b:
        copy.start()
    for copy in loads[3:]:
        copy.wait()
    reduce.finish(total)

    def into_input(at):
        value = x[at, :].astype(f32)
        scale = lax.rsqrt(jnp.mean(value * value, axis=1, keepdims=True) + norm_epsilon)
        inner = gain[...] * total[at, :]
        moment = jnp.mean(value * inner, axis=1, keepdims=True)
        input_grad[at, :] = (
            dresid[at, :] + scale * inner - value * scale * (scale * scale * moment)
        )

    in_tiles(tokens, into_input)
    for copy in a + a_down + b + across:
        copy.wait()


def last(n, m, dqkv, w, x, dresid, gain, norm_t, ffn, downs, wo, vec, ident):
    width, length = norm_t.shape
    tokens = length // n
    cols = w.shape[1] // SLOT * HALF
    strip = width // (n * m)
    vmem = pl.BlockSpec(memory_space=pltpu.VMEM)
    hbm = pl.BlockSpec(memory_space=ANY)
    return pl.pallas_call(
        functools.partial(last_body, n, m),
        out_shape=(
            jax.ShapeDtypeStruct((tokens, width), f32),
            jax.ShapeDtypeStruct((3, ffn.shape[1] // n, ffn.shape[2] * n), ffn.dtype),
            jax.ShapeDtypeStruct((n, strip, cols), bf16),
            jax.ShapeDtypeStruct(wo.shape, wo.dtype),
            jax.ShapeDtypeStruct(vec.shape, vec.dtype),
        ),
        in_specs=[hbm] * 4 + [vmem] + [hbm] * 5,
        out_specs=[vmem] + [hbm] * 4,
        scratch_shapes=[
            pltpu.VMEM(dqkv.shape, bf16),
            pltpu.VMEM(w.shape, bf16),
            pltpu.VMEM(x.shape, bf16),
            pltpu.VMEM(dresid.shape, f32),
            pltpu.VMEM(downs.shape, bf16),
            pltpu.VMEM(downs.shape[1:], bf16),
            pltpu.VMEM((w.shape[1], cols), bf16),
        ]
        + Reduce.scratch(tokens, width)
        + [
            pltpu.VMEM((tokens, width), f32),
            pltpu.VMEM((4, tokens, width), bf16),
            pltpu.VMEM((width, length), bf16),
            pltpu.VMEM((n, m, strip, cols), bf16),
            pltpu.VMEM((m, n, strip, cols), bf16),
            pltpu.VMEM((n, strip, cols), bf16),
            pltpu.SemaphoreType.DMA((3, 2, n - 1)),
            pltpu.SemaphoreType.DMA((3, 2, m - 1)),
            pltpu.SemaphoreType.DMA((11,)),
        ],
        compiler_params=pltpu.CompilerParams(
            collective_id=ident, has_side_effects=True, vmem_limit_bytes=VMEM_LIMIT
        ),
        cost_estimate=COST,
        name="last",
    )(dqkv, w, x, dresid, gain, norm_t, ffn, downs, wo, vec)


def column(row):
    return jnp.broadcast_to(row, (8, row.shape[1])).T[:, :1]


def lanes_of_columns(shape, of):
    column = lax.broadcasted_iota(jnp.int32, shape, of).astype(f32)
    lane = lax.broadcasted_iota(jnp.int32, shape, 1 - of).astype(f32)
    half = jnp.floor((column + 0.5) * (1.0 / HALF))
    return jnp.where(lane == column + half * (SLOT - HALF), 1.0, 0.0).astype(bf16)


def gain_row(tiles, which, strip):
    stacked = tiles.reshape(-1, LANES).astype(bf16)
    count = stacked.shape[0] // 8
    shape = (LANES, count * strip)
    lane = lax.broadcasted_iota(jnp.int32, shape, 1).astype(f32)
    owner = jnp.floor((lane + 0.5) * (1.0 / strip))
    inside = lane - owner * strip
    pick = lax.broadcasted_iota(jnp.int32, shape, 0).astype(f32) == inside
    spread_out = jnp.dot(
        stacked, jnp.where(pick, 1.0, 0.0).astype(bf16), preferred_element_type=f32
    )
    shape = spread_out.shape
    lane = lax.broadcasted_iota(jnp.int32, shape, 1).astype(f32)
    owner = jnp.floor((lane + 0.5) * (1.0 / strip))
    row = lax.broadcasted_iota(jnp.int32, shape, 0).astype(f32)
    mine = row == owner * 8.0 + which
    return jnp.sum(jnp.where(mine, spread_out, 0.0), axis=0, keepdims=True)


def entry_body(
    n, m, heads, strip, x, doc_ids, positions, wq, wk, wv, one, two, wg, wu, wd, wo, inverse,
    norm_t, q, k, v, cosine, sine, w, gain_one, gain_two, docs, ffn, down, wo_z,
    blocks, norms, turned, places_all, w_all, gains_all, q_here, k_here, v_here, cos_here, sin_here,
    places, wqkv, gains, widen, sx, lx, rem, sz, sn, loc,
):
    plane = Plane(n, m)
    greet(plane, True)
    tokens = x.shape[0]
    start = 0
    for weight in (wq, wk, wv):
        each = weight.shape[1] // n
        for i in range(n):
            wqkv[i, :, start : start + each] = weight[:, i * each : (i + 1) * each]
        start += each
    gains[...] = jnp.zeros_like(gains)
    gains[0:1, :strip] = one[...].astype(f32)
    gains[1:2, :strip] = two[...].astype(f32)
    places[0:1, :] = doc_ids[...]
    places[1:2, :] = positions[...]
    meet(plane, True)
    gather = Gathers(plane, x, lambda i: blocks.at[i], sx, lx, 2)
    first = []
    for i, (src, dst) in enumerate(((gains, gains_all), (wqkv, w_all))):
        first += exchange(
            plane,
            lambda s, src=src, i=i: src.at[s] if i else src,
            lambda s, dst=dst: dst.at[s, plane.t],
            rem.at[i, 0],
            rem.at[i, 1],
            loc.at[1 + i],
        )
    few = exchange(
        plane, lambda i: places, lambda i: places_all.at[i], rem.at[2, 0], rem.at[2, 1], loc.at[3]
    )
    for copy in first + few:
        copy.start()
    gather.start()
    across = []
    for i, ref in enumerate((gains_all, w_all)):

        def slot(t, ref=ref):
            return ref.at[:, plane.t]

        across.append(fan(plane, slot, slot, sz.at[i, 0], sz.at[i, 1]))
    across.append(fan(plane, lambda t: wo, lambda t: wo_z.at[t], sz.at[2, 0], sz.at[2, 1]))
    own_wo = pltpu.make_async_copy(wo, wo_z.at[plane.t], loc.at[4])
    own_wo.start()
    for copy in first:
        copy.wait()
    for copy in across[0] + across[1]:
        copy.start()
    widen[...] = lanes_of_columns(widen.shape, 0)
    moves = []
    width, rows = wg.shape[1] // n, wg.shape[0]
    for j, weight in enumerate((wg, wu, wd)):
        moves += exchange(
            plane,
            lambda i, weight=weight: weight.at[:, pl.ds(pl.multiple_of(i * width, width), width)],
            lambda i, dst=ffn.at[j] if j < 2 else down: dst.at[
                pl.ds(pl.multiple_of(i * rows, rows), rows), :
            ],
            rem.at[3 + j, 0],
            rem.at[3 + j, 1],
            loc.at[5 + j],
        )
    for copy in few + across[0]:
        copy.wait()
    tiles = gains_all[...]
    gain_one[...] = gain_row(tiles, 0, strip)
    gain_two[...] = gain_row(tiles, 1, strip)
    gather.wait_own()

    def number(it):
        return plane.number(it // 2, lax.rem(it, 2))

    def store(it, at):
        span = pl.ds(pl.multiple_of(number(it) * tokens, tokens), tokens)
        return pltpu.make_async_copy(turned.at[at], norm_t.at[:, span], sn.at[at])

    def normalize(it, carry):
        b = number(it)
        at = lax.rem(it, 2)

        @pl.when(it == 1)
        def _():
            gather.wait_swap()

        @pl.when(it == 2)
        def _():
            gather.relay_near()

        @pl.when(it == 3)
        def _():
            gather.wait_share(1)

        @pl.when(it == 5)
        def _():
            gather.wait_share(0)

        @pl.when(it == 6)
        def _():
            gather.relay_far()
            for copy in moves + across[2]:
                copy.start()

        @pl.when(it == 7)
        def _():
            gather.wait_share(2)

        @pl.when(it >= 2)
        def _():
            store(it - 2, at).wait()

        value = blocks[b].astype(f32)
        scale = lax.rsqrt(jnp.mean(value * value, axis=1, keepdims=True) + norm_epsilon)
        low = (value * scale * gain_one[...]).astype(bf16)
        norms[b] = low
        turned[at] = low.T
        store(it, at).start()
        here = pl.ds(pl.multiple_of(b * tokens, tokens), tokens)
        docs[:, here] = places_all[b, 0:1, :]
        angles = column(places_all[b, 1:2, :].astype(f32)) * inverse[...]
        lanes = lax.broadcasted_iota(jnp.int32, angles.shape, 1)
        sin = jnp.sin(angles)
        cos_here[here, :] = jnp.cos(angles)
        sin_here[here, :] = jnp.where(lanes < SLOT, -sin, sin)
        return carry

    lax.fori_loop(0, n, normalize, 0)
    outs = [
        pltpu.make_async_copy(cos_here, cosine, loc.at[8]),
        pltpu.make_async_copy(sin_here, sine, loc.at[9]),
        pltpu.make_async_copy(q_here, q, loc.at[10]),
        pltpu.make_async_copy(k_here, k, loc.at[11]),
        pltpu.make_async_copy(v_here, v, loc.at[12]),
    ]
    for copy in outs[:2]:
        copy.start()
    for copy in across[1]:
        copy.wait()

    def widened(s, carry):
        at = pl.ds(pl.multiple_of(s * m * strip, m * strip), m * strip)
        narrow = w_all[s].reshape(m * strip, w_all.shape[3])
        w[at, :] = jnp.dot(narrow, widen[...], preferred_element_type=f32).astype(bf16)
        return carry

    lax.fori_loop(0, n, widened, 0)

    def project(b, carry):
        here = pl.ds(pl.multiple_of(b * tokens, tokens), tokens)
        out = jnp.dot(norms[b], w[...], preferred_element_type=f32)
        cos, sin = cos_here[here, :], sin_here[here, :]
        for h in range(heads + 1):
            part = out[:, h * LANES : (h + 1) * LANES]
            rotated = (part * cos + pltpu.roll(part, SLOT, 1) * sin).astype(bf16)
            if h < heads:
                q_here[h, here, :] = rotated
            else:
                k_here[here, :] = rotated
        v_here[here, :] = out[:, (heads + 1) * LANES :].astype(bf16)
        return carry

    lax.fori_loop(0, n, project, 0)
    for copy in outs[2:]:
        copy.start()
    gather.wait_sends()
    store(n - 2, 0).wait()
    store(n - 1, 1).wait()
    own_wo.wait()
    for copy in across[2] + moves + outs:
        copy.wait()


def entry(n, m, heads, x, docs, positions, wq, wk, wv, one, two, wg, wu, wd, wo, inverse, ident):
    tokens, width = x.shape
    length = n * tokens
    strip = wq.shape[0]
    each = (wq.shape[1] + wk.shape[1] + wv.shape[1]) // n
    wide = each // HALF * SLOT
    rows, cols = wg.shape
    vmem = pl.BlockSpec(memory_space=pltpu.VMEM)
    hbm = pl.BlockSpec(memory_space=ANY)
    return pl.pallas_call(
        functools.partial(entry_body, n, m, heads, strip),
        out_shape=(
            jax.ShapeDtypeStruct((width, length), bf16),
            jax.ShapeDtypeStruct((heads, length, LANES), bf16),
            jax.ShapeDtypeStruct((length, LANES), bf16),
            jax.ShapeDtypeStruct((length, LANES), bf16),
            jax.ShapeDtypeStruct((length, LANES), f32),
            jax.ShapeDtypeStruct((length, LANES), f32),
            jax.ShapeDtypeStruct((width, wide), bf16),
            jax.ShapeDtypeStruct((1, width), f32),
            jax.ShapeDtypeStruct((1, width), f32),
            jax.ShapeDtypeStruct((1, length), jnp.int32),
            jax.ShapeDtypeStruct((2, rows * n, cols // n), wg.dtype),
            jax.ShapeDtypeStruct((rows * n, cols // n), wg.dtype),
            jax.ShapeDtypeStruct((m,) + wo.shape, wo.dtype),
        ),
        in_specs=[hbm] + [vmem] * 7 + [hbm] * 4 + [vmem],
        out_specs=[hbm] * 6 + [vmem] * 4 + [hbm] * 3,
        scratch_shapes=[
            pltpu.VMEM((n, tokens, width), bf16),
            pltpu.VMEM((n, tokens, width), bf16),
            pltpu.VMEM((2, width, tokens), bf16),
            pltpu.VMEM((n, 2, tokens), jnp.int32),
            pltpu.VMEM((n, m, strip, each), bf16),
            pltpu.VMEM((n, m, 8, LANES), f32),
            pltpu.VMEM((heads, length, LANES), bf16),
            pltpu.VMEM((length, LANES), bf16),
            pltpu.VMEM((length, LANES), bf16),
            pltpu.VMEM((length, LANES), f32),
            pltpu.VMEM((length, LANES), f32),
            pltpu.VMEM((2, tokens), jnp.int32),
            pltpu.VMEM((n, strip, each), bf16),
            pltpu.VMEM((8, LANES), f32),
            pltpu.VMEM((each, wide), bf16),
            *Gathers.scratch(2),
            pltpu.SemaphoreType.DMA((6, 2, n - 1)),
            pltpu.SemaphoreType.DMA((3, 2, m - 1)),
            pltpu.SemaphoreType.DMA((2,)),
            pltpu.SemaphoreType.DMA((13,)),
        ],
        compiler_params=pltpu.CompilerParams(
            collective_id=ident, has_side_effects=True, vmem_limit_bytes=VMEM_LIMIT
        ),
        cost_estimate=COST,
        name="entry",
    )(x, docs, positions, wq, wk, wv, one, two, wg, wu, wd, wo, inverse)


BLOCK = 512
NT = (((1,), (1,)), ((), ()))
LOG2E = 1.4426950408889634


def allowed_block(first_key, first_query, begin, causal):
    keys = first_key + lax.broadcasted_iota(jnp.int32, (BLOCK, BLOCK), 0)
    ok = keys >= begin
    if causal:
        queries = first_query + lax.broadcasted_iota(jnp.int32, (BLOCK, BLOCK), 1)
        ok = ok & (keys <= queries)
    return ok


def begins(docs):
    begin = jnp.zeros(docs.shape, jnp.int32)
    for d in range(3):
        count = jnp.sum((docs == d).astype(f32), axis=1, keepdims=True).astype(jnp.int32)
        begin = begin + jnp.where(docs > d, count, 0)
    return begin


def spread_rows(wo, wo_here):
    halves, filled, width = wo.shape
    for i in range(halves):
        wo_here[i * SLOT : i * SLOT + filled, :] = wo[i]
        wo_here[i * SLOT + filled : (i + 1) * SLOT, :] = jnp.zeros((SLOT - filled, width), bf16)


def attend_body(
    n, m, factor, q, k, v, docs, wo, go, x, gain, ffn,
    o_out, lse, start, low_out, go_all, resid, norm, ffn_all,
    o, low, vt, top, total, acc, wo_here, go_here,
    pair, near, far, sr, lr, stage, sg, lg, sz, loc,
):
    plane = Plane(n, m)
    rows = x.shape[0]
    heads = q.shape[0]
    greet(plane, True)
    gather = Gathers(plane, go, lambda i: go_here.at[i], sg, lg, 2)
    reduce = Reduce(plane, None, pair, near, far, sr, None, stage)
    spread_rows(wo, wo_here)
    vt[...] = v[...].T
    start[...] = begins(docs[...])
    meet(plane, True)
    gather.start()
    chain = Chain(plane, ffn, lambda t: ffn_all.at[t], sz)
    chain.start()
    own_ffn = pltpu.make_async_copy(ffn, ffn_all.at[plane.t], loc.at[3])
    own_ffn.start()

    def chips(step, carry):
        kk = 3 - step
        i = plane.number(kk, 0) // 2
        here = pl.ds(pl.multiple_of(i * BLOCK, BLOCK), BLOCK)
        begin = start[:, here]

        def head(h, carry):
            query = q[h, here, :]
            top[...] = jnp.full_like(top, mask_fill_value)
            total[...] = jnp.zeros_like(total)
            acc[...] = jnp.zeros_like(acc)

            def keys(j, causal):
                at = pl.ds(pl.multiple_of(j * BLOCK, BLOCK), BLOCK)
                raw = lax.dot_general(k[at, :], query, NT, preferred_element_type=f32)
                ok = allowed_block(j * BLOCK, i * BLOCK, begin, causal)
                scores = jnp.where(ok, raw * factor, mask_fill_value)
                new_top = jnp.maximum(top[...], jnp.max(scores, axis=0, keepdims=True))
                weights = jnp.exp2(scores - new_top)
                keep = jnp.exp2(top[...] - new_top)
                total[...] = total[...] * keep + jnp.sum(weights, axis=0, keepdims=True)
                acc[...] = acc[...] * keep + jnp.dot(
                    vt[:, at], weights.astype(bf16), preferred_element_type=f32
                )
                top[...] = new_top

            def loop(j, carry):
                keys(j, False)
                return carry

            lax.fori_loop(0, i, loop, 0)
            keys(i, True)
            out = (acc[...] / total[...]).T
            o[h, here, :] = out
            low[here, pl.ds(pl.multiple_of(h * LANES, LANES), LANES)] = out.astype(bf16)
            lse[h, :, here] = top[...] + jnp.log2(total[...])
            return carry

        lax.fori_loop(0, heads, head, 0)

        @pl.when(step == 1)
        def _():
            reduce.join(3)
            reduce.out[0].start()

        @pl.when(step == 3)
        def _():
            reduce.join(1)
            reduce.out[1].start()

        for other in (1, 0):
            b = plane.number(kk, other)
            at = pl.ds(pl.multiple_of(b * rows, rows), rows)
            part = jnp.dot(low[at, :], wo_here[...], preferred_element_type=f32).astype(bf16)
            if other:
                stage[kk] = part
                for which in range(4):

                    @pl.when(kk == which)
                    def _(which=which):
                        reduce.swaps[Reduce.THEIRS[which]].start()

            else:
                pair[kk] = part
        return carry

    lax.fori_loop(0, 4, chips, 0)
    outs = [
        pltpu.make_async_copy(o, o_out, loc.at[0]),
        pltpu.make_async_copy(low, low_out, loc.at[1]),
    ]
    for copy in outs:
        copy.start()
    gather.relay_near()
    chain.step(1)
    reduce.ready()
    reduce.first(resid, x)
    reduce.send_fro()
    for hop in range(2, m - 1):
        chain.step(hop)
    gather.relay_far()
    reduce.finish(resid)

    def normalize(at):
        value = resid[at, :]
        scale = lax.rsqrt(jnp.mean(value * value, axis=1, keepdims=True) + norm_epsilon)
        norm[at, :] = (value * scale * gain[...]).astype(bf16)

    in_tiles(rows, normalize)
    gather.finish()
    outs.append(pltpu.make_async_copy(go_here, go_all, loc.at[2]))
    outs[-1].start()
    chain.step(m - 1)
    chain.wait_sends()
    own_ffn.wait()
    for copy in outs:
        copy.wait()


def attend(n, m, factor, q, k, v, docs, wo, go, x, gain, ffn, ident):
    heads, length, _ = q.shape
    rows, width = x.shape
    hbm = pl.BlockSpec(memory_space=ANY)
    vmem = pl.BlockSpec(memory_space=pltpu.VMEM)
    return pl.pallas_call(
        functools.partial(attend_body, n, m, factor),
        out_shape=(
            jax.ShapeDtypeStruct((heads, length, LANES), f32),
            jax.ShapeDtypeStruct((heads, 1, length), f32),
            jax.ShapeDtypeStruct((1, length), jnp.int32),
            jax.ShapeDtypeStruct((length, heads * LANES), bf16),
            jax.ShapeDtypeStruct((n,) + go.shape, go.dtype),
            jax.ShapeDtypeStruct((rows, width), f32),
            jax.ShapeDtypeStruct((rows, width), bf16),
            jax.ShapeDtypeStruct((m,) + ffn.shape, bf16),
        ),
        in_specs=[vmem] * 5 + [hbm] + [vmem] * 2 + [hbm],
        out_specs=[hbm, vmem, vmem, hbm, hbm, vmem, vmem, hbm],
        scratch_shapes=[
            pltpu.VMEM((heads, length, LANES), f32),
            pltpu.VMEM((length, heads * LANES), bf16),
            pltpu.VMEM((LANES, length), bf16),
            pltpu.VMEM((1, BLOCK), f32),
            pltpu.VMEM((1, BLOCK), f32),
            pltpu.VMEM((LANES, BLOCK), f32),
            pltpu.VMEM((heads * LANES, width), bf16),
            pltpu.VMEM((n,) + go.shape, go.dtype),
        ]
        + Reduce.scratch(rows, width)
        + [pltpu.VMEM((4, rows, width), bf16)]
        + Gathers.scratch(2)
        + [pltpu.SemaphoreType.DMA((4, m)), pltpu.SemaphoreType.DMA((4,))],
        compiler_params=pltpu.CompilerParams(
            collective_id=ident, has_side_effects=True, vmem_limit_bytes=VMEM_LIMIT
        ),
        cost_estimate=COST,
        name="attend",
    )(q, k, v, docs, wo, go, x, gain, ffn)


def attend_back_body(
    n, m, factor, scale, q_in, k_in, v_in, o_in, lse, begin, cos_in, sin_in, low_in,
    hid_in, down_in, ffn, wo, dnorm, resid, grad, gain,
    out, layer, terms, dresid, gain_out, ffn_sum,
    q, k, v, o, cosine, sine, low, kt, dqt, dk, dv, delta, go, every, dbranch, wo_here,
    hid_low, w_down, stage, pair, near, far, sr, lr, held, gain_sum, gain_cut, gain_got,
    sums, add, own, got, ss, ls, sg, lg, sv, loc,
):
    plane = Plane(n, m)
    heads, length, _ = q.shape
    rows, width = dnorm.shape
    strip = gain_out.shape[2]
    loads = [
        pltpu.make_async_copy(a, b, loc.at[i])
        for i, (a, b) in enumerate(
            (
                (q_in, q), (k_in, k), (v_in, v), (o_in, o),
                (cos_in, cosine), (sin_in, sine), (low_in, low),
            )
        )
    ]
    for copy in loads:
        copy.start()
    greet(plane, True)
    moves = [
        pltpu.make_async_copy(hid_in, hid_low, loc.at[8]),
        pltpu.make_async_copy(down_in, w_down, loc.at[9]),
    ]
    for copy in moves:
        copy.start()
    one = Reduce(plane, None, pair, near, far, sr, None, stage)
    gather = Gathers(plane, dbranch, lambda i: every.at[i], sg, lg, 2)
    gain_copies = exchange(
        plane, lambda i: gain_cut.at[i], lambda i: gain_got.at[i], sv.at[0], sv.at[1], loc.at[7]
    )
    gain_sum[...] = jnp.zeros_like(gain_sum)

    def into_branch(at):
        value, up = resid[at, :], dnorm[at, :]
        scale_two = lax.rsqrt(jnp.mean(value * value, axis=1, keepdims=True) + norm_epsilon)
        inner = gain[...] * up
        moment = jnp.mean(value * inner, axis=1, keepdims=True)
        turned = value * scale_two
        got = (
            grad[at, :].astype(f32) + scale_two * inner - turned * (scale_two * scale_two * moment)
        )
        dresid[at, :] = got
        dbranch[at, :] = got.astype(bf16)
        gain_sum[...] += up * turned

    in_tiles(rows, into_branch)
    meet(plane, True)
    gather.start()
    scatter = Scatter(plane, ffn, sums, add, own, got, ss, ls)
    scatter.start()
    total_gain = jnp.sum(gain_sum[...], axis=0, keepdims=True)
    for i in range(n):
        gain_cut[i] = total_gain[:, i * (width // n) : (i + 1) * (width // n)]
    for copy in gain_copies:
        copy.start()
    spread_rows(wo, wo_here)
    for copy in moves:
        copy.wait()

    def mix(it, carry):
        kk = 3 - it // 2
        other = 1 - lax.rem(it, 2)
        b = plane.number(kk, other)
        at = pl.ds(pl.multiple_of(b * rows, rows), rows)
        part = lax.dot_general(
            hid_low[at, :], w_down[...], NT, preferred_element_type=f32
        ).astype(bf16)

        @pl.when(other == 0)
        def _():
            pair[kk] = part

        @pl.when(other == 1)
        def _():
            stage[kk] = part

        for which in range(4):

            @pl.when(it == 2 * (3 - which))
            def _(which=which):
                one.swaps[Reduce.THEIRS[which]].start()

        return carry

    lax.fori_loop(0, n, mix, 0)
    for copy in loads:
        copy.wait()
    kt[...] = k[...].T
    dk[...] = jnp.zeros_like(dk)
    dv[...] = jnp.zeros_like(dv)

    def unturn(value, at):
        return value * cosine[at, :] - pltpu.roll(value, SLOT, 1) * sine[at, :]

    def chips(kk, carry):
        @pl.when(kk == 0)
        def _():
            gather.wait_own()
            gather.wait_swap()

        @pl.when(kk == 1)
        def _():
            gather.relay_near()
            gather.wait_share(1)
            scatter.relay(0, 0)

        @pl.when(kk == 2)
        def _():
            one.send_to()
            gather.wait_share(0)
            scatter.relay(0, 1)

        @pl.when(kk == 3)
        def _():
            one.ready()
            one.first(held, resid)
            gather.relay_far()
            gather.wait_share(2)
            scatter.relay(1, 0)

        i = plane.number(kk, 0) // 2
        here = pl.ds(pl.multiple_of(i * BLOCK, BLOCK), BLOCK)
        for other in range(2):
            b = plane.number(kk, other)
            at = pl.ds(pl.multiple_of(b * rows, rows), rows)
            value = lax.dot_general(every[b], wo_here[...], NT, preferred_element_type=f32)
            for h in range(heads):
                go[h, at, :] = value[:, h * LANES : (h + 1) * LANES].astype(bf16)

        def head(h, carry):
            query = q[h, here, :]
            grads = go[h, here, :]
            delta[...] = jnp.sum((grads.astype(f32) * o[h, here, :]).T, axis=0, keepdims=True)
            dqt[...] = jnp.zeros_like(dqt)

            def keys(j, causal):
                at = pl.ds(pl.multiple_of(j * BLOCK, BLOCK), BLOCK)
                raw = lax.dot_general(k[at, :], query, NT, preferred_element_type=f32)
                ok = allowed_block(j * BLOCK, i * BLOCK, begin[:, here], causal)
                probs = jnp.where(ok, jnp.exp2(raw * factor - lse[h, :, here]), 0.0)
                dprob = lax.dot_general(v[at, :], grads, NT, preferred_element_type=f32)
                dscore = (probs * (dprob - delta[...])).astype(bf16)
                dv[at, :] += jnp.dot(probs.astype(bf16), grads, preferred_element_type=f32)
                dk[at, :] += jnp.dot(dscore, query, preferred_element_type=f32)
                dqt[...] += jnp.dot(kt[:, at], dscore, preferred_element_type=f32)

            def loop(j, carry):
                keys(j, False)
                return carry

            lax.fori_loop(0, i, loop, 0)
            keys(i, True)
            got = unturn(dqt[...].T * scale, here).astype(bf16)
            out[here, pl.ds(pl.multiple_of(h * LANES, LANES), LANES)] = got
            return carry

        lax.fori_loop(0, heads, head, 0)
        return carry

    lax.fori_loop(0, 4, chips, 0)
    scatter.relay(1, 1)

    def write(i, carry):
        at = pl.ds(pl.multiple_of(i * BLOCK, BLOCK), BLOCK)
        turned = unturn(dk[at, :] * scale, at).astype(bf16)
        out[at, heads * LANES : (heads + 1) * LANES] = turned
        out[at, (heads + 1) * LANES :] = dv[at, :].astype(bf16)
        return carry

    lax.fori_loop(0, length // BLOCK, write, 0)
    one.send_fro()
    across = every.reshape(length, width)
    part = 512

    def into_terms(i, carry):
        at = pl.ds(pl.multiple_of(i * part, part), part)
        value = lax.dot_general(
            low[...], across[:, at], (((0,), (0,)), ((), ())), preferred_element_type=f32
        ).astype(bf16)
        for half in range(terms.shape[0]):
            terms[half, :, at] = value[half * SLOT : half * SLOT + HALF]
        return carry

    lax.fori_loop(0, width // part, into_terms, 0)
    for copy in gain_copies:
        copy.wait()
    all_gain = gain_got[0]
    for i in range(1, n):
        all_gain = all_gain + gain_got[i]
    for t in range(m):
        gain_out[t] = all_gain[:, t * strip : (t + 1) * strip]
    gather.wait_sends()
    one.finish(held, layer)
    scatter.finish()
    back = pltpu.make_async_copy(sums, ffn_sum, loc.at[10])
    back.start()
    back.wait()


def attend_back(
    n, m, factor, scale, q, k, v, o, lse, begin, cosine, sine, low,
    hid_low, w_down, ffn, wo, dnorm, resid, grad, gain, ident,
):
    heads, length, _ = q.shape
    rows, width = dnorm.shape
    strip = width // (n * m)
    hbm = pl.BlockSpec(memory_space=ANY)
    vmem = pl.BlockSpec(memory_space=pltpu.VMEM)
    return pl.pallas_call(
        functools.partial(attend_back_body, n, m, factor, scale),
        out_shape=(
            jax.ShapeDtypeStruct((length, (heads + 2) * LANES), bf16),
            jax.ShapeDtypeStruct((rows, width), bf16),
            jax.ShapeDtypeStruct(wo.shape, bf16),
            jax.ShapeDtypeStruct((rows, width), f32),
            jax.ShapeDtypeStruct((m, 1, strip), f32),
            jax.ShapeDtypeStruct(ffn.shape[1:], bf16),
        ),
        in_specs=[hbm] * 4 + [vmem] * 2 + [hbm] * 6 + [vmem] * 5,
        out_specs=[vmem] * 5 + [hbm],
        scratch_shapes=[
            pltpu.VMEM(q.shape, bf16),
            pltpu.VMEM(k.shape, bf16),
            pltpu.VMEM(v.shape, bf16),
            pltpu.VMEM(o.shape, f32),
            pltpu.VMEM(cosine.shape, f32),
            pltpu.VMEM(sine.shape, f32),
            pltpu.VMEM(low.shape, bf16),
            pltpu.VMEM((LANES, length), bf16),
            pltpu.VMEM((LANES, BLOCK), f32),
            pltpu.VMEM((length, LANES), f32),
            pltpu.VMEM((length, LANES), f32),
            pltpu.VMEM((1, BLOCK), f32),
            pltpu.VMEM((heads, length, LANES), bf16),
            pltpu.VMEM((n, rows, width), bf16),
            pltpu.VMEM((rows, width), bf16),
            pltpu.VMEM((heads * LANES, width), bf16),
            pltpu.VMEM(hid_low.shape, bf16),
            pltpu.VMEM(w_down.shape, bf16),
            pltpu.VMEM((4, rows, width), bf16),
        ]
        + Reduce.scratch(rows, width)
        + [
            pltpu.VMEM((rows, width), f32),
            pltpu.VMEM((TILE, width), f32),
            pltpu.VMEM((n, 1, width // n), f32),
            pltpu.VMEM((n, 1, width // n), f32),
            pltpu.VMEM(ffn.shape[1:], bf16),
        ]
        + Scatter.scratch(ffn.shape[1:])
        + Gathers.scratch(2)
        + [pltpu.SemaphoreType.DMA((2, n - 1)), pltpu.SemaphoreType.DMA((11,))],
        compiler_params=pltpu.CompilerParams(
            collective_id=ident, has_side_effects=True, vmem_limit_bytes=VMEM_LIMIT
        ),
        cost_estimate=COST,
        name="attend_back",
    )(
        q, k, v, o, lse, begin, cosine, sine, low, hid_low, w_down, ffn, wo, dnorm, resid, grad, gain
    )


def feed_body(
    n, m, mine, go, w_in, down, dnorm, grads, hid_out, down_out, down_parts,
    rows, rows_t, go_t, go_two, w, w_down, gates, h, hid_low, down_held, down_sum,
    pair, near, far, stage,
    sg, lg, sr, loc, sw, so, sd, sz, sf,
):
    plane = Plane(n, m)
    tokens, width = rows.shape[1:]
    hid = down.shape[1]
    half = m * hid
    greet(plane, True)
    gather = Gathers(plane, mine, lambda i: rows.at[i], sg, lg, 2)
    reduce = Reduce(plane, None, pair, near, far, sr, None, stage)

    def columns(ref, j, t):
        return ref.at[:, j * half + t * hid : j * half + (t + 1) * hid]

    weights = [
        pltpu.make_async_copy(w_in.at[t, j], columns(w, j, t), sw.at[j, t])
        for j in range(2)
        for t in range(m)
    ]
    for copy in weights:
        copy.start()
    meet(plane, True)
    gather.start()

    def down_at(ref, t):
        return ref.at[:, pl.ds(pl.multiple_of(t * hid, hid), hid)]

    chain = Chain(plane, down, lambda t: down_at(w_down, t), sz)
    chain.start()
    own_down = pltpu.make_async_copy(down, down_at(w_down, plane.t), loc.at[0])
    own_down.start()
    gather.wait_own()
    for copy in weights:
        copy.wait()

    def span(b):
        return pl.ds(pl.multiple_of(b * tokens, tokens), tokens)

    def down_grad(kk, keep):
        chip = plane.number(kk, 0) // 2
        at = pl.ds(pl.multiple_of(chip * 2 * tokens, 2 * tokens), 2 * tokens)

        def part(i, carry):
            line = pl.ds(pl.multiple_of(i * 256, 256), 256)
            value = jnp.dot(go_t[line, at], hid_low[at, :], preferred_element_type=f32)
            keep(line, value)
            return carry

        lax.fori_loop(0, width // 256, part, 0)

    def set_down(line, value):
        down_sum[line, :] = value

    def add_down(line, value):
        down_sum[line, :] += value

    def hold_down(line, value):
        down_held[line, :] = (down_sum[line, :] + value).astype(bf16)

    def early_go(it, slot):
        b = plane.number(it // 2, lax.rem(it, 2))
        return pltpu.make_async_copy(go.at[b], go_two.at[slot], so.at[slot])

    def forward(it, carry):
        b = plane.number(it // 2, lax.rem(it, 2))

        @pl.when(it == 1)
        def _():
            gather.wait_swap()

        @pl.when(it == 2)
        def _():
            down_grad(0, set_down)
            chain.step(1)
            gather.relay_near()

        @pl.when(it == 3)
        def _():
            gather.wait_share(1)

        @pl.when(it == 4)
        def _():
            chain.step(2)

        @pl.when(it == 5)
        def _():
            gather.wait_share(0)

        @pl.when(it == 6)
        def _():
            down_grad(1, add_down)
            down_grad(2, add_down)
            gather.relay_far()

        @pl.when(it == 7)
        def _():
            gather.wait_share(2)

        slot = lax.rem(it, 2)

        @pl.when(it < n - 1)
        def _():
            early_go(it + 1, 1 - slot).start()

        row = rows[b]
        both = jnp.dot(row, w[...], preferred_element_type=f32)
        gates[span(b), :] = both
        gate, up = both[:, :half], both[:, half:]
        hid_low[span(b), :] = (gate * jax.nn.sigmoid(gate) * up).astype(bf16)
        rows_t[:, span(b)] = row.T
        early_go(it, slot).wait()
        go_t[:, span(b)] = go_two[slot].T
        return carry

    early_go(0, 0).start()
    lax.fori_loop(0, n, forward, 0)

    def number(it):
        return plane.number(3 - it // 2, 1 - lax.rem(it, 2))

    def load_go(it, slot):
        return pltpu.make_async_copy(go.at[number(it)], go_two.at[slot], so.at[slot])

    load_go(0, 0).start()
    down_grad(3, hold_down)
    outs = fan(
        plane, lambda t: down_at(down_held, t), lambda t: down_parts.at[t], sf.at[0], sf.at[1]
    )
    outs.append(
        pltpu.make_async_copy(down_at(down_held, plane.t), down_parts.at[plane.t], loc.at[1])
    )
    outs.append(pltpu.make_async_copy(hid_low, hid_out, loc.at[2]))
    for copy in outs:
        copy.start()
    for hop in range(3, m):
        chain.step(hop)
    own_down.wait()
    outs.append(pltpu.make_async_copy(w_down, down_out, loc.at[3]))
    outs[-1].start()

    def backward(it, carry):
        slot = lax.rem(it, 2)
        k = 3 - it // 2
        b = number(it)

        @pl.when(it == 2)
        def _():
            reduce.join(3)
            reduce.out[0].start()

        @pl.when(it == 6)
        def _():
            reduce.join(1)
            reduce.out[1].start()

        @pl.when(it == 7)
        def _():
            reduce.ready()
            reduce.send_fro()

        @pl.when(it < n - 1)
        def _():
            load_go(it + 1, 1 - slot).start()

        load_go(it, slot).wait()

        gate = gates[span(b), :half]
        up = gates[span(b), half:]
        dhidden = jnp.dot(go_two[slot], w_down[...], preferred_element_type=f32)
        sig = jax.nn.sigmoid(gate)
        dgate = (dhidden * up * sig * (1.0 + gate * (1.0 - sig))).astype(bf16)
        dup = (dhidden * gate * sig).astype(bf16)
        h[span(b), :half] = dgate
        h[span(b), half:] = dup
        part = lax.dot_general(h[span(b), :], w[...], NT, preferred_element_type=f32)
        part = part.astype(bf16)

        @pl.when(lax.rem(it, 2) == 1)
        def _():
            pair[k] = part

        @pl.when(lax.rem(it, 2) == 0)
        def _():
            stage[k] = part

        for kk in range(4):

            @pl.when(it == 2 * (3 - kk))
            def _(kk=kk):
                reduce.swaps[Reduce.THEIRS[kk]].start()

        return carry

    lax.fori_loop(0, n, backward, 0)

    def weight_grad(i, carry):
        at = pl.ds(pl.multiple_of(i * 256, 256), 256)
        value = jnp.dot(rows_t[at, :], h[...], preferred_element_type=f32)
        w[at, :] = value.astype(bf16)
        return carry

    lax.fori_loop(0, width // 256, weight_grad, 0)
    ends = [
        pltpu.make_async_copy(columns(w, j, t), grads.at[t, j], sd.at[j, t])
        for j in range(2)
        for t in range(m)
    ]
    for copy in ends:
        copy.start()
    reduce.first(dnorm)
    gather.wait_sends()
    chain.wait_sends()
    reduce.finish(dnorm)
    for copy in outs + ends:
        copy.wait()


def feed(n, m, norm, go, w_in, down, ident):
    tokens, width = norm.shape
    hid = down.shape[1]
    length = n * tokens
    half = m * hid
    hbm = pl.BlockSpec(memory_space=ANY)
    return pl.pallas_call(
        functools.partial(feed_body, n, m),
        out_shape=(
            jax.ShapeDtypeStruct((tokens, width), f32),
            jax.ShapeDtypeStruct((m, 2, width, hid), bf16),
            jax.ShapeDtypeStruct((length, half), bf16),
            jax.ShapeDtypeStruct((width, half), bf16),
            jax.ShapeDtypeStruct((m, width, hid), bf16),
        ),
        in_specs=[hbm] * 4,
        out_specs=[pl.BlockSpec(memory_space=pltpu.VMEM)] + [hbm] * 4,
        scratch_shapes=[
            pltpu.VMEM((n, tokens, width), bf16),
            pltpu.VMEM((width, length), bf16),
            pltpu.VMEM((width, length), bf16),
            pltpu.VMEM((2, tokens, width), bf16),
            pltpu.VMEM((width, 2 * half), bf16),
            pltpu.VMEM((width, half), bf16),
            pltpu.VMEM((length, 2 * half), f32),
            pltpu.VMEM((length, 2 * half), bf16),
            pltpu.VMEM((length, half), bf16),
            pltpu.VMEM((width, half), bf16),
            pltpu.VMEM((width, half), f32),
        ]
        + [pltpu.VMEM((slots, tokens, width), bf16) for slots in Reduce.SLOTS]
        + [
            pltpu.VMEM((4, tokens, width), bf16),
            *Gathers.scratch(2),
            pltpu.SemaphoreType.DMA((4, 4)),
            pltpu.SemaphoreType.DMA((4,)),
            pltpu.SemaphoreType.DMA((2, m)),
            pltpu.SemaphoreType.DMA((2,)),
            pltpu.SemaphoreType.DMA((2, m)),
            pltpu.SemaphoreType.DMA((4, m)),
            pltpu.SemaphoreType.DMA((2, m - 1)),
        ],
        compiler_params=pltpu.CompilerParams(
            collective_id=ident, has_side_effects=True, vmem_limit_bytes=VMEM_LIMIT
        ),
        cost_estimate=COST,
        name="feed",
    )(norm, go, w_in, down)


def fast_layer(n, m):
    def on_plane(
        layer_input,
        doc_ids,
        positions,
        first_gain,
        query_weight,
        key_weight,
        value_weight,
        output_weight,
        second_gain,
        gate_weight,
        up_weight,
        down_weight,
        out_grad,
    ):
        x = layer_input[0]
        width = x.shape[1]
        heads = QUERY_HEADS // n
        scale = 1.0 / math.sqrt(HEAD_SIZE)
        factor = scale * LOG2E
        strip = query_weight.shape[0]

        lane = np.arange(LANES) % SLOT
        inverse = np.where(lane < HALF, rope_base ** (-(lane * 2.0 / HEAD_SIZE)), 0.0)
        (
            norm_t, q, k, v, cosine, sine, wqkv, gain_one, gain_two, docs,
            ffn_mine, down_mine, output_rows,
        ) = entry(
            n, m, heads, x, doc_ids, positions, query_weight, key_weight, value_weight,
            first_gain.reshape(1, strip), second_gain.reshape(1, strip),
            gate_weight, up_weight, down_weight, output_weight,
            jnp.asarray(inverse[None], f32), 0,
        )
        o, lse, begin, low, grad_all, resid, norm_two, ffn_all = attend(
            n, m, factor, q, k, v, docs, output_rows, out_grad[0], x, gain_two, ffn_mine, 9
        )
        dnorm_two, ffn_terms, hid_low, w_down, down_parts = feed(
            n, m, norm_two, grad_all, ffn_all, down_mine, 2
        )
        dqkv, layer_output, output_terms, dresid, gain_part, ffn_sum = attend_back(
            n, m, factor, scale, q, k, v, o, lse, begin, cosine, sine, low, hid_low, w_down, ffn_terms,
            output_rows, dnorm_two, resid, out_grad[0], gain_two, 3,
        )
        input_grad, ffn_out, qkv_out, output_parts, gain_sums = last(
            n, m, dqkv, wqkv, x, dresid, gain_one, norm_t, ffn_sum, down_parts,
            output_terms, gain_part, 6,
        )
        output_grad = jnp.sum(output_parts.astype(f32), axis=0)

        gate_grad, up_grad, down_grad = [ffn_out[i].astype(f32) for i in range(3)]
        kv = HEAD_SIZE * KEY_VALUE_HEADS // n
        split = heads * HEAD_SIZE

        def columns(a, b):
            return qkv_out[:, :, a:b].transpose(1, 0, 2).reshape(strip, -1).astype(f32)

        query_grad = columns(0, split)
        key_grad = columns(split, split + kv)
        value_grad = columns(split + kv, split + 2 * kv)

        one = (
            jnp.sum(query_weight.astype(f32) * query_grad, axis=1)
            + jnp.sum(key_weight.astype(f32) * key_grad, axis=1)
            + jnp.sum(value_weight.astype(f32) * value_grad, axis=1)
        )
        first_gain_grad = one / first_gain.astype(f32)
        second_gain_grad = jnp.sum(gain_sums, axis=(0, 1))
        return (
            layer_output[None],
            input_grad[None],
            first_gain_grad,
            query_grad,
            key_grad,
            value_grad,
            output_grad,
            second_gain_grad,
            gate_grad,
            up_grad,
            down_grad,
        )

    return on_plane


def solution(mesh):
    n, m = mesh.shape["seq"], mesh.shape["tp"]
    fits = n == KEY_VALUE_HEADS == 8 and m == 4
    return jax.shard_map(
        fast_layer(n, m) if fits else on_device,
        mesh=mesh,
        in_specs=(
            P("tp", "seq", None),
            P("tp", "seq"),
            P("tp", "seq"),
            P(("seq", "tp")),
            P(("seq", "tp"), None),
            P(("seq", "tp"), None),
            P(("seq", "tp"), None),
            P(("seq", "tp"), None),
            P(("seq", "tp")),
            P("seq", "tp"),
            P("seq", "tp"),
            P("seq", "tp"),
            P("tp", "seq", None),
        ),
        out_specs=(
            P("tp", "seq", None),
            P("tp", "seq", None),
            P(("seq", "tp")),
            P(("seq", "tp"), None),
            P(("seq", "tp"), None),
            P(("seq", "tp"), None),
            P(("seq", "tp"), None),
            P(("seq", "tp")),
            P("seq", "tp"),
            P("seq", "tp"),
            P("seq", "tp"),
        ),
        check_vma=False,
    )
```

```python
import functools
import math

import jax
import jax.numpy as jnp
import numpy as np
from jax import lax
from jax.experimental import pallas as pl
from jax.experimental.pallas import tpu as pltpu
from jax.sharding import PartitionSpec as P

QUERY_HEADS = 16
KEY_VALUE_HEADS = 8
HEAD_SIZE = 96


norm_epsilon = 1e-05
rope_base = 100000.0
mask_fill_value = -1e30


def rope_tables(places):
    half = HEAD_SIZE // 2
    inverse = rope_base ** (-(jnp.arange(half, dtype=jnp.float32) * 2.0 / HEAD_SIZE))
    angles = places.astype(jnp.float32)[:, None] * inverse[None, :]
    return (jnp.cos(angles), jnp.sin(angles))


def apply_rotary(value_rows, cosine_table, sine_table, heads, direction):
    sequence_length = value_rows.shape[0]
    split = value_rows.reshape(sequence_length, heads, 2, HEAD_SIZE // 2)
    first = split[:, :, 0]
    second = split[:, :, 1]
    cosine = cosine_table[:, None, :]
    sine = direction * sine_table[:, None, :]
    turned = jnp.stack([first * cosine - second * sine, second * cosine + first * sine], axis=2)
    return turned.reshape(sequence_length, heads * HEAD_SIZE)


def outer_product(left, right):
    return lax.dot_general(
        left, right, (((0,), (0,)), ((), ())), preferred_element_type=jnp.float32
    )


def times_transpose(left, right):
    return lax.dot_general(
        left, right, (((1,), (1,)), ((), ())), preferred_element_type=jnp.float32
    )


def norm_backward(inputs, scale, gain, upstream):
    inner = gain * upstream
    moment = jnp.mean(inputs * inner, axis=1, keepdims=True)
    return (
        scale * inner - inputs * scale * scale * scale * moment,
        jnp.sum(upstream * inputs * scale, axis=0),
    )


def on_device(
    layer_input,
    doc_ids,
    positions,
    first_gain,
    query_weight,
    key_weight,
    value_weight,
    output_weight,
    second_gain,
    gate_weight,
    up_weight,
    down_weight,
    out_grad,
):
    token_rows = layer_input.shape[1]
    query_groups = QUERY_HEADS // KEY_VALUE_HEADS
    scale_of_scores = 1.0 / math.sqrt(HEAD_SIZE)
    inputs_f = layer_input[0].astype(jnp.float32)
    my_docs = doc_ids[0]
    gain_one, query_full, complete_keys, value_full, output_full, gain_two = (
        lax.all_gather(first_gain, ("seq", "tp"), axis=0, tiled=True),
        lax.all_gather(query_weight, ("seq", "tp"), axis=0, tiled=True),
        lax.all_gather(key_weight, ("seq", "tp"), axis=0, tiled=True),
        lax.all_gather(value_weight, ("seq", "tp"), axis=0, tiled=True),
        lax.all_gather(output_weight, ("seq", "tp"), axis=0, tiled=True),
        lax.all_gather(second_gain, ("seq", "tp"), axis=0, tiled=True),
    )
    gain_one_f = gain_one.astype(jnp.float32)
    gain_two_f = gain_two.astype(jnp.float32)
    scale_one = lax.rsqrt(jnp.mean(inputs_f * inputs_f, axis=1, keepdims=True) + norm_epsilon)
    first_normalized = (inputs_f * scale_one * gain_one_f).astype(jnp.bfloat16)
    cosine_table, sine_table = rope_tables(positions[0])
    rotated_query = apply_rotary(
        jnp.dot(first_normalized, query_full, preferred_element_type=jnp.float32),
        cosine_table,
        sine_table,
        QUERY_HEADS,
        1.0,
    ).astype(jnp.bfloat16)
    key_rot = apply_rotary(
        jnp.dot(first_normalized, complete_keys, preferred_element_type=jnp.float32),
        cosine_table,
        sine_table,
        KEY_VALUE_HEADS,
        1.0,
    ).astype(jnp.bfloat16)
    value_low = jnp.dot(first_normalized, value_full, preferred_element_type=jnp.float32).astype(
        jnp.bfloat16
    )
    gathered_keys, gathered_values, doc_all = (
        lax.all_gather(key_rot, "seq", axis=0, tiled=True),
        lax.all_gather(value_low, "seq", axis=0, tiled=True),
        lax.all_gather(my_docs.astype(jnp.bfloat16), "seq", axis=0, tiled=True),
    )
    sequence_length = gathered_keys.shape[0]
    block_number = math.gcd(512, sequence_length)
    block_count = sequence_length // block_number
    query_index = lax.axis_index("seq") * token_rows + jnp.arange(token_rows, dtype=jnp.int32)
    my_doc_f = my_docs.astype(jnp.float32)
    heads_of_query = rotated_query.reshape(token_rows, KEY_VALUE_HEADS, query_groups, HEAD_SIZE)
    layer_entries = (
        gathered_keys.reshape(block_count, block_number, KEY_VALUE_HEADS, HEAD_SIZE),
        gathered_values.reshape(block_count, block_number, KEY_VALUE_HEADS, HEAD_SIZE),
        doc_all.astype(jnp.float32).reshape(block_count, block_number),
        jnp.arange(block_count, dtype=jnp.int32) * block_number,
    )

    def allowed_of(doc_piece, start):
        key_index = start + jnp.arange(block_number, dtype=jnp.int32)
        return (key_index[None, :] <= query_index[:, None]) & (
            doc_piece[None, :] == my_doc_f[:, None]
        )

    def scores_of(key_piece, allowed):
        raw = (
            jnp.einsum(
                "tgrd,kgd->tgrk", heads_of_query, key_piece, preferred_element_type=jnp.float32
            )
            * scale_of_scores
        )
        return jnp.where(allowed[:, None, None, :], raw, mask_fill_value)

    def total_step(carry, item):
        key_piece, value_piece, doc_piece, start = item
        allowed = allowed_of(doc_piece, start)

        def total_work(state):
            top, total = state
            scores = scores_of(key_piece, allowed)
            new_top = jnp.maximum(top, jnp.max(scores, axis=3))
            weights = jnp.where(
                allowed[:, None, None, :], jnp.exp(scores - new_top[..., None]), 0.0
            )
            return (new_top, total * jnp.exp(top - new_top) + jnp.sum(weights, axis=3))

        return (lax.cond(jnp.any(allowed), total_work, lambda state: state, carry), None)

    start_state = (
        jnp.full((token_rows, KEY_VALUE_HEADS, query_groups), mask_fill_value, jnp.float32),
        jnp.zeros((token_rows, KEY_VALUE_HEADS, query_groups), jnp.float32),
    )
    (top, total), unused_result = lax.scan(total_step, start_state, layer_entries)
    log_total = top + jnp.log(total)

    def probs_of(key_piece, allowed):
        scores = scores_of(key_piece, allowed)
        return jnp.where(allowed[:, None, None, :], jnp.exp(scores - log_total[..., None]), 0.0)

    def output_update(accum, item):
        key_piece, value_piece, doc_piece, start = item
        allowed = allowed_of(doc_piece, start)

        def output_work(state):
            probs = probs_of(key_piece, allowed).astype(jnp.bfloat16)
            return state + jnp.einsum(
                "tgrk,kgd->tgrd", probs, value_piece, preferred_element_type=jnp.float32
            )

        return (lax.cond(jnp.any(allowed), output_work, lambda state: state, accum), None)

    heads_output, unused_result = lax.scan(
        output_update,
        jnp.zeros((token_rows, KEY_VALUE_HEADS, query_groups, HEAD_SIZE), jnp.float32),
        layer_entries,
    )
    attn_low = heads_output.reshape(token_rows, QUERY_HEADS * HEAD_SIZE).astype(jnp.bfloat16)
    resid = inputs_f + jnp.dot(attn_low, output_full, preferred_element_type=jnp.float32)
    scale_two = lax.rsqrt(jnp.mean(resid * resid, axis=1, keepdims=True) + norm_epsilon)
    normed_two = (resid * scale_two * gain_two_f).astype(jnp.bfloat16)
    rows_all = lax.all_gather(normed_two, "tp", axis=0, tiled=True)
    gate_cols, up_cols, down_cols = (
        lax.all_gather(gate_weight, "seq", axis=0, tiled=True),
        lax.all_gather(up_weight, "seq", axis=0, tiled=True),
        lax.all_gather(down_weight, "seq", axis=0, tiled=True),
    )
    gate_pre = jnp.dot(rows_all, gate_cols, preferred_element_type=jnp.float32)
    up_pre = jnp.dot(rows_all, up_cols, preferred_element_type=jnp.float32)
    gate_sig = jax.nn.sigmoid(gate_pre)
    gate_act = gate_pre * gate_sig
    hidden = (gate_act * up_pre).astype(jnp.bfloat16)
    mixed = lax.psum_scatter(
        times_transpose(hidden, down_cols).astype(jnp.bfloat16),
        "tp",
        scatter_dimension=0,
        tiled=True,
    ).astype(jnp.float32)
    layer_output = (resid + mixed).astype(jnp.bfloat16)[None]
    grad_low = out_grad[0]
    grad_f = grad_low.astype(jnp.float32)
    grad_all = lax.all_gather(grad_low, "tp", axis=0, tiled=True)
    dhidden = jnp.dot(grad_all, down_cols, preferred_element_type=jnp.float32)
    dgate = (dhidden * up_pre * gate_sig * (1.0 + gate_pre * (1.0 - gate_sig))).astype(jnp.bfloat16)
    dup = (dhidden * gate_act).astype(jnp.bfloat16)
    gate_term = outer_product(rows_all, dgate)
    up_term = outer_product(rows_all, dup)
    down_term_grad = outer_product(grad_all, hidden)
    dnorm_two = lax.psum_scatter(
        (times_transpose(dgate, gate_cols) + times_transpose(dup, up_cols)).astype(jnp.bfloat16),
        "tp",
        scatter_dimension=0,
        tiled=True,
    ).astype(jnp.float32)
    gate_grad, up_grad, down_grad = (
        lax.psum_scatter(
            gate_term.astype(jnp.bfloat16), "seq", scatter_dimension=0, tiled=True
        ).astype(jnp.float32),
        lax.psum_scatter(
            up_term.astype(jnp.bfloat16), "seq", scatter_dimension=0, tiled=True
        ).astype(jnp.float32),
        lax.psum_scatter(
            down_term_grad.astype(jnp.bfloat16), "seq", scatter_dimension=0, tiled=True
        ).astype(jnp.float32),
    )
    resid_part, gain_two_term = norm_backward(resid, scale_two, gain_two_f, dnorm_two)
    dresid = grad_f + resid_part
    dbranch = dresid.astype(jnp.bfloat16)
    output_term = outer_product(attn_low, dbranch)
    heads_gradient = times_transpose(dbranch, output_full).astype(jnp.bfloat16)
    grouped_heads_gradient = heads_gradient.reshape(
        token_rows, KEY_VALUE_HEADS, query_groups, HEAD_SIZE
    )
    delta = jnp.sum(grouped_heads_gradient.astype(jnp.float32) * heads_output, axis=3)

    def gradient_update(dquery, item):
        key_piece, value_piece, doc_piece, start = item
        allowed = allowed_of(doc_piece, start)

        def gradient_work(state):
            probs = probs_of(key_piece, allowed)
            value_piece_grad = jnp.einsum(
                "tgrk,tgrd->kgd",
                probs.astype(jnp.bfloat16),
                grouped_heads_gradient,
                preferred_element_type=jnp.float32,
            )
            prob_grad = jnp.einsum(
                "tgrd,kgd->tgrk",
                grouped_heads_gradient,
                value_piece,
                preferred_element_type=jnp.float32,
            )
            score_grad = (probs * (prob_grad - delta[..., None])).astype(jnp.bfloat16)
            key_piece_grad = jnp.einsum(
                "tgrk,tgrd->kgd", score_grad, heads_of_query, preferred_element_type=jnp.float32
            )
            updated = state + jnp.einsum(
                "tgrk,kgd->tgrd", score_grad, key_piece, preferred_element_type=jnp.float32
            )
            return (updated, (key_piece_grad, value_piece_grad))

        def skip(state):
            blank_tensor = jnp.zeros((block_number, KEY_VALUE_HEADS, HEAD_SIZE), jnp.float32)
            return (state, (blank_tensor, blank_tensor))

        return lax.cond(jnp.any(allowed), gradient_work, skip, dquery)

    dquery, (key_contributions, value_contributions) = lax.scan(
        gradient_update,
        jnp.zeros((token_rows, KEY_VALUE_HEADS, query_groups, HEAD_SIZE), jnp.float32),
        layer_entries,
    )
    gathered_key_contributions = (
        key_contributions.reshape(sequence_length, KEY_VALUE_HEADS * HEAD_SIZE) * scale_of_scores
    )
    gathered_value_contributions = value_contributions.reshape(
        sequence_length, KEY_VALUE_HEADS * HEAD_SIZE
    )
    local_keys, value_mine = (
        lax.psum_scatter(
            gathered_key_contributions.astype(jnp.bfloat16), "seq", scatter_dimension=0, tiled=True
        ).astype(jnp.float32),
        lax.psum_scatter(
            gathered_value_contributions.astype(jnp.bfloat16),
            "seq",
            scatter_dimension=0,
            tiled=True,
        ).astype(jnp.float32),
    )
    dq_pre = apply_rotary(
        dquery.reshape(token_rows, QUERY_HEADS * HEAD_SIZE) * scale_of_scores,
        cosine_table,
        sine_table,
        QUERY_HEADS,
        -1.0,
    ).astype(jnp.bfloat16)
    key_gradient_unrotated = apply_rotary(
        local_keys, cosine_table, sine_table, KEY_VALUE_HEADS, -1.0
    ).astype(jnp.bfloat16)
    dv_pre = value_mine.astype(jnp.bfloat16)
    dnorm_one = (
        times_transpose(dq_pre, query_full)
        + times_transpose(key_gradient_unrotated, complete_keys)
        + times_transpose(dv_pre, value_full)
    )
    input_part, gain_one_term = norm_backward(inputs_f, scale_one, gain_one_f, dnorm_one)
    input_grad = (dresid + input_part)[None]
    query_term = outer_product(first_normalized, dq_pre)
    key_term = outer_product(first_normalized, key_gradient_unrotated)
    value_term = outer_product(first_normalized, dv_pre)
    first_gain_grad, query_grad, key_grad, value_grad, output_grad, second_gain_grad = (
        lax.psum_scatter(gain_one_term, ("seq", "tp"), scatter_dimension=0, tiled=True),
        lax.psum_scatter(query_term, ("seq", "tp"), scatter_dimension=0, tiled=True),
        lax.psum_scatter(key_term, ("seq", "tp"), scatter_dimension=0, tiled=True),
        lax.psum_scatter(value_term, ("seq", "tp"), scatter_dimension=0, tiled=True),
        lax.psum_scatter(output_term, ("seq", "tp"), scatter_dimension=0, tiled=True),
        lax.psum_scatter(gain_two_term, ("seq", "tp"), scatter_dimension=0, tiled=True),
    )
    return (
        layer_output,
        input_grad,
        first_gain_grad,
        query_grad,
        key_grad,
        value_grad,
        output_grad,
        second_gain_grad,
        gate_grad,
        up_grad,
        down_grad,
    )


MESH = pl.DeviceIdType.MESH
ANY = pl.ANY
HALF = HEAD_SIZE // 2
LANES = 128
SLOT = LANES // 2
f32 = jnp.float32
bf16 = jnp.bfloat16
VMEM_LIMIT = 62 << 20
COST = pl.CostEstimate(flops=1_000_000, transcendentals=0, bytes_accessed=100_000)


class Plane:
    def __init__(self, n, m):
        self.n, self.m, self.chips = n, m, n // 2
        self.s = lax.axis_index("seq")
        self.t = lax.axis_index("tp")
        self.q = self.s // 2
        self.c = lax.rem(self.s, 2)

        across = self.q + 1 - 2 * lax.rem(self.q, 2)
        along = lax.rem(self.q + 2, 4)
        self.to = across * (1 - self.c) + along * self.c
        self.fro = across * self.c + along * (1 - self.c)
        self.far = 3 - self.q
        self.order = (self.q, self.to, self.fro, self.far)

    def device(self, s):
        return (s, self.t)

    def same(self, chip):
        return (2 * chip + self.c, self.t)

    def number(self, k, other):
        c, q = self.c, self.q
        low, high = lax.rem(k, 2), k // 2
        dx = low * (1 - c) + high * c
        dy = high * (1 - c) + low * c
        x, y = lax.rem(q, 2), q // 2
        chip = 2 * (y + dy - 2 * y * dy) + x + dx - 2 * x * dx
        return 2 * chip + c + other * (1 - 2 * c)

    def sibling(self):
        return (2 * self.q + 1 - self.c, self.t)

    def ahead(self, k):
        return lax.rem(self.q + k, self.chips)

    def behind(self, k):
        return lax.rem(self.q + self.chips - k, self.chips)

    def seq_ahead(self, k):
        return lax.rem(self.s + k, self.n)

    def seq_behind(self, k):
        return lax.rem(self.s + self.n - k, self.n)

    def tp_ahead(self, k):
        return (self.s, lax.rem(self.t + k, self.m))

    def tp_behind(self, k):
        return lax.rem(self.t + self.m - k, self.m)


def greet(plane, with_tp):
    barrier = pltpu.get_barrier_semaphore()
    for k in range(1, plane.n):
        pl.semaphore_signal(
            barrier, inc=1, device_id=plane.device(plane.seq_ahead(k)), device_id_type=MESH
        )
    if with_tp:
        for k in range(1, plane.m):
            pl.semaphore_signal(barrier, inc=1, device_id=plane.tp_ahead(k), device_id_type=MESH)


def meet(plane, with_tp):
    count = plane.n - 1 + (plane.m - 1 if with_tp else 0)
    pl.semaphore_wait(pltpu.get_barrier_semaphore(), count)


def remote(src, dst, send, recv, device):
    return pltpu.make_async_remote_copy(
        src_ref=src,
        dst_ref=dst,
        send_sem=send,
        recv_sem=recv,
        device_id=device,
        device_id_type=MESH,
    )


class Gather:
    COPIES = 7

    def __init__(self, plane, src, dst_of, send, recv, local):
        to, fro, far, c = plane.to, plane.fro, plane.far, plane.c
        here = dst_of(plane.s)
        self.own = pltpu.make_async_copy(src, here, local)

        def block(chip):
            return dst_of(2 * chip + c)

        def copy(i, a, b, device):
            return remote(a, b, send.at[i], recv.at[i], device)

        sibling = plane.sibling()
        self.swap = copy(0, src, here, sibling)
        self.ahead = copy(1, src, here, plane.same(to))
        self.back = copy(2, src, here, plane.same(fro))
        self.relay = copy(3, block(fro), block(fro), plane.same(to))
        self.share = [
            copy(4, block(to), block(to), sibling),
            copy(5, block(fro), block(fro), sibling),
            copy(6, block(far), block(far), sibling),
        ]

    def start(self):
        self.back.start()
        self.ahead.start()

    def start_here(self):
        self.swap.start()
        self.own.start()

    def relay_near(self):
        self.back.wait_recv()
        self.relay.start()
        self.share[1].start()
        self.ahead.wait_recv()
        self.share[0].start()

    def relay_far(self):
        self.relay.wait_recv()
        self.share[2].start()

    def wait_sends(self):
        for copy in [self.swap, self.ahead, self.back, self.relay] + self.share:
            copy.wait_send()


class Gathers:
    def __init__(self, plane, src, dst_of, sems, local, pieces):
        rows = src.shape[0] // pieces
        self.parts = []
        for i in range(pieces):
            at = pl.ds(i * rows, rows)
            self.parts.append(
                Gather(
                    plane,
                    src.at[at],
                    lambda d, at=at: dst_of(d).at[at],
                    sems.at[i, 0],
                    sems.at[i, 1],
                    local.at[i],
                )
            )

    def start(self):
        for part in self.parts:
            part.start()
        for part in self.parts:
            part.start_here()

    def relay_near(self):
        for part in self.parts:
            part.relay_near()

    def relay_far(self):
        for part in self.parts:
            part.relay_far()

    def wait_own(self):
        for part in self.parts:
            part.own.wait()

    def wait_swap(self):
        for part in self.parts:
            part.swap.wait_recv()

    def wait_share(self, i):
        for part in self.parts:
            part.share[i].wait_recv()

    def wait_sends(self):
        for part in self.parts:
            part.wait_sends()

    def finish(self):
        self.wait_own()
        self.wait_swap()
        for i in range(3):
            self.wait_share(i)
        self.wait_sends()

    @staticmethod
    def scratch(pieces):
        return [
            pltpu.SemaphoreType.DMA((pieces, 2, Gather.COPIES)),
            pltpu.SemaphoreType.DMA((pieces,)),
        ]


class Chain:
    def __init__(self, plane, mine, slot_of, sems):
        self.plane, self.mine, self.slot_of, self.sems = plane, mine, slot_of, sems

    def copy(self, way, hop, to):
        plane, row = self.plane, 0 if way > 0 else 2
        slot = self.slot_of(plane.t - way * hop)
        return remote(
            self.mine if hop == 0 else slot,
            slot,
            self.sems.at[row, hop],
            self.sems.at[row + 1, hop],
            (plane.s, to),
        )

    def inside(self, way, hop):
        t, m = self.plane.t, self.plane.m
        holds = t >= hop if way > 0 else t < m - hop
        passes = t < m - 1 if way > 0 else t > 0
        return holds, passes

    def start(self):
        self.pass_on(0)

    def pass_on(self, hop):
        for way in (1, -1):
            holds, passes = self.inside(way, hop)

            @pl.when(holds & passes)
            def _(way=way):
                self.copy(way, hop, self.plane.t + way).start()

    def step(self, hop):
        plane = self.plane
        for way in (1, -1):
            holds, _ = self.inside(way, hop)

            @pl.when(holds)
            def _(way=way):
                row = 0 if way > 0 else 2
                slot = self.slot_of(plane.t - way * hop)
                remote(
                    slot,
                    slot,
                    self.sems.at[row, hop - 1],
                    self.sems.at[row + 1, hop - 1],
                    (plane.s, plane.t - way),
                ).wait_recv()

        if hop < plane.m - 1:
            self.pass_on(hop)

    def wait_sends(self):
        for hop in range(self.plane.m - 1):
            for way in (1, -1):
                holds, passes = self.inside(way, hop)

                @pl.when(holds & passes)
                def _(way=way, hop=hop):
                    self.copy(way, hop, self.plane.t + way).wait_send()


class Scatter:
    def __init__(self, plane, parts, total, add, own, got, sems, loc):
        t = plane.t
        self.plane, self.total = plane, total
        self.add, self.own, self.got, self.loc = add, own, got, loc
        self.inner = (t == 1) | (t == 2)
        self.outer = (t == 0) | (t == 3)
        up = t // 2
        self.near = t + 1 - 2 * lax.rem(t, 2)
        self.far_outer = 3 - 3 * up
        self.far_inner = 2 - up
        self.parts, self.sems = parts, sems

    def copy(self, i, j, src, dst, to):
        return remote(
            src, dst, self.sems.at[0, i, j], self.sems.at[1, i, j], (self.plane.s, to)
        )

    def first(self, i, j):
        chunk = (self.far_outer, self.far_inner, self.near)[i]
        dst = self.got.at[0, j] if i == 2 else self.add.at[i, j]
        return self.copy(i, j, self.parts.at[chunk, j], dst, self.near)

    def back(self, j):
        return self.copy(2, j, self.parts.at[self.near, j], self.got.at[0, j], self.near)

    def sent(self, i, j):
        to = self.far_inner if i else self.far_outer
        return remote(
            self.add.at[i, j],
            self.got.at[1, j],
            self.sems.at[0, 3 + i, j],
            self.sems.at[1, 3, j],
            (self.plane.s, to),
        )

    def load(self, i, j):
        chunk = (self.far_outer, self.far_inner, self.plane.t)[i]
        dst = self.total.at[j] if i == 2 else self.own.at[i, j]
        return pltpu.make_async_copy(self.parts.at[chunk, j], dst, self.loc.at[i, j])

    def start(self):
        for j in range(2):
            self.load(2, j).start()

        @pl.when(self.outer)
        def _():
            for i in range(3):
                for j in range(2):
                    self.first(i, j).start()

        @pl.when(self.inner)
        def _():
            for j in range(2):
                self.back(j).start()
            for i in range(2):
                for j in range(2):
                    self.load(i, j).start()

    def relay(self, i, j):
        @pl.when(self.inner)
        def _():
            self.first(i, j).wait_recv()
            self.load(i, j).wait()
            add, own = self.add, self.own

            def both(at):
                value = add[i, j, at, :].astype(f32) + own[i, j, at, :].astype(f32)
                add[i, j, at, :] = value.astype(bf16)

            in_tiles(add.shape[2], both, 256)
            self.sent(i, j).start()

    def finish(self):
        total, got = self.total, self.got
        for j in range(2):
            self.load(2, j).wait()
            self.back(j).wait_recv()
            self.sent(0, j).wait_recv()

            def sums(at, j=j):
                value = total[j, at, :].astype(f32) + got[0, j, at, :].astype(f32)
                total[j, at, :] = (value + got[1, j, at, :].astype(f32)).astype(bf16)

            in_tiles(total.shape[1], sums, 256)

        @pl.when(self.outer)
        def _():
            for i in range(3):
                for j in range(2):
                    self.first(i, j).wait_send()

        @pl.when(self.inner)
        def _():
            for j in range(2):
                self.back(j).wait_send()
                for i in range(2):
                    self.sent(i, j).wait_send()

    @staticmethod
    def scratch(shape):
        return [
            pltpu.VMEM((2,) + shape, bf16),
            pltpu.VMEM((2,) + shape, bf16),
            pltpu.VMEM((2,) + shape, bf16),
            pltpu.SemaphoreType.DMA((2, 5, 2)),
            pltpu.SemaphoreType.DMA((3, 2)),
        ]


def fan(plane, src_of, dst_of, send, recv):
    copies = []
    for k in range(1, plane.m):
        device = plane.tp_ahead(k)
        copies.append(
            remote(src_of(device[1]), dst_of(plane.t), send.at[k - 1], recv.at[k - 1], device)
        )
    return copies


def exchange(plane, src_of, dst_of, send, recv, local):
    own = pltpu.make_async_copy(src_of(plane.s), dst_of(plane.s), local)
    copies = []
    for k in range(1, plane.n):
        peer = plane.seq_ahead(k)
        copies.append(
            remote(
                src_of(peer), dst_of(plane.s), send.at[k - 1], recv.at[k - 1], plane.device(peer)
            )
        )
    return [own] + copies


TILE = 16


def in_tiles(rows, body, tile=TILE):
    def one(i, carry):
        body(pl.ds(pl.multiple_of(i * tile, tile), tile))
        return carry

    lax.fori_loop(0, rows // tile, one, 0)


class Reduce:
    SLOTS = (4, 4, 3)

    THEIRS = (0, 2, 1, 3)

    def __init__(self, plane, part_of, pair, near, far, sems, loc, stage=None):
        c = plane.c
        self.pair, self.near, self.far = pair, near, far
        self.rows = pair.shape[1]
        self.swaps, self.loads = {}, {}
        for k in range(4):
            mine = self.THEIRS[k]
            chip = plane.order[mine]
            source = part_of(2 * chip + 1 - c) if stage is None else stage.at[mine]
            self.swaps[k] = remote(
                source, near.at[k], sems.at[0, k], sems.at[1, k], plane.sibling()
            )
            if stage is None:
                self.loads[k] = pltpu.make_async_copy(
                    part_of(2 * plane.order[k] + c), pair.at[k], loc.at[k]
                )

        def out(i, k, chip):
            return remote(
                pair.at[k], far.at[i], sems.at[2, i], sems.at[3, i], plane.same(chip)
            )

        self.out = [out(0, 3, plane.to), out(1, 1, plane.to), out(2, 2, plane.fro)]

    def start(self, *which):
        for k in which:
            self.swaps[k].start()
            self.loads[k].start()

    def landed(self, k):
        self.swaps[k].wait()
        if self.loads:
            self.loads[k].wait()

    def join(self, k):
        pair, near = self.pair, self.near
        self.landed(k)

        def add(at):
            both = pair[k, at, :].astype(f32) + near[k, at, :].astype(f32)
            pair[k, at, :] = both.astype(bf16)

        in_tiles(self.rows, add)

    def send_to(self):
        self.join(3)
        self.out[0].start()
        self.join(1)
        self.out[1].start()

    def ready(self):
        self.landed(2)

    def send_fro(self):
        pair, near, far = self.pair, self.near, self.far
        self.out[0].wait_recv()

        def add(at):
            both = pair[2, at, :].astype(f32) + near[2, at, :].astype(f32)
            pair[2, at, :] = (both + far[0, at, :].astype(f32)).astype(bf16)

        in_tiles(self.rows, add)
        self.out[2].start()

    def first(self, total, more=None):
        pair, near = self.pair, self.near
        self.landed(0)

        def add(at):
            value = pair[0, at, :].astype(f32) + near[0, at, :].astype(f32)
            total[at, :] = value if more is None else value + more[at, :].astype(f32)

        in_tiles(self.rows, add)

    def finish(self, total, out=None):
        far = self.far
        out = total if out is None else out
        self.out[0].wait_send()
        self.out[1].wait()
        self.out[2].wait()

        def add(at):
            value = total[at, :] + far[1, at, :].astype(f32) + far[2, at, :].astype(f32)
            out[at, :] = value.astype(out.dtype)

        in_tiles(self.rows, add)

    @staticmethod
    def scratch(rows, width):
        return [pltpu.VMEM((slots, rows, width), bf16) for slots in Reduce.SLOTS] + [
            pltpu.SemaphoreType.DMA((4, 4)),
            pltpu.SemaphoreType.DMA((4,)),
        ]


def last_body(
    n, m, dqkv_in, w_in, norm_t, ffn, downs, wo, vec,
    total, ffn_out, qkv_out, wo_out, vec_out,
    dqkv, w, down_here, down_sum, narrow, pair, near, far, sr, lr, stage, norms, mine, got, summed, sems, st, loc,
):
    plane = Plane(n, m)
    greet(plane, True)
    loads = [
        pltpu.make_async_copy(a, b, loc.at[5 + i])
        for i, (a, b) in enumerate(
            ((dqkv_in, dqkv), (w_in, w), (downs, down_here))
        )
    ]
    load = pltpu.make_async_copy(norm_t, norms, loc.at[0])
    for copy in loads + [load]:
        copy.start()
    narrow[...] = lanes_of_columns(narrow.shape, 1)
    meet(plane, True)
    rows, width = ffn_out.shape[1], ffn.shape[2]
    across = fan(plane, lambda t: wo.at[t], lambda t: wo_out.at[t], st.at[1, 0], st.at[1, 1])
    across += fan(plane, lambda t: vec.at[t], lambda t: vec_out.at[t], st.at[2, 0], st.at[2, 1])
    across += [
        pltpu.make_async_copy(wo.at[plane.t], wo_out.at[plane.t], loc.at[1]),
        pltpu.make_async_copy(vec.at[plane.t], vec_out.at[plane.t], loc.at[2]),
    ]
    for copy in across:
        copy.start()
    a = exchange(
        plane,
        lambda i: ffn.at[:, pl.ds(pl.multiple_of(i * rows, rows), rows), :],
        lambda i: ffn_out.at[
            pl.ds(0, 2), :, pl.ds(pl.multiple_of(i * width, width), width)
        ],
        sems.at[0, 0],
        sems.at[0, 1],
        loc.at[3],
    )
    a_down = exchange(
        plane,
        lambda i: down_sum.at[pl.ds(pl.multiple_of(i * rows, rows), rows), :],
        lambda i: ffn_out.at[2, :, pl.ds(pl.multiple_of(i * width, width), width)],
        sems.at[2, 0],
        sems.at[2, 1],
        loc.at[10],
    )
    for copy in a:
        copy.start()
    reduce = Reduce(plane, None, pair, near, far, sr, lr, stage)
    tokens = pair.shape[1]
    for copy in loads[:2]:
        copy.wait()

    def blocks(it, carry):
        k = 3 - it // 2
        other = 1 - lax.rem(it, 2)
        b = plane.number(k, other)
        here = pl.ds(pl.multiple_of(b * tokens, tokens), tokens)
        part = lax.dot_general(dqkv[here, :], w[...], NT, preferred_element_type=f32).astype(bf16)

        @pl.when(other == 0)
        def _():
            pair[k] = part

        @pl.when(other == 1)
        def _():
            stage[k] = part

        for kk in range(4):

            @pl.when(it == 2 * (3 - kk))
            def _(kk=kk):
                reduce.swaps[Reduce.THEIRS[kk]].start()

        return carry

    lax.fori_loop(0, n, blocks, 0)
    reduce.send_to()
    loads[2].wait()

    def add_down(at):
        value = down_here[0, at, :].astype(f32)
        for t in range(1, m):
            value = value + down_here[t, at, :].astype(f32)
        down_sum[at, :] = value.astype(bf16)

    in_tiles(down_sum.shape[0], add_down)
    for copy in a_down:
        copy.start()
    load.wait()
    strip = summed.shape[1]

    def weight_grads(s, carry):
        at = pl.ds(pl.multiple_of(s * m * strip, m * strip), m * strip)
        value = jnp.dot(norms[at, :], dqkv[...], preferred_element_type=f32).astype(bf16)
        value = jnp.dot(value, narrow[...], preferred_element_type=f32).astype(bf16)
        for t in range(m):
            mine[s, t] = value[t * strip : (t + 1) * strip]
        return carry

    lax.fori_loop(0, n, weight_grads, 0)
    over = fan(plane, lambda t: mine.at[:, t], lambda t: got.at[t], st.at[0, 0], st.at[0, 1])
    for copy in over:
        copy.start()
    reduce.ready()
    reduce.first(total)
    reduce.send_fro()
    for copy in over:
        copy.wait()

    def add(s, carry):
        value = mine[s, plane.t].astype(f32)
        for k in range(1, m):
            value = value + got[plane.tp_behind(k), s].astype(f32)
        summed[s] = value.astype(bf16)
        return carry

    lax.fori_loop(0, n, add, 0)
    b = exchange(
        plane,
        lambda i: summed.at[i],
        lambda i: qkv_out.at[i],
        sems.at[1, 0],
        sems.at[1, 1],
        loc.at[4],
    )
    for copy in b:
        copy.start()
    reduce.finish(total)
    for copy in a + a_down + b + across:
        copy.wait()


def last(n, m, dqkv, w, norm_t, ffn, downs, wo, vec, ident):
    width, length = norm_t.shape
    tokens = length // n
    cols = w.shape[1] // SLOT * HALF
    strip = width // (n * m)
    vmem = pl.BlockSpec(memory_space=pltpu.VMEM)
    hbm = pl.BlockSpec(memory_space=ANY)
    return pl.pallas_call(
        functools.partial(last_body, n, m),
        out_shape=(
            jax.ShapeDtypeStruct((tokens, width), f32),
            jax.ShapeDtypeStruct((3, ffn.shape[1] // n, ffn.shape[2] * n), ffn.dtype),
            jax.ShapeDtypeStruct((n, strip, cols), bf16),
            jax.ShapeDtypeStruct(wo.shape, wo.dtype),
            jax.ShapeDtypeStruct(vec.shape, vec.dtype),
        ),
        in_specs=[hbm] * 7,
        out_specs=[vmem] + [hbm] * 4,
        scratch_shapes=[
            pltpu.VMEM(dqkv.shape, bf16),
            pltpu.VMEM(w.shape, bf16),
            pltpu.VMEM(downs.shape, bf16),
            pltpu.VMEM(downs.shape[1:], bf16),
            pltpu.VMEM((w.shape[1], cols), bf16),
        ]
        + Reduce.scratch(tokens, width)
        + [
            pltpu.VMEM((4, tokens, width), bf16),
            pltpu.VMEM((width, length), bf16),
            pltpu.VMEM((n, m, strip, cols), bf16),
            pltpu.VMEM((m, n, strip, cols), bf16),
            pltpu.VMEM((n, strip, cols), bf16),
            pltpu.SemaphoreType.DMA((3, 2, n - 1)),
            pltpu.SemaphoreType.DMA((3, 2, m - 1)),
            pltpu.SemaphoreType.DMA((11,)),
        ],
        compiler_params=pltpu.CompilerParams(
            collective_id=ident, has_side_effects=True, vmem_limit_bytes=VMEM_LIMIT
        ),
        cost_estimate=COST,
        name="last",
    )(dqkv, w, norm_t, ffn, downs, wo, vec)


def column(row):
    return jnp.broadcast_to(row, (8, row.shape[1])).T[:, :1]


def lanes_of_columns(shape, of):
    column = lax.broadcasted_iota(jnp.int32, shape, of).astype(f32)
    lane = lax.broadcasted_iota(jnp.int32, shape, 1 - of).astype(f32)
    half = jnp.floor((column + 0.5) * (1.0 / HALF))
    return jnp.where(lane == column + half * (SLOT - HALF), 1.0, 0.0).astype(bf16)


def gain_row(tiles, which, strip):
    stacked = tiles.reshape(-1, LANES).astype(bf16)
    count = stacked.shape[0] // 8
    shape = (LANES, count * strip)
    lane = lax.broadcasted_iota(jnp.int32, shape, 1).astype(f32)
    owner = jnp.floor((lane + 0.5) * (1.0 / strip))
    inside = lane - owner * strip
    pick = lax.broadcasted_iota(jnp.int32, shape, 0).astype(f32) == inside
    spread_out = jnp.dot(
        stacked, jnp.where(pick, 1.0, 0.0).astype(bf16), preferred_element_type=f32
    )
    shape = spread_out.shape
    lane = lax.broadcasted_iota(jnp.int32, shape, 1).astype(f32)
    owner = jnp.floor((lane + 0.5) * (1.0 / strip))
    row = lax.broadcasted_iota(jnp.int32, shape, 0).astype(f32)
    mine = row == owner * 8.0 + which
    return jnp.sum(jnp.where(mine, spread_out, 0.0), axis=0, keepdims=True)


def entry_body(
    n, m, heads, strip, x, doc_ids, positions, wq, wk, wv, one, two, wg, wu, wd, wo, inverse,
    norm_t, q, k, v, cosine, sine, w, gain_one, gain_two, docs, ffn, down, wo_z,
    blocks, norms, turned, places_all, w_all, gains_all, q_here, k_here, v_here, cos_here, sin_here,
    places, wqkv, gains, widen, sx, lx, rem, sz, sn, loc,
):
    plane = Plane(n, m)
    greet(plane, True)
    tokens = x.shape[0]
    start = 0
    for weight in (wq, wk, wv):
        each = weight.shape[1] // n
        for i in range(n):
            wqkv[i, :, start : start + each] = weight[:, i * each : (i + 1) * each]
        start += each
    gains[...] = jnp.zeros_like(gains)
    gains[0:1, :strip] = one[...].astype(f32)
    gains[1:2, :strip] = two[...].astype(f32)
    places[0:1, :] = doc_ids[...]
    places[1:2, :] = positions[...]
    meet(plane, True)
    gather = Gathers(plane, x, lambda i: blocks.at[i], sx, lx, 1)
    first = []
    for i, (src, dst) in enumerate(((gains, gains_all), (wqkv, w_all))):
        first += exchange(
            plane,
            lambda s, src=src, i=i: src.at[s] if i else src,
            lambda s, dst=dst: dst.at[s, plane.t],
            rem.at[i, 0],
            rem.at[i, 1],
            loc.at[1 + i],
        )
    few = exchange(
        plane, lambda i: places, lambda i: places_all.at[i], rem.at[2, 0], rem.at[2, 1], loc.at[3]
    )
    for copy in first + few:
        copy.start()
    gather.start()
    across = []
    for i, ref in enumerate((gains_all, w_all)):

        def slot(t, ref=ref):
            return ref.at[:, plane.t]

        across.append(fan(plane, slot, slot, sz.at[i, 0], sz.at[i, 1]))
    across.append(fan(plane, lambda t: wo, lambda t: wo_z.at[t], sz.at[2, 0], sz.at[2, 1]))
    own_wo = pltpu.make_async_copy(wo, wo_z.at[plane.t], loc.at[4])
    own_wo.start()
    for copy in first:
        copy.wait()
    for copy in across[0] + across[1]:
        copy.start()
    widen[...] = lanes_of_columns(widen.shape, 0)
    moves = []
    width, rows = wg.shape[1] // n, wg.shape[0]
    for j, weight in enumerate((wg, wu, wd)):
        moves += exchange(
            plane,
            lambda i, weight=weight: weight.at[:, pl.ds(pl.multiple_of(i * width, width), width)],
            lambda i, dst=ffn.at[j] if j < 2 else down: dst.at[
                pl.ds(pl.multiple_of(i * rows, rows), rows), :
            ],
            rem.at[3 + j, 0],
            rem.at[3 + j, 1],
            loc.at[5 + j],
        )
    for copy in few + across[0]:
        copy.wait()
    tiles = gains_all[...]
    gain_one[...] = gain_row(tiles, 0, strip)
    gain_two[...] = gain_row(tiles, 1, strip)
    gather.wait_own()

    def number(it):
        return plane.number(it // 2, lax.rem(it, 2))

    def store(it, at):
        span = pl.ds(pl.multiple_of(number(it) * tokens, tokens), tokens)
        return pltpu.make_async_copy(turned.at[at], norm_t.at[:, span], sn.at[at])

    def normalize(it, carry):
        b = number(it)
        at = lax.rem(it, 2)

        @pl.when(it == 1)
        def _():
            gather.wait_swap()

        @pl.when(it == 2)
        def _():
            gather.relay_near()

        @pl.when(it == 3)
        def _():
            gather.wait_share(1)

        @pl.when(it == 5)
        def _():
            gather.wait_share(0)

        @pl.when(it == 6)
        def _():
            gather.relay_far()
            for copy in moves + across[2]:
                copy.start()

        @pl.when(it == 7)
        def _():
            gather.wait_share(2)

        @pl.when(it >= 2)
        def _():
            store(it - 2, at).wait()

        value = blocks[b].astype(f32)
        scale = lax.rsqrt(jnp.mean(value * value, axis=1, keepdims=True) + norm_epsilon)
        low = (value * scale * gain_one[...]).astype(bf16)
        norms[b] = low
        turned[at] = low.T
        store(it, at).start()
        here = pl.ds(pl.multiple_of(b * tokens, tokens), tokens)
        docs[:, here] = places_all[b, 0:1, :]
        angles = column(places_all[b, 1:2, :].astype(f32)) * inverse[...]
        lanes = lax.broadcasted_iota(jnp.int32, angles.shape, 1)
        sin = jnp.sin(angles)
        cos_here[here, :] = jnp.cos(angles)
        sin_here[here, :] = jnp.where(lanes < SLOT, -sin, sin)
        return carry

    lax.fori_loop(0, n, normalize, 0)
    outs = [
        pltpu.make_async_copy(cos_here, cosine, loc.at[8]),
        pltpu.make_async_copy(sin_here, sine, loc.at[9]),
        pltpu.make_async_copy(q_here, q, loc.at[10]),
        pltpu.make_async_copy(k_here, k, loc.at[11]),
        pltpu.make_async_copy(v_here, v, loc.at[12]),
    ]
    for copy in outs[:2]:
        copy.start()
    for copy in across[1]:
        copy.wait()

    def widened(s, carry):
        at = pl.ds(pl.multiple_of(s * m * strip, m * strip), m * strip)
        narrow = w_all[s].reshape(m * strip, w_all.shape[3])
        w[at, :] = jnp.dot(narrow, widen[...], preferred_element_type=f32).astype(bf16)
        return carry

    lax.fori_loop(0, n, widened, 0)

    def project(b, carry):
        here = pl.ds(pl.multiple_of(b * tokens, tokens), tokens)
        out = jnp.dot(norms[b], w[...], preferred_element_type=f32)
        cos, sin = cos_here[here, :], sin_here[here, :]
        for h in range(heads + 1):
            part = out[:, h * LANES : (h + 1) * LANES]
            rotated = (part * cos + pltpu.roll(part, SLOT, 1) * sin).astype(bf16)
            if h < heads:
                q_here[h, here, :] = rotated
            else:
                k_here[here, :] = rotated
        v_here[here, :] = out[:, (heads + 1) * LANES :].astype(bf16)
        return carry

    lax.fori_loop(0, n, project, 0)
    for copy in outs[2:]:
        copy.start()
    gather.wait_sends()
    store(n - 2, 0).wait()
    store(n - 1, 1).wait()
    own_wo.wait()
    for copy in across[2] + moves + outs:
        copy.wait()


def entry(n, m, heads, x, docs, positions, wq, wk, wv, one, two, wg, wu, wd, wo, inverse, ident):
    tokens, width = x.shape
    length = n * tokens
    strip = wq.shape[0]
    each = (wq.shape[1] + wk.shape[1] + wv.shape[1]) // n
    wide = each // HALF * SLOT
    rows, cols = wg.shape
    vmem = pl.BlockSpec(memory_space=pltpu.VMEM)
    hbm = pl.BlockSpec(memory_space=ANY)
    return pl.pallas_call(
        functools.partial(entry_body, n, m, heads, strip),
        out_shape=(
            jax.ShapeDtypeStruct((width, length), bf16),
            jax.ShapeDtypeStruct((heads, length, LANES), bf16),
            jax.ShapeDtypeStruct((length, LANES), bf16),
            jax.ShapeDtypeStruct((length, LANES), bf16),
            jax.ShapeDtypeStruct((length, LANES), f32),
            jax.ShapeDtypeStruct((length, LANES), f32),
            jax.ShapeDtypeStruct((width, wide), bf16),
            jax.ShapeDtypeStruct((1, width), f32),
            jax.ShapeDtypeStruct((1, width), f32),
            jax.ShapeDtypeStruct((1, length), jnp.int32),
            jax.ShapeDtypeStruct((2, rows * n, cols // n), wg.dtype),
            jax.ShapeDtypeStruct((rows * n, cols // n), wg.dtype),
            jax.ShapeDtypeStruct((m,) + wo.shape, wo.dtype),
        ),
        in_specs=[hbm] + [vmem] * 7 + [hbm] * 4 + [vmem],
        out_specs=[hbm] * 6 + [vmem] * 4 + [hbm] * 3,
        scratch_shapes=[
            pltpu.VMEM((n, tokens, width), bf16),
            pltpu.VMEM((n, tokens, width), bf16),
            pltpu.VMEM((2, width, tokens), bf16),
            pltpu.VMEM((n, 2, tokens), jnp.int32),
            pltpu.VMEM((n, m, strip, each), bf16),
            pltpu.VMEM((n, m, 8, LANES), f32),
            pltpu.VMEM((heads, length, LANES), bf16),
            pltpu.VMEM((length, LANES), bf16),
            pltpu.VMEM((length, LANES), bf16),
            pltpu.VMEM((length, LANES), f32),
            pltpu.VMEM((length, LANES), f32),
            pltpu.VMEM((2, tokens), jnp.int32),
            pltpu.VMEM((n, strip, each), bf16),
            pltpu.VMEM((8, LANES), f32),
            pltpu.VMEM((each, wide), bf16),
            *Gathers.scratch(1),
            pltpu.SemaphoreType.DMA((6, 2, n - 1)),
            pltpu.SemaphoreType.DMA((3, 2, m - 1)),
            pltpu.SemaphoreType.DMA((2,)),
            pltpu.SemaphoreType.DMA((13,)),
        ],
        compiler_params=pltpu.CompilerParams(
            collective_id=ident, has_side_effects=True, vmem_limit_bytes=VMEM_LIMIT
        ),
        cost_estimate=COST,
        name="entry",
    )(x, docs, positions, wq, wk, wv, one, two, wg, wu, wd, wo, inverse)


BLOCK = 512
NT = (((1,), (1,)), ((), ()))
LOG2E = 1.4426950408889634


def allowed_block(first_key, first_query, begin, causal):
    keys = first_key + lax.broadcasted_iota(jnp.int32, (BLOCK, BLOCK), 0)
    ok = keys >= begin
    if causal:
        queries = first_query + lax.broadcasted_iota(jnp.int32, (BLOCK, BLOCK), 1)
        ok = ok & (keys <= queries)
    return ok


def begins(docs):
    begin = jnp.zeros(docs.shape, jnp.int32)
    for d in range(3):
        count = jnp.sum((docs == d).astype(f32), axis=1, keepdims=True).astype(jnp.int32)
        begin = begin + jnp.where(docs > d, count, 0)
    return begin


def spread_rows(wo, wo_here):
    halves, filled, width = wo.shape
    for i in range(halves):
        wo_here[i * SLOT : i * SLOT + filled, :] = wo[i]
        wo_here[i * SLOT + filled : (i + 1) * SLOT, :] = jnp.zeros((SLOT - filled, width), bf16)


def attend_body(
    n, m, factor, q, k, v, docs, wo, go, x, gain, ffn,
    o_out, lse, start, low_out, go_all, resid, norm, ffn_all,
    o, low, vt, top, total, acc, wo_here, go_here,
    pair, near, far, sr, lr, stage, sg, lg, sz, loc,
):
    plane = Plane(n, m)
    rows = x.shape[0]
    heads = q.shape[0]
    greet(plane, True)
    gather = Gathers(plane, go, lambda i: go_here.at[i], sg, lg, 2)
    reduce = Reduce(plane, None, pair, near, far, sr, None, stage)
    spread_rows(wo, wo_here)
    vt[...] = v[...].T
    start[...] = begins(docs[...])
    meet(plane, True)
    gather.start()
    chain = Chain(plane, ffn, lambda t: ffn_all.at[t], sz)
    chain.start()
    own_ffn = pltpu.make_async_copy(ffn, ffn_all.at[plane.t], loc.at[3])
    own_ffn.start()

    def chips(step, carry):
        kk = 3 - step
        i = plane.number(kk, 0) // 2
        here = pl.ds(pl.multiple_of(i * BLOCK, BLOCK), BLOCK)
        begin = start[:, here]

        def head(h, carry):
            query = q[h, here, :]
            top[...] = jnp.full_like(top, mask_fill_value)
            total[...] = jnp.zeros_like(total)
            acc[...] = jnp.zeros_like(acc)

            def keys(j, causal):
                at = pl.ds(pl.multiple_of(j * BLOCK, BLOCK), BLOCK)
                raw = lax.dot_general(k[at, :], query, NT, preferred_element_type=f32)
                ok = allowed_block(j * BLOCK, i * BLOCK, begin, causal)
                scores = jnp.where(ok, raw * factor, mask_fill_value)
                new_top = jnp.maximum(top[...], jnp.max(scores, axis=0, keepdims=True))
                weights = jnp.exp2(scores - new_top)
                keep = jnp.exp2(top[...] - new_top)
                total[...] = total[...] * keep + jnp.sum(weights, axis=0, keepdims=True)
                acc[...] = acc[...] * keep + jnp.dot(
                    vt[:, at], weights.astype(bf16), preferred_element_type=f32
                )
                top[...] = new_top

            def loop(j, carry):
                keys(j, False)
                return carry

            lax.fori_loop(0, i, loop, 0)
            keys(i, True)
            out = (acc[...] / total[...]).T
            o[h, here, :] = out
            low[here, pl.ds(pl.multiple_of(h * LANES, LANES), LANES)] = out.astype(bf16)
            lse[h, :, here] = top[...] + jnp.log2(total[...])
            return carry

        lax.fori_loop(0, heads, head, 0)

        @pl.when(step == 1)
        def _():
            reduce.join(3)
            reduce.out[0].start()

        @pl.when(step == 3)
        def _():
            reduce.join(1)
            reduce.out[1].start()

        for other in (1, 0):
            b = plane.number(kk, other)
            at = pl.ds(pl.multiple_of(b * rows, rows), rows)
            part = jnp.dot(low[at, :], wo_here[...], preferred_element_type=f32).astype(bf16)
            if other:
                stage[kk] = part
                for which in range(4):

                    @pl.when(kk == which)
                    def _(which=which):
                        reduce.swaps[Reduce.THEIRS[which]].start()

            else:
                pair[kk] = part
        return carry

    lax.fori_loop(0, 4, chips, 0)
    outs = [
        pltpu.make_async_copy(o, o_out, loc.at[0]),
        pltpu.make_async_copy(low, low_out, loc.at[1]),
    ]
    for copy in outs:
        copy.start()
    gather.relay_near()
    chain.step(1)
    reduce.ready()
    reduce.first(resid, x)
    reduce.send_fro()
    for hop in range(2, m - 1):
        chain.step(hop)
    gather.relay_far()
    reduce.finish(resid)

    def normalize(at):
        value = resid[at, :]
        scale = lax.rsqrt(jnp.mean(value * value, axis=1, keepdims=True) + norm_epsilon)
        norm[at, :] = (value * scale * gain[...]).astype(bf16)

    in_tiles(rows, normalize)
    gather.finish()
    outs.append(pltpu.make_async_copy(go_here, go_all, loc.at[2]))
    outs[-1].start()
    chain.step(m - 1)
    chain.wait_sends()
    own_ffn.wait()
    for copy in outs:
        copy.wait()


def attend(n, m, factor, q, k, v, docs, wo, go, x, gain, ffn, ident):
    heads, length, _ = q.shape
    rows, width = x.shape
    hbm = pl.BlockSpec(memory_space=ANY)
    vmem = pl.BlockSpec(memory_space=pltpu.VMEM)
    return pl.pallas_call(
        functools.partial(attend_body, n, m, factor),
        out_shape=(
            jax.ShapeDtypeStruct((heads, length, LANES), f32),
            jax.ShapeDtypeStruct((heads, 1, length), f32),
            jax.ShapeDtypeStruct((1, length), jnp.int32),
            jax.ShapeDtypeStruct((length, heads * LANES), bf16),
            jax.ShapeDtypeStruct((n,) + go.shape, go.dtype),
            jax.ShapeDtypeStruct((rows, width), f32),
            jax.ShapeDtypeStruct((rows, width), bf16),
            jax.ShapeDtypeStruct((m,) + ffn.shape, bf16),
        ),
        in_specs=[vmem] * 5 + [hbm] + [vmem] * 2 + [hbm],
        out_specs=[hbm, vmem, vmem, hbm, hbm, vmem, vmem, hbm],
        scratch_shapes=[
            pltpu.VMEM((heads, length, LANES), f32),
            pltpu.VMEM((length, heads * LANES), bf16),
            pltpu.VMEM((LANES, length), bf16),
            pltpu.VMEM((1, BLOCK), f32),
            pltpu.VMEM((1, BLOCK), f32),
            pltpu.VMEM((LANES, BLOCK), f32),
            pltpu.VMEM((heads * LANES, width), bf16),
            pltpu.VMEM((n,) + go.shape, go.dtype),
        ]
        + Reduce.scratch(rows, width)
        + [pltpu.VMEM((4, rows, width), bf16)]
        + Gathers.scratch(2)
        + [pltpu.SemaphoreType.DMA((4, m)), pltpu.SemaphoreType.DMA((4,))],
        compiler_params=pltpu.CompilerParams(
            collective_id=ident, has_side_effects=True, vmem_limit_bytes=VMEM_LIMIT
        ),
        cost_estimate=COST,
        name="attend",
    )(q, k, v, docs, wo, go, x, gain, ffn)


def attend_back_body(
    n, m, factor, scale, q_in, k_in, v_in, o_in, lse, begin, cos_in, sin_in, low_in,
    hid_in, down_in, ffn, wo, dnorm, resid, grad, gain,
    out, layer, terms, dresid, gain_out, ffn_sum,
    q, k, v, o, cosine, sine, low, kt, dqt, dk, dv, delta, go, every, dbranch, wo_here,
    hid_low, w_down, stage, pair, near, far, sr, lr, held, gain_sum, gain_cut, gain_got,
    sums, add, own, got, ss, ls, sg, lg, sv, loc,
):
    plane = Plane(n, m)
    heads, length, _ = q.shape
    rows, width = dnorm.shape
    strip = gain_out.shape[2]
    loads = [
        pltpu.make_async_copy(a, b, loc.at[i])
        for i, (a, b) in enumerate(
            (
                (q_in, q), (k_in, k), (v_in, v), (o_in, o),
                (cos_in, cosine), (sin_in, sine), (low_in, low),
            )
        )
    ]
    for copy in loads:
        copy.start()
    greet(plane, True)
    moves = [
        pltpu.make_async_copy(hid_in, hid_low, loc.at[8]),
        pltpu.make_async_copy(down_in, w_down, loc.at[9]),
    ]
    for copy in moves:
        copy.start()
    one = Reduce(plane, None, pair, near, far, sr, None, stage)
    gather = Gathers(plane, dbranch, lambda i: every.at[i], sg, lg, 2)
    gain_copies = exchange(
        plane, lambda i: gain_cut.at[i], lambda i: gain_got.at[i], sv.at[0], sv.at[1], loc.at[7]
    )
    gain_sum[...] = jnp.zeros_like(gain_sum)

    def into_branch(at):
        value, up = resid[at, :], dnorm[at, :]
        scale_two = lax.rsqrt(jnp.mean(value * value, axis=1, keepdims=True) + norm_epsilon)
        inner = gain[...] * up
        moment = jnp.mean(value * inner, axis=1, keepdims=True)
        turned = value * scale_two
        got = (
            grad[at, :].astype(f32) + scale_two * inner - turned * (scale_two * scale_two * moment)
        )
        dresid[at, :] = got
        dbranch[at, :] = got.astype(bf16)
        gain_sum[...] += up * turned

    in_tiles(rows, into_branch)
    meet(plane, True)
    gather.start()
    scatter = Scatter(plane, ffn, sums, add, own, got, ss, ls)
    scatter.start()
    total_gain = jnp.sum(gain_sum[...], axis=0, keepdims=True)
    for i in range(n):
        gain_cut[i] = total_gain[:, i * (width // n) : (i + 1) * (width // n)]
    for copy in gain_copies:
        copy.start()
    spread_rows(wo, wo_here)
    for copy in moves:
        copy.wait()

    def mix(it, carry):
        kk = 3 - it // 2
        other = 1 - lax.rem(it, 2)
        b = plane.number(kk, other)
        at = pl.ds(pl.multiple_of(b * rows, rows), rows)
        part = lax.dot_general(
            hid_low[at, :], w_down[...], NT, preferred_element_type=f32
        ).astype(bf16)

        @pl.when(other == 0)
        def _():
            pair[kk] = part

        @pl.when(other == 1)
        def _():
            stage[kk] = part

        for which in range(4):

            @pl.when(it == 2 * (3 - which))
            def _(which=which):
                one.swaps[Reduce.THEIRS[which]].start()

        return carry

    lax.fori_loop(0, n, mix, 0)
    for copy in loads:
        copy.wait()
    kt[...] = k[...].T
    dk[...] = jnp.zeros_like(dk)
    dv[...] = jnp.zeros_like(dv)

    def unturn(value, at):
        return value * cosine[at, :] - pltpu.roll(value, SLOT, 1) * sine[at, :]

    def chips(kk, carry):
        @pl.when(kk == 0)
        def _():
            gather.wait_own()
            gather.wait_swap()

        @pl.when(kk == 1)
        def _():
            gather.relay_near()
            gather.wait_share(1)
            scatter.relay(0, 0)

        @pl.when(kk == 2)
        def _():
            one.send_to()
            gather.wait_share(0)
            scatter.relay(0, 1)

        @pl.when(kk == 3)
        def _():
            one.ready()
            one.first(held, resid)
            gather.relay_far()
            gather.wait_share(2)
            scatter.relay(1, 0)

        i = plane.number(kk, 0) // 2
        here = pl.ds(pl.multiple_of(i * BLOCK, BLOCK), BLOCK)
        for other in range(2):
            b = plane.number(kk, other)
            at = pl.ds(pl.multiple_of(b * rows, rows), rows)
            value = lax.dot_general(every[b], wo_here[...], NT, preferred_element_type=f32)
            for h in range(heads):
                go[h, at, :] = value[:, h * LANES : (h + 1) * LANES].astype(bf16)

        def head(h, carry):
            query = q[h, here, :]
            grads = go[h, here, :]
            delta[...] = jnp.sum((grads.astype(f32) * o[h, here, :]).T, axis=0, keepdims=True)
            dqt[...] = jnp.zeros_like(dqt)

            def keys(j, causal):
                at = pl.ds(pl.multiple_of(j * BLOCK, BLOCK), BLOCK)
                raw = lax.dot_general(k[at, :], query, NT, preferred_element_type=f32)
                ok = allowed_block(j * BLOCK, i * BLOCK, begin[:, here], causal)
                probs = jnp.where(ok, jnp.exp2(raw * factor - lse[h, :, here]), 0.0)
                dprob = lax.dot_general(v[at, :], grads, NT, preferred_element_type=f32)
                dscore = (probs * (dprob - delta[...])).astype(bf16)
                dv[at, :] += jnp.dot(probs.astype(bf16), grads, preferred_element_type=f32)
                dk[at, :] += jnp.dot(dscore, query, preferred_element_type=f32)
                dqt[...] += jnp.dot(kt[:, at], dscore, preferred_element_type=f32)

            def loop(j, carry):
                keys(j, False)
                return carry

            lax.fori_loop(0, i, loop, 0)
            keys(i, True)
            got = unturn(dqt[...].T * scale, here).astype(bf16)
            out[here, pl.ds(pl.multiple_of(h * LANES, LANES), LANES)] = got
            return carry

        lax.fori_loop(0, heads, head, 0)
        return carry

    lax.fori_loop(0, 4, chips, 0)
    scatter.relay(1, 1)

    def write(i, carry):
        at = pl.ds(pl.multiple_of(i * BLOCK, BLOCK), BLOCK)
        turned = unturn(dk[at, :] * scale, at).astype(bf16)
        out[at, heads * LANES : (heads + 1) * LANES] = turned
        out[at, (heads + 1) * LANES :] = dv[at, :].astype(bf16)
        return carry

    lax.fori_loop(0, length // BLOCK, write, 0)
    one.send_fro()
    across = every.reshape(length, width)
    part = 512

    def into_terms(i, carry):
        at = pl.ds(pl.multiple_of(i * part, part), part)
        value = lax.dot_general(
            low[...], across[:, at], (((0,), (0,)), ((), ())), preferred_element_type=f32
        ).astype(bf16)
        for half in range(terms.shape[0]):
            terms[half, :, at] = value[half * SLOT : half * SLOT + HALF]
        return carry

    lax.fori_loop(0, width // part, into_terms, 0)
    for copy in gain_copies:
        copy.wait()
    all_gain = gain_got[0]
    for i in range(1, n):
        all_gain = all_gain + gain_got[i]
    for t in range(m):
        gain_out[t] = all_gain[:, t * strip : (t + 1) * strip]
    gather.wait_sends()
    one.finish(held, layer)
    scatter.finish()
    back = pltpu.make_async_copy(sums, ffn_sum, loc.at[10])
    back.start()
    back.wait()


def attend_back(
    n, m, factor, scale, q, k, v, o, lse, begin, cosine, sine, low,
    hid_low, w_down, ffn, wo, dnorm, resid, grad, gain, ident,
):
    heads, length, _ = q.shape
    rows, width = dnorm.shape
    strip = width // (n * m)
    hbm = pl.BlockSpec(memory_space=ANY)
    vmem = pl.BlockSpec(memory_space=pltpu.VMEM)
    return pl.pallas_call(
        functools.partial(attend_back_body, n, m, factor, scale),
        out_shape=(
            jax.ShapeDtypeStruct((length, (heads + 2) * LANES), bf16),
            jax.ShapeDtypeStruct((rows, width), bf16),
            jax.ShapeDtypeStruct(wo.shape, bf16),
            jax.ShapeDtypeStruct((rows, width), f32),
            jax.ShapeDtypeStruct((m, 1, strip), f32),
            jax.ShapeDtypeStruct(ffn.shape[1:], bf16),
        ),
        in_specs=[hbm] * 4 + [vmem] * 2 + [hbm] * 6 + [vmem] * 5,
        out_specs=[vmem] * 5 + [hbm],
        scratch_shapes=[
            pltpu.VMEM(q.shape, bf16),
            pltpu.VMEM(k.shape, bf16),
            pltpu.VMEM(v.shape, bf16),
            pltpu.VMEM(o.shape, f32),
            pltpu.VMEM(cosine.shape, f32),
            pltpu.VMEM(sine.shape, f32),
            pltpu.VMEM(low.shape, bf16),
            pltpu.VMEM((LANES, length), bf16),
            pltpu.VMEM((LANES, BLOCK), f32),
            pltpu.VMEM((length, LANES), f32),
            pltpu.VMEM((length, LANES), f32),
            pltpu.VMEM((1, BLOCK), f32),
            pltpu.VMEM((heads, length, LANES), bf16),
            pltpu.VMEM((n, rows, width), bf16),
            pltpu.VMEM((rows, width), bf16),
            pltpu.VMEM((heads * LANES, width), bf16),
            pltpu.VMEM(hid_low.shape, bf16),
            pltpu.VMEM(w_down.shape, bf16),
            pltpu.VMEM((4, rows, width), bf16),
        ]
        + Reduce.scratch(rows, width)
        + [
            pltpu.VMEM((rows, width), f32),
            pltpu.VMEM((TILE, width), f32),
            pltpu.VMEM((n, 1, width // n), f32),
            pltpu.VMEM((n, 1, width // n), f32),
            pltpu.VMEM(ffn.shape[1:], bf16),
        ]
        + Scatter.scratch(ffn.shape[1:])
        + Gathers.scratch(2)
        + [pltpu.SemaphoreType.DMA((2, n - 1)), pltpu.SemaphoreType.DMA((11,))],
        compiler_params=pltpu.CompilerParams(
            collective_id=ident, has_side_effects=True, vmem_limit_bytes=VMEM_LIMIT
        ),
        cost_estimate=COST,
        name="attend_back",
    )(
        q, k, v, o, lse, begin, cosine, sine, low, hid_low, w_down, ffn, wo, dnorm, resid, grad, gain
    )


def feed_body(
    n, m, mine, go, w_in, down, dnorm, grads, hid_out, down_out, down_parts,
    rows, rows_t, go_t, go_two, w, w_down, gates, h, hid_low, down_held, down_sum,
    pair, near, far, stage,
    sg, lg, sr, loc, sw, so, sd, sz, sf,
):
    plane = Plane(n, m)
    tokens, width = rows.shape[1:]
    hid = down.shape[1]
    half = m * hid
    greet(plane, True)
    gather = Gathers(plane, mine, lambda i: rows.at[i], sg, lg, 2)
    reduce = Reduce(plane, None, pair, near, far, sr, None, stage)

    def columns(ref, j, t):
        return ref.at[:, j * half + t * hid : j * half + (t + 1) * hid]

    weights = [
        pltpu.make_async_copy(w_in.at[t, j], columns(w, j, t), sw.at[j, t])
        for j in range(2)
        for t in range(m)
    ]
    for copy in weights:
        copy.start()
    meet(plane, True)
    gather.start()

    def down_at(ref, t):
        return ref.at[:, pl.ds(pl.multiple_of(t * hid, hid), hid)]

    chain = Chain(plane, down, lambda t: down_at(w_down, t), sz)
    chain.start()
    own_down = pltpu.make_async_copy(down, down_at(w_down, plane.t), loc.at[0])
    own_down.start()
    gather.wait_own()
    for copy in weights:
        copy.wait()

    def span(b):
        return pl.ds(pl.multiple_of(b * tokens, tokens), tokens)

    def down_grad(kk, keep):
        chip = plane.number(kk, 0) // 2
        at = pl.ds(pl.multiple_of(chip * 2 * tokens, 2 * tokens), 2 * tokens)

        def part(i, carry):
            line = pl.ds(pl.multiple_of(i * 256, 256), 256)
            value = jnp.dot(go_t[line, at], hid_low[at, :], preferred_element_type=f32)
            keep(line, value)
            return carry

        lax.fori_loop(0, width // 256, part, 0)

    def set_down(line, value):
        down_sum[line, :] = value

    def add_down(line, value):
        down_sum[line, :] += value

    def hold_down(line, value):
        down_held[line, :] = (down_sum[line, :] + value).astype(bf16)

    def early_go(it, slot):
        b = plane.number(it // 2, lax.rem(it, 2))
        return pltpu.make_async_copy(go.at[b], go_two.at[slot], so.at[slot])

    def forward(it, carry):
        b = plane.number(it // 2, lax.rem(it, 2))

        @pl.when(it == 1)
        def _():
            gather.wait_swap()

        @pl.when(it == 2)
        def _():
            down_grad(0, set_down)
            chain.step(1)
            gather.relay_near()

        @pl.when(it == 3)
        def _():
            gather.wait_share(1)

        @pl.when(it == 4)
        def _():
            chain.step(2)

        @pl.when(it == 5)
        def _():
            gather.wait_share(0)

        @pl.when(it == 6)
        def _():
            down_grad(1, add_down)
            down_grad(2, add_down)
            gather.relay_far()

        @pl.when(it == 7)
        def _():
            gather.wait_share(2)

        slot = lax.rem(it, 2)

        @pl.when(it < n - 1)
        def _():
            early_go(it + 1, 1 - slot).start()

        row = rows[b]
        both = jnp.dot(row, w[...], preferred_element_type=f32)
        gates[span(b), :] = both
        gate, up = both[:, :half], both[:, half:]
        hid_low[span(b), :] = (gate * jax.nn.sigmoid(gate) * up).astype(bf16)
        rows_t[:, span(b)] = row.T
        early_go(it, slot).wait()
        go_t[:, span(b)] = go_two[slot].T
        return carry

    early_go(0, 0).start()
    lax.fori_loop(0, n, forward, 0)

    def number(it):
        return plane.number(3 - it // 2, 1 - lax.rem(it, 2))

    def load_go(it, slot):
        return pltpu.make_async_copy(go.at[number(it)], go_two.at[slot], so.at[slot])

    load_go(0, 0).start()
    down_grad(3, hold_down)
    outs = fan(
        plane, lambda t: down_at(down_held, t), lambda t: down_parts.at[t], sf.at[0], sf.at[1]
    )
    outs.append(
        pltpu.make_async_copy(down_at(down_held, plane.t), down_parts.at[plane.t], loc.at[1])
    )
    outs.append(pltpu.make_async_copy(hid_low, hid_out, loc.at[2]))
    for copy in outs:
        copy.start()
    for hop in range(3, m):
        chain.step(hop)
    own_down.wait()
    outs.append(pltpu.make_async_copy(w_down, down_out, loc.at[3]))
    outs[-1].start()

    def backward(it, carry):
        slot = lax.rem(it, 2)
        k = 3 - it // 2
        b = number(it)

        @pl.when(it == 2)
        def _():
            reduce.join(3)
            reduce.out[0].start()

        @pl.when(it == 6)
        def _():
            reduce.join(1)
            reduce.out[1].start()

        @pl.when(it == 7)
        def _():
            reduce.ready()
            reduce.send_fro()

        @pl.when(it < n - 1)
        def _():
            load_go(it + 1, 1 - slot).start()

        load_go(it, slot).wait()

        gate = gates[span(b), :half]
        up = gates[span(b), half:]
        dhidden = jnp.dot(go_two[slot], w_down[...], preferred_element_type=f32)
        sig = jax.nn.sigmoid(gate)
        dgate = (dhidden * up * sig * (1.0 + gate * (1.0 - sig))).astype(bf16)
        dup = (dhidden * gate * sig).astype(bf16)
        h[span(b), :half] = dgate
        h[span(b), half:] = dup
        part = lax.dot_general(h[span(b), :], w[...], NT, preferred_element_type=f32)
        part = part.astype(bf16)

        @pl.when(lax.rem(it, 2) == 1)
        def _():
            pair[k] = part

        @pl.when(lax.rem(it, 2) == 0)
        def _():
            stage[k] = part

        for kk in range(4):

            @pl.when(it == 2 * (3 - kk))
            def _(kk=kk):
                reduce.swaps[Reduce.THEIRS[kk]].start()

        return carry

    lax.fori_loop(0, n, backward, 0)

    def weight_grad(i, carry):
        at = pl.ds(pl.multiple_of(i * 256, 256), 256)
        value = jnp.dot(rows_t[at, :], h[...], preferred_element_type=f32)
        w[at, :] = value.astype(bf16)
        return carry

    lax.fori_loop(0, width // 256, weight_grad, 0)
    ends = [
        pltpu.make_async_copy(columns(w, j, t), grads.at[t, j], sd.at[j, t])
        for j in range(2)
        for t in range(m)
    ]
    for copy in ends:
        copy.start()
    reduce.first(dnorm)
    gather.wait_sends()
    chain.wait_sends()
    reduce.finish(dnorm)
    for copy in outs + ends:
        copy.wait()


def feed(n, m, norm, go, w_in, down, ident):
    tokens, width = norm.shape
    hid = down.shape[1]
    length = n * tokens
    half = m * hid
    hbm = pl.BlockSpec(memory_space=ANY)
    return pl.pallas_call(
        functools.partial(feed_body, n, m),
        out_shape=(
            jax.ShapeDtypeStruct((tokens, width), f32),
            jax.ShapeDtypeStruct((m, 2, width, hid), bf16),
            jax.ShapeDtypeStruct((length, half), bf16),
            jax.ShapeDtypeStruct((width, half), bf16),
            jax.ShapeDtypeStruct((m, width, hid), bf16),
        ),
        in_specs=[hbm] * 4,
        out_specs=[pl.BlockSpec(memory_space=pltpu.VMEM)] + [hbm] * 4,
        scratch_shapes=[
            pltpu.VMEM((n, tokens, width), bf16),
            pltpu.VMEM((width, length), bf16),
            pltpu.VMEM((width, length), bf16),
            pltpu.VMEM((2, tokens, width), bf16),
            pltpu.VMEM((width, 2 * half), bf16),
            pltpu.VMEM((width, half), bf16),
            pltpu.VMEM((length, 2 * half), f32),
            pltpu.VMEM((length, 2 * half), bf16),
            pltpu.VMEM((length, half), bf16),
            pltpu.VMEM((width, half), bf16),
            pltpu.VMEM((width, half), f32),
        ]
        + [pltpu.VMEM((slots, tokens, width), bf16) for slots in Reduce.SLOTS]
        + [
            pltpu.VMEM((4, tokens, width), bf16),
            *Gathers.scratch(2),
            pltpu.SemaphoreType.DMA((4, 4)),
            pltpu.SemaphoreType.DMA((4,)),
            pltpu.SemaphoreType.DMA((2, m)),
            pltpu.SemaphoreType.DMA((2,)),
            pltpu.SemaphoreType.DMA((2, m)),
            pltpu.SemaphoreType.DMA((4, m)),
            pltpu.SemaphoreType.DMA((2, m - 1)),
        ],
        compiler_params=pltpu.CompilerParams(
            collective_id=ident, has_side_effects=True, vmem_limit_bytes=VMEM_LIMIT
        ),
        cost_estimate=COST,
        name="feed",
    )(norm, go, w_in, down)


def results_body(
    dnorm, dresid, x, gain, layer_in, ffn, qkv, wo, vec, wq, wk, wv, one,
    layer, input_grad, first, query, key, value, output, second, gate, up, down,
):
    step = pl.program_id(0)

    def into_input(at):
        token = x[at, :].astype(f32)
        scale = lax.rsqrt(jnp.mean(token * token, axis=1, keepdims=True) + norm_epsilon)
        inner = gain[...] * dnorm[at, :]
        moment = jnp.mean(token * inner, axis=1, keepdims=True)
        input_grad[at, :] = (
            dresid[at, :] + scale * inner - token * scale * (scale * scale * moment)
        )
        layer[at, :] = layer_in[at, :]

    in_tiles(x.shape[0], into_input)
    for i, ref in enumerate((gate, up, down)):
        ref[...] = ffn[i].astype(f32)

    @pl.when(step == 0)
    def _():
        groups, strip, _ = qkv.shape
        start = 0
        sums = jnp.zeros((strip, 1), f32)
        for ref, weight in ((query, wq), (key, wk), (value, wv)):
            each = ref.shape[1] // groups
            for g in range(groups):
                ref[:, g * each : (g + 1) * each] = qkv[g, :, start : start + each].astype(f32)
            start += each
            sums += jnp.sum(weight[...].astype(f32) * ref[...], axis=1, keepdims=True)
        row = jnp.broadcast_to(sums, (strip, LANES)).T[0:1, :strip]
        first[...] = row / one[...].astype(f32)
        total = wo[0].astype(f32)
        gains = vec[0]
        for t in range(1, wo.shape[0]):
            total += wo[t].astype(f32)
            gains += vec[t]
        output[...] = total
        second[...] = gains


def results(dnorm, dresid, x, gain, layer, ffn, qkv, wo, vec, wq, wk, wv, one):
    tokens, width = x.shape
    rows, cols = ffn.shape[1:]
    strip = wq.shape[0]
    steps = 2

    def tiled(count, columns):
        return pl.BlockSpec((count // steps, columns), lambda i: (i, 0))

    def fixed(*shape):
        return pl.BlockSpec(shape, lambda i: (0,) * len(shape))

    return pl.pallas_call(
        results_body,
        grid=(steps,),
        out_shape=(
            jax.ShapeDtypeStruct((tokens, width), bf16),
            jax.ShapeDtypeStruct((tokens, width), f32),
            jax.ShapeDtypeStruct((1, strip), f32),
            jax.ShapeDtypeStruct(wq.shape, f32),
            jax.ShapeDtypeStruct(wk.shape, f32),
            jax.ShapeDtypeStruct(wv.shape, f32),
            jax.ShapeDtypeStruct((strip, width), f32),
            jax.ShapeDtypeStruct((1, strip), f32),
            jax.ShapeDtypeStruct((rows, cols), f32),
            jax.ShapeDtypeStruct((rows, cols), f32),
            jax.ShapeDtypeStruct((rows, cols), f32),
        ),
        in_specs=[
            tiled(tokens, width),
            tiled(tokens, width),
            tiled(tokens, width),
            fixed(1, width),
            tiled(tokens, width),
            pl.BlockSpec((3, rows // steps, cols), lambda i: (0, i, 0)),
            fixed(*qkv.shape),
            fixed(*wo.shape),
            fixed(*vec.shape),
            fixed(*wq.shape),
            fixed(*wk.shape),
            fixed(*wv.shape),
            fixed(1, strip),
        ],
        out_specs=[
            tiled(tokens, width),
            tiled(tokens, width),
            fixed(1, strip),
            fixed(*wq.shape),
            fixed(*wk.shape),
            fixed(*wv.shape),
            fixed(strip, width),
            fixed(1, strip),
            tiled(rows, cols),
            tiled(rows, cols),
            tiled(rows, cols),
        ],
        compiler_params=pltpu.CompilerParams(vmem_limit_bytes=VMEM_LIMIT),
        cost_estimate=COST,
        name="results",
    )(dnorm, dresid, x, gain, layer, ffn, qkv, wo, vec, wq, wk, wv, one)


def fast_layer(n, m):
    def on_plane(
        layer_input,
        doc_ids,
        positions,
        first_gain,
        query_weight,
        key_weight,
        value_weight,
        output_weight,
        second_gain,
        gate_weight,
        up_weight,
        down_weight,
        out_grad,
    ):
        x = layer_input[0]
        width = x.shape[1]
        heads = QUERY_HEADS // n
        scale = 1.0 / math.sqrt(HEAD_SIZE)
        factor = scale * LOG2E
        strip = query_weight.shape[0]

        lane = np.arange(LANES) % SLOT
        inverse = np.where(lane < HALF, rope_base ** (-(lane * 2.0 / HEAD_SIZE)), 0.0)
        (
            norm_t, q, k, v, cosine, sine, wqkv, gain_one, gain_two, docs,
            ffn_mine, down_mine, output_rows,
        ) = entry(
            n, m, heads, x, doc_ids, positions, query_weight, key_weight, value_weight,
            first_gain.reshape(1, strip), second_gain.reshape(1, strip),
            gate_weight, up_weight, down_weight, output_weight,
            jnp.asarray(inverse[None], f32), 0,
        )
        o, lse, begin, low, grad_all, resid, norm_two, ffn_all = attend(
            n, m, factor, q, k, v, docs, output_rows, out_grad[0], x, gain_two, ffn_mine, 9
        )
        dnorm_two, ffn_terms, hid_low, w_down, down_parts = feed(
            n, m, norm_two, grad_all, ffn_all, down_mine, 2
        )
        dqkv, layer_output, output_terms, dresid, gain_part, ffn_sum = attend_back(
            n, m, factor, scale, q, k, v, o, lse, begin, cosine, sine, low, hid_low, w_down, ffn_terms,
            output_rows, dnorm_two, resid, out_grad[0], gain_two, 3,
        )
        dnorm_one, ffn_out, qkv_out, output_parts, gain_sums = last(
            n, m, dqkv, wqkv, norm_t, ffn_sum, down_parts, output_terms, gain_part, 6
        )
        (
            layer_output, input_grad, first_gain_grad, query_grad, key_grad, value_grad,
            output_grad, second_gain_grad, gate_grad, up_grad, down_grad,
        ) = results(
            dnorm_one, dresid, x, gain_one, layer_output, ffn_out, qkv_out, output_parts,
            gain_sums, query_weight, key_weight, value_weight, first_gain.reshape(1, strip),
        )
        return (
            layer_output[None],
            input_grad[None],
            first_gain_grad.reshape(strip),
            query_grad,
            key_grad,
            value_grad,
            output_grad,
            second_gain_grad.reshape(strip),
            gate_grad,
            up_grad,
            down_grad,
        )

    return on_plane


def solution(mesh):
    n, m = mesh.shape["seq"], mesh.shape["tp"]
    fits = n == KEY_VALUE_HEADS == 8 and m == 4
    return jax.shard_map(
        fast_layer(n, m) if fits else on_device,
        mesh=mesh,
        in_specs=(
            P("tp", "seq", None),
            P("tp", "seq"),
            P("tp", "seq"),
            P(("seq", "tp")),
            P(("seq", "tp"), None),
            P(("seq", "tp"), None),
            P(("seq", "tp"), None),
            P(("seq", "tp"), None),
            P(("seq", "tp")),
            P("seq", "tp"),
            P("seq", "tp"),
            P("seq", "tp"),
            P("tp", "seq", None),
        ),
        out_specs=(
            P("tp", "seq", None),
            P("tp", "seq", None),
            P(("seq", "tp")),
            P(("seq", "tp"), None),
            P(("seq", "tp"), None),
            P(("seq", "tp"), None),
            P(("seq", "tp"), None),
            P(("seq", "tp")),
            P("seq", "tp"),
            P("seq", "tp"),
            P("seq", "tp"),
        ),
        check_vma=False,
    )
```

```python
import functools
import math

import jax
import jax.numpy as jnp
import numpy as np
from jax import lax
from jax.experimental import pallas as pl
from jax.experimental.pallas import tpu as pltpu
from jax.sharding import PartitionSpec as P

QUERY_HEADS = 16
KEY_VALUE_HEADS = 8
HEAD_SIZE = 96


norm_epsilon = 1e-05
rope_base = 100000.0
mask_fill_value = -1e30


def rope_tables(places):
    half = HEAD_SIZE // 2
    inverse = rope_base ** (-(jnp.arange(half, dtype=jnp.float32) * 2.0 / HEAD_SIZE))
    angles = places.astype(jnp.float32)[:, None] * inverse[None, :]
    return (jnp.cos(angles), jnp.sin(angles))


def apply_rotary(value_rows, cosine_table, sine_table, heads, direction):
    sequence_length = value_rows.shape[0]
    split = value_rows.reshape(sequence_length, heads, 2, HEAD_SIZE // 2)
    first = split[:, :, 0]
    second = split[:, :, 1]
    cosine = cosine_table[:, None, :]
    sine = direction * sine_table[:, None, :]
    turned = jnp.stack([first * cosine - second * sine, second * cosine + first * sine], axis=2)
    return turned.reshape(sequence_length, heads * HEAD_SIZE)


def outer_product(left, right):
    return lax.dot_general(
        left, right, (((0,), (0,)), ((), ())), preferred_element_type=jnp.float32
    )


def times_transpose(left, right):
    return lax.dot_general(
        left, right, (((1,), (1,)), ((), ())), preferred_element_type=jnp.float32
    )


def norm_backward(inputs, scale, gain, upstream):
    inner = gain * upstream
    moment = jnp.mean(inputs * inner, axis=1, keepdims=True)
    return (
        scale * inner - inputs * scale * scale * scale * moment,
        jnp.sum(upstream * inputs * scale, axis=0),
    )


def on_device(
    layer_input,
    doc_ids,
    positions,
    first_gain,
    query_weight,
    key_weight,
    value_weight,
    output_weight,
    second_gain,
    gate_weight,
    up_weight,
    down_weight,
    out_grad,
):
    token_rows = layer_input.shape[1]
    query_groups = QUERY_HEADS // KEY_VALUE_HEADS
    scale_of_scores = 1.0 / math.sqrt(HEAD_SIZE)
    inputs_f = layer_input[0].astype(jnp.float32)
    my_docs = doc_ids[0]
    gain_one, query_full, complete_keys, value_full, output_full, gain_two = (
        lax.all_gather(first_gain, ("seq", "tp"), axis=0, tiled=True),
        lax.all_gather(query_weight, ("seq", "tp"), axis=0, tiled=True),
        lax.all_gather(key_weight, ("seq", "tp"), axis=0, tiled=True),
        lax.all_gather(value_weight, ("seq", "tp"), axis=0, tiled=True),
        lax.all_gather(output_weight, ("seq", "tp"), axis=0, tiled=True),
        lax.all_gather(second_gain, ("seq", "tp"), axis=0, tiled=True),
    )
    gain_one_f = gain_one.astype(jnp.float32)
    gain_two_f = gain_two.astype(jnp.float32)
    scale_one = lax.rsqrt(jnp.mean(inputs_f * inputs_f, axis=1, keepdims=True) + norm_epsilon)
    first_normalized = (inputs_f * scale_one * gain_one_f).astype(jnp.bfloat16)
    cosine_table, sine_table = rope_tables(positions[0])
    rotated_query = apply_rotary(
        jnp.dot(first_normalized, query_full, preferred_element_type=jnp.float32),
        cosine_table,
        sine_table,
        QUERY_HEADS,
        1.0,
    ).astype(jnp.bfloat16)
    key_rot = apply_rotary(
        jnp.dot(first_normalized, complete_keys, preferred_element_type=jnp.float32),
        cosine_table,
        sine_table,
        KEY_VALUE_HEADS,
        1.0,
    ).astype(jnp.bfloat16)
    value_low = jnp.dot(first_normalized, value_full, preferred_element_type=jnp.float32).astype(
        jnp.bfloat16
    )
    gathered_keys, gathered_values, doc_all = (
        lax.all_gather(key_rot, "seq", axis=0, tiled=True),
        lax.all_gather(value_low, "seq", axis=0, tiled=True),
        lax.all_gather(my_docs.astype(jnp.bfloat16), "seq", axis=0, tiled=True),
    )
    sequence_length = gathered_keys.shape[0]
    block_number = math.gcd(512, sequence_length)
    block_count = sequence_length // block_number
    query_index = lax.axis_index("seq") * token_rows + jnp.arange(token_rows, dtype=jnp.int32)
    my_doc_f = my_docs.astype(jnp.float32)
    heads_of_query = rotated_query.reshape(token_rows, KEY_VALUE_HEADS, query_groups, HEAD_SIZE)
    layer_entries = (
        gathered_keys.reshape(block_count, block_number, KEY_VALUE_HEADS, HEAD_SIZE),
        gathered_values.reshape(block_count, block_number, KEY_VALUE_HEADS, HEAD_SIZE),
        doc_all.astype(jnp.float32).reshape(block_count, block_number),
        jnp.arange(block_count, dtype=jnp.int32) * block_number,
    )

    def allowed_of(doc_piece, start):
        key_index = start + jnp.arange(block_number, dtype=jnp.int32)
        return (key_index[None, :] <= query_index[:, None]) & (
            doc_piece[None, :] == my_doc_f[:, None]
        )

    def scores_of(key_piece, allowed):
        raw = (
            jnp.einsum(
                "tgrd,kgd->tgrk", heads_of_query, key_piece, preferred_element_type=jnp.float32
            )
            * scale_of_scores
        )
        return jnp.where(allowed[:, None, None, :], raw, mask_fill_value)

    def total_step(carry, item):
        key_piece, value_piece, doc_piece, start = item
        allowed = allowed_of(doc_piece, start)

        def total_work(state):
            top, total = state
            scores = scores_of(key_piece, allowed)
            new_top = jnp.maximum(top, jnp.max(scores, axis=3))
            weights = jnp.where(
                allowed[:, None, None, :], jnp.exp(scores - new_top[..., None]), 0.0
            )
            return (new_top, total * jnp.exp(top - new_top) + jnp.sum(weights, axis=3))

        return (lax.cond(jnp.any(allowed), total_work, lambda state: state, carry), None)

    start_state = (
        jnp.full((token_rows, KEY_VALUE_HEADS, query_groups), mask_fill_value, jnp.float32),
        jnp.zeros((token_rows, KEY_VALUE_HEADS, query_groups), jnp.float32),
    )
    (top, total), unused_result = lax.scan(total_step, start_state, layer_entries)
    log_total = top + jnp.log(total)

    def probs_of(key_piece, allowed):
        scores = scores_of(key_piece, allowed)
        return jnp.where(allowed[:, None, None, :], jnp.exp(scores - log_total[..., None]), 0.0)

    def output_update(accum, item):
        key_piece, value_piece, doc_piece, start = item
        allowed = allowed_of(doc_piece, start)

        def output_work(state):
            probs = probs_of(key_piece, allowed).astype(jnp.bfloat16)
            return state + jnp.einsum(
                "tgrk,kgd->tgrd", probs, value_piece, preferred_element_type=jnp.float32
            )

        return (lax.cond(jnp.any(allowed), output_work, lambda state: state, accum), None)

    heads_output, unused_result = lax.scan(
        output_update,
        jnp.zeros((token_rows, KEY_VALUE_HEADS, query_groups, HEAD_SIZE), jnp.float32),
        layer_entries,
    )
    attn_low = heads_output.reshape(token_rows, QUERY_HEADS * HEAD_SIZE).astype(jnp.bfloat16)
    resid = inputs_f + jnp.dot(attn_low, output_full, preferred_element_type=jnp.float32)
    scale_two = lax.rsqrt(jnp.mean(resid * resid, axis=1, keepdims=True) + norm_epsilon)
    normed_two = (resid * scale_two * gain_two_f).astype(jnp.bfloat16)
    rows_all = lax.all_gather(normed_two, "tp", axis=0, tiled=True)
    gate_cols, up_cols, down_cols = (
        lax.all_gather(gate_weight, "seq", axis=0, tiled=True),
        lax.all_gather(up_weight, "seq", axis=0, tiled=True),
        lax.all_gather(down_weight, "seq", axis=0, tiled=True),
    )
    gate_pre = jnp.dot(rows_all, gate_cols, preferred_element_type=jnp.float32)
    up_pre = jnp.dot(rows_all, up_cols, preferred_element_type=jnp.float32)
    gate_sig = jax.nn.sigmoid(gate_pre)
    gate_act = gate_pre * gate_sig
    hidden = (gate_act * up_pre).astype(jnp.bfloat16)
    mixed = lax.psum_scatter(
        times_transpose(hidden, down_cols).astype(jnp.bfloat16),
        "tp",
        scatter_dimension=0,
        tiled=True,
    ).astype(jnp.float32)
    layer_output = (resid + mixed).astype(jnp.bfloat16)[None]
    grad_low = out_grad[0]
    grad_f = grad_low.astype(jnp.float32)
    grad_all = lax.all_gather(grad_low, "tp", axis=0, tiled=True)
    dhidden = jnp.dot(grad_all, down_cols, preferred_element_type=jnp.float32)
    dgate = (dhidden * up_pre * gate_sig * (1.0 + gate_pre * (1.0 - gate_sig))).astype(jnp.bfloat16)
    dup = (dhidden * gate_act).astype(jnp.bfloat16)
    gate_term = outer_product(rows_all, dgate)
    up_term = outer_product(rows_all, dup)
    down_term_grad = outer_product(grad_all, hidden)
    dnorm_two = lax.psum_scatter(
        (times_transpose(dgate, gate_cols) + times_transpose(dup, up_cols)).astype(jnp.bfloat16),
        "tp",
        scatter_dimension=0,
        tiled=True,
    ).astype(jnp.float32)
    gate_grad, up_grad, down_grad = (
        lax.psum_scatter(
            gate_term.astype(jnp.bfloat16), "seq", scatter_dimension=0, tiled=True
        ).astype(jnp.float32),
        lax.psum_scatter(
            up_term.astype(jnp.bfloat16), "seq", scatter_dimension=0, tiled=True
        ).astype(jnp.float32),
        lax.psum_scatter(
            down_term_grad.astype(jnp.bfloat16), "seq", scatter_dimension=0, tiled=True
        ).astype(jnp.float32),
    )
    resid_part, gain_two_term = norm_backward(resid, scale_two, gain_two_f, dnorm_two)
    dresid = grad_f + resid_part
    dbranch = dresid.astype(jnp.bfloat16)
    output_term = outer_product(attn_low, dbranch)
    heads_gradient = times_transpose(dbranch, output_full).astype(jnp.bfloat16)
    grouped_heads_gradient = heads_gradient.reshape(
        token_rows, KEY_VALUE_HEADS, query_groups, HEAD_SIZE
    )
    delta = jnp.sum(grouped_heads_gradient.astype(jnp.float32) * heads_output, axis=3)

    def gradient_update(dquery, item):
        key_piece, value_piece, doc_piece, start = item
        allowed = allowed_of(doc_piece, start)

        def gradient_work(state):
            probs = probs_of(key_piece, allowed)
            value_piece_grad = jnp.einsum(
                "tgrk,tgrd->kgd",
                probs.astype(jnp.bfloat16),
                grouped_heads_gradient,
                preferred_element_type=jnp.float32,
            )
            prob_grad = jnp.einsum(
                "tgrd,kgd->tgrk",
                grouped_heads_gradient,
                value_piece,
                preferred_element_type=jnp.float32,
            )
            score_grad = (probs * (prob_grad - delta[..., None])).astype(jnp.bfloat16)
            key_piece_grad = jnp.einsum(
                "tgrk,tgrd->kgd", score_grad, heads_of_query, preferred_element_type=jnp.float32
            )
            updated = state + jnp.einsum(
                "tgrk,kgd->tgrd", score_grad, key_piece, preferred_element_type=jnp.float32
            )
            return (updated, (key_piece_grad, value_piece_grad))

        def skip(state):
            blank_tensor = jnp.zeros((block_number, KEY_VALUE_HEADS, HEAD_SIZE), jnp.float32)
            return (state, (blank_tensor, blank_tensor))

        return lax.cond(jnp.any(allowed), gradient_work, skip, dquery)

    dquery, (key_contributions, value_contributions) = lax.scan(
        gradient_update,
        jnp.zeros((token_rows, KEY_VALUE_HEADS, query_groups, HEAD_SIZE), jnp.float32),
        layer_entries,
    )
    gathered_key_contributions = (
        key_contributions.reshape(sequence_length, KEY_VALUE_HEADS * HEAD_SIZE) * scale_of_scores
    )
    gathered_value_contributions = value_contributions.reshape(
        sequence_length, KEY_VALUE_HEADS * HEAD_SIZE
    )
    local_keys, value_mine = (
        lax.psum_scatter(
            gathered_key_contributions.astype(jnp.bfloat16), "seq", scatter_dimension=0, tiled=True
        ).astype(jnp.float32),
        lax.psum_scatter(
            gathered_value_contributions.astype(jnp.bfloat16),
            "seq",
            scatter_dimension=0,
            tiled=True,
        ).astype(jnp.float32),
    )
    dq_pre = apply_rotary(
        dquery.reshape(token_rows, QUERY_HEADS * HEAD_SIZE) * scale_of_scores,
        cosine_table,
        sine_table,
        QUERY_HEADS,
        -1.0,
    ).astype(jnp.bfloat16)
    key_gradient_unrotated = apply_rotary(
        local_keys, cosine_table, sine_table, KEY_VALUE_HEADS, -1.0
    ).astype(jnp.bfloat16)
    dv_pre = value_mine.astype(jnp.bfloat16)
    dnorm_one = (
        times_transpose(dq_pre, query_full)
        + times_transpose(key_gradient_unrotated, complete_keys)
        + times_transpose(dv_pre, value_full)
    )
    input_part, gain_one_term = norm_backward(inputs_f, scale_one, gain_one_f, dnorm_one)
    input_grad = (dresid + input_part)[None]
    query_term = outer_product(first_normalized, dq_pre)
    key_term = outer_product(first_normalized, key_gradient_unrotated)
    value_term = outer_product(first_normalized, dv_pre)
    first_gain_grad, query_grad, key_grad, value_grad, output_grad, second_gain_grad = (
        lax.psum_scatter(gain_one_term, ("seq", "tp"), scatter_dimension=0, tiled=True),
        lax.psum_scatter(query_term, ("seq", "tp"), scatter_dimension=0, tiled=True),
        lax.psum_scatter(key_term, ("seq", "tp"), scatter_dimension=0, tiled=True),
        lax.psum_scatter(value_term, ("seq", "tp"), scatter_dimension=0, tiled=True),
        lax.psum_scatter(output_term, ("seq", "tp"), scatter_dimension=0, tiled=True),
        lax.psum_scatter(gain_two_term, ("seq", "tp"), scatter_dimension=0, tiled=True),
    )
    return (
        layer_output,
        input_grad,
        first_gain_grad,
        query_grad,
        key_grad,
        value_grad,
        output_grad,
        second_gain_grad,
        gate_grad,
        up_grad,
        down_grad,
    )


MESH = pl.DeviceIdType.MESH
ANY = pl.ANY
HALF = HEAD_SIZE // 2
LANES = 128
SLOT = LANES // 2
f32 = jnp.float32
bf16 = jnp.bfloat16
VMEM_LIMIT = 62 << 20
COST = pl.CostEstimate(flops=1_000_000, transcendentals=0, bytes_accessed=100_000)


class Plane:
    def __init__(self, n, m):
        self.n, self.m, self.chips = n, m, n // 2
        self.s = lax.axis_index("seq")
        self.t = lax.axis_index("tp")
        self.q = self.s // 2
        self.c = lax.rem(self.s, 2)

        across = self.q + 1 - 2 * lax.rem(self.q, 2)
        along = lax.rem(self.q + 2, 4)
        self.to = across * (1 - self.c) + along * self.c
        self.fro = across * self.c + along * (1 - self.c)
        self.far = 3 - self.q
        self.order = (self.q, self.to, self.fro, self.far)

    def device(self, s):
        return (s, self.t)

    def same(self, chip):
        return (2 * chip + self.c, self.t)

    def number(self, k, other):
        c, q = self.c, self.q
        low, high = lax.rem(k, 2), k // 2
        dx = low * (1 - c) + high * c
        dy = high * (1 - c) + low * c
        x, y = lax.rem(q, 2), q // 2
        chip = 2 * (y + dy - 2 * y * dy) + x + dx - 2 * x * dx
        return 2 * chip + c + other * (1 - 2 * c)

    def sibling(self):
        return (2 * self.q + 1 - self.c, self.t)

    def ahead(self, k):
        return lax.rem(self.q + k, self.chips)

    def behind(self, k):
        return lax.rem(self.q + self.chips - k, self.chips)

    def seq_ahead(self, k):
        return lax.rem(self.s + k, self.n)

    def seq_behind(self, k):
        return lax.rem(self.s + self.n - k, self.n)

    def tp_ahead(self, k):
        return (self.s, lax.rem(self.t + k, self.m))

    def tp_behind(self, k):
        return lax.rem(self.t + self.m - k, self.m)


def greet(plane, with_tp):
    barrier = pltpu.get_barrier_semaphore()
    for k in range(1, plane.n):
        pl.semaphore_signal(
            barrier, inc=1, device_id=plane.device(plane.seq_ahead(k)), device_id_type=MESH
        )
    if with_tp:
        for k in range(1, plane.m):
            pl.semaphore_signal(barrier, inc=1, device_id=plane.tp_ahead(k), device_id_type=MESH)


def meet(plane, with_tp):
    count = plane.n - 1 + (plane.m - 1 if with_tp else 0)
    pl.semaphore_wait(pltpu.get_barrier_semaphore(), count)


def remote(src, dst, send, recv, device):
    return pltpu.make_async_remote_copy(
        src_ref=src,
        dst_ref=dst,
        send_sem=send,
        recv_sem=recv,
        device_id=device,
        device_id_type=MESH,
    )


class Gather:
    COPIES = 7

    def __init__(self, plane, src, dst_of, send, recv, local):
        to, fro, far, c = plane.to, plane.fro, plane.far, plane.c
        here = dst_of(plane.s)
        self.own = pltpu.make_async_copy(src, here, local)

        def block(chip):
            return dst_of(2 * chip + c)

        def copy(i, a, b, device):
            return remote(a, b, send.at[i], recv.at[i], device)

        sibling = plane.sibling()
        self.swap = copy(0, src, here, sibling)
        self.ahead = copy(1, src, here, plane.same(to))
        self.back = copy(2, src, here, plane.same(fro))
        self.relay = copy(3, block(fro), block(fro), plane.same(to))
        self.share = [
            copy(4, block(to), block(to), sibling),
            copy(5, block(fro), block(fro), sibling),
            copy(6, block(far), block(far), sibling),
        ]

    def start(self):
        self.back.start()
        self.ahead.start()

    def start_here(self):
        self.swap.start()
        self.own.start()

    def relay_near(self):
        self.back.wait_recv()
        self.relay.start()
        self.share[1].start()
        self.ahead.wait_recv()
        self.share[0].start()

    def relay_far(self):
        self.relay.wait_recv()
        self.share[2].start()

    def wait_sends(self):
        for copy in [self.swap, self.ahead, self.back, self.relay] + self.share:
            copy.wait_send()


class Gathers:
    def __init__(self, plane, src, dst_of, sems, local, pieces):
        rows = src.shape[0] // pieces
        self.parts = []
        for i in range(pieces):
            at = pl.ds(i * rows, rows)
            self.parts.append(
                Gather(
                    plane,
                    src.at[at],
                    lambda d, at=at: dst_of(d).at[at],
                    sems.at[i, 0],
                    sems.at[i, 1],
                    local.at[i],
                )
            )

    def start(self):
        for part in self.parts:
            part.start()
        for part in self.parts:
            part.start_here()

    def relay_near(self):
        for part in self.parts:
            part.relay_near()

    def relay_far(self):
        for part in self.parts:
            part.relay_far()

    def wait_own(self):
        for part in self.parts:
            part.own.wait()

    def wait_swap(self):
        for part in self.parts:
            part.swap.wait_recv()

    def wait_share(self, i):
        for part in self.parts:
            part.share[i].wait_recv()

    def wait_sends(self):
        for part in self.parts:
            part.wait_sends()

    def finish(self):
        self.wait_own()
        self.wait_swap()
        for i in range(3):
            self.wait_share(i)
        self.wait_sends()

    @staticmethod
    def scratch(pieces):
        return [
            pltpu.SemaphoreType.DMA((pieces, 2, Gather.COPIES)),
            pltpu.SemaphoreType.DMA((pieces,)),
        ]


class Chain:
    def __init__(self, plane, mine, slot_of, sems):
        self.plane, self.mine, self.slot_of, self.sems = plane, mine, slot_of, sems

    def copy(self, way, hop, to):
        plane, row = self.plane, 0 if way > 0 else 2
        slot = self.slot_of(plane.t - way * hop)
        return remote(
            self.mine if hop == 0 else slot,
            slot,
            self.sems.at[row, hop],
            self.sems.at[row + 1, hop],
            (plane.s, to),
        )

    def inside(self, way, hop):
        t, m = self.plane.t, self.plane.m
        holds = t >= hop if way > 0 else t < m - hop
        passes = t < m - 1 if way > 0 else t > 0
        return holds, passes

    def start(self):
        self.pass_on(0)

    def pass_on(self, hop):
        for way in (1, -1):
            holds, passes = self.inside(way, hop)

            @pl.when(holds & passes)
            def _(way=way):
                self.copy(way, hop, self.plane.t + way).start()

    def step(self, hop):
        plane = self.plane
        for way in (1, -1):
            holds, _ = self.inside(way, hop)

            @pl.when(holds)
            def _(way=way):
                row = 0 if way > 0 else 2
                slot = self.slot_of(plane.t - way * hop)
                remote(
                    slot,
                    slot,
                    self.sems.at[row, hop - 1],
                    self.sems.at[row + 1, hop - 1],
                    (plane.s, plane.t - way),
                ).wait_recv()

        if hop < plane.m - 1:
            self.pass_on(hop)

    def wait_sends(self):
        for hop in range(self.plane.m - 1):
            for way in (1, -1):
                holds, passes = self.inside(way, hop)

                @pl.when(holds & passes)
                def _(way=way, hop=hop):
                    self.copy(way, hop, self.plane.t + way).wait_send()


class Scatter:
    def __init__(self, plane, parts, total, add, own, got, sems, loc):
        t = plane.t
        self.plane, self.total = plane, total
        self.add, self.own, self.got, self.loc = add, own, got, loc
        self.inner = (t == 1) | (t == 2)
        self.outer = (t == 0) | (t == 3)
        up = t // 2
        self.near = t + 1 - 2 * lax.rem(t, 2)
        self.far_outer = 3 - 3 * up
        self.far_inner = 2 - up
        self.parts, self.sems = parts, sems

    def copy(self, i, j, src, dst, to):
        return remote(
            src, dst, self.sems.at[0, i, j], self.sems.at[1, i, j], (self.plane.s, to)
        )

    def first(self, i, j):
        chunk = (self.far_outer, self.far_inner, self.near)[i]
        dst = self.got.at[0, j] if i == 2 else self.add.at[i, j]
        return self.copy(i, j, self.parts.at[chunk, j], dst, self.near)

    def back(self, j):
        return self.copy(2, j, self.parts.at[self.near, j], self.got.at[0, j], self.near)

    def sent(self, i, j):
        to = self.far_inner if i else self.far_outer
        return remote(
            self.add.at[i, j],
            self.got.at[1, j],
            self.sems.at[0, 3 + i, j],
            self.sems.at[1, 3, j],
            (self.plane.s, to),
        )

    def load(self, i, j):
        chunk = (self.far_outer, self.far_inner, self.plane.t)[i]
        dst = self.total.at[j] if i == 2 else self.own.at[i, j]
        return pltpu.make_async_copy(self.parts.at[chunk, j], dst, self.loc.at[i, j])

    def start(self):
        for j in range(2):
            self.load(2, j).start()

        @pl.when(self.outer)
        def _():
            for i in range(3):
                for j in range(2):
                    self.first(i, j).start()

        @pl.when(self.inner)
        def _():
            for j in range(2):
                self.back(j).start()
            for i in range(2):
                for j in range(2):
                    self.load(i, j).start()

    def relay(self, i, j):
        @pl.when(self.inner)
        def _():
            self.first(i, j).wait_recv()
            self.load(i, j).wait()
            add, own = self.add, self.own

            def both(at):
                value = add[i, j, at, :].astype(f32) + own[i, j, at, :].astype(f32)
                add[i, j, at, :] = value.astype(bf16)

            in_tiles(add.shape[2], both, 256)
            self.sent(i, j).start()

    def finish(self):
        total, got = self.total, self.got
        for j in range(2):
            self.load(2, j).wait()
            self.back(j).wait_recv()
            self.sent(0, j).wait_recv()

            def sums(at, j=j):
                value = total[j, at, :].astype(f32) + got[0, j, at, :].astype(f32)
                total[j, at, :] = (value + got[1, j, at, :].astype(f32)).astype(bf16)

            in_tiles(total.shape[1], sums, 256)

        @pl.when(self.outer)
        def _():
            for i in range(3):
                for j in range(2):
                    self.first(i, j).wait_send()

        @pl.when(self.inner)
        def _():
            for j in range(2):
                self.back(j).wait_send()
                for i in range(2):
                    self.sent(i, j).wait_send()

    @staticmethod
    def scratch(shape):
        return [
            pltpu.VMEM((2,) + shape, bf16),
            pltpu.VMEM((2,) + shape, bf16),
            pltpu.VMEM((2,) + shape, bf16),
            pltpu.SemaphoreType.DMA((2, 5, 2)),
            pltpu.SemaphoreType.DMA((3, 2)),
        ]


def fan(plane, src_of, dst_of, send, recv):
    copies = []
    for k in range(1, plane.m):
        device = plane.tp_ahead(k)
        copies.append(
            remote(src_of(device[1]), dst_of(plane.t), send.at[k - 1], recv.at[k - 1], device)
        )
    return copies


def exchange(plane, src_of, dst_of, send, recv, local):
    own = pltpu.make_async_copy(src_of(plane.s), dst_of(plane.s), local)
    copies = []
    for k in range(1, plane.n):
        peer = plane.seq_ahead(k)
        copies.append(
            remote(
                src_of(peer), dst_of(plane.s), send.at[k - 1], recv.at[k - 1], plane.device(peer)
            )
        )
    return [own] + copies


TILE = 32


def in_tiles(rows, body, tile=TILE):
    def one(i, carry):
        body(pl.ds(pl.multiple_of(i * tile, tile), tile))
        return carry

    lax.fori_loop(0, rows // tile, one, 0)


class Reduce:
    SLOTS = (4, 4, 3)

    THEIRS = (0, 2, 1, 3)

    def __init__(self, plane, part_of, pair, near, far, sems, loc, stage=None):
        c = plane.c
        self.pair, self.near, self.far = pair, near, far
        self.rows = pair.shape[1]
        self.swaps, self.loads = {}, {}
        for k in range(4):
            mine = self.THEIRS[k]
            chip = plane.order[mine]
            source = part_of(2 * chip + 1 - c) if stage is None else stage.at[mine]
            self.swaps[k] = remote(
                source, near.at[k], sems.at[0, k], sems.at[1, k], plane.sibling()
            )
            if stage is None:
                self.loads[k] = pltpu.make_async_copy(
                    part_of(2 * plane.order[k] + c), pair.at[k], loc.at[k]
                )

        def out(i, k, chip):
            return remote(
                pair.at[k], far.at[i], sems.at[2, i], sems.at[3, i], plane.same(chip)
            )

        self.out = [out(0, 3, plane.to), out(1, 1, plane.to), out(2, 2, plane.fro)]

    def start(self, *which):
        for k in which:
            self.swaps[k].start()
            self.loads[k].start()

    def landed(self, k):
        self.swaps[k].wait()
        if self.loads:
            self.loads[k].wait()

    def join(self, k):
        pair, near = self.pair, self.near
        self.landed(k)

        def add(at):
            both = pair[k, at, :].astype(f32) + near[k, at, :].astype(f32)
            pair[k, at, :] = both.astype(bf16)

        in_tiles(self.rows, add)

    def send_to(self):
        self.join(3)
        self.out[0].start()
        self.join(1)
        self.out[1].start()

    def ready(self):
        self.landed(2)

    def send_fro(self):
        pair, near, far = self.pair, self.near, self.far
        self.out[0].wait_recv()

        def add(at):
            both = pair[2, at, :].astype(f32) + near[2, at, :].astype(f32)
            pair[2, at, :] = (both + far[0, at, :].astype(f32)).astype(bf16)

        in_tiles(self.rows, add)
        self.out[2].start()

    def first(self, total, more=None):
        pair, near = self.pair, self.near
        self.landed(0)

        def add(at):
            value = pair[0, at, :].astype(f32) + near[0, at, :].astype(f32)
            total[at, :] = value if more is None else value + more[at, :].astype(f32)

        in_tiles(self.rows, add)

    def finish(self, total, out=None):
        far = self.far
        out = total if out is None else out
        self.out[0].wait_send()
        self.out[1].wait()
        self.out[2].wait()

        def add(at):
            value = total[at, :] + far[1, at, :].astype(f32) + far[2, at, :].astype(f32)
            out[at, :] = value.astype(out.dtype)

        in_tiles(self.rows, add)

    @staticmethod
    def scratch(rows, width):
        return [pltpu.VMEM((slots, rows, width), bf16) for slots in Reduce.SLOTS] + [
            pltpu.SemaphoreType.DMA((4, 4)),
            pltpu.SemaphoreType.DMA((4,)),
        ]


def last_body(
    n, m, dqkv_in, w_in, norm_t, ffn, downs, wo, vec,
    total, ffn_out, qkv_out, wo_out, vec_out,
    dqkv, w, down_here, down_sum, narrow, pair, near, far, sr, lr, stage, norms, mine, got, summed, sems, st, loc,
):
    plane = Plane(n, m)
    greet(plane, True)
    loads = [
        pltpu.make_async_copy(a, b, loc.at[5 + i])
        for i, (a, b) in enumerate(
            ((dqkv_in, dqkv), (w_in, w), (downs, down_here))
        )
    ]
    load = pltpu.make_async_copy(norm_t, norms, loc.at[0])
    for copy in loads + [load]:
        copy.start()
    narrow[...] = lanes_of_columns(narrow.shape, 1)
    meet(plane, True)
    rows, width = ffn_out.shape[1], ffn.shape[2]
    across = fan(plane, lambda t: wo.at[t], lambda t: wo_out.at[t], st.at[1, 0], st.at[1, 1])
    across += fan(plane, lambda t: vec.at[t], lambda t: vec_out.at[t], st.at[2, 0], st.at[2, 1])
    across += [
        pltpu.make_async_copy(wo.at[plane.t], wo_out.at[plane.t], loc.at[1]),
        pltpu.make_async_copy(vec.at[plane.t], vec_out.at[plane.t], loc.at[2]),
    ]
    for copy in across:
        copy.start()
    a = exchange(
        plane,
        lambda i: ffn.at[:, pl.ds(pl.multiple_of(i * rows, rows), rows), :],
        lambda i: ffn_out.at[
            pl.ds(0, 2), :, pl.ds(pl.multiple_of(i * width, width), width)
        ],
        sems.at[0, 0],
        sems.at[0, 1],
        loc.at[3],
    )
    a_down = exchange(
        plane,
        lambda i: down_sum.at[pl.ds(pl.multiple_of(i * rows, rows), rows), :],
        lambda i: ffn_out.at[2, :, pl.ds(pl.multiple_of(i * width, width), width)],
        sems.at[2, 0],
        sems.at[2, 1],
        loc.at[10],
    )
    for copy in a:
        copy.start()
    reduce = Reduce(plane, None, pair, near, far, sr, lr, stage)
    tokens = pair.shape[1]
    for copy in loads[:2]:
        copy.wait()

    def blocks(it, carry):
        k = 3 - it // 2
        other = 1 - lax.rem(it, 2)
        b = plane.number(k, other)
        here = pl.ds(pl.multiple_of(b * tokens, tokens), tokens)
        part = lax.dot_general(dqkv[here, :], w[...], NT, preferred_element_type=f32).astype(bf16)

        @pl.when(other == 0)
        def _():
            pair[k] = part

        @pl.when(other == 1)
        def _():
            stage[k] = part

        for kk in range(4):

            @pl.when(it == 2 * (3 - kk))
            def _(kk=kk):
                reduce.swaps[Reduce.THEIRS[kk]].start()

        return carry

    lax.fori_loop(0, n, blocks, 0)
    reduce.send_to()
    loads[2].wait()

    def add_down(at):
        value = down_here[0, at, :].astype(f32)
        for t in range(1, m):
            value = value + down_here[t, at, :].astype(f32)
        down_sum[at, :] = value.astype(bf16)

    in_tiles(down_sum.shape[0], add_down)
    for copy in a_down:
        copy.start()
    load.wait()
    strip = summed.shape[1]

    def weight_grads(s, carry):
        at = pl.ds(pl.multiple_of(s * m * strip, m * strip), m * strip)
        value = jnp.dot(norms[at, :], dqkv[...], preferred_element_type=f32).astype(bf16)
        value = jnp.dot(value, narrow[...], preferred_element_type=f32).astype(bf16)
        for t in range(m):
            mine[s, t] = value[t * strip : (t + 1) * strip]
        return carry

    lax.fori_loop(0, n, weight_grads, 0)
    over = fan(plane, lambda t: mine.at[:, t], lambda t: got.at[t], st.at[0, 0], st.at[0, 1])
    for copy in over:
        copy.start()
    reduce.ready()
    reduce.first(total)
    reduce.send_fro()
    for copy in over:
        copy.wait()

    def add(s, carry):
        value = mine[s, plane.t].astype(f32)
        for k in range(1, m):
            value = value + got[plane.tp_behind(k), s].astype(f32)
        summed[s] = value.astype(bf16)
        return carry

    lax.fori_loop(0, n, add, 0)
    b = exchange(
        plane,
        lambda i: summed.at[i],
        lambda i: qkv_out.at[i],
        sems.at[1, 0],
        sems.at[1, 1],
        loc.at[4],
    )
    for copy in b:
        copy.start()
    reduce.finish(total)
    for copy in a + a_down + b + across:
        copy.wait()


def last(n, m, dqkv, w, norm_t, ffn, downs, wo, vec, ident):
    width, length = norm_t.shape
    tokens = length // n
    cols = w.shape[1] // SLOT * HALF
    strip = width // (n * m)
    vmem = pl.BlockSpec(memory_space=pltpu.VMEM)
    hbm = pl.BlockSpec(memory_space=ANY)
    return pl.pallas_call(
        functools.partial(last_body, n, m),
        out_shape=(
            jax.ShapeDtypeStruct((tokens, width), f32),
            jax.ShapeDtypeStruct((3, ffn.shape[1] // n, ffn.shape[2] * n), ffn.dtype),
            jax.ShapeDtypeStruct((n, strip, cols), bf16),
            jax.ShapeDtypeStruct(wo.shape, wo.dtype),
            jax.ShapeDtypeStruct(vec.shape, vec.dtype),
        ),
        in_specs=[hbm] * 7,
        out_specs=[vmem] + [hbm] * 4,
        scratch_shapes=[
            pltpu.VMEM(dqkv.shape, bf16),
            pltpu.VMEM(w.shape, bf16),
            pltpu.VMEM(downs.shape, bf16),
            pltpu.VMEM(downs.shape[1:], bf16),
            pltpu.VMEM((w.shape[1], cols), bf16),
        ]
        + Reduce.scratch(tokens, width)
        + [
            pltpu.VMEM((4, tokens, width), bf16),
            pltpu.VMEM((width, length), bf16),
            pltpu.VMEM((n, m, strip, cols), bf16),
            pltpu.VMEM((m, n, strip, cols), bf16),
            pltpu.VMEM((n, strip, cols), bf16),
            pltpu.SemaphoreType.DMA((3, 2, n - 1)),
            pltpu.SemaphoreType.DMA((3, 2, m - 1)),
            pltpu.SemaphoreType.DMA((11,)),
        ],
        compiler_params=pltpu.CompilerParams(
            collective_id=ident, has_side_effects=True, vmem_limit_bytes=VMEM_LIMIT
        ),
        cost_estimate=COST,
        name="last",
    )(dqkv, w, norm_t, ffn, downs, wo, vec)


def column(row):
    return jnp.broadcast_to(row, (8, row.shape[1])).T[:, :1]


def lanes_of_columns(shape, of):
    column = lax.broadcasted_iota(jnp.int32, shape, of).astype(f32)
    lane = lax.broadcasted_iota(jnp.int32, shape, 1 - of).astype(f32)
    half = jnp.floor((column + 0.5) * (1.0 / HALF))
    return jnp.where(lane == column + half * (SLOT - HALF), 1.0, 0.0).astype(bf16)


def gain_row(tiles, which, strip):
    stacked = tiles.reshape(-1, LANES).astype(bf16)
    count = stacked.shape[0] // 8
    shape = (LANES, count * strip)
    lane = lax.broadcasted_iota(jnp.int32, shape, 1).astype(f32)
    owner = jnp.floor((lane + 0.5) * (1.0 / strip))
    inside = lane - owner * strip
    pick = lax.broadcasted_iota(jnp.int32, shape, 0).astype(f32) == inside
    spread_out = jnp.dot(
        stacked, jnp.where(pick, 1.0, 0.0).astype(bf16), preferred_element_type=f32
    )
    shape = spread_out.shape
    lane = lax.broadcasted_iota(jnp.int32, shape, 1).astype(f32)
    owner = jnp.floor((lane + 0.5) * (1.0 / strip))
    row = lax.broadcasted_iota(jnp.int32, shape, 0).astype(f32)
    mine = row == owner * 8.0 + which
    return jnp.sum(jnp.where(mine, spread_out, 0.0), axis=0, keepdims=True)


def entry_body(
    n, m, heads, strip, x, doc_ids, positions, wq, wk, wv, one, two, wg, wu, wd, wo, inverse,
    norm_t, q, k, v, cosine, sine, w, gain_one, gain_two, docs, ffn, down, wo_z,
    blocks, norms, turned, places_all, w_all, gains_all, q_here, k_here, v_here, cos_here, sin_here,
    places, wqkv, gains, widen, sx, lx, rem, sz, sn, loc,
):
    plane = Plane(n, m)
    greet(plane, True)
    tokens = x.shape[0]
    start = 0
    for weight in (wq, wk, wv):
        each = weight.shape[1] // n
        for i in range(n):
            wqkv[i, :, start : start + each] = weight[:, i * each : (i + 1) * each]
        start += each
    gains[...] = jnp.zeros_like(gains)
    gains[0:1, :strip] = one[...].astype(f32)
    gains[1:2, :strip] = two[...].astype(f32)
    places[0:1, :] = doc_ids[...]
    places[1:2, :] = positions[...]
    meet(plane, True)
    gather = Gathers(plane, x, lambda i: blocks.at[i], sx, lx, 1)
    first = []
    for i, (src, dst) in enumerate(((gains, gains_all), (wqkv, w_all))):
        first += exchange(
            plane,
            lambda s, src=src, i=i: src.at[s] if i else src,
            lambda s, dst=dst: dst.at[s, plane.t],
            rem.at[i, 0],
            rem.at[i, 1],
            loc.at[1 + i],
        )
    few = exchange(
        plane, lambda i: places, lambda i: places_all.at[i], rem.at[2, 0], rem.at[2, 1], loc.at[3]
    )
    for copy in first + few:
        copy.start()
    gather.start()
    across = []
    for i, ref in enumerate((gains_all, w_all)):

        def slot(t, ref=ref):
            return ref.at[:, plane.t]

        across.append(fan(plane, slot, slot, sz.at[i, 0], sz.at[i, 1]))
    across.append(fan(plane, lambda t: wo, lambda t: wo_z.at[t], sz.at[2, 0], sz.at[2, 1]))
    own_wo = pltpu.make_async_copy(wo, wo_z.at[plane.t], loc.at[4])
    own_wo.start()
    for copy in first:
        copy.wait()
    for copy in across[0] + across[1]:
        copy.start()
    widen[...] = lanes_of_columns(widen.shape, 0)
    moves = []
    width, rows = wg.shape[1] // n, wg.shape[0]
    for j, weight in enumerate((wg, wu, wd)):
        moves += exchange(
            plane,
            lambda i, weight=weight: weight.at[:, pl.ds(pl.multiple_of(i * width, width), width)],
            lambda i, dst=ffn.at[j] if j < 2 else down: dst.at[
                pl.ds(pl.multiple_of(i * rows, rows), rows), :
            ],
            rem.at[3 + j, 0],
            rem.at[3 + j, 1],
            loc.at[5 + j],
        )
    for copy in few + across[0]:
        copy.wait()
    tiles = gains_all[...]
    gain_one[...] = gain_row(tiles, 0, strip)
    gain_two[...] = gain_row(tiles, 1, strip)
    gather.wait_own()

    def number(it):
        return plane.number(it // 2, lax.rem(it, 2))

    def store(it, at):
        span = pl.ds(pl.multiple_of(number(it) * tokens, tokens), tokens)
        return pltpu.make_async_copy(turned.at[at], norm_t.at[:, span], sn.at[at])

    def normalize(it, carry):
        b = number(it)
        at = lax.rem(it, 2)

        @pl.when(it == 1)
        def _():
            gather.wait_swap()

        @pl.when(it == 2)
        def _():
            gather.relay_near()

        @pl.when(it == 3)
        def _():
            gather.wait_share(1)

        @pl.when(it == 5)
        def _():
            gather.wait_share(0)

        @pl.when(it == 6)
        def _():
            gather.relay_far()
            for copy in moves + across[2]:
                copy.start()

        @pl.when(it == 7)
        def _():
            gather.wait_share(2)

        @pl.when(it >= 2)
        def _():
            store(it - 2, at).wait()

        value = blocks[b].astype(f32)
        scale = lax.rsqrt(jnp.mean(value * value, axis=1, keepdims=True) + norm_epsilon)
        low = (value * scale * gain_one[...]).astype(bf16)
        norms[b] = low
        turned[at] = low.T
        store(it, at).start()
        here = pl.ds(pl.multiple_of(b * tokens, tokens), tokens)
        docs[:, here] = places_all[b, 0:1, :]
        angles = column(places_all[b, 1:2, :].astype(f32)) * inverse[...]
        lanes = lax.broadcasted_iota(jnp.int32, angles.shape, 1)
        sin = jnp.sin(angles)
        cos_here[here, :] = jnp.cos(angles)
        sin_here[here, :] = jnp.where(lanes < SLOT, -sin, sin)
        return carry

    lax.fori_loop(0, n, normalize, 0)
    outs = [
        pltpu.make_async_copy(cos_here, cosine, loc.at[8]),
        pltpu.make_async_copy(sin_here, sine, loc.at[9]),
        pltpu.make_async_copy(q_here, q, loc.at[10]),
        pltpu.make_async_copy(k_here, k, loc.at[11]),
        pltpu.make_async_copy(v_here, v, loc.at[12]),
    ]
    for copy in outs[:2]:
        copy.start()
    for copy in across[1]:
        copy.wait()

    def widened(s, carry):
        at = pl.ds(pl.multiple_of(s * m * strip, m * strip), m * strip)
        narrow = w_all[s].reshape(m * strip, w_all.shape[3])
        w[at, :] = jnp.dot(narrow, widen[...], preferred_element_type=f32).astype(bf16)
        return carry

    lax.fori_loop(0, n, widened, 0)

    def project(b, carry):
        here = pl.ds(pl.multiple_of(b * tokens, tokens), tokens)
        out = jnp.dot(norms[b], w[...], preferred_element_type=f32)
        cos, sin = cos_here[here, :], sin_here[here, :]
        for h in range(heads + 1):
            part = out[:, h * LANES : (h + 1) * LANES]
            rotated = (part * cos + pltpu.roll(part, SLOT, 1) * sin).astype(bf16)
            if h < heads:
                q_here[h, here, :] = rotated
            else:
                k_here[here, :] = rotated
        v_here[here, :] = out[:, (heads + 1) * LANES :].astype(bf16)
        return carry

    lax.fori_loop(0, n, project, 0)
    for copy in outs[2:]:
        copy.start()
    gather.wait_sends()
    store(n - 2, 0).wait()
    store(n - 1, 1).wait()
    own_wo.wait()
    for copy in across[2] + moves + outs:
        copy.wait()


def entry(n, m, heads, x, docs, positions, wq, wk, wv, one, two, wg, wu, wd, wo, inverse, ident):
    tokens, width = x.shape
    length = n * tokens
    strip = wq.shape[0]
    each = (wq.shape[1] + wk.shape[1] + wv.shape[1]) // n
    wide = each // HALF * SLOT
    rows, cols = wg.shape
    vmem = pl.BlockSpec(memory_space=pltpu.VMEM)
    hbm = pl.BlockSpec(memory_space=ANY)
    return pl.pallas_call(
        functools.partial(entry_body, n, m, heads, strip),
        out_shape=(
            jax.ShapeDtypeStruct((width, length), bf16),
            jax.ShapeDtypeStruct((heads, length, LANES), bf16),
            jax.ShapeDtypeStruct((length, LANES), bf16),
            jax.ShapeDtypeStruct((length, LANES), bf16),
            jax.ShapeDtypeStruct((length, LANES), f32),
            jax.ShapeDtypeStruct((length, LANES), f32),
            jax.ShapeDtypeStruct((width, wide), bf16),
            jax.ShapeDtypeStruct((1, width), f32),
            jax.ShapeDtypeStruct((1, width), f32),
            jax.ShapeDtypeStruct((1, length), jnp.int32),
            jax.ShapeDtypeStruct((2, rows * n, cols // n), wg.dtype),
            jax.ShapeDtypeStruct((rows * n, cols // n), wg.dtype),
            jax.ShapeDtypeStruct((m,) + wo.shape, wo.dtype),
        ),
        in_specs=[hbm] + [vmem] * 7 + [hbm] * 4 + [vmem],
        out_specs=[hbm] * 6 + [vmem] * 4 + [hbm] * 3,
        scratch_shapes=[
            pltpu.VMEM((n, tokens, width), bf16),
            pltpu.VMEM((n, tokens, width), bf16),
            pltpu.VMEM((2, width, tokens), bf16),
            pltpu.VMEM((n, 2, tokens), jnp.int32),
            pltpu.VMEM((n, m, strip, each), bf16),
            pltpu.VMEM((n, m, 8, LANES), f32),
            pltpu.VMEM((heads, length, LANES), bf16),
            pltpu.VMEM((length, LANES), bf16),
            pltpu.VMEM((length, LANES), bf16),
            pltpu.VMEM((length, LANES), f32),
            pltpu.VMEM((length, LANES), f32),
            pltpu.VMEM((2, tokens), jnp.int32),
            pltpu.VMEM((n, strip, each), bf16),
            pltpu.VMEM((8, LANES), f32),
            pltpu.VMEM((each, wide), bf16),
            *Gathers.scratch(1),
            pltpu.SemaphoreType.DMA((6, 2, n - 1)),
            pltpu.SemaphoreType.DMA((3, 2, m - 1)),
            pltpu.SemaphoreType.DMA((2,)),
            pltpu.SemaphoreType.DMA((13,)),
        ],
        compiler_params=pltpu.CompilerParams(
            collective_id=ident, has_side_effects=True, vmem_limit_bytes=VMEM_LIMIT
        ),
        cost_estimate=COST,
        name="entry",
    )(x, docs, positions, wq, wk, wv, one, two, wg, wu, wd, wo, inverse)


BLOCK = 512
NT = (((1,), (1,)), ((), ()))
LOG2E = 1.4426950408889634


def allowed_block(first_key, first_query, begin, causal):
    keys = first_key + lax.broadcasted_iota(jnp.int32, (BLOCK, BLOCK), 0)
    ok = keys >= begin
    if causal:
        queries = first_query + lax.broadcasted_iota(jnp.int32, (BLOCK, BLOCK), 1)
        ok = ok & (keys <= queries)
    return ok


def begins(docs):
    begin = jnp.zeros(docs.shape, jnp.int32)
    for d in range(3):
        count = jnp.sum((docs == d).astype(f32), axis=1, keepdims=True).astype(jnp.int32)
        begin = begin + jnp.where(docs > d, count, 0)
    return begin


def spread_rows(wo, wo_here):
    halves, filled, width = wo.shape
    for i in range(halves):
        wo_here[i * SLOT : i * SLOT + filled, :] = wo[i]
        wo_here[i * SLOT + filled : (i + 1) * SLOT, :] = jnp.zeros((SLOT - filled, width), bf16)


def attend_body(
    n, m, factor, q, k, v, docs, wo, go, x, gain, ffn,
    o_out, lse, start, low_out, go_all, resid, norm, ffn_all,
    o, low, vt, top, total, acc, wo_here, go_here,
    pair, near, far, sr, lr, stage, sg, lg, sz, loc,
):
    plane = Plane(n, m)
    rows = x.shape[0]
    heads = q.shape[0]
    greet(plane, True)
    gather = Gathers(plane, go, lambda i: go_here.at[i], sg, lg, 2)
    reduce = Reduce(plane, None, pair, near, far, sr, None, stage)
    spread_rows(wo, wo_here)
    vt[...] = v[...].T
    start[...] = begins(docs[...])
    meet(plane, True)
    gather.start()
    chain = Chain(plane, ffn, lambda t: ffn_all.at[t], sz)
    chain.start()
    own_ffn = pltpu.make_async_copy(ffn, ffn_all.at[plane.t], loc.at[3])
    own_ffn.start()

    def chips(step, carry):
        kk = 3 - step
        i = plane.number(kk, 0) // 2
        here = pl.ds(pl.multiple_of(i * BLOCK, BLOCK), BLOCK)
        begin = start[:, here]

        def head(h, carry):
            query = q[h, here, :]
            top[...] = jnp.full_like(top, mask_fill_value)
            total[...] = jnp.zeros_like(total)
            acc[...] = jnp.zeros_like(acc)

            def keys(j, causal):
                at = pl.ds(pl.multiple_of(j * BLOCK, BLOCK), BLOCK)
                raw = lax.dot_general(k[at, :], query, NT, preferred_element_type=f32)
                ok = allowed_block(j * BLOCK, i * BLOCK, begin, causal)
                scores = jnp.where(ok, raw * factor, mask_fill_value)
                new_top = jnp.maximum(top[...], jnp.max(scores, axis=0, keepdims=True))
                weights = jnp.exp2(scores - new_top)
                keep = jnp.exp2(top[...] - new_top)
                total[...] = total[...] * keep + jnp.sum(weights, axis=0, keepdims=True)
                acc[...] = acc[...] * keep + jnp.dot(
                    vt[:, at], weights.astype(bf16), preferred_element_type=f32
                )
                top[...] = new_top

            def loop(j, carry):
                keys(j, False)
                return carry

            lax.fori_loop(0, i, loop, 0)
            keys(i, True)
            out = (acc[...] / total[...]).T
            o[h, here, :] = out
            low[here, pl.ds(pl.multiple_of(h * LANES, LANES), LANES)] = out.astype(bf16)
            lse[h, :, here] = top[...] + jnp.log2(total[...])
            return carry

        lax.fori_loop(0, heads, head, 0)

        @pl.when(step == 1)
        def _():
            reduce.join(3)
            reduce.out[0].start()

        @pl.when(step == 3)
        def _():
            reduce.join(1)
            reduce.out[1].start()

        for other in (1, 0):
            b = plane.number(kk, other)
            at = pl.ds(pl.multiple_of(b * rows, rows), rows)
            part = jnp.dot(low[at, :], wo_here[...], preferred_element_type=f32).astype(bf16)
            if other:
                stage[kk] = part
                for which in range(4):

                    @pl.when(kk == which)
                    def _(which=which):
                        reduce.swaps[Reduce.THEIRS[which]].start()

            else:
                pair[kk] = part
        return carry

    lax.fori_loop(0, 4, chips, 0)
    outs = [
        pltpu.make_async_copy(o, o_out, loc.at[0]),
        pltpu.make_async_copy(low, low_out, loc.at[1]),
    ]
    for copy in outs:
        copy.start()
    gather.relay_near()
    chain.step(1)
    reduce.ready()
    reduce.first(resid, x)
    reduce.send_fro()
    for hop in range(2, m - 1):
        chain.step(hop)
    gather.relay_far()
    reduce.finish(resid)

    def normalize(at):
        value = resid[at, :]
        scale = lax.rsqrt(jnp.mean(value * value, axis=1, keepdims=True) + norm_epsilon)
        norm[at, :] = (value * scale * gain[...]).astype(bf16)

    in_tiles(rows, normalize)
    gather.finish()
    outs.append(pltpu.make_async_copy(go_here, go_all, loc.at[2]))
    outs[-1].start()
    chain.step(m - 1)
    chain.wait_sends()
    own_ffn.wait()
    for copy in outs:
        copy.wait()


def attend(n, m, factor, q, k, v, docs, wo, go, x, gain, ffn, ident):
    heads, length, _ = q.shape
    rows, width = x.shape
    hbm = pl.BlockSpec(memory_space=ANY)
    vmem = pl.BlockSpec(memory_space=pltpu.VMEM)
    return pl.pallas_call(
        functools.partial(attend_body, n, m, factor),
        out_shape=(
            jax.ShapeDtypeStruct((heads, length, LANES), f32),
            jax.ShapeDtypeStruct((heads, 1, length), f32),
            jax.ShapeDtypeStruct((1, length), jnp.int32),
            jax.ShapeDtypeStruct((length, heads * LANES), bf16),
            jax.ShapeDtypeStruct((n,) + go.shape, go.dtype),
            jax.ShapeDtypeStruct((rows, width), f32),
            jax.ShapeDtypeStruct((rows, width), bf16),
            jax.ShapeDtypeStruct((m,) + ffn.shape, bf16),
        ),
        in_specs=[vmem] * 5 + [hbm] + [vmem] * 2 + [hbm],
        out_specs=[hbm, vmem, vmem, hbm, hbm, vmem, vmem, hbm],
        scratch_shapes=[
            pltpu.VMEM((heads, length, LANES), f32),
            pltpu.VMEM((length, heads * LANES), bf16),
            pltpu.VMEM((LANES, length), bf16),
            pltpu.VMEM((1, BLOCK), f32),
            pltpu.VMEM((1, BLOCK), f32),
            pltpu.VMEM((LANES, BLOCK), f32),
            pltpu.VMEM((heads * LANES, width), bf16),
            pltpu.VMEM((n,) + go.shape, go.dtype),
        ]
        + Reduce.scratch(rows, width)
        + [pltpu.VMEM((4, rows, width), bf16)]
        + Gathers.scratch(2)
        + [pltpu.SemaphoreType.DMA((4, m)), pltpu.SemaphoreType.DMA((4,))],
        compiler_params=pltpu.CompilerParams(
            collective_id=ident, has_side_effects=True, vmem_limit_bytes=VMEM_LIMIT
        ),
        cost_estimate=COST,
        name="attend",
    )(q, k, v, docs, wo, go, x, gain, ffn)


def attend_back_body(
    n, m, factor, scale, q_in, k_in, v_in, o_in, lse, begin, cos_in, sin_in, low_in,
    hid_in, down_in, ffn, wo, dnorm, resid, grad, gain,
    out, layer, terms, dresid, gain_out, ffn_sum,
    q, k, v, o, cosine, sine, low, kt, dqt, dk, dv, delta, go, every, dbranch, wo_here,
    hid_low, w_down, stage, pair, near, far, sr, lr, held, gain_sum, gain_cut, gain_got,
    sums, add, own, got, ss, ls, sg, lg, sv, loc,
):
    plane = Plane(n, m)
    heads, length, _ = q.shape
    rows, width = dnorm.shape
    strip = gain_out.shape[2]
    loads = [
        pltpu.make_async_copy(a, b, loc.at[i])
        for i, (a, b) in enumerate(
            (
                (q_in, q), (k_in, k), (v_in, v), (o_in, o),
                (cos_in, cosine), (sin_in, sine), (low_in, low),
            )
        )
    ]
    for copy in loads:
        copy.start()
    greet(plane, True)
    moves = [
        pltpu.make_async_copy(hid_in, hid_low, loc.at[8]),
        pltpu.make_async_copy(down_in, w_down, loc.at[9]),
    ]
    for copy in moves:
        copy.start()
    one = Reduce(plane, None, pair, near, far, sr, None, stage)
    gather = Gathers(plane, dbranch, lambda i: every.at[i], sg, lg, 2)
    gain_copies = exchange(
        plane, lambda i: gain_cut.at[i], lambda i: gain_got.at[i], sv.at[0], sv.at[1], loc.at[7]
    )
    gain_sum[...] = jnp.zeros_like(gain_sum)

    def into_branch(at):
        value, up = resid[at, :], dnorm[at, :]
        scale_two = lax.rsqrt(jnp.mean(value * value, axis=1, keepdims=True) + norm_epsilon)
        inner = gain[...] * up
        moment = jnp.mean(value * inner, axis=1, keepdims=True)
        turned = value * scale_two
        got = (
            grad[at, :].astype(f32) + scale_two * inner - turned * (scale_two * scale_two * moment)
        )
        dresid[at, :] = got
        dbranch[at, :] = got.astype(bf16)
        gain_sum[...] += up * turned

    in_tiles(rows, into_branch)
    meet(plane, True)
    gather.start()
    scatter = Scatter(plane, ffn, sums, add, own, got, ss, ls)
    scatter.start()
    total_gain = jnp.sum(gain_sum[...], axis=0, keepdims=True)
    for i in range(n):
        gain_cut[i] = total_gain[:, i * (width // n) : (i + 1) * (width // n)]
    for copy in gain_copies:
        copy.start()
    spread_rows(wo, wo_here)
    for copy in moves:
        copy.wait()

    def mix(it, carry):
        kk = 3 - it // 2
        other = 1 - lax.rem(it, 2)
        b = plane.number(kk, other)
        at = pl.ds(pl.multiple_of(b * rows, rows), rows)
        part = lax.dot_general(
            hid_low[at, :], w_down[...], NT, preferred_element_type=f32
        ).astype(bf16)

        @pl.when(other == 0)
        def _():
            pair[kk] = part

        @pl.when(other == 1)
        def _():
            stage[kk] = part

        for which in range(4):

            @pl.when(it == 2 * (3 - which))
            def _(which=which):
                one.swaps[Reduce.THEIRS[which]].start()

        return carry

    lax.fori_loop(0, n, mix, 0)
    for copy in loads:
        copy.wait()
    kt[...] = k[...].T
    dk[...] = jnp.zeros_like(dk)
    dv[...] = jnp.zeros_like(dv)

    def unturn(value, at):
        return value * cosine[at, :] - pltpu.roll(value, SLOT, 1) * sine[at, :]

    def chips(kk, carry):
        @pl.when(kk == 0)
        def _():
            gather.wait_own()
            gather.wait_swap()

        @pl.when(kk == 1)
        def _():
            gather.relay_near()
            one.send_to()
            gather.wait_share(1)
            scatter.relay(0, 0)

        @pl.when(kk == 2)
        def _():
            gather.wait_share(0)
            scatter.relay(0, 1)

        @pl.when(kk == 3)
        def _():
            one.ready()
            one.first(held, resid)
            gather.relay_far()
            gather.wait_share(2)
            scatter.relay(1, 0)

        i = plane.number(kk, 0) // 2
        here = pl.ds(pl.multiple_of(i * BLOCK, BLOCK), BLOCK)
        for other in range(2):
            b = plane.number(kk, other)
            at = pl.ds(pl.multiple_of(b * rows, rows), rows)
            value = lax.dot_general(every[b], wo_here[...], NT, preferred_element_type=f32)
            for h in range(heads):
                go[h, at, :] = value[:, h * LANES : (h + 1) * LANES].astype(bf16)

        def head(h, carry):
            query = q[h, here, :]
            grads = go[h, here, :]
            delta[...] = jnp.sum((grads.astype(f32) * o[h, here, :]).T, axis=0, keepdims=True)
            dqt[...] = jnp.zeros_like(dqt)

            def keys(j, causal):
                at = pl.ds(pl.multiple_of(j * BLOCK, BLOCK), BLOCK)
                raw = lax.dot_general(k[at, :], query, NT, preferred_element_type=f32)
                ok = allowed_block(j * BLOCK, i * BLOCK, begin[:, here], causal)
                probs = jnp.where(ok, jnp.exp2(raw * factor - lse[h, :, here]), 0.0)
                dprob = lax.dot_general(v[at, :], grads, NT, preferred_element_type=f32)
                dscore = (probs * (dprob - delta[...])).astype(bf16)
                dv[at, :] += jnp.dot(probs.astype(bf16), grads, preferred_element_type=f32)
                dk[at, :] += jnp.dot(dscore, query, preferred_element_type=f32)
                dqt[...] += jnp.dot(kt[:, at], dscore, preferred_element_type=f32)

            def loop(j, carry):
                keys(j, False)
                return carry

            lax.fori_loop(0, i, loop, 0)
            keys(i, True)
            got = unturn(dqt[...].T * scale, here).astype(bf16)
            out[here, pl.ds(pl.multiple_of(h * LANES, LANES), LANES)] = got
            return carry

        lax.fori_loop(0, heads, head, 0)
        return carry

    lax.fori_loop(0, 4, chips, 0)
    scatter.relay(1, 1)

    def write(i, carry):
        at = pl.ds(pl.multiple_of(i * BLOCK, BLOCK), BLOCK)
        turned = unturn(dk[at, :] * scale, at).astype(bf16)
        out[at, heads * LANES : (heads + 1) * LANES] = turned
        out[at, (heads + 1) * LANES :] = dv[at, :].astype(bf16)
        return carry

    lax.fori_loop(0, length // BLOCK, write, 0)
    one.send_fro()
    across = every.reshape(length, width)
    part = 512

    def into_terms(i, carry):
        at = pl.ds(pl.multiple_of(i * part, part), part)
        value = lax.dot_general(
            low[...], across[:, at], (((0,), (0,)), ((), ())), preferred_element_type=f32
        ).astype(bf16)
        for half in range(terms.shape[0]):
            terms[half, :, at] = value[half * SLOT : half * SLOT + HALF]
        return carry

    lax.fori_loop(0, width // part, into_terms, 0)
    for copy in gain_copies:
        copy.wait()
    all_gain = gain_got[0]
    for i in range(1, n):
        all_gain = all_gain + gain_got[i]
    for t in range(m):
        gain_out[t] = all_gain[:, t * strip : (t + 1) * strip]
    gather.wait_sends()
    one.finish(held, layer)
    scatter.finish()
    back = pltpu.make_async_copy(sums, ffn_sum, loc.at[10])
    back.start()
    back.wait()


def attend_back(
    n, m, factor, scale, q, k, v, o, lse, begin, cosine, sine, low,
    hid_low, w_down, ffn, wo, dnorm, resid, grad, gain, ident,
):
    heads, length, _ = q.shape
    rows, width = dnorm.shape
    strip = width // (n * m)
    hbm = pl.BlockSpec(memory_space=ANY)
    vmem = pl.BlockSpec(memory_space=pltpu.VMEM)
    return pl.pallas_call(
        functools.partial(attend_back_body, n, m, factor, scale),
        out_shape=(
            jax.ShapeDtypeStruct((length, (heads + 2) * LANES), bf16),
            jax.ShapeDtypeStruct((rows, width), bf16),
            jax.ShapeDtypeStruct(wo.shape, bf16),
            jax.ShapeDtypeStruct((rows, width), f32),
            jax.ShapeDtypeStruct((m, 1, strip), f32),
            jax.ShapeDtypeStruct(ffn.shape[1:], bf16),
        ),
        in_specs=[hbm] * 4 + [vmem] * 2 + [hbm] * 6 + [vmem] * 5,
        out_specs=[vmem] * 5 + [hbm],
        scratch_shapes=[
            pltpu.VMEM(q.shape, bf16),
            pltpu.VMEM(k.shape, bf16),
            pltpu.VMEM(v.shape, bf16),
            pltpu.VMEM(o.shape, f32),
            pltpu.VMEM(cosine.shape, f32),
            pltpu.VMEM(sine.shape, f32),
            pltpu.VMEM(low.shape, bf16),
            pltpu.VMEM((LANES, length), bf16),
            pltpu.VMEM((LANES, BLOCK), f32),
            pltpu.VMEM((length, LANES), f32),
            pltpu.VMEM((length, LANES), f32),
            pltpu.VMEM((1, BLOCK), f32),
            pltpu.VMEM((heads, length, LANES), bf16),
            pltpu.VMEM((n, rows, width), bf16),
            pltpu.VMEM((rows, width), bf16),
            pltpu.VMEM((heads * LANES, width), bf16),
            pltpu.VMEM(hid_low.shape, bf16),
            pltpu.VMEM(w_down.shape, bf16),
            pltpu.VMEM((4, rows, width), bf16),
        ]
        + Reduce.scratch(rows, width)
        + [
            pltpu.VMEM((rows, width), f32),
            pltpu.VMEM((TILE, width), f32),
            pltpu.VMEM((n, 1, width // n), f32),
            pltpu.VMEM((n, 1, width // n), f32),
            pltpu.VMEM(ffn.shape[1:], bf16),
        ]
        + Scatter.scratch(ffn.shape[1:])
        + Gathers.scratch(2)
        + [pltpu.SemaphoreType.DMA((2, n - 1)), pltpu.SemaphoreType.DMA((11,))],
        compiler_params=pltpu.CompilerParams(
            collective_id=ident, has_side_effects=True, vmem_limit_bytes=VMEM_LIMIT
        ),
        cost_estimate=COST,
        name="attend_back",
    )(
        q, k, v, o, lse, begin, cosine, sine, low, hid_low, w_down, ffn, wo, dnorm, resid, grad, gain
    )


def feed_body(
    n, m, mine, go, w_in, down, dnorm, grads, hid_out, down_out, down_parts,
    rows, rows_t, go_t, go_two, w, w_down, gates, h, hid_low, down_held, down_sum,
    pair, near, far, stage,
    sg, lg, sr, loc, sw, so, sd, sz, sf,
):
    plane = Plane(n, m)
    tokens, width = rows.shape[1:]
    hid = down.shape[1]
    half = m * hid
    greet(plane, True)
    gather = Gathers(plane, mine, lambda i: rows.at[i], sg, lg, 2)
    reduce = Reduce(plane, None, pair, near, far, sr, None, stage)

    def columns(ref, j, t):
        return ref.at[:, j * half + t * hid : j * half + (t + 1) * hid]

    weights = [
        pltpu.make_async_copy(w_in.at[t, j], columns(w, j, t), sw.at[j, t])
        for j in range(2)
        for t in range(m)
    ]
    for copy in weights:
        copy.start()
    meet(plane, True)
    gather.start()

    def down_at(ref, t):
        return ref.at[:, pl.ds(pl.multiple_of(t * hid, hid), hid)]

    chain = Chain(plane, down, lambda t: down_at(w_down, t), sz)
    chain.start()
    own_down = pltpu.make_async_copy(down, down_at(w_down, plane.t), loc.at[0])
    own_down.start()
    gather.wait_own()
    for copy in weights:
        copy.wait()

    def span(b):
        return pl.ds(pl.multiple_of(b * tokens, tokens), tokens)

    def down_grad(kk, keep):
        chip = plane.number(kk, 0) // 2
        at = pl.ds(pl.multiple_of(chip * 2 * tokens, 2 * tokens), 2 * tokens)

        def part(i, carry):
            line = pl.ds(pl.multiple_of(i * 256, 256), 256)
            value = jnp.dot(go_t[line, at], hid_low[at, :], preferred_element_type=f32)
            keep(line, value)
            return carry

        lax.fori_loop(0, width // 256, part, 0)

    def set_down(line, value):
        down_sum[line, :] = value

    def add_down(line, value):
        down_sum[line, :] += value

    def hold_down(line, value):
        down_held[line, :] = (down_sum[line, :] + value).astype(bf16)

    def early_go(it, slot):
        b = plane.number(it // 2, lax.rem(it, 2))
        return pltpu.make_async_copy(go.at[b], go_two.at[slot], so.at[slot])

    def forward(it, carry):
        b = plane.number(it // 2, lax.rem(it, 2))

        @pl.when(it == 1)
        def _():
            gather.wait_swap()

        @pl.when(it == 2)
        def _():
            down_grad(0, set_down)
            chain.step(1)
            gather.relay_near()

        @pl.when(it == 3)
        def _():
            gather.wait_share(1)

        @pl.when(it == 4)
        def _():
            chain.step(2)

        @pl.when(it == 5)
        def _():
            gather.wait_share(0)

        @pl.when(it == 6)
        def _():
            down_grad(1, add_down)
            down_grad(2, add_down)
            gather.relay_far()

        @pl.when(it == 7)
        def _():
            gather.wait_share(2)

        slot = lax.rem(it, 2)

        @pl.when(it < n - 1)
        def _():
            early_go(it + 1, 1 - slot).start()

        row = rows[b]
        both = jnp.dot(row, w[...], preferred_element_type=f32)
        gates[span(b), :] = both
        gate, up = both[:, :half], both[:, half:]
        hid_low[span(b), :] = (gate * jax.nn.sigmoid(gate) * up).astype(bf16)
        rows_t[:, span(b)] = row.T
        early_go(it, slot).wait()
        go_t[:, span(b)] = go_two[slot].T
        return carry

    early_go(0, 0).start()
    lax.fori_loop(0, n, forward, 0)

    def number(it):
        return plane.number(3 - it // 2, 1 - lax.rem(it, 2))

    def load_go(it, slot):
        return pltpu.make_async_copy(go.at[number(it)], go_two.at[slot], so.at[slot])

    load_go(0, 0).start()
    down_grad(3, hold_down)
    outs = fan(
        plane, lambda t: down_at(down_held, t), lambda t: down_parts.at[t], sf.at[0], sf.at[1]
    )
    outs.append(
        pltpu.make_async_copy(down_at(down_held, plane.t), down_parts.at[plane.t], loc.at[1])
    )
    outs.append(pltpu.make_async_copy(hid_low, hid_out, loc.at[2]))
    for copy in outs:
        copy.start()
    for hop in range(3, m):
        chain.step(hop)
    own_down.wait()
    outs.append(pltpu.make_async_copy(w_down, down_out, loc.at[3]))
    outs[-1].start()

    def backward(it, carry):
        slot = lax.rem(it, 2)
        k = 3 - it // 2
        b = number(it)

        @pl.when(it == 2)
        def _():
            reduce.join(3)
            reduce.out[0].start()

        @pl.when(it == 6)
        def _():
            reduce.join(1)
            reduce.out[1].start()

        @pl.when(it == 7)
        def _():
            reduce.ready()
            reduce.send_fro()

        @pl.when(it < n - 1)
        def _():
            load_go(it + 1, 1 - slot).start()

        load_go(it, slot).wait()

        gate = gates[span(b), :half]
        up = gates[span(b), half:]
        dhidden = jnp.dot(go_two[slot], w_down[...], preferred_element_type=f32)
        sig = jax.nn.sigmoid(gate)
        dgate = (dhidden * up * sig * (1.0 + gate * (1.0 - sig))).astype(bf16)
        dup = (dhidden * gate * sig).astype(bf16)
        h[span(b), :half] = dgate
        h[span(b), half:] = dup
        part = lax.dot_general(h[span(b), :], w[...], NT, preferred_element_type=f32)
        part = part.astype(bf16)

        @pl.when(lax.rem(it, 2) == 1)
        def _():
            pair[k] = part

        @pl.when(lax.rem(it, 2) == 0)
        def _():
            stage[k] = part

        for kk in range(4):

            @pl.when(it == 2 * (3 - kk))
            def _(kk=kk):
                reduce.swaps[Reduce.THEIRS[kk]].start()

        return carry

    lax.fori_loop(0, n, backward, 0)

    def weight_grad(i, carry):
        at = pl.ds(pl.multiple_of(i * 256, 256), 256)
        value = jnp.dot(rows_t[at, :], h[...], preferred_element_type=f32)
        w[at, :] = value.astype(bf16)
        return carry

    lax.fori_loop(0, width // 256, weight_grad, 0)
    ends = [
        pltpu.make_async_copy(columns(w, j, t), grads.at[t, j], sd.at[j, t])
        for j in range(2)
        for t in range(m)
    ]
    for copy in ends:
        copy.start()
    reduce.first(dnorm)
    gather.wait_sends()
    chain.wait_sends()
    reduce.finish(dnorm)
    for copy in outs + ends:
        copy.wait()


def feed(n, m, norm, go, w_in, down, ident):
    tokens, width = norm.shape
    hid = down.shape[1]
    length = n * tokens
    half = m * hid
    hbm = pl.BlockSpec(memory_space=ANY)
    return pl.pallas_call(
        functools.partial(feed_body, n, m),
        out_shape=(
            jax.ShapeDtypeStruct((tokens, width), f32),
            jax.ShapeDtypeStruct((m, 2, width, hid), bf16),
            jax.ShapeDtypeStruct((length, half), bf16),
            jax.ShapeDtypeStruct((width, half), bf16),
            jax.ShapeDtypeStruct((m, width, hid), bf16),
        ),
        in_specs=[hbm] * 4,
        out_specs=[pl.BlockSpec(memory_space=pltpu.VMEM)] + [hbm] * 4,
        scratch_shapes=[
            pltpu.VMEM((n, tokens, width), bf16),
            pltpu.VMEM((width, length), bf16),
            pltpu.VMEM((width, length), bf16),
            pltpu.VMEM((2, tokens, width), bf16),
            pltpu.VMEM((width, 2 * half), bf16),
            pltpu.VMEM((width, half), bf16),
            pltpu.VMEM((length, 2 * half), f32),
            pltpu.VMEM((length, 2 * half), bf16),
            pltpu.VMEM((length, half), bf16),
            pltpu.VMEM((width, half), bf16),
            pltpu.VMEM((width, half), f32),
        ]
        + [pltpu.VMEM((slots, tokens, width), bf16) for slots in Reduce.SLOTS]
        + [
            pltpu.VMEM((4, tokens, width), bf16),
            *Gathers.scratch(2),
            pltpu.SemaphoreType.DMA((4, 4)),
            pltpu.SemaphoreType.DMA((4,)),
            pltpu.SemaphoreType.DMA((2, m)),
            pltpu.SemaphoreType.DMA((2,)),
            pltpu.SemaphoreType.DMA((2, m)),
            pltpu.SemaphoreType.DMA((4, m)),
            pltpu.SemaphoreType.DMA((2, m - 1)),
        ],
        compiler_params=pltpu.CompilerParams(
            collective_id=ident, has_side_effects=True, vmem_limit_bytes=VMEM_LIMIT
        ),
        cost_estimate=COST,
        name="feed",
    )(norm, go, w_in, down)


def results_body(
    dnorm, dresid, x, gain, layer_in, ffn, qkv, wo, vec, wq, wk, wv, one,
    layer, input_grad, first, query, key, value, output, second, gate, up, down,
):
    step = pl.program_id(0)

    def into_input(at):
        token = x[at, :].astype(f32)
        scale = lax.rsqrt(jnp.mean(token * token, axis=1, keepdims=True) + norm_epsilon)
        inner = gain[...] * dnorm[at, :]
        moment = jnp.mean(token * inner, axis=1, keepdims=True)
        input_grad[at, :] = (
            dresid[at, :] + scale * inner - token * scale * (scale * scale * moment)
        )
        layer[at, :] = layer_in[at, :]

    in_tiles(x.shape[0], into_input)
    for i, ref in enumerate((gate, up, down)):
        ref[...] = ffn[i].astype(f32)

    @pl.when(step == 0)
    def _():
        groups, strip, _ = qkv.shape
        start = 0
        sums = jnp.zeros((strip, 1), f32)
        for ref, weight in ((query, wq), (key, wk), (value, wv)):
            each = ref.shape[1] // groups
            for g in range(groups):
                ref[:, g * each : (g + 1) * each] = qkv[g, :, start : start + each].astype(f32)
            start += each
            sums += jnp.sum(weight[...].astype(f32) * ref[...], axis=1, keepdims=True)
        row = jnp.broadcast_to(sums, (strip, LANES)).T[0:1, :strip]
        first[...] = row / one[...].astype(f32)
        total = wo[0].astype(f32)
        gains = vec[0]
        for t in range(1, wo.shape[0]):
            total += wo[t].astype(f32)
            gains += vec[t]
        output[...] = total
        second[...] = gains


def results(dnorm, dresid, x, gain, layer, ffn, qkv, wo, vec, wq, wk, wv, one):
    tokens, width = x.shape
    rows, cols = ffn.shape[1:]
    strip = wq.shape[0]
    steps = 2

    def tiled(count, columns):
        return pl.BlockSpec((count // steps, columns), lambda i: (i, 0))

    def fixed(*shape):
        return pl.BlockSpec(shape, lambda i: (0,) * len(shape))

    return pl.pallas_call(
        results_body,
        grid=(steps,),
        out_shape=(
            jax.ShapeDtypeStruct((tokens, width), bf16),
            jax.ShapeDtypeStruct((tokens, width), f32),
            jax.ShapeDtypeStruct((1, strip), f32),
            jax.ShapeDtypeStruct(wq.shape, f32),
            jax.ShapeDtypeStruct(wk.shape, f32),
            jax.ShapeDtypeStruct(wv.shape, f32),
            jax.ShapeDtypeStruct((strip, width), f32),
            jax.ShapeDtypeStruct((1, strip), f32),
            jax.ShapeDtypeStruct((rows, cols), f32),
            jax.ShapeDtypeStruct((rows, cols), f32),
            jax.ShapeDtypeStruct((rows, cols), f32),
        ),
        in_specs=[
            tiled(tokens, width),
            tiled(tokens, width),
            tiled(tokens, width),
            fixed(1, width),
            tiled(tokens, width),
            pl.BlockSpec((3, rows // steps, cols), lambda i: (0, i, 0)),
            fixed(*qkv.shape),
            fixed(*wo.shape),
            fixed(*vec.shape),
            fixed(*wq.shape),
            fixed(*wk.shape),
            fixed(*wv.shape),
            fixed(1, strip),
        ],
        out_specs=[
            tiled(tokens, width),
            tiled(tokens, width),
            fixed(1, strip),
            fixed(*wq.shape),
            fixed(*wk.shape),
            fixed(*wv.shape),
            fixed(strip, width),
            fixed(1, strip),
            tiled(rows, cols),
            tiled(rows, cols),
            tiled(rows, cols),
        ],
        compiler_params=pltpu.CompilerParams(vmem_limit_bytes=VMEM_LIMIT),
        cost_estimate=COST,
        name="results",
    )(dnorm, dresid, x, gain, layer, ffn, qkv, wo, vec, wq, wk, wv, one)


def fast_layer(n, m):
    def on_plane(
        layer_input,
        doc_ids,
        positions,
        first_gain,
        query_weight,
        key_weight,
        value_weight,
        output_weight,
        second_gain,
        gate_weight,
        up_weight,
        down_weight,
        out_grad,
    ):
        x = layer_input[0]
        width = x.shape[1]
        heads = QUERY_HEADS // n
        scale = 1.0 / math.sqrt(HEAD_SIZE)
        factor = scale * LOG2E
        strip = query_weight.shape[0]

        lane = np.arange(LANES) % SLOT
        inverse = np.where(lane < HALF, rope_base ** (-(lane * 2.0 / HEAD_SIZE)), 0.0)
        (
            norm_t, q, k, v, cosine, sine, wqkv, gain_one, gain_two, docs,
            ffn_mine, down_mine, output_rows,
        ) = entry(
            n, m, heads, x, doc_ids, positions, query_weight, key_weight, value_weight,
            first_gain.reshape(1, strip), second_gain.reshape(1, strip),
            gate_weight, up_weight, down_weight, output_weight,
            jnp.asarray(inverse[None], f32), 0,
        )
        o, lse, begin, low, grad_all, resid, norm_two, ffn_all = attend(
            n, m, factor, q, k, v, docs, output_rows, out_grad[0], x, gain_two, ffn_mine, 9
        )
        dnorm_two, ffn_terms, hid_low, w_down, down_parts = feed(
            n, m, norm_two, grad_all, ffn_all, down_mine, 2
        )
        dqkv, layer_output, output_terms, dresid, gain_part, ffn_sum = attend_back(
            n, m, factor, scale, q, k, v, o, lse, begin, cosine, sine, low, hid_low, w_down, ffn_terms,
            output_rows, dnorm_two, resid, out_grad[0], gain_two, 3,
        )
        dnorm_one, ffn_out, qkv_out, output_parts, gain_sums = last(
            n, m, dqkv, wqkv, norm_t, ffn_sum, down_parts, output_terms, gain_part, 6
        )
        (
            layer_output, input_grad, first_gain_grad, query_grad, key_grad, value_grad,
            output_grad, second_gain_grad, gate_grad, up_grad, down_grad,
        ) = results(
            dnorm_one, dresid, x, gain_one, layer_output, ffn_out, qkv_out, output_parts,
            gain_sums, query_weight, key_weight, value_weight, first_gain.reshape(1, strip),
        )
        return (
            layer_output[None],
            input_grad[None],
            first_gain_grad.reshape(strip),
            query_grad,
            key_grad,
            value_grad,
            output_grad,
            second_gain_grad.reshape(strip),
            gate_grad,
            up_grad,
            down_grad,
        )

    return on_plane


def solution(mesh):
    n, m = mesh.shape["seq"], mesh.shape["tp"]
    fits = n == KEY_VALUE_HEADS == 8 and m == 4
    return jax.shard_map(
        fast_layer(n, m) if fits else on_device,
        mesh=mesh,
        in_specs=(
            P("tp", "seq", None),
            P("tp", "seq"),
            P("tp", "seq"),
            P(("seq", "tp")),
            P(("seq", "tp"), None),
            P(("seq", "tp"), None),
            P(("seq", "tp"), None),
            P(("seq", "tp"), None),
            P(("seq", "tp")),
            P("seq", "tp"),
            P("seq", "tp"),
            P("seq", "tp"),
            P("tp", "seq", None),
        ),
        out_specs=(
            P("tp", "seq", None),
            P("tp", "seq", None),
            P(("seq", "tp")),
            P(("seq", "tp"), None),
            P(("seq", "tp"), None),
            P(("seq", "tp"), None),
            P(("seq", "tp"), None),
            P(("seq", "tp")),
            P("seq", "tp"),
            P("seq", "tp"),
            P("seq", "tp"),
        ),
        check_vma=False,
    )
```

```python
import functools
import math

import jax
import jax.numpy as jnp
import numpy as np
from jax import lax
from jax.experimental import pallas as pl
from jax.experimental.pallas import tpu as pltpu
from jax.sharding import PartitionSpec as P

QUERY_HEADS = 16
KEY_VALUE_HEADS = 8
HEAD_SIZE = 96


norm_epsilon = 1e-05
rope_base = 100000.0
mask_fill_value = -1e30


def rope_tables(places):
    half = HEAD_SIZE // 2
    inverse = rope_base ** (-(jnp.arange(half, dtype=jnp.float32) * 2.0 / HEAD_SIZE))
    angles = places.astype(jnp.float32)[:, None] * inverse[None, :]
    return (jnp.cos(angles), jnp.sin(angles))


def apply_rotary(value_rows, cosine_table, sine_table, heads, direction):
    sequence_length = value_rows.shape[0]
    split = value_rows.reshape(sequence_length, heads, 2, HEAD_SIZE // 2)
    first = split[:, :, 0]
    second = split[:, :, 1]
    cosine = cosine_table[:, None, :]
    sine = direction * sine_table[:, None, :]
    turned = jnp.stack([first * cosine - second * sine, second * cosine + first * sine], axis=2)
    return turned.reshape(sequence_length, heads * HEAD_SIZE)


def outer_product(left, right):
    return lax.dot_general(
        left, right, (((0,), (0,)), ((), ())), preferred_element_type=jnp.float32
    )


def times_transpose(left, right):
    return lax.dot_general(
        left, right, (((1,), (1,)), ((), ())), preferred_element_type=jnp.float32
    )


def norm_backward(inputs, scale, gain, upstream):
    inner = gain * upstream
    moment = jnp.mean(inputs * inner, axis=1, keepdims=True)
    return (
        scale * inner - inputs * scale * scale * scale * moment,
        jnp.sum(upstream * inputs * scale, axis=0),
    )


def on_device(
    layer_input,
    doc_ids,
    positions,
    first_gain,
    query_weight,
    key_weight,
    value_weight,
    output_weight,
    second_gain,
    gate_weight,
    up_weight,
    down_weight,
    out_grad,
):
    token_rows = layer_input.shape[1]
    query_groups = QUERY_HEADS // KEY_VALUE_HEADS
    scale_of_scores = 1.0 / math.sqrt(HEAD_SIZE)
    inputs_f = layer_input[0].astype(jnp.float32)
    my_docs = doc_ids[0]
    gain_one, query_full, complete_keys, value_full, output_full, gain_two = (
        lax.all_gather(first_gain, ("seq", "tp"), axis=0, tiled=True),
        lax.all_gather(query_weight, ("seq", "tp"), axis=0, tiled=True),
        lax.all_gather(key_weight, ("seq", "tp"), axis=0, tiled=True),
        lax.all_gather(value_weight, ("seq", "tp"), axis=0, tiled=True),
        lax.all_gather(output_weight, ("seq", "tp"), axis=0, tiled=True),
        lax.all_gather(second_gain, ("seq", "tp"), axis=0, tiled=True),
    )
    gain_one_f = gain_one.astype(jnp.float32)
    gain_two_f = gain_two.astype(jnp.float32)
    scale_one = lax.rsqrt(jnp.mean(inputs_f * inputs_f, axis=1, keepdims=True) + norm_epsilon)
    first_normalized = (inputs_f * scale_one * gain_one_f).astype(jnp.bfloat16)
    cosine_table, sine_table = rope_tables(positions[0])
    rotated_query = apply_rotary(
        jnp.dot(first_normalized, query_full, preferred_element_type=jnp.float32),
        cosine_table,
        sine_table,
        QUERY_HEADS,
        1.0,
    ).astype(jnp.bfloat16)
    key_rot = apply_rotary(
        jnp.dot(first_normalized, complete_keys, preferred_element_type=jnp.float32),
        cosine_table,
        sine_table,
        KEY_VALUE_HEADS,
        1.0,
    ).astype(jnp.bfloat16)
    value_low = jnp.dot(first_normalized, value_full, preferred_element_type=jnp.float32).astype(
        jnp.bfloat16
    )
    gathered_keys, gathered_values, doc_all = (
        lax.all_gather(key_rot, "seq", axis=0, tiled=True),
        lax.all_gather(value_low, "seq", axis=0, tiled=True),
        lax.all_gather(my_docs.astype(jnp.bfloat16), "seq", axis=0, tiled=True),
    )
    sequence_length = gathered_keys.shape[0]
    block_number = math.gcd(512, sequence_length)
    block_count = sequence_length // block_number
    query_index = lax.axis_index("seq") * token_rows + jnp.arange(token_rows, dtype=jnp.int32)
    my_doc_f = my_docs.astype(jnp.float32)
    heads_of_query = rotated_query.reshape(token_rows, KEY_VALUE_HEADS, query_groups, HEAD_SIZE)
    layer_entries = (
        gathered_keys.reshape(block_count, block_number, KEY_VALUE_HEADS, HEAD_SIZE),
        gathered_values.reshape(block_count, block_number, KEY_VALUE_HEADS, HEAD_SIZE),
        doc_all.astype(jnp.float32).reshape(block_count, block_number),
        jnp.arange(block_count, dtype=jnp.int32) * block_number,
    )

    def allowed_of(doc_piece, start):
        key_index = start + jnp.arange(block_number, dtype=jnp.int32)
        return (key_index[None, :] <= query_index[:, None]) & (
            doc_piece[None, :] == my_doc_f[:, None]
        )

    def scores_of(key_piece, allowed):
        raw = (
            jnp.einsum(
                "tgrd,kgd->tgrk", heads_of_query, key_piece, preferred_element_type=jnp.float32
            )
            * scale_of_scores
        )
        return jnp.where(allowed[:, None, None, :], raw, mask_fill_value)

    def total_step(carry, item):
        key_piece, value_piece, doc_piece, start = item
        allowed = allowed_of(doc_piece, start)

        def total_work(state):
            top, total = state
            scores = scores_of(key_piece, allowed)
            new_top = jnp.maximum(top, jnp.max(scores, axis=3))
            weights = jnp.where(
                allowed[:, None, None, :], jnp.exp(scores - new_top[..., None]), 0.0
            )
            return (new_top, total * jnp.exp(top - new_top) + jnp.sum(weights, axis=3))

        return (lax.cond(jnp.any(allowed), total_work, lambda state: state, carry), None)

    start_state = (
        jnp.full((token_rows, KEY_VALUE_HEADS, query_groups), mask_fill_value, jnp.float32),
        jnp.zeros((token_rows, KEY_VALUE_HEADS, query_groups), jnp.float32),
    )
    (top, total), unused_result = lax.scan(total_step, start_state, layer_entries)
    log_total = top + jnp.log(total)

    def probs_of(key_piece, allowed):
        scores = scores_of(key_piece, allowed)
        return jnp.where(allowed[:, None, None, :], jnp.exp(scores - log_total[..., None]), 0.0)

    def output_update(accum, item):
        key_piece, value_piece, doc_piece, start = item
        allowed = allowed_of(doc_piece, start)

        def output_work(state):
            probs = probs_of(key_piece, allowed).astype(jnp.bfloat16)
            return state + jnp.einsum(
                "tgrk,kgd->tgrd", probs, value_piece, preferred_element_type=jnp.float32
            )

        return (lax.cond(jnp.any(allowed), output_work, lambda state: state, accum), None)

    heads_output, unused_result = lax.scan(
        output_update,
        jnp.zeros((token_rows, KEY_VALUE_HEADS, query_groups, HEAD_SIZE), jnp.float32),
        layer_entries,
    )
    attn_low = heads_output.reshape(token_rows, QUERY_HEADS * HEAD_SIZE).astype(jnp.bfloat16)
    resid = inputs_f + jnp.dot(attn_low, output_full, preferred_element_type=jnp.float32)
    scale_two = lax.rsqrt(jnp.mean(resid * resid, axis=1, keepdims=True) + norm_epsilon)
    normed_two = (resid * scale_two * gain_two_f).astype(jnp.bfloat16)
    rows_all = lax.all_gather(normed_two, "tp", axis=0, tiled=True)
    gate_cols, up_cols, down_cols = (
        lax.all_gather(gate_weight, "seq", axis=0, tiled=True),
        lax.all_gather(up_weight, "seq", axis=0, tiled=True),
        lax.all_gather(down_weight, "seq", axis=0, tiled=True),
    )
    gate_pre = jnp.dot(rows_all, gate_cols, preferred_element_type=jnp.float32)
    up_pre = jnp.dot(rows_all, up_cols, preferred_element_type=jnp.float32)
    gate_sig = jax.nn.sigmoid(gate_pre)
    gate_act = gate_pre * gate_sig
    hidden = (gate_act * up_pre).astype(jnp.bfloat16)
    mixed = lax.psum_scatter(
        times_transpose(hidden, down_cols).astype(jnp.bfloat16),
        "tp",
        scatter_dimension=0,
        tiled=True,
    ).astype(jnp.float32)
    layer_output = (resid + mixed).astype(jnp.bfloat16)[None]
    grad_low = out_grad[0]
    grad_f = grad_low.astype(jnp.float32)
    grad_all = lax.all_gather(grad_low, "tp", axis=0, tiled=True)
    dhidden = jnp.dot(grad_all, down_cols, preferred_element_type=jnp.float32)
    dgate = (dhidden * up_pre * gate_sig * (1.0 + gate_pre * (1.0 - gate_sig))).astype(jnp.bfloat16)
    dup = (dhidden * gate_act).astype(jnp.bfloat16)
    gate_term = outer_product(rows_all, dgate)
    up_term = outer_product(rows_all, dup)
    down_term_grad = outer_product(grad_all, hidden)
    dnorm_two = lax.psum_scatter(
        (times_transpose(dgate, gate_cols) + times_transpose(dup, up_cols)).astype(jnp.bfloat16),
        "tp",
        scatter_dimension=0,
        tiled=True,
    ).astype(jnp.float32)
    gate_grad, up_grad, down_grad = (
        lax.psum_scatter(
            gate_term.astype(jnp.bfloat16), "seq", scatter_dimension=0, tiled=True
        ).astype(jnp.float32),
        lax.psum_scatter(
            up_term.astype(jnp.bfloat16), "seq", scatter_dimension=0, tiled=True
        ).astype(jnp.float32),
        lax.psum_scatter(
            down_term_grad.astype(jnp.bfloat16), "seq", scatter_dimension=0, tiled=True
        ).astype(jnp.float32),
    )
    resid_part, gain_two_term = norm_backward(resid, scale_two, gain_two_f, dnorm_two)
    dresid = grad_f + resid_part
    dbranch = dresid.astype(jnp.bfloat16)
    output_term = outer_product(attn_low, dbranch)
    heads_gradient = times_transpose(dbranch, output_full).astype(jnp.bfloat16)
    grouped_heads_gradient = heads_gradient.reshape(
        token_rows, KEY_VALUE_HEADS, query_groups, HEAD_SIZE
    )
    delta = jnp.sum(grouped_heads_gradient.astype(jnp.float32) * heads_output, axis=3)

    def gradient_update(dquery, item):
        key_piece, value_piece, doc_piece, start = item
        allowed = allowed_of(doc_piece, start)

        def gradient_work(state):
            probs = probs_of(key_piece, allowed)
            value_piece_grad = jnp.einsum(
                "tgrk,tgrd->kgd",
                probs.astype(jnp.bfloat16),
                grouped_heads_gradient,
                preferred_element_type=jnp.float32,
            )
            prob_grad = jnp.einsum(
                "tgrd,kgd->tgrk",
                grouped_heads_gradient,
                value_piece,
                preferred_element_type=jnp.float32,
            )
            score_grad = (probs * (prob_grad - delta[..., None])).astype(jnp.bfloat16)
            key_piece_grad = jnp.einsum(
                "tgrk,tgrd->kgd", score_grad, heads_of_query, preferred_element_type=jnp.float32
            )
            updated = state + jnp.einsum(
                "tgrk,kgd->tgrd", score_grad, key_piece, preferred_element_type=jnp.float32
            )
            return (updated, (key_piece_grad, value_piece_grad))

        def skip(state):
            blank_tensor = jnp.zeros((block_number, KEY_VALUE_HEADS, HEAD_SIZE), jnp.float32)
            return (state, (blank_tensor, blank_tensor))

        return lax.cond(jnp.any(allowed), gradient_work, skip, dquery)

    dquery, (key_contributions, value_contributions) = lax.scan(
        gradient_update,
        jnp.zeros((token_rows, KEY_VALUE_HEADS, query_groups, HEAD_SIZE), jnp.float32),
        layer_entries,
    )
    gathered_key_contributions = (
        key_contributions.reshape(sequence_length, KEY_VALUE_HEADS * HEAD_SIZE) * scale_of_scores
    )
    gathered_value_contributions = value_contributions.reshape(
        sequence_length, KEY_VALUE_HEADS * HEAD_SIZE
    )
    local_keys, value_mine = (
        lax.psum_scatter(
            gathered_key_contributions.astype(jnp.bfloat16), "seq", scatter_dimension=0, tiled=True
        ).astype(jnp.float32),
        lax.psum_scatter(
            gathered_value_contributions.astype(jnp.bfloat16),
            "seq",
            scatter_dimension=0,
            tiled=True,
        ).astype(jnp.float32),
    )
    dq_pre = apply_rotary(
        dquery.reshape(token_rows, QUERY_HEADS * HEAD_SIZE) * scale_of_scores,
        cosine_table,
        sine_table,
        QUERY_HEADS,
        -1.0,
    ).astype(jnp.bfloat16)
    key_gradient_unrotated = apply_rotary(
        local_keys, cosine_table, sine_table, KEY_VALUE_HEADS, -1.0
    ).astype(jnp.bfloat16)
    dv_pre = value_mine.astype(jnp.bfloat16)
    dnorm_one = (
        times_transpose(dq_pre, query_full)
        + times_transpose(key_gradient_unrotated, complete_keys)
        + times_transpose(dv_pre, value_full)
    )
    input_part, gain_one_term = norm_backward(inputs_f, scale_one, gain_one_f, dnorm_one)
    input_grad = (dresid + input_part)[None]
    query_term = outer_product(first_normalized, dq_pre)
    key_term = outer_product(first_normalized, key_gradient_unrotated)
    value_term = outer_product(first_normalized, dv_pre)
    first_gain_grad, query_grad, key_grad, value_grad, output_grad, second_gain_grad = (
        lax.psum_scatter(gain_one_term, ("seq", "tp"), scatter_dimension=0, tiled=True),
        lax.psum_scatter(query_term, ("seq", "tp"), scatter_dimension=0, tiled=True),
        lax.psum_scatter(key_term, ("seq", "tp"), scatter_dimension=0, tiled=True),
        lax.psum_scatter(value_term, ("seq", "tp"), scatter_dimension=0, tiled=True),
        lax.psum_scatter(output_term, ("seq", "tp"), scatter_dimension=0, tiled=True),
        lax.psum_scatter(gain_two_term, ("seq", "tp"), scatter_dimension=0, tiled=True),
    )
    return (
        layer_output,
        input_grad,
        first_gain_grad,
        query_grad,
        key_grad,
        value_grad,
        output_grad,
        second_gain_grad,
        gate_grad,
        up_grad,
        down_grad,
    )


MESH = pl.DeviceIdType.MESH
ANY = pl.ANY
HALF = HEAD_SIZE // 2
LANES = 128
SLOT = LANES // 2
f32 = jnp.float32
bf16 = jnp.bfloat16
VMEM_LIMIT = 62 << 20
COST = pl.CostEstimate(flops=1_000_000, transcendentals=0, bytes_accessed=100_000)


class Plane:
    def __init__(self, n, m):
        self.n, self.m, self.chips = n, m, n // 2
        self.s = lax.axis_index("seq")
        self.t = lax.axis_index("tp")
        self.q = self.s // 2
        self.c = lax.rem(self.s, 2)

        across = self.q + 1 - 2 * lax.rem(self.q, 2)
        along = lax.rem(self.q + 2, 4)
        self.to = across * (1 - self.c) + along * self.c
        self.fro = across * self.c + along * (1 - self.c)
        self.far = 3 - self.q
        self.order = (self.q, self.to, self.fro, self.far)

    def device(self, s):
        return (s, self.t)

    def same(self, chip):
        return (2 * chip + self.c, self.t)

    def number(self, k, other):
        c, q = self.c, self.q
        low, high = lax.rem(k, 2), k // 2
        dx = low * (1 - c) + high * c
        dy = high * (1 - c) + low * c
        x, y = lax.rem(q, 2), q // 2
        chip = 2 * (y + dy - 2 * y * dy) + x + dx - 2 * x * dx
        return 2 * chip + c + other * (1 - 2 * c)

    def sibling(self):
        return (2 * self.q + 1 - self.c, self.t)

    def ahead(self, k):
        return lax.rem(self.q + k, self.chips)

    def behind(self, k):
        return lax.rem(self.q + self.chips - k, self.chips)

    def seq_ahead(self, k):
        return lax.rem(self.s + k, self.n)

    def seq_behind(self, k):
        return lax.rem(self.s + self.n - k, self.n)

    def tp_ahead(self, k):
        return (self.s, lax.rem(self.t + k, self.m))

    def tp_behind(self, k):
        return lax.rem(self.t + self.m - k, self.m)


def greet(plane, with_tp):
    barrier = pltpu.get_barrier_semaphore()
    for k in range(1, plane.n):
        pl.semaphore_signal(
            barrier, inc=1, device_id=plane.device(plane.seq_ahead(k)), device_id_type=MESH
        )
    if with_tp:
        for k in range(1, plane.m):
            pl.semaphore_signal(barrier, inc=1, device_id=plane.tp_ahead(k), device_id_type=MESH)


def meet(plane, with_tp):
    count = plane.n - 1 + (plane.m - 1 if with_tp else 0)
    pl.semaphore_wait(pltpu.get_barrier_semaphore(), count)


def remote(src, dst, send, recv, device):
    return pltpu.make_async_remote_copy(
        src_ref=src,
        dst_ref=dst,
        send_sem=send,
        recv_sem=recv,
        device_id=device,
        device_id_type=MESH,
    )


class Gather:
    COPIES = 7

    def __init__(self, plane, src, dst_of, send, recv, local):
        to, fro, far, c = plane.to, plane.fro, plane.far, plane.c
        here = dst_of(plane.s)
        self.own = pltpu.make_async_copy(src, here, local)

        def block(chip):
            return dst_of(2 * chip + c)

        def copy(i, a, b, device):
            return remote(a, b, send.at[i], recv.at[i], device)

        sibling = plane.sibling()
        self.swap = copy(0, src, here, sibling)
        self.ahead = copy(1, src, here, plane.same(to))
        self.back = copy(2, src, here, plane.same(fro))
        self.relay = copy(3, block(fro), block(fro), plane.same(to))
        self.share = [
            copy(4, block(to), block(to), sibling),
            copy(5, block(fro), block(fro), sibling),
            copy(6, block(far), block(far), sibling),
        ]

    def start(self):
        self.back.start()
        self.ahead.start()

    def start_here(self):
        self.swap.start()
        self.own.start()

    def relay_near(self):
        self.back.wait_recv()
        self.relay.start()
        self.share[1].start()
        self.ahead.wait_recv()
        self.share[0].start()

    def relay_far(self):
        self.relay.wait_recv()
        self.share[2].start()

    def wait_sends(self):
        for copy in [self.swap, self.ahead, self.back, self.relay] + self.share:
            copy.wait_send()


class Gathers:
    def __init__(self, plane, src, dst_of, sems, local, pieces):
        rows = src.shape[0] // pieces
        self.parts = []
        for i in range(pieces):
            at = pl.ds(i * rows, rows)
            self.parts.append(
                Gather(
                    plane,
                    src.at[at],
                    lambda d, at=at: dst_of(d).at[at],
                    sems.at[i, 0],
                    sems.at[i, 1],
                    local.at[i],
                )
            )

    def start(self):
        for part in self.parts:
            part.start()
        for part in self.parts:
            part.start_here()

    def relay_near(self):
        for part in self.parts:
            part.relay_near()

    def relay_far(self):
        for part in self.parts:
            part.relay_far()

    def wait_own(self):
        for part in self.parts:
            part.own.wait()

    def wait_swap(self):
        for part in self.parts:
            part.swap.wait_recv()

    def wait_share(self, i):
        for part in self.parts:
            part.share[i].wait_recv()

    def wait_sends(self):
        for part in self.parts:
            part.wait_sends()

    def finish(self):
        self.wait_own()
        self.wait_swap()
        for i in range(3):
            self.wait_share(i)
        self.wait_sends()

    @staticmethod
    def scratch(pieces):
        return [
            pltpu.SemaphoreType.DMA((pieces, 2, Gather.COPIES)),
            pltpu.SemaphoreType.DMA((pieces,)),
        ]


class Chain:
    def __init__(self, plane, mine, slot_of, sems):
        self.plane, self.mine, self.slot_of, self.sems = plane, mine, slot_of, sems

    def copy(self, way, hop, to):
        plane, row = self.plane, 0 if way > 0 else 2
        slot = self.slot_of(plane.t - way * hop)
        return remote(
            self.mine if hop == 0 else slot,
            slot,
            self.sems.at[row, hop],
            self.sems.at[row + 1, hop],
            (plane.s, to),
        )

    def inside(self, way, hop):
        t, m = self.plane.t, self.plane.m
        holds = t >= hop if way > 0 else t < m - hop
        passes = t < m - 1 if way > 0 else t > 0
        return holds, passes

    def start(self):
        self.pass_on(0)

    def pass_on(self, hop):
        for way in (1, -1):
            holds, passes = self.inside(way, hop)

            @pl.when(holds & passes)
            def _(way=way):
                self.copy(way, hop, self.plane.t + way).start()

    def step(self, hop):
        plane = self.plane
        for way in (1, -1):
            holds, _ = self.inside(way, hop)

            @pl.when(holds)
            def _(way=way):
                row = 0 if way > 0 else 2
                slot = self.slot_of(plane.t - way * hop)
                remote(
                    slot,
                    slot,
                    self.sems.at[row, hop - 1],
                    self.sems.at[row + 1, hop - 1],
                    (plane.s, plane.t - way),
                ).wait_recv()

        if hop < plane.m - 1:
            self.pass_on(hop)

    def wait_sends(self):
        for hop in range(self.plane.m - 1):
            for way in (1, -1):
                holds, passes = self.inside(way, hop)

                @pl.when(holds & passes)
                def _(way=way, hop=hop):
                    self.copy(way, hop, self.plane.t + way).wait_send()


class Scatter:
    def __init__(self, plane, parts, total, add, own, got, sems, loc):
        t = plane.t
        self.plane, self.total = plane, total
        self.add, self.own, self.got, self.loc = add, own, got, loc
        self.inner = (t == 1) | (t == 2)
        self.outer = (t == 0) | (t == 3)
        up = t // 2
        self.near = t + 1 - 2 * lax.rem(t, 2)
        self.far_outer = 3 - 3 * up
        self.far_inner = 2 - up
        self.parts, self.sems = parts, sems

    def copy(self, i, j, src, dst, to):
        return remote(
            src, dst, self.sems.at[0, i, j], self.sems.at[1, i, j], (self.plane.s, to)
        )

    def first(self, i, j):
        chunk = (self.far_outer, self.far_inner, self.near)[i]
        dst = self.got.at[0, j] if i == 2 else self.add.at[i, j]
        return self.copy(i, j, self.parts.at[chunk, j], dst, self.near)

    def back(self, j):
        return self.copy(2, j, self.parts.at[self.near, j], self.got.at[0, j], self.near)

    def sent(self, i, j):
        to = self.far_inner if i else self.far_outer
        return remote(
            self.add.at[i, j],
            self.got.at[1, j],
            self.sems.at[0, 3 + i, j],
            self.sems.at[1, 3, j],
            (self.plane.s, to),
        )

    def load(self, i, j):
        chunk = (self.far_outer, self.far_inner, self.plane.t)[i]
        dst = self.total.at[j] if i == 2 else self.own.at[i, j]
        return pltpu.make_async_copy(self.parts.at[chunk, j], dst, self.loc.at[i, j])

    def start(self):
        for j in range(2):
            self.load(2, j).start()

        @pl.when(self.outer)
        def _():
            for i in range(3):
                for j in range(2):
                    self.first(i, j).start()

        @pl.when(self.inner)
        def _():
            for j in range(2):
                self.back(j).start()
            for i in range(2):
                for j in range(2):
                    self.load(i, j).start()

    def relay(self, i, j):
        @pl.when(self.inner)
        def _():
            self.first(i, j).wait_recv()
            self.load(i, j).wait()
            add, own = self.add, self.own

            def both(at):
                value = add[i, j, at, :].astype(f32) + own[i, j, at, :].astype(f32)
                add[i, j, at, :] = value.astype(bf16)

            in_tiles(add.shape[2], both, 256)
            self.sent(i, j).start()

    def finish(self):
        total, got = self.total, self.got
        for j in range(2):
            self.load(2, j).wait()
            self.back(j).wait_recv()
            self.sent(0, j).wait_recv()

            def sums(at, j=j):
                value = total[j, at, :].astype(f32) + got[0, j, at, :].astype(f32)
                total[j, at, :] = (value + got[1, j, at, :].astype(f32)).astype(bf16)

            in_tiles(total.shape[1], sums, 256)

        @pl.when(self.outer)
        def _():
            for i in range(3):
                for j in range(2):
                    self.first(i, j).wait_send()

        @pl.when(self.inner)
        def _():
            for j in range(2):
                self.back(j).wait_send()
                for i in range(2):
                    self.sent(i, j).wait_send()

    @staticmethod
    def scratch(shape):
        return [
            pltpu.VMEM((2,) + shape, bf16),
            pltpu.VMEM((2,) + shape, bf16),
            pltpu.VMEM((2,) + shape, bf16),
            pltpu.SemaphoreType.DMA((2, 5, 2)),
            pltpu.SemaphoreType.DMA((3, 2)),
        ]


def fan(plane, src_of, dst_of, send, recv):
    copies = []
    for k in range(1, plane.m):
        device = plane.tp_ahead(k)
        copies.append(
            remote(src_of(device[1]), dst_of(plane.t), send.at[k - 1], recv.at[k - 1], device)
        )
    return copies


def exchange(plane, src_of, dst_of, send, recv, local):
    own = pltpu.make_async_copy(src_of(plane.s), dst_of(plane.s), local)
    copies = []
    for k in range(1, plane.n):
        peer = plane.seq_ahead(k)
        copies.append(
            remote(
                src_of(peer), dst_of(plane.s), send.at[k - 1], recv.at[k - 1], plane.device(peer)
            )
        )
    return [own] + copies


TILE = 32


def in_tiles(rows, body, tile=TILE):
    def one(i, carry):
        body(pl.ds(pl.multiple_of(i * tile, tile), tile))
        return carry

    lax.fori_loop(0, rows // tile, one, 0)


class Reduce:
    SLOTS = (4, 4, 3)

    THEIRS = (0, 2, 1, 3)

    def __init__(self, plane, part_of, pair, near, far, sems, loc, stage=None):
        c = plane.c
        self.pair, self.near, self.far = pair, near, far
        self.rows = pair.shape[1]
        self.swaps, self.loads = {}, {}
        for k in range(4):
            mine = self.THEIRS[k]
            chip = plane.order[mine]
            source = part_of(2 * chip + 1 - c) if stage is None else stage.at[mine]
            self.swaps[k] = remote(
                source, near.at[k], sems.at[0, k], sems.at[1, k], plane.sibling()
            )
            if stage is None:
                self.loads[k] = pltpu.make_async_copy(
                    part_of(2 * plane.order[k] + c), pair.at[k], loc.at[k]
                )

        def out(i, k, chip):
            return remote(
                pair.at[k], far.at[i], sems.at[2, i], sems.at[3, i], plane.same(chip)
            )

        self.out = [out(0, 3, plane.to), out(1, 1, plane.to), out(2, 2, plane.fro)]

    def start(self, *which):
        for k in which:
            self.swaps[k].start()
            self.loads[k].start()

    def landed(self, k):
        self.swaps[k].wait()
        if self.loads:
            self.loads[k].wait()

    def join(self, k):
        pair, near = self.pair, self.near
        self.landed(k)

        def add(at):
            both = pair[k, at, :].astype(f32) + near[k, at, :].astype(f32)
            pair[k, at, :] = both.astype(bf16)

        in_tiles(self.rows, add)

    def send_to(self):
        self.join(3)
        self.out[0].start()
        self.join(1)
        self.out[1].start()

    def ready(self):
        self.landed(2)

    def send_fro(self):
        pair, near, far = self.pair, self.near, self.far
        self.out[0].wait_recv()

        def add(at):
            both = pair[2, at, :].astype(f32) + near[2, at, :].astype(f32)
            pair[2, at, :] = (both + far[0, at, :].astype(f32)).astype(bf16)

        in_tiles(self.rows, add)
        self.out[2].start()

    def first(self, total, more=None):
        pair, near = self.pair, self.near
        self.landed(0)

        def add(at):
            value = pair[0, at, :].astype(f32) + near[0, at, :].astype(f32)
            total[at, :] = value if more is None else value + more[at, :].astype(f32)

        in_tiles(self.rows, add)

    def finish(self, total, out=None):
        far = self.far
        out = total if out is None else out
        self.out[0].wait_send()
        self.out[1].wait()
        self.out[2].wait()

        def add(at):
            value = total[at, :] + far[1, at, :].astype(f32) + far[2, at, :].astype(f32)
            out[at, :] = value.astype(out.dtype)

        in_tiles(self.rows, add)

    @staticmethod
    def scratch(rows, width):
        return [pltpu.VMEM((slots, rows, width), bf16) for slots in Reduce.SLOTS] + [
            pltpu.SemaphoreType.DMA((4, 4)),
            pltpu.SemaphoreType.DMA((4,)),
        ]


def last_body(
    n, m, dqkv_in, w_in, norm_t, ffn, downs, wo, vec,
    total, ffn_out, qkv_out, wo_out, vec_out,
    dqkv, w, down_here, down_sum, narrow, pair, near, far, sr, lr, stage, norms, mine, got, summed, sems, st, loc,
):
    plane = Plane(n, m)
    greet(plane, True)
    loads = [
        pltpu.make_async_copy(a, b, loc.at[5 + i])
        for i, (a, b) in enumerate(
            ((dqkv_in, dqkv), (w_in, w), (downs, down_here))
        )
    ]
    load = pltpu.make_async_copy(norm_t, norms, loc.at[0])
    for copy in loads + [load]:
        copy.start()
    narrow[...] = lanes_of_columns(narrow.shape, 1)
    meet(plane, True)
    rows, width = ffn_out.shape[1], ffn.shape[2]
    across = fan(plane, lambda t: wo.at[t], lambda t: wo_out.at[t], st.at[1, 0], st.at[1, 1])
    across += fan(plane, lambda t: vec.at[t], lambda t: vec_out.at[t], st.at[2, 0], st.at[2, 1])
    across += [
        pltpu.make_async_copy(wo.at[plane.t], wo_out.at[plane.t], loc.at[1]),
        pltpu.make_async_copy(vec.at[plane.t], vec_out.at[plane.t], loc.at[2]),
    ]
    for copy in across:
        copy.start()
    a = exchange(
        plane,
        lambda i: ffn.at[:, pl.ds(pl.multiple_of(i * rows, rows), rows), :],
        lambda i: ffn_out.at[
            pl.ds(0, 2), :, pl.ds(pl.multiple_of(i * width, width), width)
        ],
        sems.at[0, 0],
        sems.at[0, 1],
        loc.at[3],
    )
    a_down = exchange(
        plane,
        lambda i: down_sum.at[pl.ds(pl.multiple_of(i * rows, rows), rows), :],
        lambda i: ffn_out.at[2, :, pl.ds(pl.multiple_of(i * width, width), width)],
        sems.at[2, 0],
        sems.at[2, 1],
        loc.at[10],
    )
    for copy in a:
        copy.start()
    reduce = Reduce(plane, None, pair, near, far, sr, lr, stage)
    tokens = pair.shape[1]
    for copy in loads[:2]:
        copy.wait()

    def blocks(it, carry):
        k = 3 - it // 2
        other = 1 - lax.rem(it, 2)
        b = plane.number(k, other)
        here = pl.ds(pl.multiple_of(b * tokens, tokens), tokens)
        part = lax.dot_general(dqkv[here, :], w[...], NT, preferred_element_type=f32).astype(bf16)

        @pl.when(other == 0)
        def _():
            pair[k] = part

        @pl.when(other == 1)
        def _():
            stage[k] = part

        for kk in range(4):

            @pl.when(it == 2 * (3 - kk))
            def _(kk=kk):
                reduce.swaps[Reduce.THEIRS[kk]].start()

        return carry

    lax.fori_loop(0, n, blocks, 0)
    reduce.send_to()
    loads[2].wait()

    def add_down(at):
        value = down_here[0, at, :].astype(f32)
        for t in range(1, m):
            value = value + down_here[t, at, :].astype(f32)
        down_sum[at, :] = value.astype(bf16)

    in_tiles(down_sum.shape[0], add_down)
    for copy in a_down:
        copy.start()
    load.wait()
    strip = summed.shape[1]

    def weight_grads(s, carry):
        at = pl.ds(pl.multiple_of(s * m * strip, m * strip), m * strip)
        value = jnp.dot(norms[at, :], dqkv[...], preferred_element_type=f32).astype(bf16)
        value = jnp.dot(value, narrow[...], preferred_element_type=f32).astype(bf16)
        for t in range(m):
            mine[s, t] = value[t * strip : (t + 1) * strip]
        return carry

    lax.fori_loop(0, n, weight_grads, 0)
    over = fan(plane, lambda t: mine.at[:, t], lambda t: got.at[t], st.at[0, 0], st.at[0, 1])
    for copy in over:
        copy.start()
    reduce.ready()
    reduce.first(total)
    reduce.send_fro()
    for copy in over:
        copy.wait()

    def add(s, carry):
        value = mine[s, plane.t].astype(f32)
        for k in range(1, m):
            value = value + got[plane.tp_behind(k), s].astype(f32)
        summed[s] = value.astype(bf16)
        return carry

    lax.fori_loop(0, n, add, 0)
    b = exchange(
        plane,
        lambda i: summed.at[i],
        lambda i: qkv_out.at[i],
        sems.at[1, 0],
        sems.at[1, 1],
        loc.at[4],
    )
    for copy in b:
        copy.start()
    reduce.finish(total)
    for copy in a + a_down + b + across:
        copy.wait()


def last(n, m, dqkv, w, norm_t, ffn, downs, wo, vec, ident):
    width, length = norm_t.shape
    tokens = length // n
    cols = w.shape[1] // SLOT * HALF
    strip = width // (n * m)
    vmem = pl.BlockSpec(memory_space=pltpu.VMEM)
    hbm = pl.BlockSpec(memory_space=ANY)
    return pl.pallas_call(
        functools.partial(last_body, n, m),
        out_shape=(
            jax.ShapeDtypeStruct((tokens, width), f32),
            jax.ShapeDtypeStruct((3, ffn.shape[1] // n, ffn.shape[2] * n), ffn.dtype),
            jax.ShapeDtypeStruct((n, strip, cols), bf16),
            jax.ShapeDtypeStruct(wo.shape, wo.dtype),
            jax.ShapeDtypeStruct(vec.shape, vec.dtype),
        ),
        in_specs=[hbm] * 7,
        out_specs=[vmem] + [hbm] * 4,
        scratch_shapes=[
            pltpu.VMEM(dqkv.shape, bf16),
            pltpu.VMEM(w.shape, bf16),
            pltpu.VMEM(downs.shape, bf16),
            pltpu.VMEM(downs.shape[1:], bf16),
            pltpu.VMEM((w.shape[1], cols), bf16),
        ]
        + Reduce.scratch(tokens, width)
        + [
            pltpu.VMEM((4, tokens, width), bf16),
            pltpu.VMEM((width, length), bf16),
            pltpu.VMEM((n, m, strip, cols), bf16),
            pltpu.VMEM((m, n, strip, cols), bf16),
            pltpu.VMEM((n, strip, cols), bf16),
            pltpu.SemaphoreType.DMA((3, 2, n - 1)),
            pltpu.SemaphoreType.DMA((3, 2, m - 1)),
            pltpu.SemaphoreType.DMA((11,)),
        ],
        compiler_params=pltpu.CompilerParams(
            collective_id=ident, has_side_effects=True, vmem_limit_bytes=VMEM_LIMIT
        ),
        cost_estimate=COST,
        name="last",
    )(dqkv, w, norm_t, ffn, downs, wo, vec)


def column(row):
    return jnp.broadcast_to(row, (8, row.shape[1])).T[:, :1]


def lanes_of_columns(shape, of):
    column = lax.broadcasted_iota(jnp.int32, shape, of).astype(f32)
    lane = lax.broadcasted_iota(jnp.int32, shape, 1 - of).astype(f32)
    half = jnp.floor((column + 0.5) * (1.0 / HALF))
    return jnp.where(lane == column + half * (SLOT - HALF), 1.0, 0.0).astype(bf16)


def gain_row(tiles, which, strip):
    stacked = tiles.reshape(-1, LANES).astype(bf16)
    count = stacked.shape[0] // 8
    shape = (LANES, count * strip)
    lane = lax.broadcasted_iota(jnp.int32, shape, 1).astype(f32)
    owner = jnp.floor((lane + 0.5) * (1.0 / strip))
    inside = lane - owner * strip
    pick = lax.broadcasted_iota(jnp.int32, shape, 0).astype(f32) == inside
    spread_out = jnp.dot(
        stacked, jnp.where(pick, 1.0, 0.0).astype(bf16), preferred_element_type=f32
    )
    shape = spread_out.shape
    lane = lax.broadcasted_iota(jnp.int32, shape, 1).astype(f32)
    owner = jnp.floor((lane + 0.5) * (1.0 / strip))
    row = lax.broadcasted_iota(jnp.int32, shape, 0).astype(f32)
    mine = row == owner * 8.0 + which
    return jnp.sum(jnp.where(mine, spread_out, 0.0), axis=0, keepdims=True)


def entry_body(
    n, m, heads, strip, x, doc_ids, positions, wq, wk, wv, one, two, wg, wu, wd, wo, inverse,
    norm_t, q, k, v, cosine, sine, w, gain_one, gain_two, docs, ffn, down, wo_z,
    blocks, norms, turned, places_all, w_all, gains_all, q_here, k_here, v_here, cos_here, sin_here,
    places, wqkv, gains, widen, sx, lx, rem, sz, sn, loc,
):
    plane = Plane(n, m)
    greet(plane, True)
    tokens = x.shape[0]
    start = 0
    for weight in (wq, wk, wv):
        each = weight.shape[1] // n
        for i in range(n):
            wqkv[i, :, start : start + each] = weight[:, i * each : (i + 1) * each]
        start += each
    gains[...] = jnp.zeros_like(gains)
    gains[0:1, :strip] = one[...].astype(f32)
    gains[1:2, :strip] = two[...].astype(f32)
    places[0:1, :] = doc_ids[...]
    places[1:2, :] = positions[...]
    meet(plane, True)
    gather = Gathers(plane, x, lambda i: blocks.at[i], sx, lx, 1)
    first = []
    for i, (src, dst) in enumerate(((gains, gains_all), (wqkv, w_all))):
        first += exchange(
            plane,
            lambda s, src=src, i=i: src.at[s] if i else src,
            lambda s, dst=dst: dst.at[s, plane.t],
            rem.at[i, 0],
            rem.at[i, 1],
            loc.at[1 + i],
        )
    few = exchange(
        plane, lambda i: places, lambda i: places_all.at[i], rem.at[2, 0], rem.at[2, 1], loc.at[3]
    )
    for copy in first + few:
        copy.start()
    gather.start()
    across = []
    for i, ref in enumerate((gains_all, w_all)):

        def slot(t, ref=ref):
            return ref.at[:, plane.t]

        across.append(fan(plane, slot, slot, sz.at[i, 0], sz.at[i, 1]))
    across.append(fan(plane, lambda t: wo, lambda t: wo_z.at[t], sz.at[2, 0], sz.at[2, 1]))
    own_wo = pltpu.make_async_copy(wo, wo_z.at[plane.t], loc.at[4])
    own_wo.start()
    for copy in first:
        copy.wait()
    for copy in across[0] + across[1]:
        copy.start()
    widen[...] = lanes_of_columns(widen.shape, 0)
    moves = []
    width, rows = wg.shape[1] // n, wg.shape[0]
    for j, weight in enumerate((wg, wu, wd)):
        moves += exchange(
            plane,
            lambda i, weight=weight: weight.at[:, pl.ds(pl.multiple_of(i * width, width), width)],
            lambda i, dst=ffn.at[j] if j < 2 else down: dst.at[
                pl.ds(pl.multiple_of(i * rows, rows), rows), :
            ],
            rem.at[3 + j, 0],
            rem.at[3 + j, 1],
            loc.at[5 + j],
        )
    for copy in few + across[0]:
        copy.wait()
    tiles = gains_all[...]
    gain_one[...] = gain_row(tiles, 0, strip)
    gain_two[...] = gain_row(tiles, 1, strip)
    gather.wait_own()

    def number(it):
        return plane.number(it // 2, lax.rem(it, 2))

    def store(it, at):
        span = pl.ds(pl.multiple_of(number(it) * tokens, tokens), tokens)
        return pltpu.make_async_copy(turned.at[at], norm_t.at[:, span], sn.at[at])

    def normalize(it, carry):
        b = number(it)
        at = lax.rem(it, 2)

        @pl.when(it == 1)
        def _():
            gather.wait_swap()

        @pl.when(it == 2)
        def _():
            gather.relay_near()

        @pl.when(it == 3)
        def _():
            gather.wait_share(1)

        @pl.when(it == 5)
        def _():
            gather.wait_share(0)

        @pl.when(it == 6)
        def _():
            gather.relay_far()
            for copy in moves + across[2]:
                copy.start()

        @pl.when(it == 7)
        def _():
            gather.wait_share(2)

        @pl.when(it >= 2)
        def _():
            store(it - 2, at).wait()

        value = blocks[b].astype(f32)
        scale = lax.rsqrt(jnp.mean(value * value, axis=1, keepdims=True) + norm_epsilon)
        low = (value * scale * gain_one[...]).astype(bf16)
        norms[b] = low
        turned[at] = low.T
        store(it, at).start()
        here = pl.ds(pl.multiple_of(b * tokens, tokens), tokens)
        docs[:, here] = places_all[b, 0:1, :]
        angles = column(places_all[b, 1:2, :].astype(f32)) * inverse[...]
        lanes = lax.broadcasted_iota(jnp.int32, angles.shape, 1)
        sin = jnp.sin(angles)
        cos_here[here, :] = jnp.cos(angles)
        sin_here[here, :] = jnp.where(lanes < SLOT, -sin, sin)
        return carry

    lax.fori_loop(0, n, normalize, 0)
    outs = [
        pltpu.make_async_copy(cos_here, cosine, loc.at[8]),
        pltpu.make_async_copy(sin_here, sine, loc.at[9]),
        pltpu.make_async_copy(q_here, q, loc.at[10]),
        pltpu.make_async_copy(k_here, k, loc.at[11]),
        pltpu.make_async_copy(v_here, v, loc.at[12]),
    ]
    for copy in outs[:2]:
        copy.start()
    for copy in across[1]:
        copy.wait()

    def widened(s, carry):
        at = pl.ds(pl.multiple_of(s * m * strip, m * strip), m * strip)
        narrow = w_all[s].reshape(m * strip, w_all.shape[3])
        w[at, :] = jnp.dot(narrow, widen[...], preferred_element_type=f32).astype(bf16)
        return carry

    lax.fori_loop(0, n, widened, 0)

    def project(b, carry):
        here = pl.ds(pl.multiple_of(b * tokens, tokens), tokens)
        out = jnp.dot(norms[b], w[...], preferred_element_type=f32)
        cos, sin = cos_here[here, :], sin_here[here, :]
        for h in range(heads + 1):
            part = out[:, h * LANES : (h + 1) * LANES]
            rotated = (part * cos + pltpu.roll(part, SLOT, 1) * sin).astype(bf16)
            if h < heads:
                q_here[h, here, :] = rotated
            else:
                k_here[here, :] = rotated
        v_here[here, :] = out[:, (heads + 1) * LANES :].astype(bf16)
        return carry

    lax.fori_loop(0, n, project, 0)
    for copy in outs[2:]:
        copy.start()
    gather.wait_sends()
    store(n - 2, 0).wait()
    store(n - 1, 1).wait()
    own_wo.wait()
    for copy in across[2] + moves + outs:
        copy.wait()


def entry(n, m, heads, x, docs, positions, wq, wk, wv, one, two, wg, wu, wd, wo, inverse, ident):
    tokens, width = x.shape
    length = n * tokens
    strip = wq.shape[0]
    each = (wq.shape[1] + wk.shape[1] + wv.shape[1]) // n
    wide = each // HALF * SLOT
    rows, cols = wg.shape
    vmem = pl.BlockSpec(memory_space=pltpu.VMEM)
    hbm = pl.BlockSpec(memory_space=ANY)
    return pl.pallas_call(
        functools.partial(entry_body, n, m, heads, strip),
        out_shape=(
            jax.ShapeDtypeStruct((width, length), bf16),
            jax.ShapeDtypeStruct((heads, length, LANES), bf16),
            jax.ShapeDtypeStruct((length, LANES), bf16),
            jax.ShapeDtypeStruct((length, LANES), bf16),
            jax.ShapeDtypeStruct((length, LANES), f32),
            jax.ShapeDtypeStruct((length, LANES), f32),
            jax.ShapeDtypeStruct((width, wide), bf16),
            jax.ShapeDtypeStruct((1, width), f32),
            jax.ShapeDtypeStruct((1, width), f32),
            jax.ShapeDtypeStruct((1, length), jnp.int32),
            jax.ShapeDtypeStruct((2, rows * n, cols // n), wg.dtype),
            jax.ShapeDtypeStruct((rows * n, cols // n), wg.dtype),
            jax.ShapeDtypeStruct((m,) + wo.shape, wo.dtype),
        ),
        in_specs=[hbm] + [vmem] * 7 + [hbm] * 4 + [vmem],
        out_specs=[hbm] * 6 + [vmem] * 4 + [hbm] * 3,
        scratch_shapes=[
            pltpu.VMEM((n, tokens, width), bf16),
            pltpu.VMEM((n, tokens, width), bf16),
            pltpu.VMEM((2, width, tokens), bf16),
            pltpu.VMEM((n, 2, tokens), jnp.int32),
            pltpu.VMEM((n, m, strip, each), bf16),
            pltpu.VMEM((n, m, 8, LANES), f32),
            pltpu.VMEM((heads, length, LANES), bf16),
            pltpu.VMEM((length, LANES), bf16),
            pltpu.VMEM((length, LANES), bf16),
            pltpu.VMEM((length, LANES), f32),
            pltpu.VMEM((length, LANES), f32),
            pltpu.VMEM((2, tokens), jnp.int32),
            pltpu.VMEM((n, strip, each), bf16),
            pltpu.VMEM((8, LANES), f32),
            pltpu.VMEM((each, wide), bf16),
            *Gathers.scratch(1),
            pltpu.SemaphoreType.DMA((6, 2, n - 1)),
            pltpu.SemaphoreType.DMA((3, 2, m - 1)),
            pltpu.SemaphoreType.DMA((2,)),
            pltpu.SemaphoreType.DMA((13,)),
        ],
        compiler_params=pltpu.CompilerParams(
            collective_id=ident, has_side_effects=True, vmem_limit_bytes=VMEM_LIMIT
        ),
        cost_estimate=COST,
        name="entry",
    )(x, docs, positions, wq, wk, wv, one, two, wg, wu, wd, wo, inverse)


BLOCK = 512
NT = (((1,), (1,)), ((), ()))
LOG2E = 1.4426950408889634


def allowed_block(first_key, first_query, begin, causal):
    keys = first_key + lax.broadcasted_iota(jnp.int32, (BLOCK, BLOCK), 0)
    ok = keys >= begin
    if causal:
        queries = first_query + lax.broadcasted_iota(jnp.int32, (BLOCK, BLOCK), 1)
        ok = ok & (keys <= queries)
    return ok


def begins(docs):
    begin = jnp.zeros(docs.shape, jnp.int32)
    for d in range(3):
        count = jnp.sum((docs == d).astype(f32), axis=1, keepdims=True).astype(jnp.int32)
        begin = begin + jnp.where(docs > d, count, 0)
    return begin


def spread_rows(wo, wo_here):
    halves, filled, width = wo.shape
    for i in range(halves):
        wo_here[i * SLOT : i * SLOT + filled, :] = wo[i]
        wo_here[i * SLOT + filled : (i + 1) * SLOT, :] = jnp.zeros((SLOT - filled, width), bf16)


def attend_body(
    n, m, factor, q, k, v, docs, wo, go, x, gain, ffn,
    o_out, lse, start, low_out, go_all, resid, norm, ffn_all,
    o, low, vt, top, total, acc, wo_here, go_here,
    pair, near, far, sr, lr, stage, sg, lg, sz, loc,
):
    plane = Plane(n, m)
    rows = x.shape[0]
    heads = q.shape[0]
    greet(plane, True)
    gather = Gathers(plane, go, lambda i: go_here.at[i], sg, lg, 2)
    reduce = Reduce(plane, None, pair, near, far, sr, None, stage)
    spread_rows(wo, wo_here)
    vt[...] = v[...].T
    start[...] = begins(docs[...])
    meet(plane, True)
    gather.start()
    chain = Chain(plane, ffn, lambda t: ffn_all.at[t], sz)
    chain.start()
    own_ffn = pltpu.make_async_copy(ffn, ffn_all.at[plane.t], loc.at[3])
    own_ffn.start()

    def chips(step, carry):
        kk = 3 - step
        i = plane.number(kk, 0) // 2
        here = pl.ds(pl.multiple_of(i * BLOCK, BLOCK), BLOCK)
        begin = start[:, here]

        def head(h, carry):
            query = q[h, here, :]
            top[...] = jnp.full_like(top, mask_fill_value)
            total[...] = jnp.zeros_like(total)
            acc[...] = jnp.zeros_like(acc)

            def keys(j, causal):
                at = pl.ds(pl.multiple_of(j * BLOCK, BLOCK), BLOCK)
                raw = lax.dot_general(k[at, :], query, NT, preferred_element_type=f32)
                ok = allowed_block(j * BLOCK, i * BLOCK, begin, causal)
                scores = jnp.where(ok, raw * factor, mask_fill_value)
                new_top = jnp.maximum(top[...], jnp.max(scores, axis=0, keepdims=True))
                weights = jnp.exp2(scores - new_top)
                keep = jnp.exp2(top[...] - new_top)
                total[...] = total[...] * keep + jnp.sum(weights, axis=0, keepdims=True)
                acc[...] = acc[...] * keep + jnp.dot(
                    vt[:, at], weights.astype(bf16), preferred_element_type=f32
                )
                top[...] = new_top

            def loop(j, carry):
                keys(j, False)
                return carry

            lax.fori_loop(0, i, loop, 0)
            keys(i, True)
            out = (acc[...] / total[...]).T
            o[h, here, :] = out
            low[here, pl.ds(pl.multiple_of(h * LANES, LANES), LANES)] = out.astype(bf16)
            lse[h, :, here] = top[...] + jnp.log2(total[...])
            return carry

        lax.fori_loop(0, heads, head, 0)

        @pl.when(step == 1)
        def _():
            reduce.join(3)
            reduce.out[0].start()

        @pl.when(step == 3)
        def _():
            reduce.join(1)
            reduce.out[1].start()

        for other in (1, 0):
            b = plane.number(kk, other)
            at = pl.ds(pl.multiple_of(b * rows, rows), rows)
            part = jnp.dot(low[at, :], wo_here[...], preferred_element_type=f32).astype(bf16)
            if other:
                stage[kk] = part
                for which in range(4):

                    @pl.when(kk == which)
                    def _(which=which):
                        reduce.swaps[Reduce.THEIRS[which]].start()

            else:
                pair[kk] = part
        return carry

    lax.fori_loop(0, 4, chips, 0)
    outs = [
        pltpu.make_async_copy(o, o_out, loc.at[0]),
        pltpu.make_async_copy(low, low_out, loc.at[1]),
    ]
    for copy in outs:
        copy.start()
    gather.relay_near()
    chain.step(1)
    reduce.ready()
    reduce.first(resid, x)
    reduce.send_fro()
    for hop in range(2, m - 1):
        chain.step(hop)
    gather.relay_far()
    reduce.finish(resid)

    def normalize(at):
        value = resid[at, :]
        scale = lax.rsqrt(jnp.mean(value * value, axis=1, keepdims=True) + norm_epsilon)
        norm[at, :] = (value * scale * gain[...]).astype(bf16)

    in_tiles(rows, normalize)
    gather.finish()
    outs.append(pltpu.make_async_copy(go_here, go_all, loc.at[2]))
    outs[-1].start()
    chain.step(m - 1)
    chain.wait_sends()
    own_ffn.wait()
    for copy in outs:
        copy.wait()


def attend(n, m, factor, q, k, v, docs, wo, go, x, gain, ffn, ident):
    heads, length, _ = q.shape
    rows, width = x.shape
    hbm = pl.BlockSpec(memory_space=ANY)
    vmem = pl.BlockSpec(memory_space=pltpu.VMEM)
    return pl.pallas_call(
        functools.partial(attend_body, n, m, factor),
        out_shape=(
            jax.ShapeDtypeStruct((heads, length, LANES), f32),
            jax.ShapeDtypeStruct((heads, 1, length), f32),
            jax.ShapeDtypeStruct((1, length), jnp.int32),
            jax.ShapeDtypeStruct((length, heads * LANES), bf16),
            jax.ShapeDtypeStruct((n,) + go.shape, go.dtype),
            jax.ShapeDtypeStruct((rows, width), f32),
            jax.ShapeDtypeStruct((rows, width), bf16),
            jax.ShapeDtypeStruct((m,) + ffn.shape, bf16),
        ),
        in_specs=[vmem] * 5 + [hbm] + [vmem] * 2 + [hbm],
        out_specs=[hbm, vmem, vmem, hbm, hbm, vmem, vmem, hbm],
        scratch_shapes=[
            pltpu.VMEM((heads, length, LANES), f32),
            pltpu.VMEM((length, heads * LANES), bf16),
            pltpu.VMEM((LANES, length), bf16),
            pltpu.VMEM((1, BLOCK), f32),
            pltpu.VMEM((1, BLOCK), f32),
            pltpu.VMEM((LANES, BLOCK), f32),
            pltpu.VMEM((heads * LANES, width), bf16),
            pltpu.VMEM((n,) + go.shape, go.dtype),
        ]
        + Reduce.scratch(rows, width)
        + [pltpu.VMEM((4, rows, width), bf16)]
        + Gathers.scratch(2)
        + [pltpu.SemaphoreType.DMA((4, m)), pltpu.SemaphoreType.DMA((4,))],
        compiler_params=pltpu.CompilerParams(
            collective_id=ident, has_side_effects=True, vmem_limit_bytes=VMEM_LIMIT
        ),
        cost_estimate=COST,
        name="attend",
    )(q, k, v, docs, wo, go, x, gain, ffn)


def attend_back_body(
    n, m, factor, scale, q_in, k_in, v_in, o_in, lse, begin, cos_in, sin_in, low_in,
    hid_in, down_in, ffn, wo, dnorm, resid, grad, gain,
    out, layer, terms, dresid, gain_out, ffn_sum,
    q, k, v, o, cosine, sine, low, kt, dqt, dk, dv, delta, go, every, dbranch, wo_here,
    hid_low, w_down, stage, pair, near, far, sr, lr, held, gain_sum, gain_cut, gain_got,
    sums, add, own, got, ss, ls, sg, lg, sv, loc,
):
    plane = Plane(n, m)
    heads, length, _ = q.shape
    rows, width = dnorm.shape
    strip = gain_out.shape[2]
    loads = [
        pltpu.make_async_copy(a, b, loc.at[i])
        for i, (a, b) in enumerate(
            (
                (q_in, q), (k_in, k), (v_in, v), (o_in, o),
                (cos_in, cosine), (sin_in, sine), (low_in, low),
            )
        )
    ]
    for copy in loads:
        copy.start()
    greet(plane, True)
    moves = [
        pltpu.make_async_copy(hid_in, hid_low, loc.at[8]),
        pltpu.make_async_copy(down_in, w_down, loc.at[9]),
    ]
    for copy in moves:
        copy.start()
    one = Reduce(plane, None, pair, near, far, sr, None, stage)
    gather = Gathers(plane, dbranch, lambda i: every.at[i], sg, lg, 2)
    gain_copies = exchange(
        plane, lambda i: gain_cut.at[i], lambda i: gain_got.at[i], sv.at[0], sv.at[1], loc.at[7]
    )
    gain_sum[...] = jnp.zeros_like(gain_sum)

    def into_branch(at):
        value, up = resid[at, :], dnorm[at, :]
        scale_two = lax.rsqrt(jnp.mean(value * value, axis=1, keepdims=True) + norm_epsilon)
        inner = gain[...] * up
        moment = jnp.mean(value * inner, axis=1, keepdims=True)
        turned = value * scale_two
        got = (
            grad[at, :].astype(f32) + scale_two * inner - turned * (scale_two * scale_two * moment)
        )
        dresid[at, :] = got
        dbranch[at, :] = got.astype(bf16)
        gain_sum[...] += up * turned

    in_tiles(rows, into_branch)
    meet(plane, True)
    gather.start()
    scatter = Scatter(plane, ffn, sums, add, own, got, ss, ls)
    scatter.start()
    total_gain = jnp.sum(gain_sum[...], axis=0, keepdims=True)
    for i in range(n):
        gain_cut[i] = total_gain[:, i * (width // n) : (i + 1) * (width // n)]
    for copy in gain_copies:
        copy.start()
    spread_rows(wo, wo_here)
    for copy in moves:
        copy.wait()

    def mix(it, carry):
        kk = 3 - it // 2
        other = 1 - lax.rem(it, 2)
        b = plane.number(kk, other)
        at = pl.ds(pl.multiple_of(b * rows, rows), rows)
        part = lax.dot_general(
            hid_low[at, :], w_down[...], NT, preferred_element_type=f32
        ).astype(bf16)

        @pl.when(other == 0)
        def _():
            pair[kk] = part

        @pl.when(other == 1)
        def _():
            stage[kk] = part

        for which in range(4):

            @pl.when(it == 2 * (3 - which))
            def _(which=which):
                one.swaps[Reduce.THEIRS[which]].start()

        return carry

    lax.fori_loop(0, n, mix, 0)
    for copy in loads:
        copy.wait()
    kt[...] = k[...].T
    dk[...] = jnp.zeros_like(dk)
    dv[...] = jnp.zeros_like(dv)

    def unturn(value, at):
        return value * cosine[at, :] - pltpu.roll(value, SLOT, 1) * sine[at, :]

    def chips(kk, carry):
        @pl.when(kk == 0)
        def _():
            gather.wait_own()
            gather.wait_swap()

        @pl.when(kk == 1)
        def _():
            gather.relay_near()
            one.send_to()
            gather.wait_share(1)
            scatter.relay(0, 0)

        @pl.when(kk == 2)
        def _():
            gather.wait_share(0)
            scatter.relay(0, 1)

        @pl.when(kk == 3)
        def _():
            one.ready()
            one.first(held, resid)
            gather.relay_far()
            gather.wait_share(2)
            scatter.relay(1, 0)

        i = plane.number(kk, 0) // 2
        here = pl.ds(pl.multiple_of(i * BLOCK, BLOCK), BLOCK)
        for other in range(2):
            b = plane.number(kk, other)
            at = pl.ds(pl.multiple_of(b * rows, rows), rows)
            value = lax.dot_general(every[b], wo_here[...], NT, preferred_element_type=f32)
            for h in range(heads):
                go[h, at, :] = value[:, h * LANES : (h + 1) * LANES].astype(bf16)

        def head(h, carry):
            query = q[h, here, :]
            grads = go[h, here, :]
            delta[...] = jnp.sum((grads.astype(f32) * o[h, here, :]).T, axis=0, keepdims=True)
            dqt[...] = jnp.zeros_like(dqt)

            def keys(j, causal):
                at = pl.ds(pl.multiple_of(j * BLOCK, BLOCK), BLOCK)
                raw = lax.dot_general(k[at, :], query, NT, preferred_element_type=f32)
                ok = allowed_block(j * BLOCK, i * BLOCK, begin[:, here], causal)
                probs = jnp.where(ok, jnp.exp2(raw * factor - lse[h, :, here]), 0.0)
                dprob = lax.dot_general(v[at, :], grads, NT, preferred_element_type=f32)
                dscore = (probs * (dprob - delta[...])).astype(bf16)
                dv[at, :] += jnp.dot(probs.astype(bf16), grads, preferred_element_type=f32)
                dk[at, :] += jnp.dot(dscore, query, preferred_element_type=f32)
                dqt[...] += jnp.dot(kt[:, at], dscore, preferred_element_type=f32)

            def loop(j, carry):
                keys(j, False)
                return carry

            lax.fori_loop(0, i, loop, 0)
            keys(i, True)
            got = unturn(dqt[...].T * scale, here).astype(bf16)
            out[here, pl.ds(pl.multiple_of(h * LANES, LANES), LANES)] = got
            return carry

        lax.fori_loop(0, heads, head, 0)
        return carry

    lax.fori_loop(0, 4, chips, 0)
    scatter.relay(1, 1)

    def write(i, carry):
        at = pl.ds(pl.multiple_of(i * BLOCK, BLOCK), BLOCK)
        turned = unturn(dk[at, :] * scale, at).astype(bf16)
        out[at, heads * LANES : (heads + 1) * LANES] = turned
        out[at, (heads + 1) * LANES :] = dv[at, :].astype(bf16)
        return carry

    lax.fori_loop(0, length // BLOCK, write, 0)
    one.send_fro()
    across = every.reshape(length, width)
    part = 512

    def into_terms(i, carry):
        at = pl.ds(pl.multiple_of(i * part, part), part)
        value = lax.dot_general(
            low[...], across[:, at], (((0,), (0,)), ((), ())), preferred_element_type=f32
        ).astype(bf16)
        for half in range(terms.shape[0]):
            terms[half, :, at] = value[half * SLOT : half * SLOT + HALF]
        return carry

    lax.fori_loop(0, width // part, into_terms, 0)
    for copy in gain_copies:
        copy.wait()
    all_gain = gain_got[0]
    for i in range(1, n):
        all_gain = all_gain + gain_got[i]
    for t in range(m):
        gain_out[t] = all_gain[:, t * strip : (t + 1) * strip]
    gather.wait_sends()
    one.finish(held, layer)
    scatter.finish()
    back = pltpu.make_async_copy(sums, ffn_sum, loc.at[10])
    back.start()
    back.wait()


def attend_back(
    n, m, factor, scale, q, k, v, o, lse, begin, cosine, sine, low,
    hid_low, w_down, ffn, wo, dnorm, resid, grad, gain, ident,
):
    heads, length, _ = q.shape
    rows, width = dnorm.shape
    strip = width // (n * m)
    hbm = pl.BlockSpec(memory_space=ANY)
    vmem = pl.BlockSpec(memory_space=pltpu.VMEM)
    return pl.pallas_call(
        functools.partial(attend_back_body, n, m, factor, scale),
        out_shape=(
            jax.ShapeDtypeStruct((length, (heads + 2) * LANES), bf16),
            jax.ShapeDtypeStruct((rows, width), bf16),
            jax.ShapeDtypeStruct(wo.shape, bf16),
            jax.ShapeDtypeStruct((rows, width), f32),
            jax.ShapeDtypeStruct((m, 1, strip), f32),
            jax.ShapeDtypeStruct(ffn.shape[1:], bf16),
        ),
        in_specs=[hbm] * 4 + [vmem] * 2 + [hbm] * 6 + [vmem] * 5,
        out_specs=[vmem] * 5 + [hbm],
        scratch_shapes=[
            pltpu.VMEM(q.shape, bf16),
            pltpu.VMEM(k.shape, bf16),
            pltpu.VMEM(v.shape, bf16),
            pltpu.VMEM(o.shape, f32),
            pltpu.VMEM(cosine.shape, f32),
            pltpu.VMEM(sine.shape, f32),
            pltpu.VMEM(low.shape, bf16),
            pltpu.VMEM((LANES, length), bf16),
            pltpu.VMEM((LANES, BLOCK), f32),
            pltpu.VMEM((length, LANES), f32),
            pltpu.VMEM((length, LANES), f32),
            pltpu.VMEM((1, BLOCK), f32),
            pltpu.VMEM((heads, length, LANES), bf16),
            pltpu.VMEM((n, rows, width), bf16),
            pltpu.VMEM((rows, width), bf16),
            pltpu.VMEM((heads * LANES, width), bf16),
            pltpu.VMEM(hid_low.shape, bf16),
            pltpu.VMEM(w_down.shape, bf16),
            pltpu.VMEM((4, rows, width), bf16),
        ]
        + Reduce.scratch(rows, width)
        + [
            pltpu.VMEM((rows, width), f32),
            pltpu.VMEM((TILE, width), f32),
            pltpu.VMEM((n, 1, width // n), f32),
            pltpu.VMEM((n, 1, width // n), f32),
            pltpu.VMEM(ffn.shape[1:], bf16),
        ]
        + Scatter.scratch(ffn.shape[1:])
        + Gathers.scratch(2)
        + [pltpu.SemaphoreType.DMA((2, n - 1)), pltpu.SemaphoreType.DMA((11,))],
        compiler_params=pltpu.CompilerParams(
            collective_id=ident, has_side_effects=True, vmem_limit_bytes=VMEM_LIMIT
        ),
        cost_estimate=COST,
        name="attend_back",
    )(
        q, k, v, o, lse, begin, cosine, sine, low, hid_low, w_down, ffn, wo, dnorm, resid, grad, gain
    )


def feed_body(
    n, m, mine, go, w_in, down, dnorm, grads, hid_out, down_out, down_parts,
    rows, rows_t, go_t, go_two, w, w_down, gates, h, hid_low, down_held, down_sum,
    pair, near, far, stage,
    sg, lg, sr, loc, sw, so, sd, sz, sf,
):
    plane = Plane(n, m)
    tokens, width = rows.shape[1:]
    hid = down.shape[1]
    half = m * hid
    greet(plane, True)
    gather = Gathers(plane, mine, lambda i: rows.at[i], sg, lg, 2)
    reduce = Reduce(plane, None, pair, near, far, sr, None, stage)

    def columns(ref, j, t):
        return ref.at[:, j * half + t * hid : j * half + (t + 1) * hid]

    weights = [
        pltpu.make_async_copy(w_in.at[t, j], columns(w, j, t), sw.at[j, t])
        for j in range(2)
        for t in range(m)
    ]
    for copy in weights:
        copy.start()
    meet(plane, True)
    gather.start()

    def down_at(ref, t):
        return ref.at[:, pl.ds(pl.multiple_of(t * hid, hid), hid)]

    chain = Chain(plane, down, lambda t: down_at(w_down, t), sz)
    chain.start()
    own_down = pltpu.make_async_copy(down, down_at(w_down, plane.t), loc.at[0])
    own_down.start()
    gather.wait_own()
    for copy in weights:
        copy.wait()

    def span(b):
        return pl.ds(pl.multiple_of(b * tokens, tokens), tokens)

    def down_grad(kk, keep):
        chip = plane.number(kk, 0) // 2
        at = pl.ds(pl.multiple_of(chip * 2 * tokens, 2 * tokens), 2 * tokens)

        def part(i, carry):
            line = pl.ds(pl.multiple_of(i * 256, 256), 256)
            value = jnp.dot(go_t[line, at], hid_low[at, :], preferred_element_type=f32)
            keep(line, value)
            return carry

        lax.fori_loop(0, width // 256, part, 0)

    def set_down(line, value):
        down_sum[line, :] = value

    def add_down(line, value):
        down_sum[line, :] += value

    def hold_down(line, value):
        down_held[line, :] = (down_sum[line, :] + value).astype(bf16)

    def early_go(it, slot):
        b = plane.number(it // 2, lax.rem(it, 2))
        return pltpu.make_async_copy(go.at[b], go_two.at[slot], so.at[slot])

    def forward(it, carry):
        b = plane.number(it // 2, lax.rem(it, 2))

        @pl.when(it == 1)
        def _():
            gather.wait_swap()

        @pl.when(it == 2)
        def _():
            down_grad(0, set_down)
            chain.step(1)
            gather.relay_near()

        @pl.when(it == 3)
        def _():
            gather.wait_share(1)

        @pl.when(it == 4)
        def _():
            chain.step(2)

        @pl.when(it == 5)
        def _():
            gather.wait_share(0)

        @pl.when(it == 6)
        def _():
            down_grad(1, add_down)
            down_grad(2, add_down)
            gather.relay_far()

        @pl.when(it == 7)
        def _():
            gather.wait_share(2)

        slot = lax.rem(it, 2)

        @pl.when(it < n - 1)
        def _():
            early_go(it + 1, 1 - slot).start()

        row = rows[b]
        both = jnp.dot(row, w[...], preferred_element_type=f32)
        gates[span(b), :] = both
        gate, up = both[:, :half], both[:, half:]
        hid_low[span(b), :] = (gate * jax.nn.sigmoid(gate) * up).astype(bf16)
        rows_t[:, span(b)] = row.T
        early_go(it, slot).wait()
        go_t[:, span(b)] = go_two[slot].T
        return carry

    early_go(0, 0).start()
    lax.fori_loop(0, n, forward, 0)

    def number(it):
        return plane.number(3 - it // 2, 1 - lax.rem(it, 2))

    def load_go(it, slot):
        return pltpu.make_async_copy(go.at[number(it)], go_two.at[slot], so.at[slot])

    load_go(0, 0).start()
    down_grad(3, hold_down)
    outs = fan(
        plane, lambda t: down_at(down_held, t), lambda t: down_parts.at[t], sf.at[0], sf.at[1]
    )
    outs.append(
        pltpu.make_async_copy(down_at(down_held, plane.t), down_parts.at[plane.t], loc.at[1])
    )
    outs.append(pltpu.make_async_copy(hid_low, hid_out, loc.at[2]))
    for copy in outs:
        copy.start()
    for hop in range(3, m):
        chain.step(hop)
    own_down.wait()
    outs.append(pltpu.make_async_copy(w_down, down_out, loc.at[3]))
    outs[-1].start()

    def backward(it, carry):
        slot = lax.rem(it, 2)
        k = 3 - it // 2
        b = number(it)

        @pl.when(it == 2)
        def _():
            reduce.join(3)
            reduce.out[0].start()

        @pl.when(it == 6)
        def _():
            reduce.join(1)
            reduce.out[1].start()

        @pl.when(it == 7)
        def _():
            reduce.ready()
            reduce.send_fro()

        @pl.when(it < n - 1)
        def _():
            load_go(it + 1, 1 - slot).start()

        load_go(it, slot).wait()

        gate = gates[span(b), :half]
        up = gates[span(b), half:]
        dhidden = jnp.dot(go_two[slot], w_down[...], preferred_element_type=f32)
        sig = jax.nn.sigmoid(gate)
        dgate = (dhidden * up * sig * (1.0 + gate * (1.0 - sig))).astype(bf16)
        dup = (dhidden * gate * sig).astype(bf16)
        h[span(b), :half] = dgate
        h[span(b), half:] = dup
        part = lax.dot_general(h[span(b), :], w[...], NT, preferred_element_type=f32)
        part = part.astype(bf16)

        @pl.when(lax.rem(it, 2) == 1)
        def _():
            pair[k] = part

        @pl.when(lax.rem(it, 2) == 0)
        def _():
            stage[k] = part

        for kk in range(4):

            @pl.when(it == 2 * (3 - kk))
            def _(kk=kk):
                reduce.swaps[Reduce.THEIRS[kk]].start()

        return carry

    lax.fori_loop(0, n, backward, 0)

    def weight_grad(i, carry):
        at = pl.ds(pl.multiple_of(i * 256, 256), 256)
        value = jnp.dot(rows_t[at, :], h[...], preferred_element_type=f32)
        w[at, :] = value.astype(bf16)
        return carry

    lax.fori_loop(0, width // 256, weight_grad, 0)
    ends = [
        pltpu.make_async_copy(columns(w, j, t), grads.at[t, j], sd.at[j, t])
        for j in range(2)
        for t in range(m)
    ]
    for copy in ends:
        copy.start()
    reduce.first(dnorm)
    gather.wait_sends()
    chain.wait_sends()
    reduce.finish(dnorm)
    for copy in outs + ends:
        copy.wait()


def feed(n, m, norm, go, w_in, down, ident):
    tokens, width = norm.shape
    hid = down.shape[1]
    length = n * tokens
    half = m * hid
    hbm = pl.BlockSpec(memory_space=ANY)
    return pl.pallas_call(
        functools.partial(feed_body, n, m),
        out_shape=(
            jax.ShapeDtypeStruct((tokens, width), f32),
            jax.ShapeDtypeStruct((m, 2, width, hid), bf16),
            jax.ShapeDtypeStruct((length, half), bf16),
            jax.ShapeDtypeStruct((width, half), bf16),
            jax.ShapeDtypeStruct((m, width, hid), bf16),
        ),
        in_specs=[hbm] * 4,
        out_specs=[pl.BlockSpec(memory_space=pltpu.VMEM)] + [hbm] * 4,
        scratch_shapes=[
            pltpu.VMEM((n, tokens, width), bf16),
            pltpu.VMEM((width, length), bf16),
            pltpu.VMEM((width, length), bf16),
            pltpu.VMEM((2, tokens, width), bf16),
            pltpu.VMEM((width, 2 * half), bf16),
            pltpu.VMEM((width, half), bf16),
            pltpu.VMEM((length, 2 * half), f32),
            pltpu.VMEM((length, 2 * half), bf16),
            pltpu.VMEM((length, half), bf16),
            pltpu.VMEM((width, half), bf16),
            pltpu.VMEM((width, half), f32),
        ]
        + [pltpu.VMEM((slots, tokens, width), bf16) for slots in Reduce.SLOTS]
        + [
            pltpu.VMEM((4, tokens, width), bf16),
            *Gathers.scratch(2),
            pltpu.SemaphoreType.DMA((4, 4)),
            pltpu.SemaphoreType.DMA((4,)),
            pltpu.SemaphoreType.DMA((2, m)),
            pltpu.SemaphoreType.DMA((2,)),
            pltpu.SemaphoreType.DMA((2, m)),
            pltpu.SemaphoreType.DMA((4, m)),
            pltpu.SemaphoreType.DMA((2, m - 1)),
        ],
        compiler_params=pltpu.CompilerParams(
            collective_id=ident, has_side_effects=True, vmem_limit_bytes=VMEM_LIMIT
        ),
        cost_estimate=COST,
        name="feed",
    )(norm, go, w_in, down)


def results_body(
    dnorm, dresid, x, gain, layer_in, ffn, qkv, wo, vec, wq, wk, wv, one,
    layer, input_grad, first, query, key, value, output, second, gate, up, down,
):
    step = pl.program_id(0)

    def into_input(at):
        token = x[at, :].astype(f32)
        scale = lax.rsqrt(jnp.mean(token * token, axis=1, keepdims=True) + norm_epsilon)
        inner = gain[...] * dnorm[at, :]
        moment = jnp.mean(token * inner, axis=1, keepdims=True)
        input_grad[at, :] = (
            dresid[at, :] + scale * inner - token * scale * (scale * scale * moment)
        )
        layer[at, :] = layer_in[at, :]

    in_tiles(x.shape[0], into_input, 64)
    for i, ref in enumerate((gate, up, down)):
        ref[...] = ffn[i].astype(f32)

    @pl.when(step == 0)
    def _():
        groups, strip, _ = qkv.shape
        start = 0
        sums = jnp.zeros((strip, 1), f32)
        for ref, weight in ((query, wq), (key, wk), (value, wv)):
            each = ref.shape[1] // groups
            for g in range(groups):
                ref[:, g * each : (g + 1) * each] = qkv[g, :, start : start + each].astype(f32)
            start += each
            sums += jnp.sum(weight[...].astype(f32) * ref[...], axis=1, keepdims=True)
        row = jnp.broadcast_to(sums, (strip, LANES)).T[0:1, :strip]
        first[...] = row / one[...].astype(f32)
        total = wo[0].astype(f32)
        gains = vec[0]
        for t in range(1, wo.shape[0]):
            total += wo[t].astype(f32)
            gains += vec[t]
        output[...] = total
        second[...] = gains


def results(dnorm, dresid, x, gain, layer, ffn, qkv, wo, vec, wq, wk, wv, one):
    tokens, width = x.shape
    rows, cols = ffn.shape[1:]
    strip = wq.shape[0]
    steps = 2

    def tiled(count, columns):
        return pl.BlockSpec((count // steps, columns), lambda i: (i, 0))

    def fixed(*shape):
        return pl.BlockSpec(
            shape, lambda i: (0,) * len(shape), pipeline_mode=pl.Buffered(buffer_count=1)
        )

    return pl.pallas_call(
        results_body,
        grid=(steps,),
        out_shape=(
            jax.ShapeDtypeStruct((tokens, width), bf16),
            jax.ShapeDtypeStruct((tokens, width), f32),
            jax.ShapeDtypeStruct((1, strip), f32),
            jax.ShapeDtypeStruct(wq.shape, f32),
            jax.ShapeDtypeStruct(wk.shape, f32),
            jax.ShapeDtypeStruct(wv.shape, f32),
            jax.ShapeDtypeStruct((strip, width), f32),
            jax.ShapeDtypeStruct((1, strip), f32),
            jax.ShapeDtypeStruct((rows, cols), f32),
            jax.ShapeDtypeStruct((rows, cols), f32),
            jax.ShapeDtypeStruct((rows, cols), f32),
        ),
        in_specs=[
            tiled(tokens, width),
            tiled(tokens, width),
            tiled(tokens, width),
            fixed(1, width),
            tiled(tokens, width),
            pl.BlockSpec((3, rows // steps, cols), lambda i: (0, i, 0)),
            fixed(*qkv.shape),
            fixed(*wo.shape),
            fixed(*vec.shape),
            fixed(*wq.shape),
            fixed(*wk.shape),
            fixed(*wv.shape),
            fixed(1, strip),
        ],
        out_specs=[
            tiled(tokens, width),
            tiled(tokens, width),
            fixed(1, strip),
            fixed(*wq.shape),
            fixed(*wk.shape),
            fixed(*wv.shape),
            fixed(strip, width),
            fixed(1, strip),
            tiled(rows, cols),
            tiled(rows, cols),
            tiled(rows, cols),
        ],
        compiler_params=pltpu.CompilerParams(vmem_limit_bytes=VMEM_LIMIT),
        cost_estimate=COST,
        name="results",
    )(dnorm, dresid, x, gain, layer, ffn, qkv, wo, vec, wq, wk, wv, one)


def fast_layer(n, m):
    def on_plane(
        layer_input,
        doc_ids,
        positions,
        first_gain,
        query_weight,
        key_weight,
        value_weight,
        output_weight,
        second_gain,
        gate_weight,
        up_weight,
        down_weight,
        out_grad,
    ):
        x = layer_input[0]
        width = x.shape[1]
        heads = QUERY_HEADS // n
        scale = 1.0 / math.sqrt(HEAD_SIZE)
        factor = scale * LOG2E
        strip = query_weight.shape[0]

        lane = np.arange(LANES) % SLOT
        inverse = np.where(lane < HALF, rope_base ** (-(lane * 2.0 / HEAD_SIZE)), 0.0)
        (
            norm_t, q, k, v, cosine, sine, wqkv, gain_one, gain_two, docs,
            ffn_mine, down_mine, output_rows,
        ) = entry(
            n, m, heads, x, doc_ids, positions, query_weight, key_weight, value_weight,
            first_gain.reshape(1, strip), second_gain.reshape(1, strip),
            gate_weight, up_weight, down_weight, output_weight,
            jnp.asarray(inverse[None], f32), 0,
        )
        o, lse, begin, low, grad_all, resid, norm_two, ffn_all = attend(
            n, m, factor, q, k, v, docs, output_rows, out_grad[0], x, gain_two, ffn_mine, 9
        )
        dnorm_two, ffn_terms, hid_low, w_down, down_parts = feed(
            n, m, norm_two, grad_all, ffn_all, down_mine, 2
        )
        dqkv, layer_output, output_terms, dresid, gain_part, ffn_sum = attend_back(
            n, m, factor, scale, q, k, v, o, lse, begin, cosine, sine, low, hid_low, w_down, ffn_terms,
            output_rows, dnorm_two, resid, out_grad[0], gain_two, 3,
        )
        dnorm_one, ffn_out, qkv_out, output_parts, gain_sums = last(
            n, m, dqkv, wqkv, norm_t, ffn_sum, down_parts, output_terms, gain_part, 6
        )
        (
            layer_output, input_grad, first_gain_grad, query_grad, key_grad, value_grad,
            output_grad, second_gain_grad, gate_grad, up_grad, down_grad,
        ) = results(
            dnorm_one, dresid, x, gain_one, layer_output, ffn_out, qkv_out, output_parts,
            gain_sums, query_weight, key_weight, value_weight, first_gain.reshape(1, strip),
        )
        return (
            layer_output[None],
            input_grad[None],
            first_gain_grad.reshape(strip),
            query_grad,
            key_grad,
            value_grad,
            output_grad,
            second_gain_grad.reshape(strip),
            gate_grad,
            up_grad,
            down_grad,
        )

    return on_plane


def solution(mesh):
    n, m = mesh.shape["seq"], mesh.shape["tp"]
    fits = n == KEY_VALUE_HEADS == 8 and m == 4
    return jax.shard_map(
        fast_layer(n, m) if fits else on_device,
        mesh=mesh,
        in_specs=(
            P("tp", "seq", None),
            P("tp", "seq"),
            P("tp", "seq"),
            P(("seq", "tp")),
            P(("seq", "tp"), None),
            P(("seq", "tp"), None),
            P(("seq", "tp"), None),
            P(("seq", "tp"), None),
            P(("seq", "tp")),
            P("seq", "tp"),
            P("seq", "tp"),
            P("seq", "tp"),
            P("tp", "seq", None),
        ),
        out_specs=(
            P("tp", "seq", None),
            P("tp", "seq", None),
            P(("seq", "tp")),
            P(("seq", "tp"), None),
            P(("seq", "tp"), None),
            P(("seq", "tp"), None),
            P(("seq", "tp"), None),
            P(("seq", "tp")),
            P("seq", "tp"),
            P("seq", "tp"),
            P("seq", "tp"),
        ),
        check_vma=False,
    )
```
